32 devices in a mesh: dp: 2 (over core), row: 4 (over y, x), col: 4 (over z).
Axes of the slice: x: 2, y: 2, z: 4, core: 2. Of those that a mesh axis runs over, the one named last changes fastest.
Arguments:
- block_input: bfloat16 [2048, 1024], P(('dp', 'row', 'col')), may hold values from -6 to 6
- seq_lengths: int32 [2, 5], P('dp'), may hold values from 1 to 512, 1024 in all within a row
- out_grad: bfloat16 [2048, 1024], P(('dp', 'row', 'col')), may hold values from -6 to 6
- attn_norm: float32 [1024], replicated, may hold values from 0.5 to 1.5
- query_weight: bfloat16 [1024, 1024], P('col', 'row'), may hold values from -0.1875 to 0.1875
- key_weight: bfloat16 [1024, 512], P('col', 'row'), may hold values from -0.1875 to 0.1875
- value_weight: bfloat16 [1024, 512], P('col', 'row'), may hold values from -0.1875 to 0.1875
- query_norm: float32 [64], replicated, may hold values from 0.5 to 1.5
- key_norm: float32 [64], replicated, may hold values from 0.5 to 1.5
- out_weight: bfloat16 [1024, 1024], P(('row', 'col')), may hold values from -0.75 to 0.75
- ffn_norm: float32 [1024], replicated, may hold values from 0.5 to 1.5
- gate_weight: bfloat16 [1024, 4608], P('col', 'row'), may hold values from -0.1875 to 0.1875
- up_weight: bfloat16 [1024, 4608], P('col', 'row'), may hold values from -0.1875 to 0.1875
- down_weight: bfloat16 [4608, 1024], P(('row', 'col')), may hold values from -0.09375 to 0.09375
Outputs:
- block_output: bfloat16 [2048, 1024], P(('dp', 'row', 'col'))
- input_grad: float32 [2048, 1024], P(('dp', 'row', 'col'))
- grad_attnnorm: float32 [1024], replicated
- grad_query: float32 [1024, 1024], P('col', 'row')
- grad_key: float32 [1024, 512], P('col', 'row')
- grad_value: float32 [1024, 512], P('col', 'row')
- grad_qnorm: float32 [64], replicated
- grad_knorm: float32 [64], replicated
- grad_outweight: float32 [1024, 1024], P(('row', 'col'))
- grad_ffnnorm: float32 [1024], replicated
- grad_gate: float32 [1024, 4608], P('col', 'row')
- grad_up: float32 [1024, 4608], P('col', 'row')
- grad_down: float32 [4608, 1024], P(('row', 'col'))
The draws below stay inside these ranges and needn't reach their ends.
Inputs may be any that keep to these rules, and one draw needn't show every extreme that they name: Each row of seq_lengths sums to 1024, and its largest entry is exactly 512.
All inputs are finite; a program needn't handle non-finite values.
Results may differ from the reference program's by a relative error of at most 0.012.
The reference program's roundings to bfloat16 on the way count: a program that leaves them out, or rounds other values in their place, can miss the bound.
Values may be sent and summed in bfloat16 or wider, within the bound.
A program may use at most 128 MiB of HBM per device.

```python
import math
import jax
import jax.numpy as jnp
import numpy as np
from jax import lax

D = 1024
H = 16
KV = 8
HD = 64
FF = 4608
MAXLEN = 512
T_DP = 1024
NSEQ = 5
TOKENS = 2048
QD = 1024
KD = 512
N_DP = 2


def block_scale(key, extent, pieces, least, top_value):
    factor_of, own = 1.0, jax.random.fold_in(key, 6)
    for dim, shards_of in pieces:
        draws = jnp.exp(jax.random.uniform(jax.random.fold_in(own, dim), (shards_of,), jnp.float32, least / len(pieces), top_value / len(pieces)))
        factor_of = factor_of * jnp.repeat(draws, extent[dim] // shards_of).reshape([-1 if axis == dim else 1 for axis in range(len(extent))])
    return factor_of


def profile(amount, total, most, slope):
    weights = [(1 << 20) // math.isqrt(grade ** slope) + 1 for grade in range(2, amount + 1)]
    rest, counts = total - most - (amount - 1), [1] * (amount - 1)
    while rest > 0:
        free = [i for i in range(amount - 1) if counts[i] < most]
        pool, remaining = sum([weights[i] for i in free]), rest
        for i in free:
            more = min(most - counts[i], max(1, remaining * weights[i] // pool), rest)
            counts[i] = counts[i] + more
            rest = rest - more
    return np.array([most] + counts)


def uneven_parts(own_key, amount, total, most, lean):
    if amount == 2:
        one = jax.random.randint(own_key, (), max(1, total - most), min(most, total - 1) + 1)
        return jnp.stack([one, total - one])
    tallies = jnp.asarray(profile(amount, total, most, lean), jnp.int32)
    pairs = (amount - 1) // 2
    source_of, receiver = tallies[1:1 + 2 * pairs:2], tallies[2:2 + 2 * pairs:2]
    margin = jnp.minimum(source_of - 1, most - receiver)
    shifted = jax.random.randint(jax.random.fold_in(own_key, 1), (pairs,), 0, 1 << 20) % (margin + 1)
    tallies = tallies.at[1:1 + 2 * pairs:2].set(source_of - shifted).at[2:2 + 2 * pairs:2].set(receiver + shifted)
    return tallies[jax.random.permutation(jax.random.fold_in(own_key, 2), amount)]


def noise(own_key, dims, spread, limit, shards=(), kind=jnp.bfloat16):
    drawn = jax.random.normal(own_key, dims, jnp.float32) * spread
    if len(shards) > 0:
        drawn = block_scale(own_key, dims, shards, -0.22, 0.18) * drawn
    return jnp.clip(drawn, min=-limit, max=limit).astype(kind)


def setup_inputs(seed: int = 0) -> dict:
    keys = jax.random.split(jax.random.key(seed), 15)
    return {
        "block_input": noise(keys[0], (TOKENS, D), 1.0, 6.0, ((0, 32),)),
        "seq_lengths": jax.vmap(lambda own: uneven_parts(own, NSEQ, T_DP, MAXLEN, 2))(jax.random.split(keys[1], N_DP)).reshape((N_DP, NSEQ)).astype(jnp.int32),
        "out_grad": noise(keys[2], (TOKENS, D), 1.0, 6.0, ((0, 32),)),
        "attn_norm": jnp.clip(1.0 + 0.1 * jax.random.normal(keys[3], (D,), jnp.float32), 0.5, 1.5),
        "query_weight": noise(keys[4], (D, QD), D ** -0.5, 0.1875, ((0, 4), (1, 4))),
        "key_weight": noise(keys[5], (D, KD), D ** -0.5, 0.1875, ((0, 4), (1, 4))),
        "value_weight": noise(keys[6], (D, KD), D ** -0.5, 0.1875, ((0, 4), (1, 4))),
        "query_norm": jnp.clip(1.0 + 0.1 * jax.random.normal(keys[7], (HD,), jnp.float32), 0.5, 1.5),
        "key_norm": jnp.clip(1.0 + 0.1 * jax.random.normal(keys[8], (HD,), jnp.float32), 0.5, 1.5),
        "out_weight": noise(keys[9], (QD, D), HD ** -0.5, 0.75, ((0, 16),)),
        "ffn_norm": jnp.clip(1.0 + 0.1 * jax.random.normal(keys[10], (D,), jnp.float32), 0.5, 1.5),
        "gate_weight": noise(keys[11], (D, FF), D ** -0.5, 0.1875, ((0, 4), (1, 4))),
        "up_weight": noise(keys[12], (D, FF), D ** -0.5, 0.1875, ((0, 4), (1, 4))),
        "down_weight": noise(keys[13], (FF, D), FF ** -0.5, 0.09375, ((0, 16),)),
    }


EPSILON = 1e-05
THETA = 1000000.0

def segment_info(seq_lengths, length):
    end_points = jnp.cumsum(seq_lengths).astype(jnp.int32)
    places = jnp.arange(length, dtype=jnp.int32)
    passed = (places[:, None] >= end_points[None, :]).astype(jnp.int32)
    segment = lax.optimization_barrier(jnp.sum(passed, axis=1)).astype(jnp.int32)
    begins = lax.optimization_barrier(jnp.sum(passed * seq_lengths[None, :], axis=1)).astype(jnp.int32)
    return (segment, places - begins)

def rope_tables(position, width):
    half_width = width // 2
    exponent = jnp.arange(half_width, dtype=jnp.float32) * (2.0 / width)
    frequency = jnp.exp(-math.log(THETA) * exponent)
    angles = position.astype(jnp.float32)[:, None] * frequency[None, :]
    return (jnp.cos(angles), jnp.sin(angles))

def rotate(values, cosine, sine):
    half_width = values.shape[-1] // 2
    first_half = values[:, :half_width]
    second_half = values[:, half_width:]
    return jnp.concatenate([first_half * cosine - second_half * sine, second_half * cosine + first_half * sine], axis=1)

def rotate_back(cotangent, cosine, sine):
    half_width = cotangent.shape[-1] // 2
    first_half = cotangent[:, :half_width]
    second_half = cotangent[:, half_width:]
    return jnp.concatenate([first_half * cosine + second_half * sine, second_half * cosine - first_half * sine], axis=1)

def head_norm(values, gain_vec):
    inv_rms = lax.rsqrt(lax.optimization_barrier(jnp.mean(values * values, axis=-1, keepdims=True)) + EPSILON)
    return (values * inv_rms * gain_vec, inv_rms)

def head_norm_back(cotangent, values, inv_rms, gain_vec):
    normed = values * inv_rms
    weighted = cotangent * gain_vec
    gain_grad = lax.optimization_barrier(jnp.sum(cotangent * normed, axis=0))
    inner_mean = lax.optimization_barrier(jnp.mean(weighted * normed, axis=-1, keepdims=True))
    return (inv_rms * (weighted - normed * inner_mean), gain_grad)

def attend(queries, key_rows, value_rows, segment):
    length = queries.shape[0]
    block_rows = min(512, length)
    places = jnp.arange(length, dtype=jnp.int32)
    score_scale = 1.0 / math.sqrt(queries.shape[1])

    def one_block(number):
        offset = number * block_rows
        query_block = lax.dynamic_slice_in_dim(queries, offset, block_rows, 0)
        row_segment = lax.dynamic_slice_in_dim(segment, offset, block_rows, 0)
        row_places = offset + jnp.arange(block_rows, dtype=jnp.int32)
        allowed = (row_segment[:, None] == segment[None, :]) & (places[None, :] <= row_places[:, None])
        scores = jnp.dot(query_block, key_rows.T, preferred_element_type=jnp.float32) * score_scale
        exponent = jnp.where(allowed, jnp.exp(scores), 0.0)
        log_total = jnp.log(lax.optimization_barrier(jnp.sum(exponent, axis=1)))
        probability = jnp.where(allowed, jnp.exp(scores - log_total[:, None]), 0.0).astype(jnp.bfloat16)
        output = jnp.dot(probability, value_rows, preferred_element_type=jnp.float32)
        return (output, log_total)
    outputs, totals = lax.map(one_block, jnp.arange(length // block_rows, dtype=jnp.int32))
    return (outputs.reshape(length, -1), totals.reshape(length))

def attend_back(queries, key_rows, value_rows, segment, output_rows, out_grads, log_total):
    length = queries.shape[0]
    block_rows = min(512, length)
    places = jnp.arange(length, dtype=jnp.int32)
    score_scale = 1.0 / math.sqrt(queries.shape[1])

    def one_block(carried, number):
        key_total, value_total = carried
        offset = number * block_rows
        query_block = lax.dynamic_slice_in_dim(queries, offset, block_rows, 0)
        row_segment = lax.dynamic_slice_in_dim(segment, offset, block_rows, 0)
        grad_block = lax.dynamic_slice_in_dim(out_grads, offset, block_rows, 0)
        out_block = lax.dynamic_slice_in_dim(output_rows, offset, block_rows, 0)
        total_block = lax.dynamic_slice_in_dim(log_total, offset, block_rows, 0)
        row_places = offset + jnp.arange(block_rows, dtype=jnp.int32)
        allowed = (row_segment[:, None] == segment[None, :]) & (places[None, :] <= row_places[:, None])
        scores = jnp.dot(query_block, key_rows.T, preferred_element_type=jnp.float32) * score_scale
        probability = jnp.where(allowed, jnp.exp(scores - total_block[:, None]), 0.0).astype(jnp.bfloat16)
        value_total = value_total + jnp.dot(probability.T, grad_block, preferred_element_type=jnp.float32)
        prob_grad = jnp.dot(grad_block, value_rows.T, preferred_element_type=jnp.float32)
        row_delta = lax.optimization_barrier(jnp.sum(grad_block.astype(jnp.float32) * out_block.astype(jnp.float32), axis=1, keepdims=True))
        score_grad = (score_scale * probability.astype(jnp.float32) * (prob_grad - row_delta)).astype(jnp.bfloat16)
        query_grad = jnp.dot(score_grad, key_rows, preferred_element_type=jnp.float32)
        key_total = key_total + jnp.dot(score_grad.T, query_block, preferred_element_type=jnp.float32)
        return ((key_total, value_total), query_grad)
    zero_rows = jnp.zeros((length, queries.shape[1]), jnp.float32)
    (key_grad, value_grad), query_grads = lax.scan(one_block, (zero_rows, zero_rows), jnp.arange(length // block_rows, dtype=jnp.int32))
    return (query_grads.reshape(length, -1), key_grad, value_grad)

def head_inputs(query_raw, key_raw, value_raw, query_norm, key_norm, cosine, sine):
    query_normed, query_scale = head_norm(query_raw, query_norm)
    key_normed, key_scale = head_norm(key_raw, key_norm)
    query_rot = rotate(query_normed, cosine, sine).astype(jnp.bfloat16)
    key_rot = rotate(key_normed, cosine, sine).astype(jnp.bfloat16)
    return (query_rot, key_rot, value_raw.astype(jnp.bfloat16), query_scale, key_scale)

def head_forward(query_raw, key_raw, value_raw, query_norm, key_norm, cosine, sine, segment):
    query_rot, key_rot, value_low, query_scale, key_scale = head_inputs(query_raw, key_raw, value_raw, query_norm, key_norm, cosine, sine)
    output, log_total = attend(query_rot, key_rot, value_low, segment)
    return (output.astype(jnp.bfloat16), log_total)

def head_backward(query_raw, key_raw, value_raw, query_norm, key_norm, cosine, sine, segment, attn_low, cat_grad, log_total):
    query_rot, key_rot, value_low, query_scale, key_scale = head_inputs(query_raw, key_raw, value_raw, query_norm, key_norm, cosine, sine)
    query_grad, key_grad, value_grad = attend_back(query_rot, key_rot, value_low, segment, attn_low, cat_grad, log_total)
    query_pre, query_gain = head_norm_back(rotate_back(query_grad, cosine, sine), query_raw, query_scale, query_norm)
    key_pre, key_gain = head_norm_back(rotate_back(key_grad, cosine, sine), key_raw, key_scale, key_norm)
    return (query_pre.astype(jnp.bfloat16), key_pre.astype(jnp.bfloat16), value_grad.astype(jnp.bfloat16), query_gain, key_gain)

def group_pass(group_input, group_lengths, group_grad, attn_norm, query_weight, key_weight, value_weight, query_norm, key_norm, out_weight, ffn_norm, gate_weight, up_weight, down_weight):
    length = group_input.shape[0]
    segment, position = segment_info(group_lengths, length)
    cosine, sine = rope_tables(position, HD)
    residual = group_input.astype(jnp.float32)
    normed_in, scale_in = head_norm(residual, attn_norm)
    first_act = normed_in.astype(jnp.bfloat16)
    query_all = jnp.dot(first_act, query_weight, preferred_element_type=jnp.float32).reshape(length, H, HD).transpose(1, 0, 2)
    key_all = jnp.dot(first_act, key_weight, preferred_element_type=jnp.float32).reshape(length, KV, HD).transpose(1, 0, 2)
    value_all = jnp.dot(first_act, value_weight, preferred_element_type=jnp.float32).reshape(length, KV, HD).transpose(1, 0, 2)
    key_rep = jnp.repeat(key_all, 2, axis=0)
    value_rep = jnp.repeat(value_all, 2, axis=0)

    def forward_head(head_item):
        return head_forward(head_item[0], head_item[1], head_item[2], query_norm, key_norm, cosine, sine, segment)
    attn_heads, log_totals = lax.map(forward_head, (query_all, key_rep, value_rep))
    attn_cat = attn_heads.transpose(1, 0, 2).reshape(length, H * HD)
    middle = residual + jnp.dot(attn_cat, out_weight, preferred_element_type=jnp.float32)
    normed_mid, scale_mid = head_norm(middle, ffn_norm)
    second_act = normed_mid.astype(jnp.bfloat16)
    gating = jnp.dot(second_act, gate_weight, preferred_element_type=jnp.float32)
    upward = jnp.dot(second_act, up_weight, preferred_element_type=jnp.float32)
    sigmoid_gate = jax.nn.sigmoid(gating)
    activated = gating * sigmoid_gate
    hidden = (activated * upward).astype(jnp.bfloat16)
    result_sum = middle + jnp.dot(hidden, down_weight, preferred_element_type=jnp.float32)
    group_output = result_sum.astype(jnp.bfloat16)
    grad_down = jnp.dot(hidden.T, group_grad, preferred_element_type=jnp.float32)
    hidden_grad = jnp.dot(group_grad, down_weight.T, preferred_element_type=jnp.float32)
    gate_low = (hidden_grad * upward * sigmoid_gate * (1.0 + gating * (1.0 - sigmoid_gate))).astype(jnp.bfloat16)
    up_low = (hidden_grad * activated).astype(jnp.bfloat16)
    grad_gate = jnp.dot(second_act.T, gate_low, preferred_element_type=jnp.float32)
    grad_up = jnp.dot(second_act.T, up_low, preferred_element_type=jnp.float32)
    act_grad2 = jnp.dot(gate_low, gate_weight.T, preferred_element_type=jnp.float32) + jnp.dot(up_low, up_weight.T, preferred_element_type=jnp.float32)
    middle_back, ffn_gain_grad = head_norm_back(act_grad2, middle, scale_mid, ffn_norm)
    middle_grad = group_grad.astype(jnp.float32) + middle_back
    middle_low = middle_grad.astype(jnp.bfloat16)
    grad_outweight = jnp.dot(attn_cat.T, middle_low, preferred_element_type=jnp.float32)
    cat_grad = jnp.dot(middle_low, out_weight.T, preferred_element_type=jnp.float32).astype(jnp.bfloat16)
    cat_heads = cat_grad.reshape(length, H, HD).transpose(1, 0, 2)

    def backward_head(head_item):
        return head_backward(head_item[0], head_item[1], head_item[2], query_norm, key_norm, cosine, sine, segment, head_item[3], head_item[4], head_item[5])
    query_low, key_low, value_low, query_gains, key_gains = lax.map(backward_head, (query_all, key_rep, value_rep, attn_heads, cat_heads, log_totals))
    query_cat = query_low.transpose(1, 0, 2).reshape(length, H * HD)
    key_even = key_low[0::2].transpose(1, 0, 2).reshape(length, KV * HD)
    key_odd = key_low[1::2].transpose(1, 0, 2).reshape(length, KV * HD)
    value_even = value_low[0::2].transpose(1, 0, 2).reshape(length, KV * HD)
    value_odd = value_low[1::2].transpose(1, 0, 2).reshape(length, KV * HD)
    grad_query = jnp.dot(first_act.T, query_cat, preferred_element_type=jnp.float32)
    grad_key = jnp.dot(first_act.T, key_even, preferred_element_type=jnp.float32) + jnp.dot(first_act.T, key_odd, preferred_element_type=jnp.float32)
    grad_value = jnp.dot(first_act.T, value_even, preferred_element_type=jnp.float32) + jnp.dot(first_act.T, value_odd, preferred_element_type=jnp.float32)
    act_grad1 = jnp.dot(query_cat, query_weight.T, preferred_element_type=jnp.float32)
    act_grad1 = act_grad1 + jnp.dot(key_even, key_weight.T, preferred_element_type=jnp.float32) + jnp.dot(key_odd, key_weight.T, preferred_element_type=jnp.float32)
    act_grad1 = act_grad1 + jnp.dot(value_even, value_weight.T, preferred_element_type=jnp.float32) + jnp.dot(value_odd, value_weight.T, preferred_element_type=jnp.float32)
    input_back, attn_gain_grad = head_norm_back(act_grad1, residual, scale_in, attn_norm)
    input_grad = middle_grad + input_back
    gradients = (attn_gain_grad, grad_query, grad_key, grad_value, lax.optimization_barrier(jnp.sum(query_gains, axis=0)), lax.optimization_barrier(jnp.sum(key_gains, axis=0)), grad_outweight, ffn_gain_grad, grad_gate, grad_up, grad_down)
    return (group_output, input_grad, gradients)

def reference(block_input, seq_lengths, out_grad, attn_norm, query_weight, key_weight, value_weight, query_norm, key_norm, out_weight, ffn_norm, gate_weight, up_weight, down_weight):
    groups = seq_lengths.shape[0]
    width = block_input.shape[1]
    inputs = block_input.reshape(groups, -1, width)
    cotangents = out_grad.reshape(groups, -1, width)
    weights = (attn_norm, query_weight, key_weight, value_weight, query_norm, key_norm, out_weight, ffn_norm, gate_weight, up_weight, down_weight)
    zero_grads = tuple((jnp.zeros(weight_item.shape, jnp.float32) for weight_item in weights))

    def scan_step(carried, group_item):
        group_output, input_grad, gradients = group_pass(group_item[0], group_item[1], group_item[2], attn_norm, query_weight, key_weight, value_weight, query_norm, key_norm, out_weight, ffn_norm, gate_weight, up_weight, down_weight)
        summed = tuple((carried_item + grad_item for carried_item, grad_item in zip(carried, gradients)))
        return (summed, (group_output, input_grad))
    totals, (outputs, input_grads) = lax.scan(scan_step, zero_grads, (inputs, seq_lengths, cotangents))
    return (outputs.reshape(-1, width), input_grads.reshape(-1, width), totals[0], totals[1], totals[2], totals[3], totals[4], totals[5], totals[6], totals[7], totals[8], totals[9], totals[10])
```

```python
import functools
import math

import jax
import jax.numpy as jnp
from jax import lax
from jax.experimental import pallas as pl
from jax.experimental.pallas import tpu as pltpu
from jax.sharding import PartitionSpec as P

EPSILON = 1e-05
THETA = 1000000.0


def segment_info(seq_lengths, length):
    order = jnp.arange(seq_lengths.shape[0], dtype=jnp.int32)
    up_to = order[:, None] <= order[None, :]
    end_points = jnp.sum(jnp.where(up_to, seq_lengths[:, None], 0), axis=0)
    places = jnp.arange(length, dtype=jnp.int32)
    passed = (places[:, None] >= end_points[None, :]).astype(jnp.int32)
    segment = jnp.sum(passed, axis=1)
    begins = jnp.sum(passed * seq_lengths[None, :], axis=1)
    return (segment, places - begins)


def rope_tables(position, width):
    half_width = width // 2
    exponent = jnp.arange(half_width, dtype=jnp.float32) * (2.0 / width)
    frequency = jnp.exp(-math.log(THETA) * exponent)
    angles = position.astype(jnp.float32)[:, None] * frequency[None, :]
    return (jnp.cos(angles), jnp.sin(angles))


def head_norm(values, gain_vec):
    inv_rms = lax.rsqrt(jnp.mean(values * values, axis=-1, keepdims=True) + EPSILON)
    return (values * inv_rms * gain_vec, inv_rms)


def head_norm_back(cotangent, values, inv_rms, gain_vec):
    normed = values * inv_rms
    weighted = cotangent * gain_vec
    gain_grad = jnp.sum(cotangent * normed, axis=0)
    inner_mean = jnp.mean(weighted * normed, axis=-1, keepdims=True)
    return (inv_rms * (weighted - normed * inner_mean), gain_grad)


def swap_halves(values):
    half_width = values.shape[-1] // 2
    return jnp.concatenate([values[:, half_width:], values[:, :half_width]], axis=1)


def block_probability(query_block, key_rows, begins, offset, low, shift):
    score_scale = 1.0 / math.sqrt(query_block.shape[1])
    scores = dot(query_block, key_rows, 1, 1) * score_scale
    places = low + lax.broadcasted_iota(jnp.int32, scores.shape, 1)
    row_places = offset + lax.broadcasted_iota(jnp.int32, scores.shape, 0)
    allowed = (places >= begins) & (places <= row_places)
    if shift is None:
        shift = jnp.log(jnp.sum(jnp.where(allowed, jnp.exp(scores), 0.0), axis=1, keepdims=True))
    probability = jnp.where(allowed, jnp.exp(scores - shift), 0.0).astype(jnp.bfloat16)
    return probability, shift


def spans(length, longest):
    block = min(256, length)
    return [
        (offset, max(0, (offset - longest) // 128 * 128), block)
        for offset in range(0, length, block)
    ]


def attend_kernel(longest, sums, gains, cosine, sine, begins, *outs):
    query_rot, key_rot, value_low, low_rows, low_cols, totals = outs
    length, head_dim = query_rot.shape
    for place, target in ((0, query_rot), (1, key_rot)):
        normed = head_norm(
            sums[:, place * head_dim : (place + 1) * head_dim], gains[place : place + 1, :]
        )[0]
        target[...] = (normed * cosine[...] + swap_halves(normed) * sine[...]).astype(jnp.bfloat16)
    value_low[...] = sums[:, 2 * head_dim : 3 * head_dim].astype(jnp.bfloat16)
    for offset, low, block in spans(length, longest):
        rows, keys = slice(offset, offset + block), slice(low, offset + block)
        probability, total = block_probability(
            query_rot[rows, :], key_rot[keys, :], begins[rows, :], offset, low, None
        )
        totals[rows, :] = total
        low_rows[rows, :] = dot(probability, value_low[keys, :]).astype(jnp.bfloat16)
        low_cols[:, rows] = dot(value_low[keys, :], probability, 0, 1).astype(jnp.bfloat16)


def attend_back_kernel(longest, *refs):
    query_rot, key_rot, value_low, low_rows, totals, grads = refs[:6]
    sums, gains, cosine, sine, begins = refs[6:11]
    slot, gain_out, query_acc, key_acc, value_acc = refs[11:]
    length, head_dim = query_rot.shape
    score_scale = 1.0 / math.sqrt(head_dim)
    key_acc[...] = jnp.zeros_like(key_acc)
    value_acc[...] = jnp.zeros_like(value_acc)
    for offset, low, block in spans(length, longest):
        rows, keys = slice(offset, offset + block), slice(low, offset + block)
        probability, _ = block_probability(
            query_rot[rows, :], key_rot[keys, :], begins[rows, :], offset, low, totals[rows, :]
        )
        grad_block = grads[rows, :]
        value_acc[keys, :] += dot(probability, grad_block, 0, 0)
        row_delta = jnp.sum(
            grad_block.astype(jnp.float32) * low_rows[rows, :].astype(jnp.float32),
            axis=1,
            keepdims=True,
        )
        prob_grad = dot(grad_block, value_low[keys, :], 1, 1)
        score_grad = (
            score_scale * probability.astype(jnp.float32) * (prob_grad - row_delta)
        ).astype(jnp.bfloat16)
        query_acc[rows, :] = dot(score_grad, key_rot[keys, :])
        key_acc[keys, :] += dot(score_grad, query_rot[rows, :], 0, 0)
    parts = []
    for place, source in ((0, query_acc), (1, key_acc)):
        raw = sums[:, place * head_dim : (place + 1) * head_dim]
        gain = gains[place : place + 1, :]
        inv_rms = head_norm(raw, gain)[1]
        cotangent = source[...] * cosine[...] - swap_halves(source[...]) * sine[...]
        low_part, gain_grad = head_norm_back(cotangent, raw, inv_rms, gain)
        parts.append(low_part.astype(jnp.bfloat16))
        gain_out[place : place + 1, :] = gain_grad[None, :]
    parts.append(value_acc[...].astype(jnp.bfloat16))
    for place in range(3):
        slot[:, place * head_dim : (place + 1) * head_dim] = parts[place]


def local_kernel(body, args, outs, scratch=()):
    vmem = pl.BlockSpec(memory_space=pltpu.VMEM)
    return pl.pallas_call(
        body,
        out_shape=outs,
        in_specs=[vmem] * len(args),
        out_specs=[vmem] * len(outs),
        scratch_shapes=list(scratch),
    )(*args)


def pack_slots_kernel(cols, head_dim, query, key, value, out):
    for col in range(cols):
        half = col // 2
        out[col, :, :head_dim] = query[:, col * head_dim : (col + 1) * head_dim]
        for place, source in ((1, key), (2, value)):
            out[col, :, place * head_dim : (place + 1) * head_dim] = source[
                :, half * head_dim : (half + 1) * head_dim
            ]


def pack_wide_kernel(cols, gate, up, out):
    part = gate.shape[1] // cols
    for col in range(cols):
        out[col, :, :part] = gate[:, col * part : (col + 1) * part]
        out[col, :, part:] = up[:, col * part : (col + 1) * part]


def open_wide_kernel(cols, wide, gate, up):
    part = gate.shape[1] // cols
    for col in range(cols):
        gate[:, col * part : (col + 1) * part] = wide[col, :, :part].astype(jnp.float32)
        up[:, col * part : (col + 1) * part] = wide[col, :, part:].astype(jnp.float32)


def open_slots_kernel(cols, head_dim, slots, out):
    for col in range(cols):
        out[:, col * head_dim : (col + 1) * head_dim] = slots[col, :, :head_dim].astype(jnp.float32)
    for half in range(cols // 2):
        for place in (1, 2):
            lanes = slice(place * head_dim, (place + 1) * head_dim)
            begin = (cols + (place - 1) * (cols // 2) + half) * head_dim
            out[:, begin : begin + head_dim] = slots[2 * half, :, lanes].astype(
                jnp.float32
            ) + slots[2 * half + 1, :, lanes].astype(jnp.float32)


MESH = pl.DeviceIdType.MESH


def enter(axes):
    barrier = pltpu.get_barrier_semaphore()
    count = 0
    for axis in axes:
        size, own = lax.axis_size(axis), lax.axis_index(axis)
        for step in range(1, size):
            pl.semaphore_signal(
                barrier, inc=1, device_id={axis: lax.rem(own + step, size)}, device_id_type=MESH
            )
        count += size - 1
    pl.semaphore_wait(barrier, count)


def send(source, target, sems, place, axis, index):
    copy = pltpu.make_async_remote_copy(
        src_ref=source,
        dst_ref=target,
        send_sem=sems[0].at[place],
        recv_sem=sems[1].at[place],
        device_id={axis: index},
        device_id_type=MESH,
    )
    copy.start()
    return copy


def start_swaps(ins, outs, sems):
    cols, own = lax.axis_size("col"), lax.axis_index("col")
    copies = []
    for number in range(len(ins)):
        for step in range(1, cols):
            peer = lax.rem(own + step, cols)
            copies.append(
                send(ins[number].at[peer], outs[number].at[own], sems, (number, step), "col", peer)
            )
        outs[number][own] = ins[number][own]
    return copies


def call_kernel(body, args, outs, scratch, number):
    vmem = pl.BlockSpec(memory_space=pltpu.VMEM)
    return pl.pallas_call(
        body,
        out_shape=outs,
        in_specs=[vmem] * len(args),
        out_specs=[vmem] * len(outs),
        scratch_shapes=scratch,
        compiler_params=pltpu.CompilerParams(collective_id=number, has_side_effects=True),
    )(*args)


def dma(*shape):
    return [pltpu.SemaphoreType.DMA(shape), pltpu.SemaphoreType.DMA(shape)]


def exchange(gathers, swaps, number):
    rows, cols = lax.axis_size("row"), lax.axis_size("col")
    many, total = len(gathers), len(gathers) + len(swaps)

    def body(*refs):
        ins, outs = refs[:total], refs[total : 2 * total]
        sems, swap_sems = refs[2 * total : 2 * total + 2], refs[2 * total + 2 :]
        row, col = lax.axis_index("row"), lax.axis_index("col")
        enter(("row", "col"))
        across, copies = {}, []
        for item in range(many):
            for step in range(1, cols):
                across[item, step] = send(
                    ins[item],
                    outs[item].at[row, col],
                    sems,
                    (item, 0, step),
                    "col",
                    lax.rem(col + step, cols),
                )
        for item in range(many):
            for turn in range(1, rows):
                copies.append(
                    send(
                        ins[item],
                        outs[item].at[row, col],
                        sems,
                        (item, turn, 0),
                        "row",
                        lax.rem(row + turn, rows),
                    )
                )
        copies += start_swaps(ins[many:], outs[many:], swap_sems)
        for item in range(many):
            outs[item][row, col] = ins[item][...]
        for step in range(1, cols):
            origin = lax.rem(col + cols - step, cols)
            for item in range(many):
                across[item, step].wait()
                block = outs[item].at[row, origin]
                for turn in range(1, rows):
                    copies.append(
                        send(
                            block,
                            block,
                            sems,
                            (item, turn, step),
                            "row",
                            lax.rem(row + turn, rows),
                        )
                    )
        for copy in copies:
            copy.wait()

    outs = [jax.ShapeDtypeStruct((rows, cols) + g.shape, g.dtype) for g in gathers]
    outs += [jax.ShapeDtypeStruct(w.shape, w.dtype) for w in swaps]
    scratch = dma(many, rows, cols) + dma(max(len(swaps), 1), cols)
    return call_kernel(body, list(gathers) + list(swaps), outs, scratch, number)


def reduce_rows(partial_value, swaps, number):
    rows, cols = lax.axis_size("row"), lax.axis_size("col")
    local = partial_value.shape[0] // (rows * cols)
    width = partial_value.shape[1]
    shaped = partial_value.astype(jnp.bfloat16).reshape(rows, cols, local, width)
    many = len(swaps)

    def body(*refs):
        part, ins = refs[0], refs[1 : 1 + many]
        result, outs = refs[1 + many], refs[2 + many : 2 + 2 * many]
        first, staged, second = refs[2 + 2 * many : 5 + 2 * many]
        first_sems, second_sems = refs[5 + 2 * many : 7 + 2 * many], refs[7 + 2 * many : 9 + 2 * many]
        swap_sems = refs[9 + 2 * many :]
        row, col = lax.axis_index("row"), lax.axis_index("col")
        enter(("row", "col"))
        down, across = {}, []
        order = list(range(1, cols)) + [0]
        for step in order:
            block = lax.rem(col + step, cols)
            for turn in range(1, rows):
                peer = lax.rem(row + turn, rows)
                down[step, turn] = send(
                    part.at[peer, block],
                    first.at[turn, step],
                    first_sems,
                    (turn, step),
                    "row",
                    peer,
                )
        copies = start_swaps(ins, outs, swap_sems)
        for step in order:
            block = lax.rem(col + step, cols)
            summed = part[row, block].astype(jnp.float32)
            for turn in range(1, rows):
                down[step, turn].wait()
                summed = summed + first[turn, step].astype(jnp.float32)
            if step == 0:
                result[...] = summed
            else:
                staged[step] = summed.astype(jnp.bfloat16)
                across.append(
                    send(staged.at[step], second.at[step], second_sems, (step,), "col", block)
                )
        for step in range(1, cols):
            across[step - 1].wait()
            result[...] += second[step].astype(jnp.float32)
        for copy in copies:
            copy.wait()

    outs = [jax.ShapeDtypeStruct((local, width), jnp.float32)]
    outs += [jax.ShapeDtypeStruct(w.shape, w.dtype) for w in swaps]
    scratch = [
        pltpu.VMEM((rows, cols, local, width), jnp.bfloat16),
        pltpu.VMEM((cols, local, width), jnp.bfloat16),
        pltpu.VMEM((cols, local, width), jnp.bfloat16),
    ]
    scratch += dma(rows, cols) + dma(cols) + dma(max(many, 1), cols)
    return call_kernel(body, [shaped] + list(swaps), outs, scratch, number)


def last_sums(group_value, widths, gains, number):
    sizes = [lax.axis_size(axis) for axis in ("dp", "row", "col")]

    def body(value, gain, *refs):
        value_outs, gain_out = refs[: len(widths)], refs[len(widths)]
        value_in, landed, held = refs[len(widths) + 1 : len(widths) + 4]
        sems = refs[len(widths) + 4 :]
        value_sems, gain_sems = sems[:2], sems[2:]
        enter(("dp", "row", "col"))
        copies, groups = [], lax.axis_size("dp")
        me = lax.axis_index("dp")
        for step in range(1, groups):
            copies.append(
                send(
                    value,
                    value_in.at[step],
                    value_sems,
                    (step,),
                    "dp",
                    lax.rem(me + step, groups),
                )
            )
        held[0] = gain[...]
        for stage, axis in enumerate(("dp", "row", "col")):
            size, own = lax.axis_size(axis), lax.axis_index(axis)
            sent = [
                send(
                    held.at[stage],
                    landed.at[stage, step],
                    gain_sems,
                    (stage, step),
                    axis,
                    lax.rem(own + step, size),
                )
                for step in range(1, size)
            ]
            landed[stage, 0] = held[stage]
            for copy in sent:
                copy.wait()
            total = None
            for place in range(size):
                term = landed[stage, lax.rem(own - place + size, size)]
                total = term if total is None else total + term
            held[stage + 1] = total
        gain_out[...] = held[3]
        for copy in copies:
            copy.wait()
        total = value[...]
        for step in range(1, groups):
            total = total + value_in[step]
        begin = 0
        for size, value_out in zip(widths, value_outs):
            value_out[...] = total[:, begin : begin + size]
            begin += size

    outs = [jax.ShapeDtypeStruct((group_value.shape[0], size), jnp.float32) for size in widths]
    outs.append(jax.ShapeDtypeStruct(gains.shape, jnp.float32))
    scratch = [
        pltpu.VMEM((sizes[0],) + group_value.shape, jnp.float32),
        pltpu.VMEM((3, max(sizes)) + gains.shape, jnp.float32),
        pltpu.VMEM((4,) + gains.shape, jnp.float32),
    ]
    scratch += dma(sizes[0]) + dma(3, max(sizes))
    return call_kernel(body, [group_value, gains], outs, scratch, number)


def dot(left, right, left_dim=1, right_dim=0):
    return lax.dot_general(
        left,
        right,
        (((left_dim,), (right_dim,)), ((), ())),
        preferred_element_type=jnp.float32,
    )


def shards(
    block_input,
    seq_lengths,
    out_grad,
    attn_norm,
    query_weight,
    key_weight,
    value_weight,
    query_norm,
    key_norm,
    out_weight,
    ffn_norm,
    gate_weight,
    up_weight,
    down_weight,
):
    local_rows, width = block_input.shape
    head_dim = query_norm.shape[0]
    col_width = query_weight.shape[0]
    cols = lax.axis_size("col")
    length = local_rows * cols * lax.axis_size("row")
    place = (lax.axis_index("row") * cols + lax.axis_index("col")) * local_rows

    def own_rows(values):
        return lax.dynamic_slice_in_dim(values, place, local_rows, 0)

    out_weight_full = lax.all_gather(out_weight, ("row", "col"), axis=0, tiled=True)

    hidden_width = gate_weight.shape[1] // cols
    (slots,) = local_kernel(
        functools.partial(pack_slots_kernel, cols, head_dim),
        [query_weight, key_weight, value_weight],
        [jax.ShapeDtypeStruct((cols, col_width, 3 * head_dim), jnp.bfloat16)],
    )
    (wide,) = local_kernel(
        functools.partial(pack_wide_kernel, cols),
        [gate_weight, up_weight],
        [jax.ShapeDtypeStruct((cols, col_width, 2 * hidden_width), jnp.bfloat16)],
    )

    input_blocks, slot_blocks = exchange([block_input], [slots], 0)
    input_full = input_blocks.reshape(length, width).astype(jnp.float32)
    slot_weight = slot_blocks.reshape(width, 3 * head_dim)
    first_full = head_norm(input_full, attn_norm)[0].astype(jnp.bfloat16)
    residual = block_input.astype(jnp.float32)
    scale_in = head_norm(residual, attn_norm)[1]
    places = jnp.arange(length, dtype=jnp.int32)
    position = segment_info(seq_lengths[0], length)[1]
    begins = (places - position)[:, None]
    cosine, sine = rope_tables(position, head_dim)
    cosine = jnp.concatenate([cosine, cosine], axis=1)
    sine = jnp.concatenate([-sine, sine], axis=1)
    own_sums = dot(first_full, slot_weight)
    longest = length // 2
    head_gains = jnp.stack([query_norm, key_norm])
    row_shape = jax.ShapeDtypeStruct((length, head_dim), jnp.bfloat16)
    query_rot, key_rot, value_low, attn_low, attn_cols, log_total = local_kernel(
        functools.partial(attend_kernel, longest),
        [own_sums, head_gains, cosine, sine, begins],
        [
            row_shape,
            row_shape,
            row_shape,
            row_shape,
            jax.ShapeDtypeStruct((head_dim, length), jnp.bfloat16),
            jax.ShapeDtypeStruct((length, 1), jnp.float32),
        ],
    )
    cat_blocks, out_blocks, wide_blocks = exchange([attn_cols, out_grad], [wide], 1)
    out_full = out_blocks.reshape(length, width)
    cat_full = cat_blocks.reshape(width, length)
    wide_weight = wide_blocks.reshape(width, 2 * hidden_width)
    middle = input_full + dot(cat_full, out_weight_full, 0, 0)
    normed_mid, scale_mid = head_norm(middle, ffn_norm)
    second_full = normed_mid.astype(jnp.bfloat16)
    wide_sums = dot(second_full, wide_weight)
    gating, upward = wide_sums[:, :hidden_width], wide_sums[:, hidden_width:]
    sigmoid_gate = jax.nn.sigmoid(gating)
    activated = gating * sigmoid_gate
    hidden = (activated * upward).astype(jnp.bfloat16)
    hidden_grad = dot(out_full, down_weight, 1, 1)
    gate_low = (hidden_grad * upward * sigmoid_gate * (1.0 + gating * (1.0 - sigmoid_gate))).astype(
        jnp.bfloat16
    )
    up_low = (hidden_grad * activated).astype(jnp.bfloat16)
    wide_low = jnp.concatenate([gate_low, up_low], axis=1)
    both_parts = [
        dot(wide_low, wide_weight, 1, 1).astype(jnp.bfloat16),
        dot(hidden, down_weight).astype(jnp.bfloat16),
    ]
    (both_sums,) = reduce_rows(jnp.concatenate(both_parts, axis=1), [], 2)
    act_grad2, down_sums = both_sums[:, :width], both_sums[:, width:]
    middle_own = own_rows(middle)
    grad_down = dot(hidden, out_full, 0, 0)
    wide_grad = dot(second_full, wide_low, 0, 0).astype(jnp.bfloat16)
    middle_back, ffn_gain_grad = head_norm_back(
        act_grad2, middle_own, own_rows(scale_mid), ffn_norm
    )
    middle_grad = out_grad.astype(jnp.float32) + middle_back
    middle_blocks, wide_grads = exchange(
        [middle_grad.astype(jnp.bfloat16)],
        [wide_grad.reshape(cols, col_width, 2 * hidden_width)],
        3,
    )
    middle_full = middle_blocks.reshape(length, width)
    grad_outweight = dot(attn_low, middle_full, 0, 0)
    cat_grad = dot(middle_full, out_weight, 1, 1).astype(jnp.bfloat16)
    wide_shape = jax.ShapeDtypeStruct(gate_weight.shape, jnp.float32)
    grad_gate, grad_up = local_kernel(
        functools.partial(open_wide_kernel, cols), [wide_grads], [wide_shape, wide_shape]
    )
    block_output = (middle_own + down_sums).astype(jnp.bfloat16)
    accumulator = pltpu.VMEM((length, head_dim), jnp.float32)
    own_slot, head_gain_grads = local_kernel(
        functools.partial(attend_back_kernel, longest),
        [query_rot, key_rot, value_low, attn_low, log_total, cat_grad]
        + [own_sums, head_gains, cosine, sine, begins],
        [
            jax.ShapeDtypeStruct((length, 3 * head_dim), jnp.bfloat16),
            jax.ShapeDtypeStruct((2, head_dim), jnp.float32),
        ],
        [accumulator] * 3,
    )
    grad_outweight, grad_gate, grad_up, grad_down = lax.psum(
        (grad_outweight, grad_gate, grad_up, grad_down), "dp"
    )
    slot_grad = dot(first_full, own_slot, 0, 0).astype(jnp.bfloat16)
    act_grad1, slot_grads = reduce_rows(
        dot(own_slot, slot_weight, 1, 1),
        [slot_grad.reshape(cols, col_width, 3 * head_dim)],
        4,
    )
    widths = (cols * head_dim, cols // 2 * head_dim, cols // 2 * head_dim)
    (slot_sums,) = local_kernel(
        functools.partial(open_slots_kernel, cols, head_dim),
        [slot_grads],
        [jax.ShapeDtypeStruct((col_width, sum(widths)), jnp.float32)],
    )
    input_back, attn_gain_grad = head_norm_back(act_grad1, residual, scale_in, attn_norm)
    input_grad = middle_grad + input_back
    flat_gains = jnp.concatenate(
        [head_gain_grads.reshape(-1), jnp.zeros((width - 2 * head_dim,), jnp.float32)]
    )
    gains = jnp.stack([attn_gain_grad, ffn_gain_grad, flat_gains])
    gains = jnp.concatenate([gains, jnp.zeros((5, width), jnp.float32)], axis=0)
    grad_query, grad_key, grad_value, gain_sums = last_sums(slot_sums, widths, gains, 5)
    return (
        block_output,
        input_grad,
        gain_sums[0],
        grad_query,
        grad_key,
        grad_value,
        gain_sums[2, :head_dim],
        gain_sums[2, head_dim : 2 * head_dim],
        grad_outweight,
        gain_sums[1],
        grad_gate,
        grad_up,
        grad_down,
    )


def solution(mesh):
    placed = (
        P(("dp", "row", "col"), None),
        P("dp", None),
        P(("dp", "row", "col"), None),
        P(),
        P("col", "row"),
        P("col", "row"),
        P("col", "row"),
        P(),
        P(),
        P(("row", "col"), None),
        P(),
        P("col", "row"),
        P("col", "row"),
        P(("row", "col"), None),
    )
    return jax.shard_map(
        shards,
        mesh=mesh,
        in_specs=placed,
        out_specs=(
            P(("dp", "row", "col"), None),
            P(("dp", "row", "col"), None),
            P(),
            P("col", "row"),
            P("col", "row"),
            P("col", "row"),
            P(),
            P(),
            P(("row", "col"), None),
            P(),
            P("col", "row"),
            P("col", "row"),
            P(("row", "col"), None),
        ),
        check_vma=False,
    )
```

```python
import functools
import math

import jax
import jax.numpy as jnp
from jax import lax
from jax.experimental import pallas as pl
from jax.experimental.pallas import tpu as pltpu
from jax.sharding import PartitionSpec as P

EPSILON = 1e-05
THETA = 1000000.0


def segment_info(seq_lengths, length):
    order = jnp.arange(seq_lengths.shape[0], dtype=jnp.int32)
    up_to = order[:, None] <= order[None, :]
    end_points = jnp.sum(jnp.where(up_to, seq_lengths[:, None], 0), axis=0)
    places = jnp.arange(length, dtype=jnp.int32)
    passed = (places[:, None] >= end_points[None, :]).astype(jnp.int32)
    segment = jnp.sum(passed, axis=1)
    begins = jnp.sum(passed * seq_lengths[None, :], axis=1)
    return (segment, places - begins)


def rope_tables(position, width):
    half_width = width // 2
    exponent = jnp.arange(half_width, dtype=jnp.float32) * (2.0 / width)
    frequency = jnp.exp(-math.log(THETA) * exponent)
    angles = position.astype(jnp.float32)[:, None] * frequency[None, :]
    return (jnp.cos(angles), jnp.sin(angles))


def head_norm(values, gain_vec):
    inv_rms = lax.rsqrt(jnp.mean(values * values, axis=-1, keepdims=True) + EPSILON)
    return (values * inv_rms * gain_vec, inv_rms)


def head_norm_back(cotangent, values, inv_rms, gain_vec):
    normed = values * inv_rms
    weighted = cotangent * gain_vec
    gain_grad = jnp.sum(cotangent * normed, axis=0)
    inner_mean = jnp.mean(weighted * normed, axis=-1, keepdims=True)
    return (inv_rms * (weighted - normed * inner_mean), gain_grad)


def swap_halves(values):
    half_width = values.shape[-1] // 2
    return jnp.concatenate([values[:, half_width:], values[:, :half_width]], axis=1)


def block_probability(query_block, key_rows, begins, offset, low, shift):
    score_scale = 1.0 / math.sqrt(query_block.shape[1])
    scores = dot(query_block, key_rows, 1, 1) * score_scale
    places = low + lax.broadcasted_iota(jnp.int32, scores.shape, 1)
    row_places = offset + lax.broadcasted_iota(jnp.int32, scores.shape, 0)
    allowed = (places >= begins) & (places <= row_places)
    if shift is None:
        shift = jnp.log(jnp.sum(jnp.where(allowed, jnp.exp(scores), 0.0), axis=1, keepdims=True))
    probability = jnp.where(allowed, jnp.exp(scores - shift), 0.0).astype(jnp.bfloat16)
    return probability, shift


def spans(length, longest, block):
    return [
        (offset, max(0, (offset - longest) // 128 * 128), block)
        for offset in range(0, length, block)
    ]


def attend_kernel(longest, sums, gains, cosine, sine, begins, *outs):
    query_rot, key_rot, value_low, low_rows, low_cols, totals = outs
    length, head_dim = query_rot.shape
    for place, target in ((0, query_rot), (1, key_rot)):
        normed = head_norm(
            sums[:, place * head_dim : (place + 1) * head_dim], gains[place : place + 1, :]
        )[0]
        target[...] = (normed * cosine[...] + swap_halves(normed) * sine[...]).astype(jnp.bfloat16)
    value_low[...] = sums[:, 2 * head_dim : 3 * head_dim].astype(jnp.bfloat16)
    for offset, low, block in spans(length, longest, min(256, length)):
        rows, keys = slice(offset, offset + block), slice(low, offset + block)
        probability, total = block_probability(
            query_rot[rows, :], key_rot[keys, :], begins[rows, :], offset, low, None
        )
        totals[rows, :] = total
        low_rows[rows, :] = dot(probability, value_low[keys, :]).astype(jnp.bfloat16)
        low_cols[:, rows] = dot(value_low[keys, :], probability, 0, 1).astype(jnp.bfloat16)


def attend_back_kernel(longest, *refs):
    query_rot, key_rot, value_low, low_rows, totals, grads = refs[:6]
    sums, gains, cosine, sine, begins = refs[6:11]
    slot, gain_out, query_acc, key_acc, value_acc = refs[11:]
    length, head_dim = query_rot.shape
    score_scale = 1.0 / math.sqrt(head_dim)
    key_acc[...] = jnp.zeros_like(key_acc)
    value_acc[...] = jnp.zeros_like(value_acc)
    for offset, low, block in spans(length, longest, min(256, length)):
        rows, keys = slice(offset, offset + block), slice(low, offset + block)
        probability, _ = block_probability(
            query_rot[rows, :], key_rot[keys, :], begins[rows, :], offset, low, totals[rows, :]
        )
        grad_block = grads[rows, :]
        value_acc[keys, :] += dot(probability, grad_block, 0, 0)
        row_delta = jnp.sum(
            grad_block.astype(jnp.float32) * low_rows[rows, :].astype(jnp.float32),
            axis=1,
            keepdims=True,
        )
        prob_grad = dot(grad_block, value_low[keys, :], 1, 1)
        score_grad = (
            score_scale * probability.astype(jnp.float32) * (prob_grad - row_delta)
        ).astype(jnp.bfloat16)
        query_acc[rows, :] = dot(score_grad, key_rot[keys, :])
        key_acc[keys, :] += dot(score_grad, query_rot[rows, :], 0, 0)
    parts = []
    for place, source in ((0, query_acc), (1, key_acc)):
        raw = sums[:, place * head_dim : (place + 1) * head_dim]
        gain = gains[place : place + 1, :]
        inv_rms = head_norm(raw, gain)[1]
        cotangent = source[...] * cosine[...] - swap_halves(source[...]) * sine[...]
        low_part, gain_grad = head_norm_back(cotangent, raw, inv_rms, gain)
        parts.append(low_part.astype(jnp.bfloat16))
        gain_out[place : place + 1, :] = gain_grad[None, :]
    parts.append(value_acc[...].astype(jnp.bfloat16))
    for place in range(3):
        slot[:, place * head_dim : (place + 1) * head_dim] = parts[place]


def local_kernel(body, args, outs, scratch=()):
    vmem = pl.BlockSpec(memory_space=pltpu.VMEM)
    return pl.pallas_call(
        body,
        out_shape=outs,
        in_specs=[vmem] * len(args),
        out_specs=[vmem] * len(outs),
        scratch_shapes=list(scratch),
    )(*args)


def pack_slots_kernel(cols, head_dim, query, key, value, out):
    for col in range(cols):
        half = col // 2
        out[col, :, :head_dim] = query[:, col * head_dim : (col + 1) * head_dim]
        for place, source in ((1, key), (2, value)):
            out[col, :, place * head_dim : (place + 1) * head_dim] = source[
                :, half * head_dim : (half + 1) * head_dim
            ]


def pack_wide_kernel(cols, gate, up, out):
    part = gate.shape[1] // cols
    for col in range(cols):
        out[col, :, :part] = gate[:, col * part : (col + 1) * part]
        out[col, :, part:] = up[:, col * part : (col + 1) * part]


def open_wide_kernel(cols, wide, gate, up):
    part = gate.shape[1] // cols
    for col in range(cols):
        gate[:, col * part : (col + 1) * part] = wide[col, :, :part].astype(jnp.float32)
        up[:, col * part : (col + 1) * part] = wide[col, :, part:].astype(jnp.float32)


def open_slots_kernel(cols, head_dim, slots, out):
    for col in range(cols):
        out[:, col * head_dim : (col + 1) * head_dim] = slots[col, :, :head_dim].astype(jnp.float32)
    for half in range(cols // 2):
        for place in (1, 2):
            lanes = slice(place * head_dim, (place + 1) * head_dim)
            begin = (cols + (place - 1) * (cols // 2) + half) * head_dim
            out[:, begin : begin + head_dim] = slots[2 * half, :, lanes].astype(
                jnp.float32
            ) + slots[2 * half + 1, :, lanes].astype(jnp.float32)


MESH = pl.DeviceIdType.MESH
VMEM_LIMIT = 56 * 1024 * 1024


def enter(axes):
    barrier = pltpu.get_barrier_semaphore()
    count = 0
    for axis in axes:
        size, own = lax.axis_size(axis), lax.axis_index(axis)
        for step in range(1, size):
            pl.semaphore_signal(
                barrier, inc=1, device_id={axis: lax.rem(own + step, size)}, device_id_type=MESH
            )
        count += size - 1
    pl.semaphore_wait(barrier, count)


def send(source, target, sems, place, axis, index):
    copy = pltpu.make_async_remote_copy(
        src_ref=source,
        dst_ref=target,
        send_sem=sems[0].at[place],
        recv_sem=sems[1].at[place],
        device_id={axis: index},
        device_id_type=MESH,
    )
    copy.start()
    return copy


def neighbours():
    rows, row = lax.axis_size("row"), lax.axis_index("row")
    near = row + 1 - 2 * lax.rem(row, 2)
    far = lax.rem(row + rows // 2, rows)
    return near, far


def sibling():
    own = lax.axis_index("dp")
    return own + 1 - 2 * lax.rem(own, 2)


def greet(across=True, pair=True):
    cols, col = lax.axis_size("col"), lax.axis_index("col")
    near, far = neighbours()
    peers = [("col", lax.rem(col + step, cols)) for step in range(1, cols)]
    if across:
        peers += [("row", near), ("row", far)]
    if pair:
        peers.append(("dp", sibling()))
    barrier = pltpu.get_barrier_semaphore()
    for axis, index in peers:
        pl.semaphore_signal(barrier, inc=1, device_id={axis: index}, device_id_type=MESH)
    pl.semaphore_wait(barrier, len(peers))


class Gather:
    def __init__(self, source, block, part, sems, item):
        self.source, self.block, self.part = source, block, part
        self.sems, self.item = sems, item
        self.cols, self.col = lax.axis_size("col"), lax.axis_index("col")
        self.row = lax.axis_index("row")
        self.near, self.far = neighbours()
        self.lines, self.planes, self.relays = {}, {}, {}

    def origin(self, step):
        return lax.rem(self.col + self.cols - step, self.cols)

    def line(self):
        for step in range(1, self.cols):
            self.lines[step] = send(
                self.source,
                self.block(self.row, self.col),
                self.sems,
                (self.item, 0, step),
                "col",
                lax.rem(self.col + step, self.cols),
            )

    def plane(self, step):
        target = self.block(self.row, self.origin(step))
        if step:
            self.lines[step].wait_recv()
        for kind, peer in ((1, self.near), (2, self.far)):
            self.planes[step, kind] = send(
                target if step else self.source,
                target,
                self.sems,
                (self.item, kind, step),
                "row",
                peer,
            )

    def relay(self, step):
        for kind, source, peer in ((1, self.near, self.far), (2, self.far, self.near)):
            self.planes[step, kind].wait_recv()
            piece = self.part(source, self.origin(step), kind - 1)
            self.relays[step, kind] = send(
                piece, piece, self.sems, (self.item, kind + 2, step), "row", peer
            )

    def land(self, step):
        for kind in (1, 2):
            self.relays[step, kind].wait_recv()

    def sent(self):
        for copies in (self.lines, self.planes, self.relays):
            for copy in copies.values():
                copy.wait_send()


class Swap:
    def __init__(self, source, target, sems, item):
        self.source, self.target, self.sems, self.item = source, target, sems, item
        self.cols, self.col = lax.axis_size("col"), lax.axis_index("col")
        self.half = lax.rem(lax.axis_index("dp"), 2)
        self.lines, self.pairs = {}, {}

    def line(self):
        for step in range(1, self.cols):
            peer = lax.rem(self.col + step, self.cols)
            self.lines[step] = send(
                self.source.at[peer, self.half],
                self.target.at[self.col, self.half],
                self.sems,
                (self.item, 0, step),
                "col",
                peer,
            )

    def relay(self):
        for step in range(1, self.cols):
            self.lines[step].wait_recv()
            piece = self.target.at[lax.rem(self.col + self.cols - step, self.cols), self.half]
            self.pairs[step] = send(
                piece, piece, self.sems, (self.item, 1, step), "dp", sibling()
            )

    def land(self):
        for step in range(1, self.cols):
            self.pairs[step].wait_recv()

    def sent(self):
        for copies in (self.lines, self.pairs):
            for copy in copies.values():
                copy.wait_send()


def front_kernel(*refs):
    (own_in, own_grad, own_out, query, key, value, gate, up) = refs[:8]
    (attn_norm, gains, cosine, sine, begins) = refs[8:13]
    (in_all, grad_all, out_all, cat_all, gate_all, up_all, slot_all) = refs[13:20]
    (first, sums, query_rot, key_rot, value_low, low_rows, totals) = refs[20:27]
    (slot_part, gate_part, up_part) = refs[27:30]
    gather_sems, swap_sems, pair_sems = refs[30:32], refs[32:34], refs[34:36]
    rows, cols = lax.axis_size("row"), lax.axis_size("col")
    row, col = lax.axis_index("row"), lax.axis_index("col")
    half = lax.rem(lax.axis_index("dp"), 2)
    near, far = neighbours()
    length, head_dim = query_rot.shape
    width = own_in.shape[1]
    local = own_in.shape[0]
    block = length // rows

    def split(ref):
        count = ref.shape[2] // 2
        return (
            lambda r, c: ref.at[r, c],
            lambda r, c, k: ref.at[r, c, pl.ds(k * count, count)],
        )

    greet()
    inputs = Gather(own_in, *split(in_all), gather_sems, 0)
    inputs.line()
    inputs.plane(0)
    height = query.shape[0] // 2
    for place in range(cols):
        for piece in range(2):
            lines = slice(piece * height, (piece + 1) * height)
            lanes = slice(place // 2 * head_dim, (place // 2 + 1) * head_dim)
            slot_part[place, piece, :, :head_dim] = query[
                lines, place * head_dim : (place + 1) * head_dim
            ]
            slot_part[place, piece, :, head_dim : 2 * head_dim] = key[lines, lanes]
            slot_part[place, piece, :, 2 * head_dim :] = value[lines, lanes]
    slots = Swap(slot_part, slot_all, swap_sems, 0)
    slots.line()
    slot_all[col] = slot_part[col]
    in_all[row, col] = own_in[...]
    for step in range(1, cols):
        inputs.plane(step)
    hidden = gate.shape[1] // cols
    for source, part in ((gate, gate_part), (up, up_part)):
        for place in range(cols):
            for piece in range(2):
                part[place, piece] = source[
                    piece * height : (piece + 1) * height, place * hidden : (place + 1) * hidden
                ]
    slots.relay()
    inputs.relay(0)
    grads = Gather(own_grad, *split(grad_all), gather_sems, 1)
    grads.line()
    inputs.relay(1)
    wide = [Swap(gate_part, gate_all, swap_sems, 1), Swap(up_part, up_all, swap_sems, 2)]
    for swap in wide:
        swap.line()
    inputs.relay(2)
    count = own_out.shape[1] // 2
    outs = Gather(
        own_out.at[half],
        lambda r, c: out_all.at[r, c, half],
        lambda r, c, k: out_all.at[r, c, half, pl.ds(k * count, count)],
        gather_sems,
        2,
    )
    outs.line()
    inputs.relay(3)
    grads.plane(0)
    outs.plane(0)
    gate_all[col] = gate_part[col]
    up_all[col] = up_part[col]
    grad_all[row, col] = own_grad[...]
    out_all[row, col] = own_out[...]
    slots.land()

    def project(place):
        for c in range(cols):
            values = in_all[place, c].astype(jnp.float32)
            normed = head_norm(values, attn_norm[...])[0]
            lines = pl.ds(pl.multiple_of(place * block + c * local, local), local)
            first[lines, :] = normed.astype(jnp.bfloat16)
        lines = pl.ds(pl.multiple_of(place * block, block), block)
        sums[lines, :] = dot(first[lines, :], slot_all[...].reshape(width, 3 * head_dim))

    project(row)
    project(near)
    project(far)
    for step in range(1, cols):
        grads.plane(step)
    for step in range(cols):
        inputs.land(step)
    project(lax.rem(near + rows // 2, rows))
    for step in range(1, cols):
        outs.plane(step)
    for place, target in ((0, query_rot), (1, key_rot)):
        normed = head_norm(
            sums[:, place * head_dim : (place + 1) * head_dim], gains[place : place + 1, :]
        )[0]
        target[...] = (normed * cosine[...] + swap_halves(normed) * sine[...]).astype(jnp.bfloat16)
    value_low[...] = sums[:, 2 * head_dim : 3 * head_dim].astype(jnp.bfloat16)

    def cat(part):
        places = pl.ds(part * (rows // 2), rows // 2)
        return Gather(
            cat_all.at[places, row, col],
            lambda r, c: cat_all.at[places, r, c],
            lambda r, c, k: cat_all.at[places, r, c, pl.ds(k * head_dim // 2, head_dim // 2)],
            gather_sems,
            3 + part,
        )

    cats = []
    for offset, low, _ in spans(length, length // 2, block):
        number = offset // block
        lines, keys = slice(offset, offset + block), slice(low, offset + block)
        probability, total = block_probability(
            query_rot[lines, :], key_rot[keys, :], begins[lines, :], offset, low, None
        )
        totals[lines, :] = total
        low_rows[lines, :] = dot(probability, value_low[keys, :]).astype(jnp.bfloat16)
        cat_all[number, row, col] = dot(value_low[keys, :], probability, 0, 1).astype(jnp.bfloat16)
        if 2 * (number + 1) % rows == 0:
            cats.append(cat(2 * (number + 1) // rows - 1))
            cats[-1].line()
            cats[-1].plane(0)
        if number == 0:
            for swap in wide:
                swap.relay()
            grads.relay(0)
            grads.relay(1)
        if number == 1:
            grads.relay(2)
            grads.relay(3)
        if number == 2:
            for step in range(cols):
                outs.relay(step)
            for step in range(1, cols):
                cats[0].plane(step)
    for step in range(1, cols):
        cats[1].plane(step)
    for gather in cats:
        for step in range(cols):
            gather.relay(step)
    pairs = []
    for step in range(cols):
        outs.land(step)
    for number, place in enumerate((near, far, lax.rem(near + rows // 2, rows))):
        piece = out_all.at[place, :, half]
        pairs.append(send(piece, piece, pair_sems, (number,), "dp", sibling()))
    for step in range(1, cols):
        piece = out_all.at[row, lax.rem(col + cols - step, cols), half]
        pairs.append(send(piece, piece, pair_sems, (2 + step,), "dp", sibling()))
    for swap in wide:
        swap.land()
    for gather in [grads] + cats:
        for step in range(cols):
            gather.land(step)
    for copy in pairs:
        copy.wait()
    for item in [inputs, grads, outs, slots] + wide + cats:
        item.sent()


def front(own_in, own_grad, own_out, query, key, value, gate, up, attn_norm, gains, tables, number):
    rows, cols = lax.axis_size("row"), lax.axis_size("col")
    local, width = own_in.shape
    length, head_dim = local * rows * cols, gains.shape[1]
    hidden, height = gate.shape[1] // cols, gate.shape[0] // 2
    low = jnp.bfloat16
    blocks = jax.ShapeDtypeStruct((rows, cols, local, width), low)
    halves = own_out.shape[0] // 2
    wide = (cols, 2, height, hidden)
    slot = (cols, 2, height, 3 * head_dim)
    shape = jax.ShapeDtypeStruct
    head_rows = shape((length, head_dim), low)
    outs = [
        blocks,
        blocks,
        shape((rows, cols, 2, halves, width), low),
        shape((rows, rows, cols, head_dim, length // rows), low),
        shape(wide, low),
        shape(wide, low),
        shape(slot, low),
        shape((length, width), low),
        shape((length, 3 * head_dim), jnp.float32),
        head_rows,
        head_rows,
        head_rows,
        head_rows,
        shape((length, 1), jnp.float32),
    ]
    scratch = [pltpu.VMEM(slot, low), pltpu.VMEM(wide, low), pltpu.VMEM(wide, low)]
    scratch += dma(5, 5, cols) + dma(3, 2, cols) + dma(2 + cols)
    args = [own_in, own_grad, own_out.reshape(2, halves, width), query, key, value, gate, up]
    args += [attn_norm.reshape(1, width), gains] + list(tables)
    return call_kernel(front_kernel, args, outs, scratch, number)


def start_swaps(ins, outs, sems):
    cols, own = lax.axis_size("col"), lax.axis_index("col")
    copies = []
    for number in range(len(ins)):
        for step in range(1, cols):
            peer = lax.rem(own + step, cols)
            copies.append(
                send(ins[number].at[peer], outs[number].at[own], sems, (number, step), "col", peer)
            )
        outs[number][own] = ins[number][own]
    return copies


def call_kernel(body, args, outs, scratch, number):
    vmem = pl.BlockSpec(memory_space=pltpu.VMEM)
    return pl.pallas_call(
        body,
        out_shape=outs,
        in_specs=[vmem] * len(args),
        out_specs=[vmem] * len(outs),
        scratch_shapes=scratch,
        compiler_params=pltpu.CompilerParams(
            collective_id=number, has_side_effects=True, vmem_limit_bytes=VMEM_LIMIT
        ),
    )(*args)


def dma(*shape):
    return [pltpu.SemaphoreType.DMA(shape), pltpu.SemaphoreType.DMA(shape)]


def exchange(gathers, swaps, number):
    rows, cols = lax.axis_size("row"), lax.axis_size("col")
    many, total = len(gathers), len(gathers) + len(swaps)

    def body(*refs):
        ins, outs = refs[:total], refs[total : 2 * total]
        sems, swap_sems = refs[2 * total : 2 * total + 2], refs[2 * total + 2 :]
        row, col = lax.axis_index("row"), lax.axis_index("col")
        enter(("row", "col"))
        across, copies = {}, []
        for item in range(many):
            for step in range(1, cols):
                across[item, step] = send(
                    ins[item],
                    outs[item].at[row, col],
                    sems,
                    (item, 0, step),
                    "col",
                    lax.rem(col + step, cols),
                )
        for item in range(many):
            for turn in range(1, rows):
                copies.append(
                    send(
                        ins[item],
                        outs[item].at[row, col],
                        sems,
                        (item, turn, 0),
                        "row",
                        lax.rem(row + turn, rows),
                    )
                )
        copies += start_swaps(ins[many:], outs[many:], swap_sems)
        for item in range(many):
            outs[item][row, col] = ins[item][...]
        for step in range(1, cols):
            origin = lax.rem(col + cols - step, cols)
            for item in range(many):
                across[item, step].wait()
                block = outs[item].at[row, origin]
                for turn in range(1, rows):
                    copies.append(
                        send(
                            block,
                            block,
                            sems,
                            (item, turn, step),
                            "row",
                            lax.rem(row + turn, rows),
                        )
                    )
        for copy in copies:
            copy.wait()

    outs = [jax.ShapeDtypeStruct((rows, cols) + g.shape, g.dtype) for g in gathers]
    outs += [jax.ShapeDtypeStruct(w.shape, w.dtype) for w in swaps]
    scratch = dma(many, rows, cols) + dma(max(len(swaps), 1), cols)
    return call_kernel(body, list(gathers) + list(swaps), outs, scratch, number)


def reduce_rows(partial_value, swaps, number):
    rows, cols = lax.axis_size("row"), lax.axis_size("col")
    local = partial_value.shape[0] // (rows * cols)
    width = partial_value.shape[1]
    shaped = partial_value.astype(jnp.bfloat16).reshape(rows, cols, local, width)
    many = len(swaps)

    def body(*refs):
        part, ins = refs[0], refs[1 : 1 + many]
        result, outs = refs[1 + many], refs[2 + many : 2 + 2 * many]
        first, staged, second = refs[2 + 2 * many : 5 + 2 * many]
        first_sems, second_sems = refs[5 + 2 * many : 7 + 2 * many], refs[7 + 2 * many : 9 + 2 * many]
        swap_sems = refs[9 + 2 * many :]
        row, col = lax.axis_index("row"), lax.axis_index("col")
        enter(("row", "col"))
        down, across = {}, []
        order = list(range(1, cols)) + [0]
        for step in order:
            block = lax.rem(col + step, cols)
            for turn in range(1, rows):
                peer = lax.rem(row + turn, rows)
                down[step, turn] = send(
                    part.at[peer, block],
                    first.at[turn, step],
                    first_sems,
                    (turn, step),
                    "row",
                    peer,
                )
        copies = start_swaps(ins, outs, swap_sems)
        for step in order:
            block = lax.rem(col + step, cols)
            summed = part[row, block].astype(jnp.float32)
            for turn in range(1, rows):
                down[step, turn].wait()
                summed = summed + first[turn, step].astype(jnp.float32)
            if step == 0:
                result[...] = summed
            else:
                staged[step] = summed.astype(jnp.bfloat16)
                across.append(
                    send(staged.at[step], second.at[step], second_sems, (step,), "col", block)
                )
        for step in range(1, cols):
            across[step - 1].wait()
            result[...] += second[step].astype(jnp.float32)
        for copy in copies:
            copy.wait()

    outs = [jax.ShapeDtypeStruct((local, width), jnp.float32)]
    outs += [jax.ShapeDtypeStruct(w.shape, w.dtype) for w in swaps]
    scratch = [
        pltpu.VMEM((rows, cols, local, width), jnp.bfloat16),
        pltpu.VMEM((cols, local, width), jnp.bfloat16),
        pltpu.VMEM((cols, local, width), jnp.bfloat16),
    ]
    scratch += dma(rows, cols) + dma(cols) + dma(max(many, 1), cols)
    return call_kernel(body, [shaped] + list(swaps), outs, scratch, number)


def last_sums(group_value, widths, gains, number):
    sizes = [lax.axis_size(axis) for axis in ("dp", "row", "col")]

    def body(value, gain, *refs):
        value_outs, gain_out = refs[: len(widths)], refs[len(widths)]
        value_in, landed, held = refs[len(widths) + 1 : len(widths) + 4]
        sems = refs[len(widths) + 4 :]
        value_sems, gain_sems = sems[:2], sems[2:]
        enter(("dp", "row", "col"))
        copies, groups = [], lax.axis_size("dp")
        me = lax.axis_index("dp")
        for step in range(1, groups):
            copies.append(
                send(
                    value,
                    value_in.at[step],
                    value_sems,
                    (step,),
                    "dp",
                    lax.rem(me + step, groups),
                )
            )
        held[0] = gain[...]
        for stage, axis in enumerate(("dp", "row", "col")):
            size, own = lax.axis_size(axis), lax.axis_index(axis)
            sent = [
                send(
                    held.at[stage],
                    landed.at[stage, step],
                    gain_sems,
                    (stage, step),
                    axis,
                    lax.rem(own + step, size),
                )
                for step in range(1, size)
            ]
            landed[stage, 0] = held[stage]
            for copy in sent:
                copy.wait()
            total = None
            for place in range(size):
                term = landed[stage, lax.rem(own - place + size, size)]
                total = term if total is None else total + term
            held[stage + 1] = total
        gain_out[...] = held[3]
        for copy in copies:
            copy.wait()
        total = value[...]
        for step in range(1, groups):
            total = total + value_in[step]
        begin = 0
        for size, value_out in zip(widths, value_outs):
            value_out[...] = total[:, begin : begin + size]
            begin += size

    outs = [jax.ShapeDtypeStruct((group_value.shape[0], size), jnp.float32) for size in widths]
    outs.append(jax.ShapeDtypeStruct(gains.shape, jnp.float32))
    scratch = [
        pltpu.VMEM((sizes[0],) + group_value.shape, jnp.float32),
        pltpu.VMEM((3, max(sizes)) + gains.shape, jnp.float32),
        pltpu.VMEM((4,) + gains.shape, jnp.float32),
    ]
    scratch += dma(sizes[0]) + dma(3, max(sizes))
    return call_kernel(body, [group_value, gains], outs, scratch, number)


def dot(left, right, left_dim=1, right_dim=0):
    return lax.dot_general(
        left,
        right,
        (((left_dim,), (right_dim,)), ((), ())),
        preferred_element_type=jnp.float32,
    )


def shards(
    block_input,
    seq_lengths,
    out_grad,
    attn_norm,
    query_weight,
    key_weight,
    value_weight,
    query_norm,
    key_norm,
    out_weight,
    ffn_norm,
    gate_weight,
    up_weight,
    down_weight,
):
    local_rows, width = block_input.shape
    head_dim = query_norm.shape[0]
    col_width = query_weight.shape[0]
    cols = lax.axis_size("col")
    length = local_rows * cols * lax.axis_size("row")
    place = (lax.axis_index("row") * cols + lax.axis_index("col")) * local_rows

    def own_rows(values):
        return lax.dynamic_slice_in_dim(values, place, local_rows, 0)

    hidden_width = gate_weight.shape[1] // cols
    residual = block_input.astype(jnp.float32)
    scale_in = head_norm(residual, attn_norm)[1]
    places = jnp.arange(length, dtype=jnp.int32)
    position = segment_info(seq_lengths[0], length)[1]
    begins = (places - position)[:, None]
    cosine, sine = rope_tables(position, head_dim)
    cosine = jnp.concatenate([cosine, cosine], axis=1)
    sine = jnp.concatenate([-sine, sine], axis=1)
    longest = length // 2
    head_gains = jnp.stack([query_norm, key_norm])
    (
        input_blocks,
        out_blocks,
        out_weight_blocks,
        cat_blocks,
        gate_blocks,
        up_blocks,
        slot_blocks,
        first_full,
        own_sums,
        query_rot,
        key_rot,
        value_low,
        attn_low,
        log_total,
    ) = front(
        block_input,
        out_grad,
        out_weight,
        query_weight,
        key_weight,
        value_weight,
        gate_weight,
        up_weight,
        attn_norm,
        head_gains,
        (cosine, sine, begins),
        0,
    )
    input_full = input_blocks.reshape(length, width).astype(jnp.float32)
    slot_weight = slot_blocks.reshape(width, 3 * head_dim)
    out_full = out_blocks.reshape(length, width)
    out_weight_full = out_weight_blocks.reshape(-1, width)
    cat_full = cat_blocks.reshape(cat_blocks.shape[0], -1, cat_blocks.shape[-1])
    wide_weight = jnp.concatenate(
        [gate_blocks.reshape(width, -1), up_blocks.reshape(width, -1)], axis=1
    )
    attended = jnp.einsum(
        "bft,fd->btd", cat_full, out_weight_full, preferred_element_type=jnp.float32
    )
    middle = input_full + attended.reshape(length, width)
    normed_mid, scale_mid = head_norm(middle, ffn_norm)
    second_full = normed_mid.astype(jnp.bfloat16)
    wide_sums = dot(second_full, wide_weight)
    gating, upward = wide_sums[:, :hidden_width], wide_sums[:, hidden_width:]
    sigmoid_gate = jax.nn.sigmoid(gating)
    activated = gating * sigmoid_gate
    hidden = (activated * upward).astype(jnp.bfloat16)
    hidden_grad = dot(out_full, down_weight, 1, 1)
    gate_low = (hidden_grad * upward * sigmoid_gate * (1.0 + gating * (1.0 - sigmoid_gate))).astype(
        jnp.bfloat16
    )
    up_low = (hidden_grad * activated).astype(jnp.bfloat16)
    wide_low = jnp.concatenate([gate_low, up_low], axis=1)
    both_parts = [
        dot(wide_low, wide_weight, 1, 1).astype(jnp.bfloat16),
        dot(hidden, down_weight).astype(jnp.bfloat16),
    ]
    (both_sums,) = reduce_rows(jnp.concatenate(both_parts, axis=1), [], 2)
    act_grad2, down_sums = both_sums[:, :width], both_sums[:, width:]
    middle_own = own_rows(middle)
    grad_down = dot(hidden, out_full, 0, 0)
    wide_grad = dot(second_full, wide_low, 0, 0).astype(jnp.bfloat16)
    middle_back, ffn_gain_grad = head_norm_back(
        act_grad2, middle_own, own_rows(scale_mid), ffn_norm
    )
    middle_grad = out_grad.astype(jnp.float32) + middle_back
    middle_blocks, wide_grads = exchange(
        [middle_grad.astype(jnp.bfloat16)],
        [wide_grad.reshape(cols, col_width, 2 * hidden_width)],
        3,
    )
    middle_full = middle_blocks.reshape(length, width)
    grad_outweight = dot(attn_low, middle_full, 0, 0)
    cat_grad = dot(middle_full, out_weight, 1, 1).astype(jnp.bfloat16)
    wide_shape = jax.ShapeDtypeStruct(gate_weight.shape, jnp.float32)
    grad_gate, grad_up = local_kernel(
        functools.partial(open_wide_kernel, cols), [wide_grads], [wide_shape, wide_shape]
    )
    block_output = (middle_own + down_sums).astype(jnp.bfloat16)
    accumulator = pltpu.VMEM((length, head_dim), jnp.float32)
    own_slot, head_gain_grads = local_kernel(
        functools.partial(attend_back_kernel, longest),
        [query_rot, key_rot, value_low, attn_low, log_total, cat_grad]
        + [own_sums, head_gains, cosine, sine, begins],
        [
            jax.ShapeDtypeStruct((length, 3 * head_dim), jnp.bfloat16),
            jax.ShapeDtypeStruct((2, head_dim), jnp.float32),
        ],
        [accumulator] * 3,
    )
    grad_outweight, grad_gate, grad_up, grad_down = lax.psum(
        (grad_outweight, grad_gate, grad_up, grad_down), "dp"
    )
    slot_grad = dot(first_full, own_slot, 0, 0).astype(jnp.bfloat16)
    act_grad1, slot_grads = reduce_rows(
        dot(own_slot, slot_weight, 1, 1),
        [slot_grad.reshape(cols, col_width, 3 * head_dim)],
        4,
    )
    widths = (cols * head_dim, cols // 2 * head_dim, cols // 2 * head_dim)
    (slot_sums,) = local_kernel(
        functools.partial(open_slots_kernel, cols, head_dim),
        [slot_grads],
        [jax.ShapeDtypeStruct((col_width, sum(widths)), jnp.float32)],
    )
    input_back, attn_gain_grad = head_norm_back(act_grad1, residual, scale_in, attn_norm)
    input_grad = middle_grad + input_back
    flat_gains = jnp.concatenate(
        [head_gain_grads.reshape(-1), jnp.zeros((width - 2 * head_dim,), jnp.float32)]
    )
    gains = jnp.stack([attn_gain_grad, ffn_gain_grad, flat_gains])
    gains = jnp.concatenate([gains, jnp.zeros((5, width), jnp.float32)], axis=0)
    grad_query, grad_key, grad_value, gain_sums = last_sums(slot_sums, widths, gains, 5)
    return (
        block_output,
        input_grad,
        gain_sums[0],
        grad_query,
        grad_key,
        grad_value,
        gain_sums[2, :head_dim],
        gain_sums[2, head_dim : 2 * head_dim],
        grad_outweight,
        gain_sums[1],
        grad_gate,
        grad_up,
        grad_down,
    )


def solution(mesh):
    placed = (
        P(("dp", "row", "col"), None),
        P("dp", None),
        P(("dp", "row", "col"), None),
        P(),
        P("col", "row"),
        P("col", "row"),
        P("col", "row"),
        P(),
        P(),
        P(("row", "col"), None),
        P(),
        P("col", "row"),
        P("col", "row"),
        P(("row", "col"), None),
    )
    return jax.shard_map(
        shards,
        mesh=mesh,
        in_specs=placed,
        out_specs=(
            P(("dp", "row", "col"), None),
            P(("dp", "row", "col"), None),
            P(),
            P("col", "row"),
            P("col", "row"),
            P("col", "row"),
            P(),
            P(),
            P(("row", "col"), None),
            P(),
            P("col", "row"),
            P("col", "row"),
            P(("row", "col"), None),
        ),
        check_vma=False,
    )
```

```python
import functools
import math

import jax
import jax.numpy as jnp
from jax import lax
from jax.experimental import pallas as pl
from jax.experimental.pallas import tpu as pltpu
from jax.sharding import PartitionSpec as P

EPSILON = 1e-05
THETA = 1000000.0


def segment_info(seq_lengths, length):
    order = jnp.arange(seq_lengths.shape[0], dtype=jnp.int32)
    up_to = order[:, None] <= order[None, :]
    end_points = jnp.sum(jnp.where(up_to, seq_lengths[:, None], 0), axis=0)
    places = jnp.arange(length, dtype=jnp.int32)
    passed = (places[:, None] >= end_points[None, :]).astype(jnp.int32)
    segment = jnp.sum(passed, axis=1)
    begins = jnp.sum(passed * seq_lengths[None, :], axis=1)
    return (segment, places - begins)


def rope_tables(position, width):
    half_width = width // 2
    exponent = jnp.arange(half_width, dtype=jnp.float32) * (2.0 / width)
    frequency = jnp.exp(-math.log(THETA) * exponent)
    angles = position.astype(jnp.float32)[:, None] * frequency[None, :]
    return (jnp.cos(angles), jnp.sin(angles))


def head_norm(values, gain_vec):
    inv_rms = lax.rsqrt(jnp.mean(values * values, axis=-1, keepdims=True) + EPSILON)
    return (values * inv_rms * gain_vec, inv_rms)


def head_norm_back(cotangent, values, inv_rms, gain_vec):
    normed = values * inv_rms
    weighted = cotangent * gain_vec
    gain_grad = jnp.sum(cotangent * normed, axis=0)
    inner_mean = jnp.mean(weighted * normed, axis=-1, keepdims=True)
    return (inv_rms * (weighted - normed * inner_mean), gain_grad)


def swap_halves(values):
    half_width = values.shape[-1] // 2
    return jnp.concatenate([values[:, half_width:], values[:, :half_width]], axis=1)


def block_probability(query_block, key_rows, begins, offset, low, shift):
    score_scale = 1.0 / math.sqrt(query_block.shape[1])
    scores = dot(query_block, key_rows, 1, 1) * score_scale
    places = low + lax.broadcasted_iota(jnp.int32, scores.shape, 1)
    row_places = offset + lax.broadcasted_iota(jnp.int32, scores.shape, 0)
    allowed = (places >= begins) & (places <= row_places)
    if shift is None:
        shift = jnp.log(jnp.sum(jnp.where(allowed, jnp.exp(scores), 0.0), axis=1, keepdims=True))
    probability = jnp.where(allowed, jnp.exp(scores - shift), 0.0).astype(jnp.bfloat16)
    return probability, shift


def spans(length, longest, block):
    return [
        (offset, max(0, (offset - longest) // 128 * 128), block)
        for offset in range(0, length, block)
    ]


def attend_kernel(longest, sums, gains, cosine, sine, begins, *outs):
    query_rot, key_rot, value_low, low_rows, low_cols, totals = outs
    length, head_dim = query_rot.shape
    for place, target in ((0, query_rot), (1, key_rot)):
        normed = head_norm(
            sums[:, place * head_dim : (place + 1) * head_dim], gains[place : place + 1, :]
        )[0]
        target[...] = (normed * cosine[...] + swap_halves(normed) * sine[...]).astype(jnp.bfloat16)
    value_low[...] = sums[:, 2 * head_dim : 3 * head_dim].astype(jnp.bfloat16)
    for offset, low, block in spans(length, longest, min(256, length)):
        rows, keys = slice(offset, offset + block), slice(low, offset + block)
        probability, total = block_probability(
            query_rot[rows, :], key_rot[keys, :], begins[rows, :], offset, low, None
        )
        totals[rows, :] = total
        low_rows[rows, :] = dot(probability, value_low[keys, :]).astype(jnp.bfloat16)
        low_cols[:, rows] = dot(value_low[keys, :], probability, 0, 1).astype(jnp.bfloat16)


def attend_back_kernel(longest, *refs):
    query_rot, key_rot, value_low, low_rows, totals, grads = refs[:6]
    sums, gains, cosine, sine, begins = refs[6:11]
    slot, gain_out, query_acc, key_acc, value_acc = refs[11:]
    length, head_dim = query_rot.shape
    score_scale = 1.0 / math.sqrt(head_dim)
    key_acc[...] = jnp.zeros_like(key_acc)
    value_acc[...] = jnp.zeros_like(value_acc)
    for offset, low, block in spans(length, longest, min(256, length)):
        rows, keys = slice(offset, offset + block), slice(low, offset + block)
        probability, _ = block_probability(
            query_rot[rows, :], key_rot[keys, :], begins[rows, :], offset, low, totals[rows, :]
        )
        grad_block = grads[rows, :]
        value_acc[keys, :] += dot(probability, grad_block, 0, 0)
        row_delta = jnp.sum(
            grad_block.astype(jnp.float32) * low_rows[rows, :].astype(jnp.float32),
            axis=1,
            keepdims=True,
        )
        prob_grad = dot(grad_block, value_low[keys, :], 1, 1)
        score_grad = (
            score_scale * probability.astype(jnp.float32) * (prob_grad - row_delta)
        ).astype(jnp.bfloat16)
        query_acc[rows, :] = dot(score_grad, key_rot[keys, :])
        key_acc[keys, :] += dot(score_grad, query_rot[rows, :], 0, 0)
    parts = []
    for place, source in ((0, query_acc), (1, key_acc)):
        raw = sums[:, place * head_dim : (place + 1) * head_dim]
        gain = gains[place : place + 1, :]
        inv_rms = head_norm(raw, gain)[1]
        cotangent = source[...] * cosine[...] - swap_halves(source[...]) * sine[...]
        low_part, gain_grad = head_norm_back(cotangent, raw, inv_rms, gain)
        parts.append(low_part.astype(jnp.bfloat16))
        gain_out[place : place + 1, :] = gain_grad[None, :]
    parts.append(value_acc[...].astype(jnp.bfloat16))
    for place in range(3):
        slot[:, place * head_dim : (place + 1) * head_dim] = parts[place]


def local_kernel(body, args, outs, scratch=()):
    vmem = pl.BlockSpec(memory_space=pltpu.VMEM)
    return pl.pallas_call(
        body,
        out_shape=outs,
        in_specs=[vmem] * len(args),
        out_specs=[vmem] * len(outs),
        scratch_shapes=list(scratch),
    )(*args)


def pack_slots_kernel(cols, head_dim, query, key, value, out):
    for col in range(cols):
        half = col // 2
        out[col, :, :head_dim] = query[:, col * head_dim : (col + 1) * head_dim]
        for place, source in ((1, key), (2, value)):
            out[col, :, place * head_dim : (place + 1) * head_dim] = source[
                :, half * head_dim : (half + 1) * head_dim
            ]


def pack_wide_kernel(cols, gate, up, out):
    part = gate.shape[1] // cols
    for col in range(cols):
        out[col, :, :part] = gate[:, col * part : (col + 1) * part]
        out[col, :, part:] = up[:, col * part : (col + 1) * part]


def open_wide_kernel(cols, wide, gate, up):
    part = gate.shape[1] // cols
    for col in range(cols):
        gate[:, col * part : (col + 1) * part] = wide[col, :, :part].astype(jnp.float32)
        up[:, col * part : (col + 1) * part] = wide[col, :, part:].astype(jnp.float32)


def open_slots_kernel(cols, head_dim, slots, out):
    for col in range(cols):
        out[:, col * head_dim : (col + 1) * head_dim] = slots[col, :, :head_dim].astype(jnp.float32)
    for half in range(cols // 2):
        for place in (1, 2):
            lanes = slice(place * head_dim, (place + 1) * head_dim)
            begin = (cols + (place - 1) * (cols // 2) + half) * head_dim
            out[:, begin : begin + head_dim] = slots[2 * half, :, lanes].astype(
                jnp.float32
            ) + slots[2 * half + 1, :, lanes].astype(jnp.float32)


MESH = pl.DeviceIdType.MESH
VMEM_LIMIT = 56 * 1024 * 1024


def enter(axes):
    barrier = pltpu.get_barrier_semaphore()
    count = 0
    for axis in axes:
        size, own = lax.axis_size(axis), lax.axis_index(axis)
        for step in range(1, size):
            pl.semaphore_signal(
                barrier, inc=1, device_id={axis: lax.rem(own + step, size)}, device_id_type=MESH
            )
        count += size - 1
    pl.semaphore_wait(barrier, count)


def send(source, target, sems, place, axis, index):
    copy = pltpu.make_async_remote_copy(
        src_ref=source,
        dst_ref=target,
        send_sem=sems[0].at[place],
        recv_sem=sems[1].at[place],
        device_id={axis: index},
        device_id_type=MESH,
    )
    copy.start()
    return copy


def neighbours():
    rows, row = lax.axis_size("row"), lax.axis_index("row")
    near = row + 1 - 2 * lax.rem(row, 2)
    far = lax.rem(row + rows // 2, rows)
    return near, far


def sibling():
    own = lax.axis_index("dp")
    return own + 1 - 2 * lax.rem(own, 2)


def greet(across=True, pair=True):
    cols, col = lax.axis_size("col"), lax.axis_index("col")
    near, far = neighbours()
    peers = [("col", lax.rem(col + step, cols)) for step in range(1, cols)]
    if across:
        peers += [("row", near), ("row", far)]
    if pair:
        peers.append(("dp", sibling()))
    barrier = pltpu.get_barrier_semaphore()
    for axis, index in peers:
        pl.semaphore_signal(barrier, inc=1, device_id={axis: index}, device_id_type=MESH)
    pl.semaphore_wait(barrier, len(peers))


class Gather:
    def __init__(self, source, block, part, sems, item):
        self.source, self.block, self.part = source, block, part
        self.sems, self.item = sems, item
        self.cols, self.col = lax.axis_size("col"), lax.axis_index("col")
        self.row = lax.axis_index("row")
        self.near, self.far = neighbours()
        self.lines, self.planes, self.relays = {}, {}, {}

    def origin(self, step):
        return lax.rem(self.col + self.cols - step, self.cols)

    def line(self):
        for step in range(1, self.cols):
            self.lines[step] = send(
                self.source,
                self.block(self.row, self.col),
                self.sems,
                (self.item, 0, step),
                "col",
                lax.rem(self.col + step, self.cols),
            )

    def plane(self, step):
        target = self.block(self.row, self.origin(step))
        if step:
            self.lines[step].wait_recv()
        for kind, peer in ((1, self.near), (2, self.far)):
            self.planes[step, kind] = send(
                target if step else self.source,
                target,
                self.sems,
                (self.item, kind, step),
                "row",
                peer,
            )

    def relay(self, step):
        for kind, source, peer in ((1, self.near, self.far), (2, self.far, self.near)):
            self.planes[step, kind].wait_recv()
            piece = self.part(source, self.origin(step), kind - 1)
            self.relays[step, kind] = send(
                piece, piece, self.sems, (self.item, kind + 2, step), "row", peer
            )

    def land(self, step):
        for kind in (1, 2):
            self.relays[step, kind].wait_recv()

    def sent(self):
        for copies in (self.lines, self.planes, self.relays):
            for copy in copies.values():
                copy.wait_send()


class Swap:
    def __init__(self, source, target, sems, item):
        self.source, self.target, self.sems, self.item = source, target, sems, item
        self.cols, self.col = lax.axis_size("col"), lax.axis_index("col")
        self.half = lax.rem(lax.axis_index("dp"), 2)
        self.lines, self.pairs = {}, {}

    def line(self):
        for step in range(1, self.cols):
            peer = lax.rem(self.col + step, self.cols)
            self.lines[step] = send(
                self.source.at[peer, self.half],
                self.target.at[self.col, self.half],
                self.sems,
                (self.item, 0, step),
                "col",
                peer,
            )

    def relay(self):
        for step in range(1, self.cols):
            self.lines[step].wait_recv()
            piece = self.target.at[lax.rem(self.col + self.cols - step, self.cols), self.half]
            self.pairs[step] = send(
                piece, piece, self.sems, (self.item, 1, step), "dp", sibling()
            )

    def land(self):
        for step in range(1, self.cols):
            self.pairs[step].wait_recv()

    def sent(self):
        for copies in (self.lines, self.pairs):
            for copy in copies.values():
                copy.wait_send()


def front_kernel(*refs):
    (own_in, own_grad, own_out, query, key, value, gate, up) = refs[:8]
    (attn_norm, gains, cosine, sine, begins) = refs[8:13]
    (in_all, grad_all, out_all, cat_all, gate_all, up_all, slot_all) = refs[13:20]
    (first, sums, query_rot, key_rot, value_low, low_rows, totals) = refs[20:27]
    (slot_part, gate_part, up_part) = refs[27:30]
    gather_sems, swap_sems, pair_sems = refs[30:32], refs[32:34], refs[34:36]
    rows, cols = lax.axis_size("row"), lax.axis_size("col")
    row, col = lax.axis_index("row"), lax.axis_index("col")
    half = lax.rem(lax.axis_index("dp"), 2)
    near, far = neighbours()
    length, head_dim = query_rot.shape
    width = own_in.shape[1]
    local = own_in.shape[0]
    block = length // rows

    def split(ref):
        count = ref.shape[2] // 2
        return (
            lambda r, c: ref.at[r, c],
            lambda r, c, k: ref.at[r, c, pl.ds(k * count, count)],
        )

    greet()
    inputs = Gather(own_in, *split(in_all), gather_sems, 0)
    inputs.line()
    inputs.plane(0)
    height = query.shape[0] // 2
    for place in range(cols):
        for piece in range(2):
            lines = slice(piece * height, (piece + 1) * height)
            lanes = slice(place // 2 * head_dim, (place // 2 + 1) * head_dim)
            slot_part[place, piece, :, :head_dim] = query[
                lines, place * head_dim : (place + 1) * head_dim
            ]
            slot_part[place, piece, :, head_dim : 2 * head_dim] = key[lines, lanes]
            slot_part[place, piece, :, 2 * head_dim :] = value[lines, lanes]
    slots = Swap(slot_part, slot_all, swap_sems, 0)
    slots.line()
    slot_all[col] = slot_part[col]
    in_all[row, col] = own_in[...]
    for step in range(1, cols):
        inputs.plane(step)
    hidden = gate.shape[1] // cols
    for source, part in ((gate, gate_part), (up, up_part)):
        for place in range(cols):
            for piece in range(2):
                part[place, piece] = source[
                    piece * height : (piece + 1) * height, place * hidden : (place + 1) * hidden
                ]
    slots.relay()
    inputs.relay(0)
    grads = Gather(own_grad, *split(grad_all), gather_sems, 1)
    grads.line()
    inputs.relay(1)
    wide = [Swap(gate_part, gate_all, swap_sems, 1), Swap(up_part, up_all, swap_sems, 2)]
    for swap in wide:
        swap.line()
    inputs.relay(2)
    count = own_out.shape[1] // 2
    outs = Gather(
        own_out.at[half],
        lambda r, c: out_all.at[r, c, half],
        lambda r, c, k: out_all.at[r, c, half, pl.ds(k * count, count)],
        gather_sems,
        2,
    )
    outs.line()
    inputs.relay(3)
    grads.plane(0)
    outs.plane(0)
    gate_all[col] = gate_part[col]
    up_all[col] = up_part[col]
    grad_all[row, col] = own_grad[...]
    out_all[row, col] = own_out[...]
    slots.land()

    def project(place):
        for c in range(cols):
            values = in_all[place, c].astype(jnp.float32)
            normed = head_norm(values, attn_norm[...])[0]
            lines = pl.ds(pl.multiple_of(place * block + c * local, local), local)
            first[lines, :] = normed.astype(jnp.bfloat16)
        lines = pl.ds(pl.multiple_of(place * block, block), block)
        sums[lines, :] = dot(first[lines, :], slot_all[...].reshape(width, 3 * head_dim))

    project(row)
    project(near)
    project(far)
    for step in range(1, cols):
        grads.plane(step)
    for step in range(cols):
        inputs.land(step)
    project(lax.rem(near + rows // 2, rows))
    for step in range(1, cols):
        outs.plane(step)
    for place, target in ((0, query_rot), (1, key_rot)):
        normed = head_norm(
            sums[:, place * head_dim : (place + 1) * head_dim], gains[place : place + 1, :]
        )[0]
        target[...] = (normed * cosine[...] + swap_halves(normed) * sine[...]).astype(jnp.bfloat16)
    value_low[...] = sums[:, 2 * head_dim : 3 * head_dim].astype(jnp.bfloat16)

    def cat(part):
        places = pl.ds(part * (rows // 2), rows // 2)
        return Gather(
            cat_all.at[places, row, col],
            lambda r, c: cat_all.at[places, r, c],
            lambda r, c, k: cat_all.at[places, r, c, pl.ds(k * head_dim // 2, head_dim // 2)],
            gather_sems,
            3 + part,
        )

    cats = []
    for offset, low, _ in spans(length, length // 2, block):
        number = offset // block
        lines, keys = slice(offset, offset + block), slice(low, offset + block)
        probability, total = block_probability(
            query_rot[lines, :], key_rot[keys, :], begins[lines, :], offset, low, None
        )
        totals[lines, :] = total
        low_rows[lines, :] = dot(probability, value_low[keys, :]).astype(jnp.bfloat16)
        cat_all[number, row, col] = dot(value_low[keys, :], probability, 0, 1).astype(jnp.bfloat16)
        if 2 * (number + 1) % rows == 0:
            cats.append(cat(2 * (number + 1) // rows - 1))
            cats[-1].line()
            cats[-1].plane(0)
        if number == 0:
            for swap in wide:
                swap.relay()
            grads.relay(0)
            grads.relay(1)
        if number == 1:
            grads.relay(2)
            grads.relay(3)
        if number == 2:
            for step in range(cols):
                outs.relay(step)
            for step in range(1, cols):
                cats[0].plane(step)
    for step in range(1, cols):
        cats[1].plane(step)
    for gather in cats:
        for step in range(cols):
            gather.relay(step)
    pairs = []
    for step in range(cols):
        outs.land(step)
    for number, place in enumerate((near, far, lax.rem(near + rows // 2, rows))):
        piece = out_all.at[place, :, half]
        pairs.append(send(piece, piece, pair_sems, (number,), "dp", sibling()))
    for step in range(1, cols):
        piece = out_all.at[row, lax.rem(col + cols - step, cols), half]
        pairs.append(send(piece, piece, pair_sems, (2 + step,), "dp", sibling()))
    for swap in wide:
        swap.land()
    for gather in [grads] + cats:
        for step in range(cols):
            gather.land(step)
    for copy in pairs:
        copy.wait()
    for item in [inputs, grads, outs, slots] + wide + cats:
        item.sent()


def front(own_in, own_grad, own_out, query, key, value, gate, up, attn_norm, gains, tables, number):
    rows, cols = lax.axis_size("row"), lax.axis_size("col")
    local, width = own_in.shape
    length, head_dim = local * rows * cols, gains.shape[1]
    hidden, height = gate.shape[1] // cols, gate.shape[0] // 2
    low = jnp.bfloat16
    blocks = jax.ShapeDtypeStruct((rows, cols, local, width), low)
    halves = own_out.shape[0] // 2
    wide = (cols, 2, height, hidden)
    slot = (cols, 2, height, 3 * head_dim)
    shape = jax.ShapeDtypeStruct
    head_rows = shape((length, head_dim), low)
    outs = [
        blocks,
        blocks,
        shape((rows, cols, 2, halves, width), low),
        shape((rows, rows, cols, head_dim, length // rows), low),
        shape(wide, low),
        shape(wide, low),
        shape(slot, low),
        shape((length, width), low),
        shape((length, 3 * head_dim), jnp.float32),
        head_rows,
        head_rows,
        head_rows,
        head_rows,
        shape((length, 1), jnp.float32),
    ]
    scratch = [pltpu.VMEM(slot, low), pltpu.VMEM(wide, low), pltpu.VMEM(wide, low)]
    scratch += dma(5, 5, cols) + dma(3, 2, cols) + dma(2 + cols)
    args = [own_in, own_grad, own_out.reshape(2, halves, width), query, key, value, gate, up]
    args += [attn_norm.reshape(1, width), gains] + list(tables)
    return call_kernel(front_kernel, args, outs, scratch, number)


class Reduce:
    def __init__(self, part, relayed, planed, staged, lined, result, sems, item):
        self.part, self.relayed, self.planed = part, relayed, planed
        self.staged, self.lined, self.result = staged, lined, result
        self.sems, self.item = sems, item
        self.cols, self.col = lax.axis_size("col"), lax.axis_index("col")
        self.row = lax.axis_index("row")
        self.near, self.far = neighbours()
        self.cross = lax.rem(self.near + lax.axis_size("row") // 2, lax.axis_size("row"))
        self.count = part.shape[2] // 2
        self.relays, self.planes, self.lines = [], [], []

    def first(self):
        for kind, peer in ((0, self.near), (1, self.far)):
            self.relays.append(
                send(
                    self.part.at[self.cross, :, pl.ds(kind * self.count, self.count)],
                    self.relayed.at[kind],
                    self.sems,
                    (self.item, 1 + kind, 0),
                    "row",
                    peer,
                )
            )

    def toward(self, kind):
        peer, came = (self.near, self.far)[kind], 1 - kind
        self.relays[came].wait_recv()
        lines = slice(came * self.count, (came + 1) * self.count)
        self.part[peer, :, lines] = (
            self.part[peer, :, lines].astype(jnp.float32)
            + self.relayed[came].astype(jnp.float32)
        ).astype(jnp.bfloat16)
        self.planes.append(
            send(
                self.part.at[peer],
                self.planed.at[kind],
                self.sems,
                (self.item, 3 + kind, 0),
                "row",
                peer,
            )
        )

    def total(self, place):
        summed = self.part[self.row, place].astype(jnp.float32)
        for kind in range(2):
            summed = summed + self.planed[kind, place].astype(jnp.float32)
        return summed

    def own(self):
        for copy in self.planes:
            copy.wait_recv()
        for step in range(1, self.cols):
            place = lax.rem(self.col + step, self.cols)
            self.staged[step] = self.total(place).astype(jnp.bfloat16)
            self.lines.append(
                send(
                    self.staged.at[step],
                    self.lined.at[step],
                    self.sems,
                    (self.item, 0, step),
                    "col",
                    place,
                )
            )
        self.result[...] = self.total(self.col)

    def last(self):
        for step in range(1, self.cols):
            self.lines[step - 1].wait_recv()
            self.result[...] += self.lined[step].astype(jnp.float32)

    def sent(self):
        for copy in self.relays + self.planes + self.lines:
            copy.wait_send()


def reduce_scratch(rows, cols, local, width):
    low = jnp.bfloat16
    return [
        pltpu.VMEM((2, cols, local // 2, width), low),
        pltpu.VMEM((2, cols, local, width), low),
        pltpu.VMEM((cols, local, width), low),
        pltpu.VMEM((cols, local, width), low),
    ]


def hidden_kernel(*refs):
    in_all, grad_all, out_all, cat_all, gate_all, up_all, down, ffn_norm = refs[:8]
    act_own, down_own, middle_own = refs[8:11]
    second_all, hidden_all, gate_low_all, up_low_all = refs[11:15]
    act_part, down_part, middle_block = refs[15:18]
    act_scratch, down_scratch, sems = refs[18:22], refs[22:26], refs[26:28]
    rows, cols = lax.axis_size("row"), lax.axis_size("col")
    row, col = lax.axis_index("row"), lax.axis_index("col")
    near, far = neighbours()
    cross = lax.rem(near + rows // 2, rows)
    local, width = in_all.shape[2:]
    block = cols * local
    greet(pair=False)
    act_sum = Reduce(act_part, *act_scratch, act_own, sems, 0)
    down_sum = Reduce(down_part, *down_scratch, down_own, sems, 1)

    def work(place):
        mixed = dot(cat_all[place].reshape(width, block), out_all[...].reshape(width, width), 0, 0)
        middle = in_all[place].reshape(block, width).astype(jnp.float32) + mixed
        middle_block[...] = middle
        second = head_norm(middle, ffn_norm[...])[0].astype(jnp.bfloat16)
        second_all[place] = second
        gate_weight = gate_all[...].reshape(width, gate_all.shape[-1])
        up_weight = up_all[...].reshape(width, up_all.shape[-1])
        gating, upward = dot(second, gate_weight), dot(second, up_weight)
        hidden_grad = dot(grad_all[place].reshape(block, width), down[...], 1, 1)
        sigmoid_gate = jax.nn.sigmoid(gating)
        activated = gating * sigmoid_gate
        hidden = (activated * upward).astype(jnp.bfloat16)
        gate_low = (
            hidden_grad * upward * sigmoid_gate * (1.0 + gating * (1.0 - sigmoid_gate))
        ).astype(jnp.bfloat16)
        up_low = (hidden_grad * activated).astype(jnp.bfloat16)
        hidden_all[place] = hidden
        gate_low_all[place] = gate_low
        up_low_all[place] = up_low
        act = dot(gate_low, gate_weight, 1, 1) + dot(up_low, up_weight, 1, 1)
        act_part[place] = act.astype(jnp.bfloat16).reshape(cols, local, width)
        down_part[place] = (
            dot(hidden, down[...]).astype(jnp.bfloat16).reshape(cols, local, width)
        )

    sums = (act_sum, down_sum)
    work(cross)
    for item in sums:
        item.first()
    work(near)
    for item in sums:
        item.toward(0)
    work(far)
    for item in sums:
        item.toward(1)
    work(row)
    lines = pl.ds(pl.multiple_of(col * local, local), local)
    middle_own[...] = middle_block[lines, :]
    for item in sums:
        item.own()
    for item in sums:
        item.last()
    for item in sums:
        item.sent()


def hidden_pass(in_all, grad_all, out_all, cat_all, gate_all, up_all, down, ffn_norm, number):
    rows, cols, local, width = in_all.shape
    block, hidden = cols * local, down.shape[0]
    shape = jax.ShapeDtypeStruct
    own, low = shape((local, width), jnp.float32), jnp.bfloat16
    part = shape((rows, block, hidden), low)
    outs = [own, own, own, shape((rows, block, width), low), part, part, part]
    parts = pltpu.VMEM((rows, cols, local, width), low)
    scratch = [parts, parts, pltpu.VMEM((block, width), jnp.float32)]
    scratch += reduce_scratch(rows, cols, local, width) * 2 + dma(2, 5, cols)
    args = [in_all, grad_all, out_all, cat_all, gate_all, up_all, down, ffn_norm.reshape(1, width)]
    return call_kernel(hidden_kernel, args, outs, scratch, number)


def start_swaps(ins, outs, sems):
    cols, own = lax.axis_size("col"), lax.axis_index("col")
    copies = []
    for number in range(len(ins)):
        for step in range(1, cols):
            peer = lax.rem(own + step, cols)
            copies.append(
                send(ins[number].at[peer], outs[number].at[own], sems, (number, step), "col", peer)
            )
        outs[number][own] = ins[number][own]
    return copies


def call_kernel(body, args, outs, scratch, number):
    vmem = pl.BlockSpec(memory_space=pltpu.VMEM)
    return pl.pallas_call(
        body,
        out_shape=outs,
        in_specs=[vmem] * len(args),
        out_specs=[vmem] * len(outs),
        scratch_shapes=scratch,
        compiler_params=pltpu.CompilerParams(
            collective_id=number, has_side_effects=True, vmem_limit_bytes=VMEM_LIMIT
        ),
    )(*args)


def dma(*shape):
    return [pltpu.SemaphoreType.DMA(shape), pltpu.SemaphoreType.DMA(shape)]


def exchange(gathers, swaps, number):
    rows, cols = lax.axis_size("row"), lax.axis_size("col")
    many, total = len(gathers), len(gathers) + len(swaps)

    def body(*refs):
        ins, outs = refs[:total], refs[total : 2 * total]
        sems, swap_sems = refs[2 * total : 2 * total + 2], refs[2 * total + 2 :]
        row, col = lax.axis_index("row"), lax.axis_index("col")
        enter(("row", "col"))
        across, copies = {}, []
        for item in range(many):
            for step in range(1, cols):
                across[item, step] = send(
                    ins[item],
                    outs[item].at[row, col],
                    sems,
                    (item, 0, step),
                    "col",
                    lax.rem(col + step, cols),
                )
        for item in range(many):
            for turn in range(1, rows):
                copies.append(
                    send(
                        ins[item],
                        outs[item].at[row, col],
                        sems,
                        (item, turn, 0),
                        "row",
                        lax.rem(row + turn, rows),
                    )
                )
        copies += start_swaps(ins[many:], outs[many:], swap_sems)
        for item in range(many):
            outs[item][row, col] = ins[item][...]
        for step in range(1, cols):
            origin = lax.rem(col + cols - step, cols)
            for item in range(many):
                across[item, step].wait()
                block = outs[item].at[row, origin]
                for turn in range(1, rows):
                    copies.append(
                        send(
                            block,
                            block,
                            sems,
                            (item, turn, step),
                            "row",
                            lax.rem(row + turn, rows),
                        )
                    )
        for copy in copies:
            copy.wait()

    outs = [jax.ShapeDtypeStruct((rows, cols) + g.shape, g.dtype) for g in gathers]
    outs += [jax.ShapeDtypeStruct(w.shape, w.dtype) for w in swaps]
    scratch = dma(many, rows, cols) + dma(max(len(swaps), 1), cols)
    return call_kernel(body, list(gathers) + list(swaps), outs, scratch, number)


def reduce_rows(partial_value, swaps, number):
    rows, cols = lax.axis_size("row"), lax.axis_size("col")
    local = partial_value.shape[0] // (rows * cols)
    width = partial_value.shape[1]
    shaped = partial_value.astype(jnp.bfloat16).reshape(rows, cols, local, width)
    many = len(swaps)

    def body(*refs):
        part, ins = refs[0], refs[1 : 1 + many]
        result, outs = refs[1 + many], refs[2 + many : 2 + 2 * many]
        first, staged, second = refs[2 + 2 * many : 5 + 2 * many]
        first_sems, second_sems = refs[5 + 2 * many : 7 + 2 * many], refs[7 + 2 * many : 9 + 2 * many]
        swap_sems = refs[9 + 2 * many :]
        row, col = lax.axis_index("row"), lax.axis_index("col")
        enter(("row", "col"))
        down, across = {}, []
        order = list(range(1, cols)) + [0]
        for step in order:
            block = lax.rem(col + step, cols)
            for turn in range(1, rows):
                peer = lax.rem(row + turn, rows)
                down[step, turn] = send(
                    part.at[peer, block],
                    first.at[turn, step],
                    first_sems,
                    (turn, step),
                    "row",
                    peer,
                )
        copies = start_swaps(ins, outs, swap_sems)
        for step in order:
            block = lax.rem(col + step, cols)
            summed = part[row, block].astype(jnp.float32)
            for turn in range(1, rows):
                down[step, turn].wait()
                summed = summed + first[turn, step].astype(jnp.float32)
            if step == 0:
                result[...] = summed
            else:
                staged[step] = summed.astype(jnp.bfloat16)
                across.append(
                    send(staged.at[step], second.at[step], second_sems, (step,), "col", block)
                )
        for step in range(1, cols):
            across[step - 1].wait()
            result[...] += second[step].astype(jnp.float32)
        for copy in copies:
            copy.wait()

    outs = [jax.ShapeDtypeStruct((local, width), jnp.float32)]
    outs += [jax.ShapeDtypeStruct(w.shape, w.dtype) for w in swaps]
    scratch = [
        pltpu.VMEM((rows, cols, local, width), jnp.bfloat16),
        pltpu.VMEM((cols, local, width), jnp.bfloat16),
        pltpu.VMEM((cols, local, width), jnp.bfloat16),
    ]
    scratch += dma(rows, cols) + dma(cols) + dma(max(many, 1), cols)
    return call_kernel(body, [shaped] + list(swaps), outs, scratch, number)


def last_sums(group_value, widths, gains, number):
    sizes = [lax.axis_size(axis) for axis in ("dp", "row", "col")]

    def body(value, gain, *refs):
        value_outs, gain_out = refs[: len(widths)], refs[len(widths)]
        value_in, landed, held = refs[len(widths) + 1 : len(widths) + 4]
        sems = refs[len(widths) + 4 :]
        value_sems, gain_sems = sems[:2], sems[2:]
        enter(("dp", "row", "col"))
        copies, groups = [], lax.axis_size("dp")
        me = lax.axis_index("dp")
        for step in range(1, groups):
            copies.append(
                send(
                    value,
                    value_in.at[step],
                    value_sems,
                    (step,),
                    "dp",
                    lax.rem(me + step, groups),
                )
            )
        held[0] = gain[...]
        for stage, axis in enumerate(("dp", "row", "col")):
            size, own = lax.axis_size(axis), lax.axis_index(axis)
            sent = [
                send(
                    held.at[stage],
                    landed.at[stage, step],
                    gain_sems,
                    (stage, step),
                    axis,
                    lax.rem(own + step, size),
                )
                for step in range(1, size)
            ]
            landed[stage, 0] = held[stage]
            for copy in sent:
                copy.wait()
            total = None
            for place in range(size):
                term = landed[stage, lax.rem(own - place + size, size)]
                total = term if total is None else total + term
            held[stage + 1] = total
        gain_out[...] = held[3]
        for copy in copies:
            copy.wait()
        total = value[...]
        for step in range(1, groups):
            total = total + value_in[step]
        begin = 0
        for size, value_out in zip(widths, value_outs):
            value_out[...] = total[:, begin : begin + size]
            begin += size

    outs = [jax.ShapeDtypeStruct((group_value.shape[0], size), jnp.float32) for size in widths]
    outs.append(jax.ShapeDtypeStruct(gains.shape, jnp.float32))
    scratch = [
        pltpu.VMEM((sizes[0],) + group_value.shape, jnp.float32),
        pltpu.VMEM((3, max(sizes)) + gains.shape, jnp.float32),
        pltpu.VMEM((4,) + gains.shape, jnp.float32),
    ]
    scratch += dma(sizes[0]) + dma(3, max(sizes))
    return call_kernel(body, [group_value, gains], outs, scratch, number)


def dot(left, right, left_dim=1, right_dim=0):
    return lax.dot_general(
        left,
        right,
        (((left_dim,), (right_dim,)), ((), ())),
        preferred_element_type=jnp.float32,
    )


def shards(
    block_input,
    seq_lengths,
    out_grad,
    attn_norm,
    query_weight,
    key_weight,
    value_weight,
    query_norm,
    key_norm,
    out_weight,
    ffn_norm,
    gate_weight,
    up_weight,
    down_weight,
):
    local_rows, width = block_input.shape
    head_dim = query_norm.shape[0]
    col_width = query_weight.shape[0]
    cols = lax.axis_size("col")
    length = local_rows * cols * lax.axis_size("row")
    hidden_width = gate_weight.shape[1] // cols
    residual = block_input.astype(jnp.float32)
    scale_in = head_norm(residual, attn_norm)[1]
    places = jnp.arange(length, dtype=jnp.int32)
    position = segment_info(seq_lengths[0], length)[1]
    begins = (places - position)[:, None]
    cosine, sine = rope_tables(position, head_dim)
    cosine = jnp.concatenate([cosine, cosine], axis=1)
    sine = jnp.concatenate([-sine, sine], axis=1)
    longest = length // 2
    head_gains = jnp.stack([query_norm, key_norm])
    (
        input_blocks,
        out_blocks,
        out_weight_blocks,
        cat_blocks,
        gate_blocks,
        up_blocks,
        slot_blocks,
        first_full,
        own_sums,
        query_rot,
        key_rot,
        value_low,
        attn_low,
        log_total,
    ) = front(
        block_input,
        out_grad,
        out_weight,
        query_weight,
        key_weight,
        value_weight,
        gate_weight,
        up_weight,
        attn_norm,
        head_gains,
        (cosine, sine, begins),
        0,
    )
    act_grad2, down_sums, middle_own, second_blocks, hidden, gate_low, up_low = hidden_pass(
        input_blocks,
        out_blocks,
        out_weight_blocks,
        cat_blocks,
        gate_blocks,
        up_blocks,
        down_weight,
        ffn_norm,
        2,
    )
    slot_weight = slot_blocks.reshape(width, 3 * head_dim)
    out_full = out_blocks.reshape(length, width)
    second_full = second_blocks.reshape(length, width)
    hidden = hidden.reshape(length, -1)
    wide_low = jnp.concatenate(
        [gate_low.reshape(length, -1), up_low.reshape(length, -1)], axis=1
    )
    grad_down = dot(hidden, out_full, 0, 0)
    wide_grad = dot(second_full, wide_low, 0, 0).astype(jnp.bfloat16)
    scale_mid = head_norm(middle_own, ffn_norm)[1]
    middle_back, ffn_gain_grad = head_norm_back(
        act_grad2, middle_own, scale_mid, ffn_norm
    )
    middle_grad = out_grad.astype(jnp.float32) + middle_back
    middle_blocks, wide_grads = exchange(
        [middle_grad.astype(jnp.bfloat16)],
        [wide_grad.reshape(cols, col_width, 2 * hidden_width)],
        3,
    )
    middle_full = middle_blocks.reshape(length, width)
    grad_outweight = dot(attn_low, middle_full, 0, 0)
    cat_grad = dot(middle_full, out_weight, 1, 1).astype(jnp.bfloat16)
    wide_shape = jax.ShapeDtypeStruct(gate_weight.shape, jnp.float32)
    grad_gate, grad_up = local_kernel(
        functools.partial(open_wide_kernel, cols), [wide_grads], [wide_shape, wide_shape]
    )
    block_output = (middle_own + down_sums).astype(jnp.bfloat16)
    accumulator = pltpu.VMEM((length, head_dim), jnp.float32)
    own_slot, head_gain_grads = local_kernel(
        functools.partial(attend_back_kernel, longest),
        [query_rot, key_rot, value_low, attn_low, log_total, cat_grad]
        + [own_sums, head_gains, cosine, sine, begins],
        [
            jax.ShapeDtypeStruct((length, 3 * head_dim), jnp.bfloat16),
            jax.ShapeDtypeStruct((2, head_dim), jnp.float32),
        ],
        [accumulator] * 3,
    )
    grad_outweight, grad_gate, grad_up, grad_down = lax.psum(
        (grad_outweight, grad_gate, grad_up, grad_down), "dp"
    )
    slot_grad = dot(first_full, own_slot, 0, 0).astype(jnp.bfloat16)
    act_grad1, slot_grads = reduce_rows(
        dot(own_slot, slot_weight, 1, 1),
        [slot_grad.reshape(cols, col_width, 3 * head_dim)],
        4,
    )
    widths = (cols * head_dim, cols // 2 * head_dim, cols // 2 * head_dim)
    (slot_sums,) = local_kernel(
        functools.partial(open_slots_kernel, cols, head_dim),
        [slot_grads],
        [jax.ShapeDtypeStruct((col_width, sum(widths)), jnp.float32)],
    )
    input_back, attn_gain_grad = head_norm_back(act_grad1, residual, scale_in, attn_norm)
    input_grad = middle_grad + input_back
    flat_gains = jnp.concatenate(
        [head_gain_grads.reshape(-1), jnp.zeros((width - 2 * head_dim,), jnp.float32)]
    )
    gains = jnp.stack([attn_gain_grad, ffn_gain_grad, flat_gains])
    gains = jnp.concatenate([gains, jnp.zeros((5, width), jnp.float32)], axis=0)
    grad_query, grad_key, grad_value, gain_sums = last_sums(slot_sums, widths, gains, 5)
    return (
        block_output,
        input_grad,
        gain_sums[0],
        grad_query,
        grad_key,
        grad_value,
        gain_sums[2, :head_dim],
        gain_sums[2, head_dim : 2 * head_dim],
        grad_outweight,
        gain_sums[1],
        grad_gate,
        grad_up,
        grad_down,
    )


def solution(mesh):
    placed = (
        P(("dp", "row", "col"), None),
        P("dp", None),
        P(("dp", "row", "col"), None),
        P(),
        P("col", "row"),
        P("col", "row"),
        P("col", "row"),
        P(),
        P(),
        P(("row", "col"), None),
        P(),
        P("col", "row"),
        P("col", "row"),
        P(("row", "col"), None),
    )
    return jax.shard_map(
        shards,
        mesh=mesh,
        in_specs=placed,
        out_specs=(
            P(("dp", "row", "col"), None),
            P(("dp", "row", "col"), None),
            P(),
            P("col", "row"),
            P("col", "row"),
            P("col", "row"),
            P(),
            P(),
            P(("row", "col"), None),
            P(),
            P("col", "row"),
            P("col", "row"),
            P(("row", "col"), None),
        ),
        check_vma=False,
    )
```

```python
import functools
import math

import jax
import jax.numpy as jnp
from jax import lax
from jax.experimental import pallas as pl
from jax.experimental.pallas import tpu as pltpu
from jax.sharding import PartitionSpec as P

EPSILON = 1e-05
THETA = 1000000.0


def segment_info(seq_lengths, length):
    order = jnp.arange(seq_lengths.shape[0], dtype=jnp.int32)
    up_to = order[:, None] <= order[None, :]
    end_points = jnp.sum(jnp.where(up_to, seq_lengths[:, None], 0), axis=0)
    places = jnp.arange(length, dtype=jnp.int32)
    passed = (places[:, None] >= end_points[None, :]).astype(jnp.int32)
    segment = jnp.sum(passed, axis=1)
    begins = jnp.sum(passed * seq_lengths[None, :], axis=1)
    return (segment, places - begins)


def rope_tables(position, width):
    half_width = width // 2
    exponent = jnp.arange(half_width, dtype=jnp.float32) * (2.0 / width)
    frequency = jnp.exp(-math.log(THETA) * exponent)
    angles = position.astype(jnp.float32)[:, None] * frequency[None, :]
    return (jnp.cos(angles), jnp.sin(angles))


def head_norm(values, gain_vec):
    inv_rms = lax.rsqrt(jnp.mean(values * values, axis=-1, keepdims=True) + EPSILON)
    return (values * inv_rms * gain_vec, inv_rms)


def head_norm_back(cotangent, values, inv_rms, gain_vec):
    normed = values * inv_rms
    weighted = cotangent * gain_vec
    gain_grad = jnp.sum(cotangent * normed, axis=0)
    inner_mean = jnp.mean(weighted * normed, axis=-1, keepdims=True)
    return (inv_rms * (weighted - normed * inner_mean), gain_grad)


def swap_halves(values):
    half_width = values.shape[-1] // 2
    return jnp.concatenate([values[:, half_width:], values[:, :half_width]], axis=1)


def block_probability(query_block, key_rows, begins, offset, low, shift):
    score_scale = 1.0 / math.sqrt(query_block.shape[1])
    scores = dot(query_block, key_rows, 1, 1) * score_scale
    places = low + lax.broadcasted_iota(jnp.int32, scores.shape, 1)
    row_places = offset + lax.broadcasted_iota(jnp.int32, scores.shape, 0)
    allowed = (places >= begins) & (places <= row_places)
    if shift is None:
        shift = jnp.log(jnp.sum(jnp.where(allowed, jnp.exp(scores), 0.0), axis=1, keepdims=True))
    probability = jnp.where(allowed, jnp.exp(scores - shift), 0.0).astype(jnp.bfloat16)
    return probability, shift


def spans(length, longest, block):
    return [
        (offset, max(0, (offset - longest) // 128 * 128), block)
        for offset in range(0, length, block)
    ]


def local_kernel(body, args, outs, scratch=()):
    vmem = pl.BlockSpec(memory_space=pltpu.VMEM)
    return pl.pallas_call(
        body,
        out_shape=outs,
        in_specs=[vmem] * len(args),
        out_specs=[vmem] * len(outs),
        scratch_shapes=list(scratch),
    )(*args)


MESH = pl.DeviceIdType.MESH
VMEM_LIMIT = 56 * 1024 * 1024


def send(source, target, sems, place, axis, index):
    copy = pltpu.make_async_remote_copy(
        src_ref=source,
        dst_ref=target,
        send_sem=sems[0].at[place],
        recv_sem=sems[1].at[place],
        device_id={axis: index},
        device_id_type=MESH,
    )
    copy.start()
    return copy


def neighbours():
    rows, row = lax.axis_size("row"), lax.axis_index("row")
    near = row + 1 - 2 * lax.rem(row, 2)
    far = lax.rem(row + rows // 2, rows)
    return near, far


def sibling():
    own = lax.axis_index("dp")
    return own + 1 - 2 * lax.rem(own, 2)


def greet(corner=False):
    cols, col = lax.axis_size("col"), lax.axis_index("col")
    near, far = neighbours()
    peers = [("col", lax.rem(col + step, cols)) for step in range(1, cols)]
    peers += [("row", near), ("row", far), ("dp", sibling())]
    if corner:
        peers.append(("row", lax.rem(near + lax.axis_size("row") // 2, lax.axis_size("row"))))
    barrier = pltpu.get_barrier_semaphore()
    for axis, index in peers:
        pl.semaphore_signal(barrier, inc=1, device_id={axis: index}, device_id_type=MESH)
    pl.semaphore_wait(barrier, len(peers))


class Gather:
    def __init__(self, source, block, part, sems, item):
        self.source, self.block, self.part = source, block, part
        self.sems, self.item = sems, item
        self.cols, self.col = lax.axis_size("col"), lax.axis_index("col")
        self.row = lax.axis_index("row")
        self.near, self.far = neighbours()
        self.lines, self.planes, self.relays = {}, {}, {}

    def origin(self, step):
        return lax.rem(self.col + self.cols - step, self.cols)

    def line(self):
        for step in range(1, self.cols):
            self.lines[step] = send(
                self.source,
                self.block(self.row, self.col),
                self.sems,
                (self.item, 0, step),
                "col",
                lax.rem(self.col + step, self.cols),
            )

    def plane(self, step):
        target = self.block(self.row, self.origin(step))
        if step:
            self.lines[step].wait_recv()
        for kind, peer in ((1, self.near), (2, self.far)):
            self.planes[step, kind] = send(
                target if step else self.source,
                target,
                self.sems,
                (self.item, kind, step),
                "row",
                peer,
            )

    def relay(self, step):
        for kind, source, peer in ((1, self.near, self.far), (2, self.far, self.near)):
            self.planes[step, kind].wait_recv()
            piece = self.part(source, self.origin(step), kind - 1)
            self.relays[step, kind] = send(
                piece, piece, self.sems, (self.item, kind + 2, step), "row", peer
            )

    def land(self, step):
        for kind in (1, 2):
            self.relays[step, kind].wait_recv()

    def sent(self):
        for copies in (self.lines, self.planes, self.relays):
            for copy in copies.values():
                copy.wait_send()


class Swap:
    def __init__(self, source, target, sems, item, whole=False):
        self.source, self.target, self.sems, self.item = source, target, sems, item
        self.cols, self.col = lax.axis_size("col"), lax.axis_index("col")
        self.half = lax.rem(lax.axis_index("dp"), 2)
        self.lines, self.pairs, self.first = {}, {}, 0 if whole else 1

    def line(self):
        for step in range(1, self.cols):
            peer = lax.rem(self.col + step, self.cols)
            self.lines[step] = send(
                self.source(peer, self.half),
                self.target.at[self.col, self.half],
                self.sems,
                (self.item, 0, step),
                "col",
                peer,
            )

    def relay(self):
        for step in range(self.first, self.cols):
            if step:
                self.lines[step].wait_recv()
            piece = self.target.at[lax.rem(self.col + self.cols - step, self.cols), self.half]
            self.pairs[step] = send(
                piece, piece, self.sems, (self.item, 1, step), "dp", sibling()
            )

    def land(self):
        for copy in self.pairs.values():
            copy.wait_recv()

    def sent(self):
        for copies in (self.lines, self.pairs):
            for copy in copies.values():
                copy.wait_send()


def front_kernel(*refs):
    (own_in, own_grad, own_out, query, key, value, gate, up) = refs[:8]
    (attn_norm, gains, cosine, sine, begins) = refs[8:13]
    (in_all, grad_all, out_all, cat_all, gate_all, up_all, slot_all) = refs[13:20]
    (first, sums, query_rot, key_rot, value_low, low_rows, totals) = refs[20:27]
    (slot_part, gate_part, up_part) = refs[27:30]
    gather_sems, swap_sems, pair_sems = refs[30:32], refs[32:34], refs[34:36]
    rows, cols = lax.axis_size("row"), lax.axis_size("col")
    row, col = lax.axis_index("row"), lax.axis_index("col")
    half = lax.rem(lax.axis_index("dp"), 2)
    near, far = neighbours()
    length, head_dim = query_rot.shape
    width = own_in.shape[1]
    local = own_in.shape[0]
    block = length // rows

    def split(ref):
        count = ref.shape[2] // 2
        return (
            lambda r, c: ref.at[r, c],
            lambda r, c, k: ref.at[r, c, pl.ds(k * count, count)],
        )

    greet()
    inputs = Gather(own_in, *split(in_all), gather_sems, 0)
    inputs.line()
    inputs.plane(0)
    height = query.shape[0] // 2
    for place in range(cols):
        for piece in range(2):
            lines = slice(piece * height, (piece + 1) * height)
            lanes = slice(place // 2 * head_dim, (place // 2 + 1) * head_dim)
            slot_part[place, piece, :, :head_dim] = query[
                lines, place * head_dim : (place + 1) * head_dim
            ]
            slot_part[place, piece, :, head_dim : 2 * head_dim] = key[lines, lanes]
            slot_part[place, piece, :, 2 * head_dim :] = value[lines, lanes]
    slots = Swap(lambda c, h: slot_part.at[c, h], slot_all, swap_sems, 0)
    slots.line()
    slot_all[col] = slot_part[col]
    in_all[row, col] = own_in[...]
    for step in range(1, cols):
        inputs.plane(step)
    hidden = gate.shape[1] // cols
    for source, part in ((gate, gate_part), (up, up_part)):
        for place in range(cols):
            for piece in range(2):
                part[place, piece] = source[
                    piece * height : (piece + 1) * height, place * hidden : (place + 1) * hidden
                ]
    slots.relay()
    inputs.relay(0)
    grads = Gather(own_grad, *split(grad_all), gather_sems, 1)
    grads.line()
    inputs.relay(1)
    wide = [
        Swap(lambda c, h: gate_part.at[c, h], gate_all, swap_sems, 1),
        Swap(lambda c, h: up_part.at[c, h], up_all, swap_sems, 2),
    ]
    for swap in wide:
        swap.line()
    inputs.relay(2)
    count = own_out.shape[1] // 2
    outs = Gather(
        own_out.at[half],
        lambda r, c: out_all.at[r, c, half],
        lambda r, c, k: out_all.at[r, c, half, pl.ds(k * count, count)],
        gather_sems,
        2,
    )
    outs.line()
    inputs.relay(3)
    grads.plane(0)
    outs.plane(0)
    gate_all[col] = gate_part[col]
    up_all[col] = up_part[col]
    grad_all[row, col] = own_grad[...]
    out_all[row, col] = own_out[...]
    slots.land()

    def project(place):
        for c in range(cols):
            values = in_all[place, c].astype(jnp.float32)
            normed = head_norm(values, attn_norm[...])[0]
            first[place, c] = normed.astype(jnp.bfloat16)
        lines = pl.ds(pl.multiple_of(place * block, block), block)
        sums[lines, :] = dot(
            first[place].reshape(block, width), slot_all[...].reshape(width, 3 * head_dim)
        )

    project(row)
    project(near)
    project(far)
    for step in range(1, cols):
        grads.plane(step)
    for step in range(cols):
        inputs.land(step)
    project(lax.rem(near + rows // 2, rows))
    for step in range(1, cols):
        outs.plane(step)
    for place, target in ((0, query_rot), (1, key_rot)):
        normed = head_norm(
            sums[:, place * head_dim : (place + 1) * head_dim], gains[place : place + 1, :]
        )[0]
        target[...] = (normed * cosine[...] + swap_halves(normed) * sine[...]).astype(jnp.bfloat16)
    value_low[...] = sums[:, 2 * head_dim : 3 * head_dim].astype(jnp.bfloat16)

    def cat(part):
        places = pl.ds(part * (rows // 2), rows // 2)
        return Gather(
            cat_all.at[places, row, col],
            lambda r, c: cat_all.at[places, r, c],
            lambda r, c, k: cat_all.at[places, r, c, pl.ds(k * head_dim // 2, head_dim // 2)],
            gather_sems,
            3 + part,
        )

    cats = []
    for offset, low, _ in spans(length, length // 2, block):
        number = offset // block
        lines, keys = slice(offset, offset + block), slice(low, offset + block)
        probability, total = block_probability(
            query_rot[lines, :], key_rot[keys, :], begins[lines, :], offset, low, None
        )
        totals[lines, :] = total
        low_rows[lines, :] = dot(probability, value_low[keys, :]).astype(jnp.bfloat16)
        cat_all[number, row, col] = dot(value_low[keys, :], probability, 0, 1).astype(jnp.bfloat16)
        if 2 * (number + 1) % rows == 0:
            cats.append(cat(2 * (number + 1) // rows - 1))
            cats[-1].line()
            cats[-1].plane(0)
        if number == 0:
            for swap in wide:
                swap.relay()
            grads.relay(0)
            grads.relay(1)
        if number == 1:
            grads.relay(2)
            grads.relay(3)
        if number == 2:
            for step in range(cols):
                outs.relay(step)
            for step in range(1, cols):
                cats[0].plane(step)
    for step in range(1, cols):
        cats[1].plane(step)
    for gather in cats:
        for step in range(cols):
            gather.relay(step)
    pairs = []
    for step in range(cols):
        outs.land(step)
    for number, place in enumerate((near, far, lax.rem(near + rows // 2, rows))):
        piece = out_all.at[place, :, half]
        pairs.append(send(piece, piece, pair_sems, (number,), "dp", sibling()))
    for step in range(1, cols):
        piece = out_all.at[row, lax.rem(col + cols - step, cols), half]
        pairs.append(send(piece, piece, pair_sems, (2 + step,), "dp", sibling()))
    for swap in wide:
        swap.land()
    for gather in [grads] + cats:
        for step in range(cols):
            gather.land(step)
    for copy in pairs:
        copy.wait()
    for item in [inputs, grads, outs, slots] + wide + cats:
        item.sent()


def front(own_in, own_grad, own_out, query, key, value, gate, up, attn_norm, gains, tables, number):
    rows, cols = lax.axis_size("row"), lax.axis_size("col")
    local, width = own_in.shape
    length, head_dim = local * rows * cols, gains.shape[1]
    hidden, height = gate.shape[1] // cols, gate.shape[0] // 2
    low = jnp.bfloat16
    blocks = jax.ShapeDtypeStruct((rows, cols, local, width), low)
    halves = own_out.shape[0] // 2
    wide = (cols, 2, height, hidden)
    slot = (cols, 2, height, 3 * head_dim)
    shape = jax.ShapeDtypeStruct
    head_rows = shape((length, head_dim), low)
    outs = [
        blocks,
        blocks,
        shape((rows, cols, 2, halves, width), low),
        shape((rows, rows, cols, head_dim, length // rows), low),
        shape(wide, low),
        shape(wide, low),
        shape(slot, low),
        blocks,
        shape((length, 3 * head_dim), jnp.float32),
        head_rows,
        head_rows,
        head_rows,
        head_rows,
        shape((length, 1), jnp.float32),
    ]
    scratch = [pltpu.VMEM(slot, low), pltpu.VMEM(wide, low), pltpu.VMEM(wide, low)]
    scratch += dma(5, 5, cols) + dma(3, 2, cols) + dma(2 + cols)
    args = [own_in, own_grad, own_out.reshape(2, halves, width), query, key, value, gate, up]
    args += [attn_norm.reshape(1, width), gains] + list(tables)
    return call_kernel(front_kernel, args, outs, scratch, number)


class Reduce:
    def __init__(self, part, relayed, planed, staged, lined, result, sems, item):
        self.part, self.relayed, self.planed = part, relayed, planed
        self.staged, self.lined, self.result = staged, lined, result
        self.sems, self.item = sems, item
        self.cols = part.shape[1]
        self.col = lax.axis_index("col") if self.cols > 1 else 0
        self.row = lax.axis_index("row")
        self.near, self.far = neighbours()
        self.cross = lax.rem(self.near + lax.axis_size("row") // 2, lax.axis_size("row"))
        self.count = part.shape[2] // 2
        self.relays, self.planes, self.lines = [], [], []

    def first(self):
        for kind, peer in ((0, self.near), (1, self.far)):
            self.relays.append(
                send(
                    self.part.at[self.cross, :, pl.ds(kind * self.count, self.count)],
                    self.relayed.at[kind],
                    self.sems,
                    (self.item, 1 + kind, 0),
                    "row",
                    peer,
                )
            )

    def toward(self, kind):
        peer, came = (self.near, self.far)[kind], 1 - kind
        self.relays[came].wait_recv()
        lines = slice(came * self.count, (came + 1) * self.count)
        self.part[peer, :, lines] = (
            self.part[peer, :, lines].astype(jnp.float32)
            + self.relayed[came].astype(jnp.float32)
        ).astype(jnp.bfloat16)
        self.planes.append(
            send(
                self.part.at[peer],
                self.planed.at[kind],
                self.sems,
                (self.item, 3 + kind, 0),
                "row",
                peer,
            )
        )

    def total(self, place):
        summed = self.part[self.row, place].astype(jnp.float32)
        for kind in range(2):
            summed = summed + self.planed[kind, place].astype(jnp.float32)
        return summed

    def own(self):
        for copy in self.planes:
            copy.wait_recv()
        for step in range(1, self.cols):
            place = lax.rem(self.col + step, self.cols)
            self.staged[step] = self.total(place).astype(jnp.bfloat16)
            self.lines.append(
                send(
                    self.staged.at[step],
                    self.lined.at[step],
                    self.sems,
                    (self.item, 0, step),
                    "col",
                    place,
                )
            )
        self.result[...] = self.total(self.col)

    def last(self):
        for step in range(1, self.cols):
            self.lines[step - 1].wait_recv()
            self.result[...] += self.lined[step].astype(jnp.float32)

    def sent(self):
        for copy in self.relays + self.planes + self.lines:
            copy.wait_send()


def reduce_scratch(rows, cols, local, width):
    low = jnp.bfloat16
    return [
        pltpu.VMEM((2, cols, local // 2, width), low),
        pltpu.VMEM((2, cols, local, width), low),
        pltpu.VMEM((cols, local, width), low),
        pltpu.VMEM((cols, local, width), low),
    ]


def hidden_kernel(*refs):
    in_all, grad_all, out_all, cat_all, gate_all, up_all, down, ffn_norm = refs[:8]
    query, key, value = refs[8:11]
    act_own, middle_own, down_part, slot_all = refs[11:15]
    second_all, hidden_all, gate_low_all, up_low_all = refs[15:19]
    act_part, middle_block, slot_part = refs[19:22]
    act_scratch, sems, swap_sems = refs[22:26], refs[26:28], refs[28:30]
    rows, cols = lax.axis_size("row"), lax.axis_size("col")
    row, col = lax.axis_index("row"), lax.axis_index("col")
    near, far = neighbours()
    cross = lax.rem(near + rows // 2, rows)
    local, width = in_all.shape[2:]
    block = cols * local
    greet()
    height, begin = query.shape[0] // 2, 0
    for source in (query, key, value):
        lanes = slice(begin, begin + source.shape[1])
        for piece in range(2):
            slot_part[piece, :, lanes] = source[piece * height : (piece + 1) * height, :]
        begin += source.shape[1]
    slots = Swap(lambda c, h: slot_part.at[h], slot_all, swap_sems, 0)
    slots.line()
    slot_all[col] = slot_part[...]
    act_sum = Reduce(act_part, *act_scratch, act_own, sems, 0)

    def work(place):
        mixed = dot(cat_all[place].reshape(width, block), out_all[...].reshape(width, width), 0, 0)
        middle = in_all[place].reshape(block, width).astype(jnp.float32) + mixed
        middle_block[...] = middle
        second = head_norm(middle, ffn_norm[...])[0].astype(jnp.bfloat16)
        second_all[place] = second
        gate_weight = gate_all[...].reshape(width, gate_all.shape[-1])
        up_weight = up_all[...].reshape(width, up_all.shape[-1])
        gating, upward = dot(second, gate_weight), dot(second, up_weight)
        hidden_grad = dot(grad_all[place].reshape(block, width), down[...], 1, 1)
        sigmoid_gate = jax.nn.sigmoid(gating)
        activated = gating * sigmoid_gate
        hidden = (activated * upward).astype(jnp.bfloat16)
        gate_low = (
            hidden_grad * upward * sigmoid_gate * (1.0 + gating * (1.0 - sigmoid_gate))
        ).astype(jnp.bfloat16)
        up_low = (hidden_grad * activated).astype(jnp.bfloat16)
        hidden_all[place] = hidden
        gate_low_all[place] = gate_low
        up_low_all[place] = up_low
        act = dot(gate_low, gate_weight, 1, 1) + dot(up_low, up_weight, 1, 1)
        act_part[place] = act.astype(jnp.bfloat16).reshape(cols, local, width)
        down_part[place] = (
            dot(hidden, down[...]).astype(jnp.bfloat16).reshape(cols, local, width)
        )

    work(cross)
    act_sum.first()
    work(near)
    act_sum.toward(0)
    slots.relay()
    work(far)
    act_sum.toward(1)
    work(row)
    lines = pl.ds(pl.multiple_of(col * local, local), local)
    middle_own[...] = middle_block[lines, :]
    act_sum.own()
    slots.land()
    act_sum.last()
    act_sum.sent()
    slots.sent()


def hidden_pass(blocks, down, ffn_norm, query, key, value, number):
    rows, cols, local, width = blocks[0].shape
    block, hidden = cols * local, down.shape[0]
    shape = jax.ShapeDtypeStruct
    own, low = shape((local, width), jnp.float32), jnp.bfloat16
    part = shape((rows, block, hidden), low)
    slot = (2, query.shape[0] // 2, query.shape[1] + key.shape[1] + value.shape[1])
    outs = [own, own, shape((rows, cols, local, width), low), shape((cols,) + slot, low)]
    outs += [shape((rows, block, width), low), part, part, part]
    scratch = [
        pltpu.VMEM((rows, cols, local, width), low),
        pltpu.VMEM((block, width), jnp.float32),
        pltpu.VMEM(slot, low),
    ]
    scratch += reduce_scratch(rows, cols, local, width) + dma(1, 5, cols) + dma(1, 2, cols)
    args = list(blocks) + [down, ffn_norm.reshape(1, width), query, key, value]
    return call_kernel(hidden_kernel, args, outs, scratch, number)


class Paired:
    def __init__(self, part, came, sems, item):
        self.part, self.came, self.sems, self.item = part, came, sems, item
        self.half = lax.rem(lax.axis_index("dp"), 2)

    def pair(self):
        self.copy = send(
            self.part.at[:, 1 - self.half], self.came, self.sems, (self.item,), "dp", sibling()
        )

    def total(self, place):
        return self.part[place, self.half] + self.came[place]


def back_kernel(*refs):
    own_in, own_grad, act_own, middle_own, attn_norm, ffn_norm = refs[:6]
    out_all, cat_all, grad_all, first, second_all = refs[6:11]
    hidden_all, gate_low_all, up_low_all, down_given, slot_all = refs[11:16]
    query_rot, key_rot, value_low, low_rows, totals = refs[16:21]
    sums, gains, cosine, sine, begins = refs[21:26]
    outs, scratch = refs[26:34], refs[34:]
    block_out, in_grad, gate_got, up_got, head_got, out_sum, down_sum, gain_sum = outs
    mid_all, cat_part, grads_in, slot_mine, slots_in = scratch[:5]
    gate_sum, gate_came, gate_low, up_sum, up_came, up_low = scratch[5:11]
    head_sum, head_came, head_low = scratch[11:14]
    out_part, out_came, out_low, out_lined = scratch[14:18]
    down_grad, down_came, act_part = scratch[18:21]
    low_even, low_odd, query_acc, key_acc, value_acc = scratch[21:26]
    act_result, down_result, held, landed, down_part = scratch[26:31]
    act_scratch, down_scratch = scratch[31:35], scratch[35:39]
    sems = scratch[39:]
    mid_sems, sum_sems, swap_sems, pair_sems = sems[:2], sems[2:4], sems[4:6], sems[6:8]
    cat_sems, low_sems, out_sems, gain_sems = sems[8:10], sems[10:12], sems[12:14], sems[14:16]
    rows, cols = lax.axis_size("row"), lax.axis_size("col")
    row, col = lax.axis_index("row"), lax.axis_index("col")
    half = lax.rem(lax.axis_index("dp"), 2)
    local, width = own_in.shape
    length, head_dim = query_rot.shape
    block = cols * local
    near, far = neighbours()
    greet(corner=True)

    middle = middle_own[...]
    scale_mid = head_norm(middle, ffn_norm[...])[1]
    middle_back, ffn_gain = head_norm_back(act_own[...], middle, scale_mid, ffn_norm[...])
    middle_grad = own_grad[...].astype(jnp.float32) + middle_back
    in_grad[...] = middle_grad
    mid_all[row, col] = middle_grad.astype(jnp.bfloat16)
    mid = Gather(
        mid_all.at[row, col],
        lambda r, c: mid_all.at[r, c],
        lambda r, c, k: mid_all.at[r, c, pl.ds(k * (local // 2), local // 2)],
        mid_sems,
        0,
    )
    mid.plane(0)
    for step in range(1, cols):
        mid_all[:, lax.rem(col + step, cols)] = jnp.zeros((rows, local, width), jnp.bfloat16)
    held[0] = jnp.zeros(held.shape[1:], jnp.float32)
    held[0, 1:2, :] = ffn_gain[None, :]

    second = second_all[...].reshape(length, width)
    pieces = (cols, 2, width // cols // 2, gate_low_all.shape[-1])
    gate = Paired(gate_sum, gate_came, pair_sems, 0)
    gate_sum[...] = dot(second, gate_low_all[...].reshape(length, pieces[-1]), 0, 0).reshape(pieces)
    gate.pair()
    mid.relay(0)
    up = Paired(up_sum, up_came, pair_sems, 1)
    up_sum[...] = dot(second, up_low_all[...].reshape(length, pieces[-1]), 0, 0).reshape(pieces)
    up.pair()
    mid.land(0)

    cat_grad = dot(
        mid_all[:, col].reshape(rows * local, width),
        out_all[row].reshape(cols * head_dim, width),
        1,
        1,
    ).astype(jnp.bfloat16)
    for place in range(cols):
        cat_part[place] = cat_grad[:, place * head_dim : (place + 1) * head_dim].reshape(
            rows, local, head_dim
        )

    def turn(source, target, sems):
        return [
            send(
                source(lax.rem(col + step, cols)),
                target,
                sems,
                (step,),
                "col",
                lax.rem(col + step, cols),
            )
            for step in range(1, cols)
        ]

    cats = turn(lambda c: cat_part.at[c], grads_in.at[:, col], cat_sems)
    grads_in[:, col] = cat_part[col]
    down_part[...] = down_given[...]
    downs = Reduce(down_part, *down_scratch, down_result, sum_sems, 0)
    downs.first()

    def swap(paired, staged, got, item):
        paired.copy.wait_recv()
        for place in range(cols):
            staged[place] = paired.total(place).astype(jnp.bfloat16)
        moved = Swap(lambda c, h: staged.at[c], got, swap_sems, item, whole=True)
        moved.line()
        got[col, half] = staged[col]
        return moved

    swaps = [swap(gate, gate_low, gate_got, 0)]
    mixed = None
    for place in range(rows):
        term = dot(
            cat_all[place, row].reshape(cols * head_dim, block),
            mid_all[place].reshape(block, width),
        )
        mixed = term if mixed is None else mixed + term
    out = Paired(out_part, out_came, pair_sems, 2)
    out_part[...] = mixed.reshape(cols, 2, head_dim // 2, width)
    out.pair()
    swaps.append(swap(up, up_low, up_got, 1))
    down_grad[...] = dot(
        hidden_all[...].reshape(length, hidden_all.shape[-1]),
        grad_all[...].reshape(length, width),
        0,
        0,
    )
    down_copy = send(down_grad, down_came, pair_sems, (3,), "dp", sibling())
    for copy in cats:
        copy.wait_recv()

    score_scale = 1.0 / math.sqrt(head_dim)
    key_acc[...] = jnp.zeros_like(key_acc)
    value_acc[...] = jnp.zeros_like(value_acc)
    for offset, low, _ in spans(length, length // 2, block):
        number = offset // block
        lines, keys = slice(offset, offset + block), slice(low, offset + block)
        probability, _ = block_probability(
            query_rot[lines, :], key_rot[keys, :], begins[lines, :], offset, low, totals[lines, :]
        )
        grad_block = grads_in[number].reshape(block, head_dim)
        value_acc[keys, :] += dot(probability, grad_block, 0, 0)
        row_delta = jnp.sum(
            grad_block.astype(jnp.float32) * low_rows[lines, :].astype(jnp.float32),
            axis=1,
            keepdims=True,
        )
        prob_grad = dot(grad_block, value_low[keys, :], 1, 1)
        score_grad = (
            score_scale * probability.astype(jnp.float32) * (prob_grad - row_delta)
        ).astype(jnp.bfloat16)
        query_acc[lines, :] = dot(score_grad, key_rot[keys, :])
        key_acc[keys, :] += dot(score_grad, query_rot[lines, :], 0, 0)
        if number in (0, 1):
            downs.toward(number)
    pieces = (rows, cols, local, head_dim)
    for place, source in ((0, query_acc), (1, key_acc)):
        raw = sums[:, place * head_dim : (place + 1) * head_dim]
        gain = gains[place : place + 1, :]
        inv_rms = head_norm(raw, gain)[1]
        cotangent = source[...] * cosine[...] - swap_halves(source[...]) * sine[...]
        low_part, gain_grad = head_norm_back(cotangent, raw, inv_rms, gain)
        slot_mine[:, :, :, place * head_dim : (place + 1) * head_dim] = low_part.astype(
            jnp.bfloat16
        ).reshape(pieces)
        held[0, 2 + place : 3 + place, :head_dim] = gain_grad[None, :]
    slot_mine[:, :, :, 2 * head_dim :] = value_acc[...].astype(jnp.bfloat16).reshape(pieces)
    lows = turn(lambda c: slot_mine.at[:, c], slots_in.at[col], low_sems)
    slots_in[col] = slot_mine[:, col]

    head = Paired(head_sum, head_came, pair_sems, 4)
    head_sum[...] = dot(
        first[...].reshape(length, width), slot_mine[...].reshape(length, 3 * head_dim), 0, 0
    ).reshape(head_sum.shape)
    head.pair()
    out.copy.wait_recv()
    for place in range(cols):
        out_low[place] = out.total(place).astype(jnp.bfloat16)
    lined = [
        send(
            out_low.at[lax.rem(col + step, cols)],
            out_lined.at[step],
            out_sems,
            (step,),
            "col",
            lax.rem(col + step, cols),
        )
        for step in range(1, cols)
    ]
    for copy in lows:
        copy.wait_recv()
    for place in range(cols):
        lanes = slice(place * head_dim, (place + 1) * head_dim)
        came = slots_in[place].reshape(rows * local, 3 * head_dim)
        low_even[:, lanes] = came[:, :head_dim]
        target, offset = (low_odd, 0) if place % 2 else (low_even, cols * head_dim)
        for kind in (0, 1):
            begin = offset + (kind * (cols // 2) + place // 2) * head_dim
            target[:, begin : begin + head_dim] = came[
                :, (1 + kind) * head_dim : (2 + kind) * head_dim
            ]
    slot_weight = slot_all[...].reshape(width, slot_all.shape[-1])
    act = dot(low_even[...], slot_weight, 1, 1) + dot(
        low_odd[...], slot_weight[:, cols * head_dim :], 1, 1
    )
    act_part[...] = act.astype(jnp.bfloat16).reshape(act_part.shape)
    acts = Reduce(act_part, *act_scratch, act_result, sum_sems, 1)
    acts.first()
    downs.own()
    swaps.append(swap(head, head_low, head_got, 2))
    acts.toward(0)
    acts.toward(1)
    swaps[0].relay()
    swaps[1].relay()
    acts.own()

    residual = own_in[...].astype(jnp.float32)
    scale_in = head_norm(residual, attn_norm[...])[1]
    input_back, attn_gain = head_norm_back(act_result[...], residual, scale_in, attn_norm[...])
    in_grad[...] += input_back
    held[0, 0:1, :] = attn_gain[None, :]

    def share(stage, axis, size, own):
        copies = [
            send(
                held.at[stage],
                landed.at[stage, own],
                gain_sems,
                (stage, step),
                axis,
                lax.rem(own + step, size),
            )
            for step in range(1, size)
        ]
        landed[stage, own] = held[stage]
        return copies

    def gather_up(stage, copies, size):
        for copy in copies:
            copy.wait_recv()
        total = landed[stage, 0]
        for place in range(1, size):
            total = total + landed[stage, place]
        held[stage + 1] = total

    shares = share(0, "row", rows, row)
    downs.last()
    block_out[...] = (middle_own[...] + down_result[...]).astype(jnp.bfloat16)
    gather_up(0, shares, rows)
    more = share(1, "col", cols, col)
    out_sum[half] = out.total(col)
    for step in range(1, cols):
        lined[step - 1].wait_recv()
        out_sum[half] += out_lined[step].astype(jnp.float32)
    out_copy = send(out_sum.at[half], out_sum.at[half], pair_sems, (5,), "dp", sibling())
    swaps[2].relay()
    down_copy.wait_recv()
    down_sum[...] = down_grad[...] + down_came[...]
    gather_up(1, more, cols)
    gain_copy = send(held.at[2], landed.at[2, 0], gain_sems, (2, 0), "dp", sibling())
    for moved in swaps:
        moved.land()
    gain_copy.wait_recv()
    gain_sum[...] = held[2] + landed[2, 0]
    out_copy.wait_recv()
    for copy in cats + lows + lined + shares + more + [down_copy, out_copy, gain_copy]:
        copy.wait_send()
    for paired in (gate, up, out, head):
        paired.copy.wait_send()
    for item in [mid, downs, acts] + swaps:
        item.sent()


def back_pass(args, hidden, head_dim, number):
    rows, cols = lax.axis_size("row"), lax.axis_size("col")
    local, width = args[0].shape
    length, height = rows * cols * local, width // cols // 2
    low, full = jnp.bfloat16, jnp.float32
    shape = jax.ShapeDtypeStruct
    slot, some = 3 * head_dim, head_dim // 2
    outs = [
        shape((local, width), low),
        shape((local, width), full),
        shape((cols, 2, height, hidden), low),
        shape((cols, 2, height, hidden), low),
        shape((cols, 2, height, slot), low),
        shape((2, some, width), full),
        shape((hidden, width), full),
        shape((8, width), full),
    ]

    def vmem(kind, *dims):
        return pltpu.VMEM(dims, kind)

    scratch = [
        vmem(low, rows, cols, local, width),
        vmem(low, cols, rows, local, head_dim),
        vmem(low, rows, cols, local, head_dim),
        vmem(low, rows, cols, local, slot),
        vmem(low, cols, rows, local, slot),
    ]
    for last in (hidden, hidden, slot):
        scratch += [
            vmem(full, cols, 2, height, last),
            vmem(full, cols, height, last),
            vmem(low, cols, height, last),
        ]
    scratch += [
        vmem(full, cols, 2, some, width),
        vmem(full, cols, some, width),
        vmem(low, cols, some, width),
        vmem(low, cols, some, width),
        vmem(full, hidden, width),
        vmem(full, hidden, width),
        vmem(low, rows, 1, local, width),
        vmem(low, rows * local, 2 * cols * head_dim),
        vmem(low, rows * local, cols * head_dim),
        vmem(full, length, head_dim),
        vmem(full, length, head_dim),
        vmem(full, length, head_dim),
        vmem(full, local, width),
        vmem(full, local, width),
        vmem(full, 3, 8, width),
        vmem(full, 3, max(rows, cols), 8, width),
        vmem(low, rows, cols, local, width),
    ]
    scratch += reduce_scratch(rows, 1, local, width) + reduce_scratch(rows, cols, local, width)
    scratch += dma(1, 5, cols) + dma(2, 5, cols) + dma(3, 2, cols) + dma(6)
    scratch += dma(cols) + dma(cols) + dma(cols) + dma(3, max(rows, cols))
    return call_kernel(back_kernel, args, outs, scratch, number)


def open_kernel(cols, head_dim, gate_got, up_got, head_got, gate, up, query, key, value):
    height, part = gate_got.shape[2:]
    for piece in range(2):
        lines = slice(piece * height, (piece + 1) * height)
        for col in range(cols):
            gate[lines, col * part : (col + 1) * part] = gate_got[col, piece].astype(jnp.float32)
            up[lines, col * part : (col + 1) * part] = up_got[col, piece].astype(jnp.float32)
            query[lines, col * head_dim : (col + 1) * head_dim] = head_got[
                col, piece, :, :head_dim
            ].astype(jnp.float32)
        for pair in range(cols // 2):
            for place, target in ((1, key), (2, value)):
                lanes = slice(place * head_dim, (place + 1) * head_dim)
                target[lines, pair * head_dim : (pair + 1) * head_dim] = head_got[
                    2 * pair, piece, :, lanes
                ].astype(jnp.float32) + head_got[2 * pair + 1, piece, :, lanes].astype(jnp.float32)


def call_kernel(body, args, outs, scratch, number):
    vmem = pl.BlockSpec(memory_space=pltpu.VMEM)
    return pl.pallas_call(
        body,
        out_shape=outs,
        in_specs=[vmem] * len(args),
        out_specs=[vmem] * len(outs),
        scratch_shapes=scratch,
        compiler_params=pltpu.CompilerParams(
            collective_id=number, has_side_effects=True, vmem_limit_bytes=VMEM_LIMIT
        ),
    )(*args)


def dma(*shape):
    return [pltpu.SemaphoreType.DMA(shape), pltpu.SemaphoreType.DMA(shape)]


def dot(left, right, left_dim=1, right_dim=0):
    return lax.dot_general(
        left,
        right,
        (((left_dim,), (right_dim,)), ((), ())),
        preferred_element_type=jnp.float32,
    )


def shards(
    block_input,
    seq_lengths,
    out_grad,
    attn_norm,
    query_weight,
    key_weight,
    value_weight,
    query_norm,
    key_norm,
    out_weight,
    ffn_norm,
    gate_weight,
    up_weight,
    down_weight,
):
    local_rows, width = block_input.shape
    head_dim = query_norm.shape[0]
    cols = lax.axis_size("col")
    length = local_rows * cols * lax.axis_size("row")
    places = jnp.arange(length, dtype=jnp.int32)
    passed = (places[:, None] >= end_points[None, :]).astype(jnp.int32)
    segment = jnp.sum(passed, axis=1)
    begins = jnp.sum(passed * seq_lengths[None, :], axis=1)
    return (segment, places - begins)


def rope_tables(position, width):
    half_width = width // 2
    exponent = jnp.arange(half_width, dtype=jnp.float32) * (2.0 / width)
    frequency = jnp.exp(-math.log(THETA) * exponent)
    angles = position.astype(jnp.float32)[:, None] * frequency[None, :]
    return (jnp.cos(angles), jnp.sin(angles))


def head_norm(values, gain_vec):
    inv_rms = lax.rsqrt(jnp.mean(values * values, axis=-1, keepdims=True) + EPSILON)
    return (values * inv_rms * gain_vec, inv_rms)


def head_norm_back(cotangent, values, inv_rms, gain_vec):
    normed = values * inv_rms
    weighted = cotangent * gain_vec
    gain_grad = jnp.sum(cotangent * normed, axis=0)
    inner_mean = jnp.mean(weighted * normed, axis=-1, keepdims=True)
    return (inv_rms * (weighted - normed * inner_mean), gain_grad)


def swap_halves(values):
    half_width = values.shape[-1] // 2
    return jnp.concatenate([values[:, half_width:], values[:, :half_width]], axis=1)


def block_probability(query_block, key_rows, begins, offset, low, shift):
    score_scale = 1.0 / math.sqrt(query_block.shape[1])
    scores = dot(query_block, key_rows, 1, 1) * score_scale
    places = low + lax.broadcasted_iota(jnp.int32, scores.shape, 1)
    row_places = offset + lax.broadcasted_iota(jnp.int32, scores.shape, 0)
    allowed = (places >= begins) & (places <= row_places)
    if shift is None:
        shift = jnp.log(jnp.sum(jnp.where(allowed, jnp.exp(scores), 0.0), axis=1, keepdims=True))
    probability = jnp.where(allowed, jnp.exp(scores - shift), 0.0).astype(jnp.bfloat16)
    return probability, shift


def spans(length, longest, block):
    return [
        (offset, max(0, (offset - longest) // 128 * 128), block)
        for offset in range(0, length, block)
    ]


def local_kernel(body, args, outs, scratch=()):
    vmem = pl.BlockSpec(memory_space=pltpu.VMEM)
    return pl.pallas_call(
        body,
        out_shape=outs,
        in_specs=[vmem] * len(args),
        out_specs=[vmem] * len(outs),
        scratch_shapes=list(scratch),
    )(*args)


MESH = pl.DeviceIdType.MESH
VMEM_LIMIT = 56 * 1024 * 1024


def send(source, target, sems, place, axis, index):
    copy = pltpu.make_async_remote_copy(
        src_ref=source,
        dst_ref=target,
        send_sem=sems[0].at[place],
        recv_sem=sems[1].at[place],
        device_id={axis: index},
        device_id_type=MESH,
    )
    copy.start()
    return copy


def neighbours():
    rows, row = lax.axis_size("row"), lax.axis_index("row")
    near = row + 1 - 2 * lax.rem(row, 2)
    far = lax.rem(row + rows // 2, rows)
    return near, far


def sibling():
    own = lax.axis_index("dp")
    return own + 1 - 2 * lax.rem(own, 2)


def greet(corner=False):
    cols, col = lax.axis_size("col"), lax.axis_index("col")
    near, far = neighbours()
    peers = [("col", lax.rem(col + step, cols)) for step in range(1, cols)]
    peers += [("row", near), ("row", far), ("dp", sibling())]
    if corner:
        peers.append(("row", lax.rem(near + lax.axis_size("row") // 2, lax.axis_size("row"))))
    barrier = pltpu.get_barrier_semaphore()
    for axis, index in peers:
        pl.semaphore_signal(barrier, inc=1, device_id={axis: index}, device_id_type=MESH)
    pl.semaphore_wait(barrier, len(peers))


class Gather:
    def __init__(self, source, block, part, sems, item):
        self.source, self.block, self.part = source, block, part
        self.sems, self.item = sems, item
        self.cols, self.col = lax.axis_size("col"), lax.axis_index("col")
        self.row = lax.axis_index("row")
        self.near, self.far = neighbours()
        self.lines, self.planes, self.relays = {}, {}, {}

    def origin(self, step):
        return lax.rem(self.col + self.cols - step, self.cols)

    def line(self):
        for step in range(1, self.cols):
            self.lines[step] = send(
                self.source,
                self.block(self.row, self.col),
                self.sems,
                (self.item, 0, step),
                "col",
                lax.rem(self.col + step, self.cols),
            )

    def plane(self, step):
        target = self.block(self.row, self.origin(step))
        if step:
            self.lines[step].wait_recv()
        for kind, peer in ((1, self.near), (2, self.far)):
            self.planes[step, kind] = send(
                target if step else self.source,
                target,
                self.sems,
                (self.item, kind, step),
                "row",
                peer,
            )

    def relay(self, step):
        for kind, source, peer in ((1, self.near, self.far), (2, self.far, self.near)):
            self.planes[step, kind].wait_recv()
            piece = self.part(source, self.origin(step), kind - 1)
            self.relays[step, kind] = send(
                piece, piece, self.sems, (self.item, kind + 2, step), "row", peer
            )

    def land(self, step):
        for kind in (1, 2):
            self.relays[step, kind].wait_recv()

    def sent(self):
        for copies in (self.lines, self.planes, self.relays):
            for copy in copies.values():
                copy.wait_send()


class Swap:
    def __init__(self, source, target, sems, item, whole=False):
        self.source, self.target, self.sems, self.item = source, target, sems, item
        self.cols, self.col = lax.axis_size("col"), lax.axis_index("col")
        self.half = lax.rem(lax.axis_index("dp"), 2)
        self.lines, self.pairs, self.first = {}, {}, 0 if whole else 1

    def line(self):
        for step in range(1, self.cols):
            peer = lax.rem(self.col + step, self.cols)
            self.lines[step] = send(
                self.source(peer, self.half),
                self.target.at[self.col, self.half],
                self.sems,
                (self.item, 0, step),
                "col",
                peer,
            )

    def relay(self):
        for step in range(self.first, self.cols):
            if step:
                self.lines[step].wait_recv()
            piece = self.target.at[lax.rem(self.col + self.cols - step, self.cols), self.half]
            self.pairs[step] = send(
                piece, piece, self.sems, (self.item, 1, step), "dp", sibling()
            )

    def land(self):
        for copy in self.pairs.values():
            copy.wait_recv()

    def sent(self):
        for copies in (self.lines, self.pairs):
            for copy in copies.values():
                copy.wait_send()


def front_kernel(*refs):
    (own_in, own_grad, own_out, query, key, value, gate, up) = refs[:8]
    (attn_norm, gains, cosine, sine, begins) = refs[8:13]
    (in_all, grad_all, out_all, cat_all, gate_all, up_all, slot_all) = refs[13:20]
    (first, sums, query_rot, key_rot, value_low, low_rows, totals) = refs[20:27]
    (slot_part, gate_part, up_part) = refs[27:30]
    gather_sems, swap_sems, pair_sems = refs[30:32], refs[32:34], refs[34:36]
    rows, cols = lax.axis_size("row"), lax.axis_size("col")
    row, col = lax.axis_index("row"), lax.axis_index("col")
    half = lax.rem(lax.axis_index("dp"), 2)
    near, far = neighbours()
    length, head_dim = query_rot.shape
    width = own_in.shape[1]
    local = own_in.shape[0]
    block = length // rows

    def split(ref):
        count = ref.shape[2] // 2
        return (
            lambda r, c: ref.at[r, c],
            lambda r, c, k: ref.at[r, c, pl.ds(k * count, count)],
        )

    greet()
    inputs = Gather(own_in, *split(in_all), gather_sems, 0)
    inputs.line()
    inputs.plane(0)
    height = query.shape[0] // 2
    for place in range(cols):
        for piece in range(2):
            lines = slice(piece * height, (piece + 1) * height)
            lanes = slice(place // 2 * head_dim, (place // 2 + 1) * head_dim)
            slot_part[place, piece, :, :head_dim] = query[
                lines, place * head_dim : (place + 1) * head_dim
            ]
            slot_part[place, piece, :, head_dim : 2 * head_dim] = key[lines, lanes]
            slot_part[place, piece, :, 2 * head_dim :] = value[lines, lanes]
    slots = Swap(lambda c, h: slot_part.at[c, h], slot_all, swap_sems, 0)
    slots.line()
    slot_all[col] = slot_part[col]
    in_all[row, col] = own_in[...]
    for step in range(1, cols):
        inputs.plane(step)
    hidden = gate.shape[1] // cols
    for source, part in ((gate, gate_part), (up, up_part)):
        for place in range(cols):
            for piece in range(2):
                part[place, piece] = source[
                    piece * height : (piece + 1) * height, place * hidden : (place + 1) * hidden
                ]
    slots.relay()
    inputs.relay(0)
    grads = Gather(own_grad, *split(grad_all), gather_sems, 1)
    grads.line()
    inputs.relay(1)
    wide = [
        Swap(lambda c, h: gate_part.at[c, h], gate_all, swap_sems, 1),
        Swap(lambda c, h: up_part.at[c, h], up_all, swap_sems, 2),
    ]
    for swap in wide:
        swap.line()
    inputs.relay(2)
    count = own_out.shape[1] // 2
    outs = Gather(
        own_out.at[half],
        lambda r, c: out_all.at[r, c, half],
        lambda r, c, k: out_all.at[r, c, half, pl.ds(k * count, count)],
        gather_sems,
        2,
    )
    outs.line()
    inputs.relay(3)
    grads.plane(0)
    outs.plane(0)
    gate_all[col] = gate_part[col]
    up_all[col] = up_part[col]
    grad_all[row, col] = own_grad[...]
    out_all[row, col] = own_out[...]
    slots.land()

    def project(place):
        for c in range(cols):
            values = in_all[place, c].astype(jnp.float32)
            normed = head_norm(values, attn_norm[...])[0]
            first[place, c] = normed.astype(jnp.bfloat16)
        lines = pl.ds(pl.multiple_of(place * block, block), block)
        sums[lines, :] = dot(
            first[place].reshape(block, width), slot_all[...].reshape(width, 3 * head_dim)
        )

    project(row)
    project(near)
    project(far)
    for step in range(1, cols):
        grads.plane(step)
    for step in range(cols):
        inputs.land(step)
    project(lax.rem(near + rows // 2, rows))
    for step in range(1, cols):
        outs.plane(step)
    for place, target in ((0, query_rot), (1, key_rot)):
        normed = head_norm(
            sums[:, place * head_dim : (place + 1) * head_dim], gains[place : place + 1, :]
        )[0]
        target[...] = (normed * cosine[...] + swap_halves(normed) * sine[...]).astype(jnp.bfloat16)
    value_low[...] = sums[:, 2 * head_dim : 3 * head_dim].astype(jnp.bfloat16)

    def cat(part):
        places = pl.ds(part * (rows // 2), rows // 2)
        return Gather(
            cat_all.at[places, row, col],
            lambda r, c: cat_all.at[places, r, c],
            lambda r, c, k: cat_all.at[places, r, c, pl.ds(k * head_dim // 2, head_dim // 2)],
            gather_sems,
            3 + part,
        )

    cats = []
    for offset, low, _ in spans(length, length // 2, block):
        number = offset // block
        lines, keys = slice(offset, offset + block), slice(low, offset + block)
        probability, total = block_probability(
            query_rot[lines, :], key_rot[keys, :], begins[lines, :], offset, low, None
        )
        totals[lines, :] = total
        low_rows[lines, :] = dot(probability, value_low[keys, :]).astype(jnp.bfloat16)
        cat_all[number, row, col] = dot(value_low[keys, :], probability, 0, 1).astype(jnp.bfloat16)
        if 2 * (number + 1) % rows == 0:
            cats.append(cat(2 * (number + 1) // rows - 1))
            cats[-1].line()
            cats[-1].plane(0)
        if number == 0:
            for swap in wide:
                swap.relay()
            grads.relay(0)
            grads.relay(1)
        if number == 1:
            grads.relay(2)
            grads.relay(3)
        if number == 2:
            for step in range(cols):
                outs.relay(step)
            for step in range(1, cols):
                cats[0].plane(step)
    for step in range(1, cols):
        cats[1].plane(step)
    for gather in cats:
        for step in range(cols):
            gather.relay(step)
    pairs = []
    for step in range(cols):
        outs.land(step)
    for number, place in enumerate((near, far, lax.rem(near + rows // 2, rows))):
        piece = out_all.at[place, :, half]
        pairs.append(send(piece, piece, pair_sems, (number,), "dp", sibling()))
    for step in range(1, cols):
        piece = out_all.at[row, lax.rem(col + cols - step, cols), half]
        pairs.append(send(piece, piece, pair_sems, (2 + step,), "dp", sibling()))
    for swap in wide:
        swap.land()
    for gather in [grads] + cats:
        for step in range(cols):
            gather.land(step)
    for copy in pairs:
        copy.wait()
    for item in [inputs, grads, outs, slots] + wide + cats:
        item.sent()


def front(own_in, own_grad, own_out, query, key, value, gate, up, attn_norm, gains, tables, number):
    rows, cols = lax.axis_size("row"), lax.axis_size("col")
    local, width = own_in.shape
    length, head_dim = local * rows * cols, gains.shape[1]
    hidden, height = gate.shape[1] // cols, gate.shape[0] // 2
    low = jnp.bfloat16
    blocks = jax.ShapeDtypeStruct((rows, cols, local, width), low)
    halves = own_out.shape[0] // 2
    wide = (cols, 2, height, hidden)
    slot = (cols, 2, height, 3 * head_dim)
    shape = jax.ShapeDtypeStruct
    head_rows = shape((length, head_dim), low)
    outs = [
        blocks,
        blocks,
        shape((rows, cols, 2, halves, width), low),
        shape((rows, rows, cols, head_dim, length // rows), low),
        shape(wide, low),
        shape(wide, low),
        shape(slot, low),
        blocks,
        shape((length, 3 * head_dim), jnp.float32),
        head_rows,
        head_rows,
        head_rows,
        head_rows,
        shape((length, 1), jnp.float32),
    ]
    scratch = [pltpu.VMEM(slot, low), pltpu.VMEM(wide, low), pltpu.VMEM(wide, low)]
    scratch += dma(5, 5, cols) + dma(3, 2, cols) + dma(2 + cols)
    args = [own_in, own_grad, own_out.reshape(2, halves, width), query, key, value, gate, up]
    args += [attn_norm.reshape(1, width), gains] + list(tables)
    return call_kernel(front_kernel, args, outs, scratch, number)


class Reduce:
    def __init__(self, part, relayed, planed, staged, lined, result, sems, item):
        self.part, self.relayed, self.planed = part, relayed, planed
        self.staged, self.lined, self.result = staged, lined, result
        self.sems, self.item = sems, item
        self.cols = part.shape[1]
        self.col = lax.axis_index("col") if self.cols > 1 else 0
        self.row = lax.axis_index("row")
        self.near, self.far = neighbours()
        self.cross = lax.rem(self.near + lax.axis_size("row") // 2, lax.axis_size("row"))
        self.count = part.shape[2] // 2
        self.relays, self.planes, self.lines = [], [], []

    def first(self):
        for kind, peer in ((0, self.near), (1, self.far)):
            self.relays.append(
                send(
                    self.part.at[self.cross, :, pl.ds(kind * self.count, self.count)],
                    self.relayed.at[kind],
                    self.sems,
                    (self.item, 1 + kind, 0),
                    "row",
                    peer,
                )
            )

    def toward(self, kind):
        peer, came = (self.near, self.far)[kind], 1 - kind
        self.relays[came].wait_recv()
        lines = slice(came * self.count, (came + 1) * self.count)
        self.part[peer, :, lines] = (
            self.part[peer, :, lines].astype(jnp.float32)
            + self.relayed[came].astype(jnp.float32)
        ).astype(jnp.bfloat16)
        self.planes.append(
            send(
                self.part.at[peer],
                self.planed.at[kind],
                self.sems,
                (self.item, 3 + kind, 0),
                "row",
                peer,
            )
        )

    def total(self, place):
        summed = self.part[self.row, place].astype(jnp.float32)
        for kind in range(2):
            summed = summed + self.planed[kind, place].astype(jnp.float32)
        return summed

    def own(self):
        for copy in self.planes:
            copy.wait_recv()
        for step in range(1, self.cols):
            place = lax.rem(self.col + step, self.cols)
            self.staged[step] = self.total(place).astype(jnp.bfloat16)
            self.lines.append(
                send(
                    self.staged.at[step],
                    self.lined.at[step],
                    self.sems,
                    (self.item, 0, step),
                    "col",
                    place,
                )
            )
        self.result[...] = self.total(self.col)

    def last(self):
        for step in range(1, self.cols):
            self.lines[step - 1].wait_recv()
            self.result[...] += self.lined[step].astype(jnp.float32)

    def sent(self):
        for copy in self.relays + self.planes + self.lines:
            copy.wait_send()


def reduce_scratch(rows, cols, local, width):
    low = jnp.bfloat16
    return [
        pltpu.VMEM((2, cols, local // 2, width), low),
        pltpu.VMEM((2, cols, local, width), low),
        pltpu.VMEM((cols, local, width), low),
        pltpu.VMEM((cols, local, width), low),
    ]


def hidden_kernel(*refs):
    in_all, grad_all, out_all, cat_all, gate_all, up_all, down, ffn_norm = refs[:8]
    query, key, value = refs[8:11]
    act_own, middle_own, down_part, slot_all = refs[11:15]
    second_all, hidden_all, gate_low_all, up_low_all = refs[15:19]
    act_part, middle_block, slot_part = refs[19:22]
    act_scratch, sems, swap_sems = refs[22:26], refs[26:28], refs[28:30]
    rows, cols = lax.axis_size("row"), lax.axis_size("col")
    row, col = lax.axis_index("row"), lax.axis_index("col")
    near, far = neighbours()
    cross = lax.rem(near + rows // 2, rows)
    local, width = in_all.shape[2:]
    block = cols * local
    greet()
    height, begin = query.shape[0] // 2, 0
    for source in (query, key, value):
        lanes = slice(begin, begin + source.shape[1])
        for piece in range(2):
            slot_part[piece, :, lanes] = source[piece * height : (piece + 1) * height, :]
        begin += source.shape[1]
    slots = Swap(lambda c, h: slot_part.at[h], slot_all, swap_sems, 0)
    slots.line()
    slot_all[col] = slot_part[...]
    act_sum = Reduce(act_part, *act_scratch, act_own, sems, 0)

    def work(place):
        mixed = dot(cat_all[place].reshape(width, block), out_all[...].reshape(width, width), 0, 0)
        middle = in_all[place].reshape(block, width).astype(jnp.float32) + mixed
        middle_block[...] = middle
        second = head_norm(middle, ffn_norm[...])[0].astype(jnp.bfloat16)
        second_all[place] = second
        gate_weight = gate_all[...].reshape(width, gate_all.shape[-1])
        up_weight = up_all[...].reshape(width, up_all.shape[-1])
        gating, upward = dot(second, gate_weight), dot(second, up_weight)
        hidden_grad = dot(grad_all[place].reshape(block, width), down[...], 1, 1)
        sigmoid_gate = jax.nn.sigmoid(gating)
        activated = gating * sigmoid_gate
        hidden = (activated * upward).astype(jnp.bfloat16)
        gate_low = (
            hidden_grad * upward * sigmoid_gate * (1.0 + gating * (1.0 - sigmoid_gate))
        ).astype(jnp.bfloat16)
        up_low = (hidden_grad * activated).astype(jnp.bfloat16)
        hidden_all[place] = hidden
        gate_low_all[place] = gate_low
        up_low_all[place] = up_low
        act = dot(gate_low, gate_weight, 1, 1) + dot(up_low, up_weight, 1, 1)
        act_part[place] = act.astype(jnp.bfloat16).reshape(cols, local, width)
        down_part[place] = (
            dot(hidden, down[...]).astype(jnp.bfloat16).reshape(cols, local, width)
        )

    work(cross)
    act_sum.first()
    work(near)
    act_sum.toward(0)
    slots.relay()
    work(far)
    act_sum.toward(1)
    work(row)
    lines = pl.ds(pl.multiple_of(col * local, local), local)
    middle_own[...] = middle_block[lines, :]
    act_sum.own()
    slots.land()
    act_sum.last()
    act_sum.sent()
    slots.sent()


def hidden_pass(blocks, down, ffn_norm, query, key, value, number):
    rows, cols, local, width = blocks[0].shape
    block, hidden = cols * local, down.shape[0]
    shape = jax.ShapeDtypeStruct
    own, low = shape((local, width), jnp.float32), jnp.bfloat16
    part = shape((rows, block, hidden), low)
    slot = (2, query.shape[0] // 2, query.shape[1] + key.shape[1] + value.shape[1])
    outs = [own, own, shape((rows, cols, local, width), low), shape((cols,) + slot, low)]
    outs += [shape((rows, block, width), low), part, part, part]
    scratch = [
        pltpu.VMEM((rows, cols, local, width), low),
        pltpu.VMEM((block, width), jnp.float32),
        pltpu.VMEM(slot, low),
    ]
    scratch += reduce_scratch(rows, cols, local, width) + dma(1, 5, cols) + dma(1, 2, cols)
    args = list(blocks) + [down, ffn_norm.reshape(1, width), query, key, value]
    return call_kernel(hidden_kernel, args, outs, scratch, number)


class Paired:
    def __init__(self, part, came, sems, item):
        self.part, self.came, self.sems, self.item = part, came, sems, item
        self.half = lax.rem(lax.axis_index("dp"), 2)

    def pair(self):
        self.copy = send(
            self.part.at[:, 1 - self.half], self.came, self.sems, (self.item,), "dp", sibling()
        )

    def total(self, place):
        return self.part[place, self.half] + self.came[place]


def back_kernel(*refs):
    own_in, own_grad, act_own, middle_own, attn_norm, ffn_norm = refs[:6]
    out_all, cat_all, grad_all, first, second_all = refs[6:11]
    hidden_all, gate_low_all, up_low_all, down_given, slot_all = refs[11:16]
    query_rot, key_rot, value_low, low_rows, totals = refs[16:21]
    sums, gains, cosine, sine, begins = refs[21:26]
    outs, scratch = refs[26:34], refs[34:]
    block_out, in_grad, gate_got, up_got, head_got, out_sum, down_sum, gain_sum = outs
    mid_all, cat_part, grads_in, slot_mine, slots_in = scratch[:5]
    gate_sum, gate_came, gate_low, up_sum, up_came, up_low = scratch[5:11]
    head_sum, head_came, head_low = scratch[11:14]
    out_part, out_came, out_low, out_lined = scratch[14:18]
    down_grad, down_came, act_part = scratch[18:21]
    low_even, low_odd, query_acc, key_acc, value_acc = scratch[21:26]
    act_result, down_result, held, landed, down_part = scratch[26:31]
    act_scratch, down_scratch = scratch[31:35], scratch[35:39]
    sems = scratch[39:]
    mid_sems, sum_sems, swap_sems, pair_sems = sems[:2], sems[2:4], sems[4:6], sems[6:8]
    cat_sems, low_sems, out_sems, gain_sems = sems[8:10], sems[10:12], sems[12:14], sems[14:16]
    rows, cols = lax.axis_size("row"), lax.axis_size("col")
    row, col = lax.axis_index("row"), lax.axis_index("col")
    half = lax.rem(lax.axis_index("dp"), 2)
    local, width = own_in.shape
    length, head_dim = query_rot.shape
    block = cols * local
    near, far = neighbours()
    greet(corner=True)

    middle = middle_own[...]
    scale_mid = head_norm(middle, ffn_norm[...])[1]
    middle_back, ffn_gain = head_norm_back(act_own[...], middle, scale_mid, ffn_norm[...])
    middle_grad = own_grad[...].astype(jnp.float32) + middle_back
    in_grad[...] = middle_grad
    mid_all[row, col] = middle_grad.astype(jnp.bfloat16)
    mid = Gather(
        mid_all.at[row, col],
        lambda r, c: mid_all.at[r, c],
        lambda r, c, k: mid_all.at[r, c, pl.ds(k * (local // 2), local // 2)],
        mid_sems,
        0,
    )
    mid.plane(0)
    for step in range(1, cols):
        mid_all[:, lax.rem(col + step, cols)] = jnp.zeros((rows, local, width), jnp.bfloat16)
    held[0] = jnp.zeros(held.shape[1:], jnp.float32)
    held[0, 1:2, :] = ffn_gain[None, :]

    second = second_all[...].reshape(length, width)
    pieces = (cols, 2, width // cols // 2, gate_low_all.shape[-1])
    gate = Paired(gate_sum, gate_came, pair_sems, 0)
    gate_sum[...] = dot(second, gate_low_all[...].reshape(length, pieces[-1]), 0, 0).reshape(pieces)
    gate.pair()
    mid.relay(0)
    up = Paired(up_sum, up_came, pair_sems, 1)
    up_sum[...] = dot(second, up_low_all[...].reshape(length, pieces[-1]), 0, 0).reshape(pieces)
    up.pair()
    mid.land(0)

    cat_grad = dot(
        mid_all[:, col].reshape(rows * local, width),
        out_all[row].reshape(cols * head_dim, width),
        1,
        1,
    ).astype(jnp.bfloat16)
    for place in range(cols):
        cat_part[place] = cat_grad[:, place * head_dim : (place + 1) * head_dim].reshape(
            rows, local, head_dim
        )

    def turn(source, target, sems):
        return [
            send(
                source(lax.rem(col + step, cols)),
                target,
                sems,
                (step,),
                "col",
                lax.rem(col + step, cols),
            )
            for step in range(1, cols)
        ]

    cats = turn(lambda c: cat_part.at[c], grads_in.at[:, col], cat_sems)
    grads_in[:, col] = cat_part[col]
    down_part[...] = down_given[...]
    downs = Reduce(down_part, *down_scratch, down_result, sum_sems, 0)
    downs.first()

    def swap(paired, staged, got, item):
        paired.copy.wait_recv()
        for place in range(cols):
            staged[place] = paired.total(place).astype(jnp.bfloat16)
        moved = Swap(lambda c, h: staged.at[c], got, swap_sems, item, whole=True)
        moved.line()
        got[col, half] = staged[col]
        return moved

    swaps = [swap(gate, gate_low, gate_got, 0)]
    mixed = None
    for place in range(rows):
        term = dot(
            cat_all[place, row].reshape(cols * head_dim, block),
            mid_all[place].reshape(block, width),
        )
        mixed = term if mixed is None else mixed + term
    out = Paired(out_part, out_came, pair_sems, 2)
    out_part[...] = mixed.reshape(cols, 2, head_dim // 2, width)
    out.pair()
    swaps.append(swap(up, up_low, up_got, 1))
    down_grad[...] = dot(
        hidden_all[...].reshape(length, hidden_all.shape[-1]),
        grad_all[...].reshape(length, width),
        0,
        0,
    )
    down_copy = send(down_grad, down_came, pair_sems, (3,), "dp", sibling())
    for copy in cats:
        copy.wait_recv()

    score_scale = 1.0 / math.sqrt(head_dim)
    key_acc[...] = jnp.zeros_like(key_acc)
    value_acc[...] = jnp.zeros_like(value_acc)
    for offset, low, _ in spans(length, length // 2, block):
        number = offset // block
        lines, keys = slice(offset, offset + block), slice(low, offset + block)
        probability, _ = block_probability(
            query_rot[lines, :], key_rot[keys, :], begins[lines, :], offset, low, totals[lines, :]
        )
        grad_block = grads_in[number].reshape(block, head_dim)
        value_acc[keys, :] += dot(probability, grad_block, 0, 0)
        row_delta = jnp.sum(
            grad_block.astype(jnp.float32) * low_rows[lines, :].astype(jnp.float32),
            axis=1,
            keepdims=True,
        )
        prob_grad = dot(grad_block, value_low[keys, :], 1, 1)
        score_grad = (
            score_scale * probability.astype(jnp.float32) * (prob_grad - row_delta)
        ).astype(jnp.bfloat16)
        query_acc[lines, :] = dot(score_grad, key_rot[keys, :])
        key_acc[keys, :] += dot(score_grad, query_rot[lines, :], 0, 0)
        if number in (0, 1):
            downs.toward(number)
    pieces = (rows, cols, local, head_dim)
    for place, source in ((0, query_acc), (1, key_acc)):
        raw = sums[:, place * head_dim : (place + 1) * head_dim]
        gain = gains[place : place + 1, :]
        inv_rms = head_norm(raw, gain)[1]
        cotangent = source[...] * cosine[...] - swap_halves(source[...]) * sine[...]
        low_part, gain_grad = head_norm_back(cotangent, raw, inv_rms, gain)
        slot_mine[:, :, :, place * head_dim : (place + 1) * head_dim] = low_part.astype(
            jnp.bfloat16
        ).reshape(pieces)
        held[0, 2 + place : 3 + place, :head_dim] = gain_grad[None, :]
    slot_mine[:, :, :, 2 * head_dim :] = value_acc[...].astype(jnp.bfloat16).reshape(pieces)
    lows = turn(lambda c: slot_mine.at[:, c], slots_in.at[col], low_sems)
    slots_in[col] = slot_mine[:, col]

    head = Paired(head_sum, head_came, pair_sems, 4)
    head_sum[...] = dot(
        first[...].reshape(length, width), slot_mine[...].reshape(length, 3 * head_dim), 0, 0
    ).reshape(head_sum.shape)
    head.pair()
    out.copy.wait_recv()
    for place in range(cols):
        out_low[place] = out.total(place).astype(jnp.bfloat16)
    lined = [
        send(
            out_low.at[lax.rem(col + step, cols)],
            out_lined.at[step],
            out_sems,
            (step,),
            "col",
            lax.rem(col + step, cols),
        )
        for step in range(1, cols)
    ]
    for copy in lows:
        copy.wait_recv()
    for place in range(cols):
        lanes = slice(place * head_dim, (place + 1) * head_dim)
        came = slots_in[place].reshape(rows * local, 3 * head_dim)
        low_even[:, lanes] = came[:, :head_dim]
        target, offset = (low_odd, 0) if place % 2 else (low_even, cols * head_dim)
        for kind in (0, 1):
            begin = offset + (kind * (cols // 2) + place // 2) * head_dim
            target[:, begin : begin + head_dim] = came[
                :, (1 + kind) * head_dim : (2 + kind) * head_dim
            ]
    slot_weight = slot_all[...].reshape(width, slot_all.shape[-1])
    act = dot(low_even[...], slot_weight, 1, 1) + dot(
        low_odd[...], slot_weight[:, cols * head_dim :], 1, 1
    )
    act_part[...] = act.astype(jnp.bfloat16).reshape(act_part.shape)
    acts = Reduce(act_part, *act_scratch, act_result, sum_sems, 1)
    acts.first()
    downs.own()
    swaps.append(swap(head, head_low, head_got, 2))
    acts.toward(0)
    acts.toward(1)
    swaps[0].relay()
    swaps[1].relay()
    acts.own()

    residual = own_in[...].astype(jnp.float32)
    scale_in = head_norm(residual, attn_norm[...])[1]
    input_back, attn_gain = head_norm_back(act_result[...], residual, scale_in, attn_norm[...])
    in_grad[...] += input_back
    held[0, 0:1, :] = attn_gain[None, :]

    def share(stage, axis, size, own):
        copies = [
            send(
                held.at[stage],
                landed.at[stage, own],
                gain_sems,
                (stage, step),
                axis,
                lax.rem(own + step, size),
            )
            for step in range(1, size)
        ]
        landed[stage, own] = held[stage]
        return copies

    def gather_up(stage, copies, size):
        for copy in copies:
            copy.wait_recv()
        total = landed[stage, 0]
        for place in range(1, size):
            total = total + landed[stage, place]
        held[stage + 1] = total

    shares = share(0, "row", rows, row)
    downs.last()
    block_out[...] = (middle_own[...] + down_result[...]).astype(jnp.bfloat16)
    gather_up(0, shares, rows)
    more = share(1, "col", cols, col)
    out_sum[half] = out.total(col)
    for step in range(1, cols):
        lined[step - 1].wait_recv()
        out_sum[half] += out_lined[step].astype(jnp.float32)
    out_copy = send(out_sum.at[half], out_sum.at[half], pair_sems, (5,), "dp", sibling())
    swaps[2].relay()
    down_copy.wait_recv()
    down_sum[...] = down_grad[...] + down_came[...]
    gather_up(1, more, cols)
    gain_copy = send(held.at[2], landed.at[2, 0], gain_sems, (2, 0), "dp", sibling())
    for moved in swaps:
        moved.land()
    gain_copy.wait_recv()
    gain_sum[...] = held[2] + landed[2, 0]
    out_copy.wait_recv()
    for copy in cats + lows + lined + shares + more + [down_copy, out_copy, gain_copy]:
        copy.wait_send()
    for paired in (gate, up, out, head):
        paired.copy.wait_send()
    for item in [mid, downs, acts] + swaps:
        item.sent()


def back_pass(args, hidden, head_dim, number):
    rows, cols = lax.axis_size("row"), lax.axis_size("col")
    local, width = args[0].shape
    length, height = rows * cols * local, width // cols // 2
    low, full = jnp.bfloat16, jnp.float32
    shape = jax.ShapeDtypeStruct
    slot, some = 3 * head_dim, head_dim // 2
    outs = [
        shape((local, width), low),
        shape((local, width), full),
        shape((cols, 2, height, hidden), low),
        shape((cols, 2, height, hidden), low),
        shape((cols, 2, height, slot), low),
        shape((2, some, width), full),
        shape((hidden, width), full),
        shape((8, width), full),
    ]

    def vmem(kind, *dims):
        return pltpu.VMEM(dims, kind)

    scratch = [
        vmem(low, rows, cols, local, width),
        vmem(low, cols, rows, local, head_dim),
        vmem(low, rows, cols, local, head_dim),
        vmem(low, rows, cols, local, slot),
        vmem(low, cols, rows, local, slot),
    ]
    for last in (hidden, hidden, slot):
        scratch += [
            vmem(full, cols, 2, height, last),
            vmem(full, cols, height, last),
            vmem(low, cols, height, last),
        ]
    scratch += [
        vmem(full, cols, 2, some, width),
        vmem(full, cols, some, width),
        vmem(low, cols, some, width),
        vmem(low, cols, some, width),
        vmem(full, hidden, width),
        vmem(full, hidden, width),
        vmem(low, rows, 1, local, width),
        vmem(low, rows * local, 2 * cols * head_dim),
        vmem(low, rows * local, cols * head_dim),
        vmem(full, length, head_dim),
        vmem(full, length, head_dim),
        vmem(full, length, head_dim),
        vmem(full, local, width),
        vmem(full, local, width),
        vmem(full, 3, 8, width),
        vmem(full, 3, max(rows, cols), 8, width),
        vmem(low, rows, cols, local, width),
    ]
    scratch += reduce_scratch(rows, 1, local, width) + reduce_scratch(rows, cols, local, width)
    scratch += dma(1, 5, cols) + dma(2, 5, cols) + dma(3, 2, cols) + dma(6)
    scratch += dma(cols) + dma(cols) + dma(cols) + dma(3, max(rows, cols))
    return call_kernel(back_kernel, args, outs, scratch, number)


def open_kernel(cols, head_dim, gate_got, up_got, head_got, gate, up, query, key, value):
    height, part = gate_got.shape[2:]
    for piece in range(2):
        lines = slice(piece * height, (piece + 1) * height)
        for col in range(cols):
            gate[lines, col * part : (col + 1) * part] = gate_got[col, piece].astype(jnp.float32)
            up[lines, col * part : (col + 1) * part] = up_got[col, piece].astype(jnp.float32)
            query[lines, col * head_dim : (col + 1) * head_dim] = head_got[
                col, piece, :, :head_dim
            ].astype(jnp.float32)
        for pair in range(cols // 2):
            for place, target in ((1, key), (2, value)):
                lanes = slice(place * head_dim, (place + 1) * head_dim)
                target[lines, pair * head_dim : (pair + 1) * head_dim] = head_got[
                    2 * pair, piece, :, lanes
                ].astype(jnp.float32) + head_got[2 * pair + 1, piece, :, lanes].astype(jnp.float32)


def call_kernel(body, args, outs, scratch, number):
    vmem = pl.BlockSpec(memory_space=pltpu.VMEM)
    return pl.pallas_call(
        body,
        out_shape=outs,
        in_specs=[vmem] * len(args),
        out_specs=[vmem] * len(outs),
        scratch_shapes=scratch,
        compiler_params=pltpu.CompilerParams(
            collective_id=number, has_side_effects=True, vmem_limit_bytes=VMEM_LIMIT
        ),
    )(*args)


def dma(*shape):
    return [pltpu.SemaphoreType.DMA(shape), pltpu.SemaphoreType.DMA(shape)]


def dot(left, right, left_dim=1, right_dim=0):
    return lax.dot_general(
        left,
        right,
        (((left_dim,), (right_dim,)), ((), ())),
        preferred_element_type=jnp.float32,
    )


def shards(
    block_input,
    seq_lengths,
    out_grad,
    attn_norm,
    query_weight,
    key_weight,
    value_weight,
    query_norm,
    key_norm,
    out_weight,
    ffn_norm,
    gate_weight,
    up_weight,
    down_weight,
):
    local_rows, width = block_input.shape
    head_dim = query_norm.shape[0]
    cols = lax.axis_size("col")
    length = local_rows * cols * lax.axis_size("row")
    hidden_width = gate_weight.shape[1] // cols
    residual = block_input.astype(jnp.float32)
    scale_in = head_norm(residual, attn_norm)[1]
    places = jnp.arange(length, dtype=jnp.int32)
    position = segment_info(seq_lengths[0], length)[1]
    begins = (places - position)[:, None]
    cosine, sine = rope_tables(position, head_dim)
    cosine = jnp.concatenate([cosine, cosine], axis=1)
    sine = jnp.concatenate([-sine, sine], axis=1)
    head_gains = jnp.stack([query_norm, key_norm])
    (
        input_blocks,
        out_blocks,
        out_weight_blocks,
        cat_blocks,
        gate_blocks,
        up_blocks,
        _,
        first_blocks,
        own_sums,
        query_rot,
        key_rot,
        value_low,
        attn_low,
        log_total,
    ) = front(
        block_input,
        out_grad,
        out_weight,
        query_weight,
        key_weight,
        value_weight,
        gate_weight,
        up_weight,
        attn_norm,
        head_gains,
        (cosine, sine, begins),
        0,
    )
    act_grad2, middle_own, down_part, slot_full, second, hidden, gate_low, up_low = hidden_pass(
        [input_blocks, out_blocks, out_weight_blocks, cat_blocks, gate_blocks, up_blocks],
        down_weight,
        ffn_norm,
        query_weight,
        key_weight,
        value_weight,
        1,
    )
    outs = back_pass(
        [block_input, out_grad, act_grad2, middle_own]
        + [attn_norm.reshape(1, width), ffn_norm.reshape(1, width)]
        + [out_weight_blocks, cat_blocks, out_blocks, first_blocks, second]
        + [hidden, gate_low, up_low, down_part, slot_full]
        + [query_rot, key_rot, value_low, attn_low, log_total]
        + [own_sums, head_gains, cosine, sine, begins],
        down_weight.shape[0],
        head_dim,
        2,
    )
    block_output, input_grad, gate_got, up_got, head_got, out_sum, grad_down, gain_sums = outs
    wide_shape = jax.ShapeDtypeStruct(gate_weight.shape, jnp.float32)
    grads = local_kernel(
        functools.partial(open_kernel, cols, head_dim),
        [gate_got, up_got, head_got],
        [wide_shape, wide_shape]
        + [
            jax.ShapeDtypeStruct(weight.shape, jnp.float32)
            for weight in (query_weight, key_weight, value_weight)
        ],
    )
    sums = tuple(grads) + (out_sum.reshape(out_weight.shape), grad_down, gain_sums)
    if lax.axis_size("dp") > 2:
        sums = lax.psum(tuple(0.5 * value for value in sums), "dp")
    grad_gate, grad_up, grad_query, grad_key, grad_value, grad_outweight, grad_down, gain_sums = sums
    return (
        block_output,
        input_grad,
        gain_sums[0],
        grad_query,
        grad_key,
        grad_value,
        gain_sums[2, :head_dim],
        gain_sums[3, :head_dim],
        grad_outweight,
        gain_sums[1],
        grad_gate,
        grad_up,
        grad_down,
    )


def solution(mesh):
    placed = (
        P(("dp", "row", "col"), None),
        P("dp", None),
        P(("dp", "row", "col"), None),
        P(),
        P("col", "row"),
        P("col", "row"),
        P("col", "row"),
        P(),
        P(),
        P(("row", "col"), None),
        P(),
        P("col", "row"),
        P("col", "row"),
        P(("row", "col"), None),
    )
    return jax.shard_map(
        shards,
        mesh=mesh,
        in_specs=placed,
        out_specs=(
            P(("dp", "row", "col"), None),
            P(("dp", "row", "col"), None),
            P(),
            P("col", "row"),
            P("col", "row"),
            P("col", "row"),
            P(),
            P(),
            P(("row", "col"), None),
            P(),
            P("col", "row"),
            P("col", "row"),
            P(("row", "col"), None),
        ),
        check_vma=False,
    )
```

```python
import functools
import math

import jax
import jax.numpy as jnp
from jax import lax
from jax.experimental import pallas as pl
from jax.experimental.pallas import tpu as pltpu
from jax.sharding import PartitionSpec as P

EPSILON = 1e-05
THETA = 1000000.0


def segment_info(seq_lengths, length):
    order = jnp.arange(seq_lengths.shape[0], dtype=jnp.int32)
    up_to = order[:, None] <= order[None, :]
    end_points = jnp.sum(jnp.where(up_to, seq_lengths[:, None], 0), axis=0)
    places = jnp.arange(length, dtype=jnp.int32)
    passed = (places[:, None] >= end_points[None, :]).astype(jnp.int32)
    segment = jnp.sum(passed, axis=1)
    begins = jnp.sum(passed * seq_lengths[None, :], axis=1)
    return (segment, places - begins)


def rope_tables(position, width):
    half_width = width // 2
    exponent = jnp.arange(half_width, dtype=jnp.float32) * (2.0 / width)
    frequency = jnp.exp(-math.log(THETA) * exponent)
    angles = position.astype(jnp.float32)[:, None] * frequency[None, :]
    return (jnp.cos(angles), jnp.sin(angles))


def head_norm(values, gain_vec):
    inv_rms = lax.rsqrt(jnp.mean(values * values, axis=-1, keepdims=True) + EPSILON)
    return (values * inv_rms * gain_vec, inv_rms)


def head_norm_back(cotangent, values, inv_rms, gain_vec):
    normed = values * inv_rms
    weighted = cotangent * gain_vec
    gain_grad = jnp.sum(cotangent * normed, axis=0)
    inner_mean = jnp.mean(weighted * normed, axis=-1, keepdims=True)
    return (inv_rms * (weighted - normed * inner_mean), gain_grad)


def swap_halves(values):
    half_width = values.shape[-1] // 2
    return jnp.concatenate([values[:, half_width:], values[:, :half_width]], axis=1)


def block_probability(query_block, key_rows, begins, offset, low, shift):
    score_scale = 1.0 / math.sqrt(query_block.shape[1])
    scores = dot(query_block, key_rows, 1, 1) * score_scale
    places = low + lax.broadcasted_iota(jnp.int32, scores.shape, 1)
    row_places = offset + lax.broadcasted_iota(jnp.int32, scores.shape, 0)
    allowed = (places >= begins) & (places <= row_places)
    if shift is None:
        shift = jnp.log(jnp.sum(jnp.where(allowed, jnp.exp(scores), 0.0), axis=1, keepdims=True))
    probability = jnp.where(allowed, jnp.exp(scores - shift), 0.0).astype(jnp.bfloat16)
    return probability, shift


def spans(length, longest, block):
    return [
        (offset, max(0, (offset - longest) // 128 * 128), block)
        for offset in range(0, length, block)
    ]


def local_kernel(body, args, outs, scratch=()):
    vmem = pl.BlockSpec(memory_space=pltpu.VMEM)
    return pl.pallas_call(
        body,
        out_shape=outs,
        in_specs=[vmem] * len(args),
        out_specs=[vmem] * len(outs),
        scratch_shapes=list(scratch),
    )(*args)


MESH = pl.DeviceIdType.MESH
VMEM_LIMIT = 56 * 1024 * 1024


def send(source, target, sems, place, axis, index):
    copy = pltpu.make_async_remote_copy(
        src_ref=source,
        dst_ref=target,
        send_sem=sems[0].at[place],
        recv_sem=sems[1].at[place],
        device_id={axis: index},
        device_id_type=MESH,
    )
    copy.start()
    return copy


def neighbours():
    rows, row = lax.axis_size("row"), lax.axis_index("row")
    near = row + 1 - 2 * lax.rem(row, 2)
    far = lax.rem(row + rows // 2, rows)
    return near, far


def sibling():
    own = lax.axis_index("dp")
    return own + 1 - 2 * lax.rem(own, 2)


def greet(corner=False):
    cols, col = lax.axis_size("col"), lax.axis_index("col")
    near, far = neighbours()
    peers = [("col", lax.rem(col + step, cols)) for step in range(1, cols)]
    peers += [("row", near), ("row", far), ("dp", sibling())]
    if corner:
        peers.append(("row", lax.rem(near + lax.axis_size("row") // 2, lax.axis_size("row"))))
    barrier = pltpu.get_barrier_semaphore()
    for axis, index in peers:
        pl.semaphore_signal(barrier, inc=1, device_id={axis: index}, device_id_type=MESH)
    pl.semaphore_wait(barrier, len(peers))


class Gather:
    def __init__(self, source, block, part, sems, item):
        self.source, self.block, self.part = source, block, part
        self.sems, self.item = sems, item
        self.cols, self.col = lax.axis_size("col"), lax.axis_index("col")
        self.row = lax.axis_index("row")
        self.near, self.far = neighbours()
        self.lines, self.planes, self.relays = {}, {}, {}

    def origin(self, step):
        return lax.rem(self.col + self.cols - step, self.cols)

    def line(self):
        for step in range(1, self.cols):
            self.lines[step] = send(
                self.source,
                self.block(self.row, self.col),
                self.sems,
                (self.item, 0, step),
                "col",
                lax.rem(self.col + step, self.cols),
            )

    def plane(self, step):
        target = self.block(self.row, self.origin(step))
        if step:
            self.lines[step].wait_recv()
        for kind, peer in ((1, self.near), (2, self.far)):
            self.planes[step, kind] = send(
                target if step else self.source,
                target,
                self.sems,
                (self.item, kind, step),
                "row",
                peer,
            )

    def relay(self, step):
        for kind, source, peer in ((1, self.near, self.far), (2, self.far, self.near)):
            self.planes[step, kind].wait_recv()
            piece = self.part(source, self.origin(step), kind - 1)
            self.relays[step, kind] = send(
                piece, piece, self.sems, (self.item, kind + 2, step), "row", peer
            )

    def land(self, step):
        for kind in (1, 2):
            self.relays[step, kind].wait_recv()

    def sent(self):
        for copies in (self.lines, self.planes, self.relays):
            for copy in copies.values():
                copy.wait_send()


class Swap:
    def __init__(self, source, target, sems, item, whole=False):
        self.source, self.target, self.sems, self.item = source, target, sems, item
        self.cols, self.col = lax.axis_size("col"), lax.axis_index("col")
        self.half = lax.rem(lax.axis_index("dp"), 2)
        self.lines, self.pairs, self.first = {}, {}, 0 if whole else 1

    def line(self):
        for step in range(1, self.cols):
            peer = lax.rem(self.col + step, self.cols)
            self.lines[step] = send(
                self.source(peer, self.half),
                self.target.at[self.col, self.half],
                self.sems,
                (self.item, 0, step),
                "col",
                peer,
            )

    def relay(self):
        for step in range(self.first, self.cols):
            if step:
                self.lines[step].wait_recv()
            piece = self.target.at[lax.rem(self.col + self.cols - step, self.cols), self.half]
            self.pairs[step] = send(
                piece, piece, self.sems, (self.item, 1, step), "dp", sibling()
            )

    def land(self):
        for copy in self.pairs.values():
            copy.wait_recv()

    def sent(self):
        for copies in (self.lines, self.pairs):
            for copy in copies.values():
                copy.wait_send()


def front_kernel(*refs):
    (own_in, own_grad, own_out, query, key, value, gate, up) = refs[:8]
    (attn_norm, gains, cosine, sine, begins) = refs[8:13]
    (in_all, grad_all, out_all, cat_all, wide_all, slot_all) = refs[13:19]
    (first, sums, query_rot, key_rot, value_low, low_rows, totals) = refs[19:26]
    (slot_part, wide_part) = refs[26:28]
    gather_sems, swap_sems, pair_sems = refs[28:30], refs[30:32], refs[32:34]
    rows, cols = lax.axis_size("row"), lax.axis_size("col")
    row, col = lax.axis_index("row"), lax.axis_index("col")
    half = lax.rem(lax.axis_index("dp"), 2)
    near, far = neighbours()
    length, head_dim = query_rot.shape
    width = own_in.shape[1]
    local = own_in.shape[0]
    block = length // rows

    def split(ref):
        count = ref.shape[2] // 2
        return (
            lambda r, c: ref.at[r, c],
            lambda r, c, k: ref.at[r, c, pl.ds(k * count, count)],
        )

    greet()
    inputs = Gather(own_in, *split(in_all), gather_sems, 0)
    inputs.line()
    inputs.plane(0)
    height = query.shape[0] // 2
    for place in range(cols):
        for piece in range(2):
            lines = slice(piece * height, (piece + 1) * height)
            lanes = slice(place // 2 * head_dim, (place // 2 + 1) * head_dim)
            slot_part[place, piece, :, :head_dim] = query[
                lines, place * head_dim : (place + 1) * head_dim
            ]
            slot_part[place, piece, :, head_dim : 2 * head_dim] = key[lines, lanes]
            slot_part[place, piece, :, 2 * head_dim :] = value[lines, lanes]
    slots = Swap(lambda c, h: slot_part.at[c, h], slot_all, swap_sems, 0)
    slots.line()
    slot_all[col] = slot_part[col]
    in_all[row, col] = own_in[...]
    for step in range(1, cols):
        inputs.plane(step)
    hidden = gate.shape[1] // cols
    for kind, source in ((0, gate), (1, up)):
        for place in range(cols):
            for piece in range(2):
                wide_part[place, piece, :, kind * hidden : (kind + 1) * hidden] = source[
                    piece * height : (piece + 1) * height, place * hidden : (place + 1) * hidden
                ]
    slots.relay()
    inputs.relay(0)
    grads = Gather(own_grad, *split(grad_all), gather_sems, 1)
    grads.line()
    inputs.relay(1)
    wide = Swap(lambda c, h: wide_part.at[c, h], wide_all, swap_sems, 1)
    wide.line()
    inputs.relay(2)
    count = own_out.shape[1] // 2
    outs = Gather(
        own_out.at[half],
        lambda r, c: out_all.at[r, c, half],
        lambda r, c, k: out_all.at[r, c, half, pl.ds(k * count, count)],
        gather_sems,
        2,
    )
    outs.line()
    inputs.relay(3)
    grads.plane(0)
    outs.plane(0)
    wide_all[col] = wide_part[col]
    grad_all[row, col] = own_grad[...]
    out_all[row, col] = own_out[...]
    slots.land()

    def project(place):
        for c in range(cols):
            values = in_all[place, c].astype(jnp.float32)
            normed = head_norm(values, attn_norm[...])[0]
            first[place, c] = normed.astype(jnp.bfloat16)
        lines = pl.ds(pl.multiple_of(place * block, block), block)
        sums[lines, :] = dot(
            first[place].reshape(block, width), slot_all[...].reshape(width, 3 * head_dim)
        )

    project(row)
    project(near)
    project(far)
    for step in range(1, cols):
        grads.plane(step)
    for step in range(cols):
        inputs.land(step)
    project(lax.rem(near + rows // 2, rows))
    for step in range(1, cols):
        outs.plane(step)
    for place, target in ((0, query_rot), (1, key_rot)):
        normed = head_norm(
            sums[:, place * head_dim : (place + 1) * head_dim], gains[place : place + 1, :]
        )[0]
        target[...] = (normed * cosine[...] + swap_halves(normed) * sine[...]).astype(jnp.bfloat16)
    value_low[...] = sums[:, 2 * head_dim : 3 * head_dim].astype(jnp.bfloat16)

    def cat(part):
        places = pl.ds(part * (rows // 2), rows // 2)
        return Gather(
            cat_all.at[places, row, col],
            lambda r, c: cat_all.at[places, r, c],
            lambda r, c, k: cat_all.at[places, r, c, pl.ds(k * head_dim // 2, head_dim // 2)],
            gather_sems,
            3 + part,
        )

    cats = []
    for offset, low, _ in spans(length, length // 2, block):
        number = offset // block
        lines, keys = slice(offset, offset + block), slice(low, offset + block)
        probability, total = block_probability(
            query_rot[lines, :], key_rot[keys, :], begins[lines, :], offset, low, None
        )
        totals[lines, :] = total
        low_rows[lines, :] = dot(probability, value_low[keys, :]).astype(jnp.bfloat16)
        cat_all[number, row, col] = dot(value_low[keys, :], probability, 0, 1).astype(jnp.bfloat16)
        if 2 * (number + 1) % rows == 0:
            cats.append(cat(2 * (number + 1) // rows - 1))
            cats[-1].line()
            cats[-1].plane(0)
        if number == 0:
            wide.relay()
            grads.relay(0)
            grads.relay(1)
        if number == 1:
            grads.relay(2)
            grads.relay(3)
        if number == 2:
            for step in range(cols):
                outs.relay(step)
            for step in range(1, cols):
                cats[0].plane(step)
    for step in range(1, cols):
        cats[1].plane(step)
    for gather in cats:
        for step in range(cols):
            gather.relay(step)
    pairs = []
    for step in range(cols):
        outs.land(step)
    for number, place in enumerate((near, far, lax.rem(near + rows // 2, rows))):
        piece = out_all.at[place, :, half]
        pairs.append(send(piece, piece, pair_sems, (number,), "dp", sibling()))
    for step in range(1, cols):
        piece = out_all.at[row, lax.rem(col + cols - step, cols), half]
        pairs.append(send(piece, piece, pair_sems, (2 + step,), "dp", sibling()))
    wide.land()
    for gather in [grads] + cats:
        for step in range(cols):
            gather.land(step)
    for copy in pairs:
        copy.wait()
    for item in [inputs, grads, outs, slots, wide] + cats:
        item.sent()


def front(own_in, own_grad, own_out, query, key, value, gate, up, attn_norm, gains, tables, number):
    rows, cols = lax.axis_size("row"), lax.axis_size("col")
    local, width = own_in.shape
    length, head_dim = local * rows * cols, gains.shape[1]
    hidden, height = gate.shape[1] // cols, gate.shape[0] // 2
    low = jnp.bfloat16
    blocks = jax.ShapeDtypeStruct((rows, cols, local, width), low)
    halves = own_out.shape[0] // 2
    wide = (cols, 2, height, 2 * hidden)
    slot = (cols, 2, height, 3 * head_dim)
    shape = jax.ShapeDtypeStruct
    head_rows = shape((length, head_dim), low)
    outs = [
        blocks,
        blocks,
        shape((rows, cols, 2, halves, width), low),
        shape((rows, rows, cols, head_dim, length // rows), low),
        shape(wide, low),
        shape(slot, low),
        blocks,
        shape((length, 3 * head_dim), jnp.float32),
        head_rows,
        head_rows,
        head_rows,
        head_rows,
        shape((length, 1), jnp.float32),
    ]
    scratch = [pltpu.VMEM(slot, low), pltpu.VMEM(wide, low)]
    scratch += dma(5, 5, cols) + dma(2, 2, cols) + dma(2 + cols)
    args = [own_in, own_grad, own_out.reshape(2, halves, width), query, key, value, gate, up]
    args += [attn_norm.reshape(1, width), gains] + list(tables)
    return call_kernel(front_kernel, args, outs, scratch, number)


class Reduce:
    def __init__(self, part, relayed, planed, staged, lined, result, sems, item):
        self.part, self.relayed, self.planed = part, relayed, planed
        self.staged, self.lined, self.result = staged, lined, result
        self.sems, self.item = sems, item
        self.cols = part.shape[1]
        self.col = lax.axis_index("col") if self.cols > 1 else 0
        self.row = lax.axis_index("row")
        self.near, self.far = neighbours()
        self.cross = lax.rem(self.near + lax.axis_size("row") // 2, lax.axis_size("row"))
        self.count = part.shape[2] // 2
        self.relays, self.planes, self.lines = [], [], []

    def first(self):
        for kind, peer in ((0, self.near), (1, self.far)):
            self.relays.append(
                send(
                    self.part.at[self.cross, :, pl.ds(kind * self.count, self.count)],
                    self.relayed.at[kind],
                    self.sems,
                    (self.item, 1 + kind, 0),
                    "row",
                    peer,
                )
            )

    def toward(self, kind):
        peer, came = (self.near, self.far)[kind], 1 - kind
        self.relays[came].wait_recv()
        lines = slice(came * self.count, (came + 1) * self.count)
        self.part[peer, :, lines] = (
            self.part[peer, :, lines].astype(jnp.float32)
            + self.relayed[came].astype(jnp.float32)
        ).astype(jnp.bfloat16)
        self.planes.append(
            send(
                self.part.at[peer],
                self.planed.at[kind],
                self.sems,
                (self.item, 3 + kind, 0),
                "row",
                peer,
            )
        )

    def total(self, place):
        summed = self.part[self.row, place].astype(jnp.float32)
        for kind in range(2):
            summed = summed + self.planed[kind, place].astype(jnp.float32)
        return summed

    def own(self):
        for copy in self.planes:
            copy.wait_recv()
        for step in range(1, self.cols):
            place = lax.rem(self.col + step, self.cols)
            self.staged[step] = self.total(place).astype(jnp.bfloat16)
            self.lines.append(
                send(
                    self.staged.at[step],
                    self.lined.at[step],
                    self.sems,
                    (self.item, 0, step),
                    "col",
                    place,
                )
            )
        self.result[...] = self.total(self.col)

    def last(self):
        for step in range(1, self.cols):
            self.lines[step - 1].wait_recv()
            self.result[...] += self.lined[step].astype(jnp.float32)

    def sent(self):
        for copy in self.relays + self.planes + self.lines:
            copy.wait_send()


def reduce_scratch(rows, cols, local, width):
    low = jnp.bfloat16
    return [
        pltpu.VMEM((2, cols, local // 2, width), low),
        pltpu.VMEM((2, cols, local, width), low),
        pltpu.VMEM((cols, local, width), low),
        pltpu.VMEM((cols, local, width), low),
    ]


def hidden_kernel(*refs):
    in_all, grad_all, out_all, cat_all, wide_all, down, ffn_norm = refs[:7]
    query, key, value = refs[7:10]
    act_own, middle_own, down_part, slot_all = refs[10:14]
    second_all, hidden_all, wide_low = refs[14:17]
    act_parts, act_halves, middle_block, slot_part = refs[17:21]
    low_all, wide_sum, wide_came = refs[21:24]
    act_scratch, rest = (refs[24:28], refs[28:32]), refs[32:]
    sems, swap_sems, pair_sems = rest[:2], rest[2:4], rest[4:6]
    rows, cols = lax.axis_size("row"), lax.axis_size("col")
    row, col = lax.axis_index("row"), lax.axis_index("col")
    near, far = neighbours()
    cross = lax.rem(near + rows // 2, rows)
    local, width = in_all.shape[2:]
    block, hidden = cols * local, down.shape[0]
    greet()
    height, begin = query.shape[0] // 2, 0
    for source in (query, key, value):
        lanes = slice(begin, begin + source.shape[1])
        for piece in range(2):
            slot_part[piece, :, lanes] = source[piece * height : (piece + 1) * height, :]
        begin += source.shape[1]
    slots = Swap(lambda c, h: slot_part.at[h], slot_all, swap_sems, 0)
    slots.line()
    slot_all[col] = slot_part[...]
    acts = [
        Reduce(act_parts.at[side], *act_scratch[side], act_halves.at[side], sems, side)
        for side in range(2)
    ]

    def work(place):
        mixed = dot(cat_all[place].reshape(width, block), out_all[...].reshape(width, width), 0, 0)
        middle = in_all[place].reshape(block, width).astype(jnp.float32) + mixed
        middle_block[...] = middle
        second = head_norm(middle, ffn_norm[...])[0].astype(jnp.bfloat16)
        second_all[place] = second
        wide_weight = wide_all[...].reshape(width, 2 * hidden)
        wide_sums = dot(second, wide_weight)
        gating, upward = wide_sums[:, :hidden], wide_sums[:, hidden:]
        hidden_grad = dot(grad_all[place].reshape(block, width), down[...], 1, 1)
        sigmoid_gate = jax.nn.sigmoid(gating)
        activated = gating * sigmoid_gate
        hidden_low = (activated * upward).astype(jnp.bfloat16)
        gate_low = (
            hidden_grad * upward * sigmoid_gate * (1.0 + gating * (1.0 - sigmoid_gate))
        ).astype(jnp.bfloat16)
        up_low = (hidden_grad * activated).astype(jnp.bfloat16)
        hidden_all[place] = hidden_low
        low_all[place, :, :hidden] = gate_low
        low_all[place, :, hidden:] = up_low
        act = dot(low_all[place], wide_weight, 1, 1).astype(jnp.bfloat16)
        for side in range(2):
            act_parts[side, place] = act[
                :, side * (width // 2) : (side + 1) * (width // 2)
            ].reshape(cols, local, width // 2)

    def work_down(place):
        down_part[place] = (
            dot(hidden_all[place], down[...]).astype(jnp.bfloat16).reshape(cols, local, width)
        )

    work(cross)
    for item in acts:
        item.first()
    work_down(cross)
    work(near)
    for item in acts:
        item.toward(0)
    slots.relay()
    work(far)
    for item in acts:
        item.toward(1)
    work(row)
    lines = pl.ds(pl.multiple_of(col * local, local), local)
    middle_own[...] = middle_block[lines, :]
    acts[0].own()
    for place in (near, far, row):
        work_down(place)
    acts[1].own()
    wide = Paired(wide_sum, wide_came, pair_sems, 0)
    wide_sum[...] = dot(
        second_all[...].reshape(rows * block, width),
        low_all[...].reshape(rows * block, 2 * hidden),
        0,
        0,
    ).reshape(wide_sum.shape)
    wide.pair()
    acts[0].last()
    slots.land()
    wide.copy.wait_recv()
    for place in range(cols):
        total = wide.total(place).astype(jnp.bfloat16)
        for side in range(2):
            wide_low[side, place] = total[side * (height // 2) : (side + 1) * (height // 2), :]
    acts[1].last()
    for side in range(2):
        act_own[:, side * (width // 2) : (side + 1) * (width // 2)] = act_halves[side]
    for item in acts:
        item.sent()
    slots.sent()
    wide.copy.wait_send()


def hidden_pass(blocks, down, ffn_norm, query, key, value, number):
    rows, cols, local, width = blocks[0].shape
    block, hidden, height = cols * local, down.shape[0], query.shape[0] // 2
    shape = jax.ShapeDtypeStruct
    own, low, full = shape((local, width), jnp.float32), jnp.bfloat16, jnp.float32
    slot = (2, height, query.shape[1] + key.shape[1] + value.shape[1])
    outs = [own, own, shape((rows, cols, local, width), low), shape((cols,) + slot, low)]
    outs += [shape((rows, block, width), low), shape((rows, block, hidden), low)]
    outs += [shape((2, cols, height // 2, 2 * hidden), low)]
    scratch = [
        pltpu.VMEM((2, rows, cols, local, width // 2), low),
        pltpu.VMEM((2, local, width // 2), full),
        pltpu.VMEM((block, width), full),
        pltpu.VMEM(slot, low),
        pltpu.VMEM((rows, block, 2 * hidden), low),
        pltpu.VMEM((cols, 2, height, 2 * hidden), full),
        pltpu.VMEM((cols, height, 2 * hidden), full),
    ]
    scratch += reduce_scratch(rows, cols, local, width // 2) * 2
    scratch += dma(2, 5, cols) + dma(1, 2, cols) + dma(1)
    args = list(blocks) + [down, ffn_norm.reshape(1, width), query, key, value]
    return call_kernel(hidden_kernel, args, outs, scratch, number)


class Paired:
    def __init__(self, part, came, sems, item):
        self.part, self.came, self.sems, self.item = part, came, sems, item
        self.half = lax.rem(lax.axis_index("dp"), 2)

    def pair(self):
        self.copy = send(
            self.part.at[:, 1 - self.half], self.came, self.sems, (self.item,), "dp", sibling()
        )

    def total(self, place):
        return self.part[place, self.half] + self.came[place]


def back_kernel(*refs):
    own_in, own_grad, act_own, middle_own, attn_norm, ffn_norm = refs[:6]
    out_all, cat_all, grad_all, first = refs[6:10]
    hidden_all, wide_low, down_given, slot_all = refs[10:14]
    query_rot, key_rot, value_low, low_rows, totals = refs[14:19]
    sums, gains, cosine, sine, begins = refs[19:24]
    outs, scratch = refs[24:31], refs[31:]
    block_out, in_grad, wide_got, head_got, out_sum, down_sum, gain_sum = outs
    mid_all, cat_part, grads_in, own_slot, slot_mine, slots_in = scratch[:6]
    head_sum, head_came, head_low = scratch[6:9]
    out_part, out_came, out_low, out_lined = scratch[9:13]
    down_grad, down_came, act_part = scratch[13:16]
    low_even, low_odd, query_acc, key_acc, value_acc = scratch[16:21]
    act_result, down_result, held, landed, down_part = scratch[21:26]
    act_scratch, down_scratch = scratch[26:30], scratch[30:34]
    sems = scratch[34:]
    mid_sems, sum_sems, swap_sems, pair_sems = sems[:2], sems[2:4], sems[4:6], sems[6:8]
    cat_sems, low_sems, out_sems, gain_sems = sems[8:10], sems[10:12], sems[12:14], sems[14:16]
    rows, cols = lax.axis_size("row"), lax.axis_size("col")
    row, col = lax.axis_index("row"), lax.axis_index("col")
    half = lax.rem(lax.axis_index("dp"), 2)
    local, width = own_in.shape
    length, head_dim = query_rot.shape
    block = cols * local
    near, far = neighbours()
    greet(corner=True)

    wides = [
        Swap(
            lambda c, h, side=side: wide_low.at[side, c],
            wide_got.at[side],
            swap_sems,
            side,
            whole=True,
        )
        for side in range(2)
    ]
    wides[0].line()
    middle = middle_own[...]
    scale_mid = head_norm(middle, ffn_norm[...])[1]
    middle_back, ffn_gain = head_norm_back(act_own[...], middle, scale_mid, ffn_norm[...])
    middle_grad = own_grad[...].astype(jnp.float32) + middle_back
    in_grad[...] = middle_grad
    mid_all[row, col] = middle_grad.astype(jnp.bfloat16)
    mid = Gather(
        mid_all.at[row, col],
        lambda r, c: mid_all.at[r, c],
        lambda r, c, k: mid_all.at[r, c, pl.ds(k * (local // 2), local // 2)],
        mid_sems,
        0,
    )
    mid.plane(0)
    for step in range(1, cols):
        mid_all[:, lax.rem(col + step, cols)] = jnp.zeros((rows, local, width), jnp.bfloat16)
    held[0] = jnp.zeros(held.shape[1:], jnp.float32)
    held[0, 1:2, :] = ffn_gain[None, :]

    for side in range(2):
        wide_got[side, col, half] = wide_low[side, col]
    down_part[...] = down_given[...]
    mid.relay(0)
    down_grad[...] = dot(
        hidden_all[...].reshape(length, hidden_all.shape[-1]),
        grad_all[...].reshape(length, width),
        0,
        0,
    )
    down_copy = send(down_grad, down_came, pair_sems, (3,), "dp", sibling())
    mid.land(0)

    cat_grad = dot(
        mid_all[:, col].reshape(rows * local, width),
        out_all[row].reshape(cols * head_dim, width),
        1,
        1,
    ).astype(jnp.bfloat16)
    for place in range(cols):
        piece = cat_grad[:, place * head_dim : (place + 1) * head_dim]
        cat_part[place, :, :head_dim] = piece[: rows // 2 * local]
        cat_part[place, :, head_dim:] = piece[rows // 2 * local :]

    def turn(source, target, sems):
        return [
            send(
                source(lax.rem(col + step, cols)),
                target,
                sems,
                (step,),
                "col",
                lax.rem(col + step, cols),
            )
            for step in range(1, cols)
        ]

    cats = turn(lambda c: cat_part.at[c], grads_in.at[col], cat_sems)
    grads_in[col] = cat_part[col]
    wides[1].line()
    downs = Reduce(down_part, *down_scratch, down_result, sum_sems, 0)
    downs.first()

    mixed = None
    for place in range(rows):
        term = dot(
            cat_all[place, row].reshape(cols * head_dim, block),
            mid_all[place].reshape(block, width),
        )
        mixed = term if mixed is None else mixed + term
    out = Paired(out_part, out_came, pair_sems, 2)
    out_part[...] = mixed.reshape(cols, 2, head_dim // 2, width)
    out.pair()
    for copy in cats:
        copy.wait_recv()

    score_scale = 1.0 / math.sqrt(head_dim)
    key_acc[...] = jnp.zeros_like(key_acc)
    value_acc[...] = jnp.zeros_like(value_acc)
    for offset, low, _ in spans(length, length // 2, block):
        number = offset // block
        lines, keys = slice(offset, offset + block), slice(low, offset + block)
        probability, _ = block_probability(
            query_rot[lines, :], key_rot[keys, :], begins[lines, :], offset, low, totals[lines, :]
        )
        upper, right = number % (rows // 2) * local, number // (rows // 2) * head_dim
        grad_block = grads_in[:, upper : upper + local, right : right + head_dim].reshape(
            block, head_dim
        )
        value_acc[keys, :] += dot(probability, grad_block, 0, 0)
        row_delta = jnp.sum(
            grad_block.astype(jnp.float32) * low_rows[lines, :].astype(jnp.float32),
            axis=1,
            keepdims=True,
        )
        prob_grad = dot(grad_block, value_low[keys, :], 1, 1)
        score_grad = (
            score_scale * probability.astype(jnp.float32) * (prob_grad - row_delta)
        ).astype(jnp.bfloat16)
        query_acc[lines, :] = dot(score_grad, key_rot[keys, :])
        key_acc[keys, :] += dot(score_grad, query_rot[lines, :], 0, 0)
        if number in (0, 1):
            downs.toward(number)
    slot = 3 * head_dim

    def keep(place, value):
        own_slot[:, place * head_dim : (place + 1) * head_dim] = value
        pieces = value.reshape(rows, cols, local, head_dim)
        for number in range(rows):
            upper = number % (rows // 2) * local
            begin = number // (rows // 2) * slot + place * head_dim
            slot_mine[:, upper : upper + local, begin : begin + head_dim] = pieces[number]

    for place, source in ((0, query_acc), (1, key_acc)):
        raw = sums[:, place * head_dim : (place + 1) * head_dim]
        gain = gains[place : place + 1, :]
        inv_rms = head_norm(raw, gain)[1]
        cotangent = source[...] * cosine[...] - swap_halves(source[...]) * sine[...]
        low_part, gain_grad = head_norm_back(cotangent, raw, inv_rms, gain)
        keep(place, low_part.astype(jnp.bfloat16))
        held[0, 2 + place : 3 + place, :head_dim] = gain_grad[None, :]
    keep(2, value_acc[...].astype(jnp.bfloat16))
    lows = turn(lambda c: slot_mine.at[c], slots_in.at[col], low_sems)
    slots_in[col] = slot_mine[col]

    head = Paired(head_sum, head_came, pair_sems, 4)
    head_grad = dot(own_slot[...], first[...].reshape(length, width), 0, 0)
    for place in range(cols):
        head_sum[place] = head_grad[
            :, place * (width // cols) : (place + 1) * (width // cols)
        ].reshape(head_sum.shape[1:])
    head.pair()
    out.copy.wait_recv()
    for place in range(cols):
        out_low[place] = out.total(place).astype(jnp.bfloat16)
    lined = [
        send(
            out_low.at[lax.rem(col + step, cols)],
            out_lined.at[step],
            out_sems,
            (step,),
            "col",
            lax.rem(col + step, cols),
        )
        for step in range(1, cols)
    ]
    for copy in lows:
        copy.wait_recv()
    for place in range(cols):
        lanes = slice(place * head_dim, (place + 1) * head_dim)
        came = jnp.concatenate([slots_in[place, :, :slot], slots_in[place, :, slot:]], axis=0)
        low_even[:, lanes] = came[:, :head_dim]
        target, offset = (low_odd, 0) if place % 2 else (low_even, cols * head_dim)
        for kind in (0, 1):
            begin = offset + (kind * (cols // 2) + place // 2) * head_dim
            target[:, begin : begin + head_dim] = came[
                :, (1 + kind) * head_dim : (2 + kind) * head_dim
            ]
    slot_weight = slot_all[...].reshape(width, slot_all.shape[-1])
    act = dot(low_even[...], slot_weight, 1, 1) + dot(
        low_odd[...], slot_weight[:, cols * head_dim :], 1, 1
    )
    act_part[...] = act.astype(jnp.bfloat16).reshape(act_part.shape)
    acts = Reduce(act_part, *act_scratch, act_result, sum_sems, 1)
    acts.first()
    head.copy.wait_recv()
    for place in range(cols):
        head_low[place] = head.total(place).astype(jnp.bfloat16)
    heads = Swap(lambda c, h: head_low.at[c], head_got, swap_sems, 2, whole=True)
    heads.line()
    head_got[col, half] = head_low[col]
    downs.own()
    acts.toward(0)
    acts.toward(1)
    wides[0].relay()
    wides[1].relay()
    acts.own()

    residual = own_in[...].astype(jnp.float32)
    scale_in = head_norm(residual, attn_norm[...])[1]
    input_back, attn_gain = head_norm_back(act_result[...], residual, scale_in, attn_norm[...])
    in_grad[...] += input_back
    held[0, 0:1, :] = attn_gain[None, :]

    def share(stage, axis, size, own):
        copies = [
            send(
                held.at[stage],
                landed.at[stage, own],
                gain_sems,
                (stage, step),
                axis,
                lax.rem(own + step, size),
            )
            for step in range(1, size)
        ]
        landed[stage, own] = held[stage]
        return copies

    def gather_up(stage, copies, size):
        for copy in copies:
            copy.wait_recv()
        total = landed[stage, 0]
        for place in range(1, size):
            total = total + landed[stage, place]
        held[stage + 1] = total

    shares = share(0, "row", rows, row)
    downs.last()
    block_out[...] = (middle_own[...] + down_result[...]).astype(jnp.bfloat16)
    gather_up(0, shares, rows)
    more = share(1, "col", cols, col)
    out_sum[half] = out.total(col)
    for step in range(1, cols):
        lined[step - 1].wait_recv()
        out_sum[half] += out_lined[step].astype(jnp.float32)
    out_copy = send(out_sum.at[half], out_sum.at[half], pair_sems, (5,), "dp", sibling())
    heads.relay()
    down_copy.wait_recv()
    down_sum[...] = down_grad[...] + down_came[...]
    gather_up(1, more, cols)
    gain_copy = send(held.at[2], landed.at[2, 0], gain_sems, (2, 0), "dp", sibling())
    for moved in wides + [heads]:
        moved.land()
    gain_copy.wait_recv()
    gain_sum[...] = held[2] + landed[2, 0]
    out_copy.wait_recv()
    for copy in cats + lows + lined + shares + more + [down_copy, out_copy, gain_copy]:
        copy.wait_send()
    for paired in (out, head):
        paired.copy.wait_send()
    for item in [mid, downs, acts, heads] + wides:
        item.sent()


def back_pass(args, hidden, head_dim, number):
    rows, cols = lax.axis_size("row"), lax.axis_size("col")
    local, width = args[0].shape
    length, height = rows * cols * local, width // cols // 2
    low, full = jnp.bfloat16, jnp.float32
    shape = jax.ShapeDtypeStruct
    slot, some = 3 * head_dim, head_dim // 2
    outs = [
        shape((local, width), low),
        shape((local, width), full),
        shape((2, cols, 2, height // 2, 2 * hidden), low),
        shape((cols, 2, slot // 2, width // cols), low),
        shape((2, some, width), full),
        shape((hidden, width), full),
        shape((8, width), full),
    ]

    def vmem(kind, *dims):
        return pltpu.VMEM(dims, kind)

    scratch = [
        vmem(low, rows, cols, local, width),
        vmem(low, cols, rows // 2 * local, 2 * head_dim),
        vmem(low, cols, rows // 2 * local, 2 * head_dim),
        vmem(low, length, slot),
        vmem(low, cols, rows // 2 * local, 2 * slot),
        vmem(low, cols, rows // 2 * local, 2 * slot),
        vmem(full, cols, 2, slot // 2, width // cols),
        vmem(full, cols, slot // 2, width // cols),
        vmem(low, cols, slot // 2, width // cols),
    ]
    scratch += [
        vmem(full, cols, 2, some, width),
        vmem(full, cols, some, width),
        vmem(low, cols, some, width),
        vmem(low, cols, some, width),
        vmem(full, hidden, width),
        vmem(full, hidden, width),
        vmem(low, rows, 1, local, width),
        vmem(low, rows * local, 2 * cols * head_dim),
        vmem(low, rows * local, cols * head_dim),
        vmem(full, length, head_dim),
        vmem(full, length, head_dim),
        vmem(full, length, head_dim),
        vmem(full, local, width),
        vmem(full, local, width),
        vmem(full, 3, 8, width),
        vmem(full, 3, max(rows, cols), 8, width),
        vmem(low, rows, cols, local, width),
    ]
    scratch += reduce_scratch(rows, 1, local, width) + reduce_scratch(rows, cols, local, width)
    scratch += dma(1, 5, cols) + dma(2, 5, cols) + dma(3, 2, cols) + dma(6)
    scratch += dma(cols) + dma(cols) + dma(cols) + dma(3, max(rows, cols))
    return call_kernel(back_kernel, args, outs, scratch, number)


def open_kernel(cols, head_dim, wide_got, head_got, gate, up, query, key, value):
    height, part = wide_got.shape[3], wide_got.shape[4] // 2
    for col in range(cols):
        for piece in range(2):
            for side in range(2):
                begin = (2 * piece + side) * height
                lines = slice(begin, begin + height)
                lanes = slice(col * part, (col + 1) * part)
                gate[lines, lanes] = wide_got[side, col, piece, :, :part].astype(jnp.float32)
                up[lines, lanes] = wide_got[side, col, piece, :, part:].astype(jnp.float32)
    turned = []
    for col in range(cols):
        stacked = head_got[col].reshape(3 * head_dim, head_got.shape[3]).astype(jnp.float32)
        turned.append(
            [stacked[kind * head_dim : (kind + 1) * head_dim].T for kind in range(3)]
        )
        query[:, col * head_dim : (col + 1) * head_dim] = turned[col][0]
    for pair in range(cols // 2):
        for place, target in ((1, key), (2, value)):
            target[:, pair * head_dim : (pair + 1) * head_dim] = (
                turned[2 * pair][place] + turned[2 * pair + 1][place]
            )


def call_kernel(body, args, outs, scratch, number):
    vmem = pl.BlockSpec(memory_space=pltpu.VMEM)
    return pl.pallas_call(
        body,
        out_shape=outs,
        in_specs=[vmem] * len(args),
        out_specs=[vmem] * len(outs),
        scratch_shapes=scratch,
        compiler_params=pltpu.CompilerParams(
            collective_id=number, has_side_effects=True, vmem_limit_bytes=VMEM_LIMIT
        ),
    )(*args)


def dma(*shape):
    return [pltpu.SemaphoreType.DMA(shape), pltpu.SemaphoreType.DMA(shape)]


def dot(left, right, left_dim=1, right_dim=0):
    return lax.dot_general(
        left,
        right,
        (((left_dim,), (right_dim,)), ((), ())),
        preferred_element_type=jnp.float32,
    )


def shards(
    block_input,
    seq_lengths,
    out_grad,
    attn_norm,
    query_weight,
    key_weight,
    value_weight,
    query_norm,
    key_norm,
    out_weight,
    ffn_norm,
    gate_weight,
    up_weight,
    down_weight,
):
    local_rows, width = block_input.shape
    head_dim = query_norm.shape[0]
    cols = lax.axis_size("col")
    length = local_rows * cols * lax.axis_size("row")
    places = jnp.arange(length, dtype=jnp.int32)
    position = segment_info(seq_lengths[0], length)[1]
    begins = (places - position)[:, None]
    cosine, sine = rope_tables(position, head_dim)
    cosine = jnp.concatenate([cosine, cosine], axis=1)
    sine = jnp.concatenate([-sine, sine], axis=1)
    head_gains = jnp.stack([query_norm, key_norm])
    (
        input_blocks,
        out_blocks,
        out_weight_blocks,
        cat_blocks,
        wide_blocks,
        _,
        first_blocks,
        own_sums,
        query_rot,
        key_rot,
        value_low,
        attn_low,
        log_total,
    ) = front(
        block_input,
        out_grad,
        out_weight,
        query_weight,
        key_weight,
        value_weight,
        gate_weight,
        up_weight,
        attn_norm,
        head_gains,
        (cosine, sine, begins),
        0,
    )
    act_grad2, middle_own, down_part, slot_full, _, hidden, wide_low = hidden_pass(
        [input_blocks, out_blocks, out_weight_blocks, cat_blocks, wide_blocks],
        down_weight,
        ffn_norm,
        query_weight,
        key_weight,
        value_weight,
        1,
    )
    outs = back_pass(
        [block_input, out_grad, act_grad2, middle_own]
        + [attn_norm.reshape(1, width), ffn_norm.reshape(1, width)]
        + [out_weight_blocks, cat_blocks, out_blocks, first_blocks]
        + [hidden, wide_low, down_part, slot_full]
        + [query_rot, key_rot, value_low, attn_low, log_total]
        + [own_sums, head_gains, cosine, sine, begins],
        down_weight.shape[0],
        head_dim,
        2,
    )
    block_output, input_grad, wide_got, head_got, out_sum, grad_down, gain_sums = outs
    wide_shape = jax.ShapeDtypeStruct(gate_weight.shape, jnp.float32)
    grads = local_kernel(
        functools.partial(open_kernel, cols, head_dim),
        [wide_got, head_got],
        [wide_shape, wide_shape]
        + [
            jax.ShapeDtypeStruct(weight.shape, jnp.float32)
            for weight in (query_weight, key_weight, value_weight)
        ],
    )
    sums = tuple(grads) + (out_sum.reshape(out_weight.shape), grad_down, gain_sums)
    if lax.axis_size("dp") > 2:
        sums = lax.psum(tuple(0.5 * value for value in sums), "dp")
    grad_gate, grad_up, grad_query, grad_key, grad_value, grad_outweight, grad_down, gain_sums = sums
    return (
        block_output,
        input_grad,
        gain_sums[0],
        grad_query,
        grad_key,
        grad_value,
        gain_sums[2, :head_dim],
        gain_sums[3, :head_dim],
        grad_outweight,
        gain_sums[1],
        grad_gate,
        grad_up,
        grad_down,
    )


def solution(mesh):
    placed = (
        P(("dp", "row", "col"), None),
        P("dp", None),
        P(("dp", "row", "col"), None),
        P(),
        P("col", "row"),
        P("col", "row"),
        P("col", "row"),
        P(),
        P(),
        P(("row", "col"), None),
        P(),
        P("col", "row"),
        P("col", "row"),
        P(("row", "col"), None),
    )
    return jax.shard_map(
        shards,
        mesh=mesh,
        in_specs=placed,
        out_specs=(
            P(("dp", "row", "col"), None),
            P(("dp", "row", "col"), None),
            P(),
            P("col", "row"),
            P("col", "row"),
            P("col", "row"),
            P(),
            P(),
            P(("row", "col"), None),
            P(),
            P("col", "row"),
            P("col", "row"),
            P(("row", "col"), None),
        ),
        check_vma=False,
    )
```

```python
import functools
import math

import jax
import jax.numpy as jnp
from jax import lax
from jax.experimental import pallas as pl
from jax.experimental.pallas import tpu as pltpu
from jax.sharding import PartitionSpec as P

EPSILON = 1e-05
THETA = 1000000.0


def rope_frequency(width):
    half_width = width // 2
    exponent = jnp.arange(half_width, dtype=jnp.float32) * (2.0 / width)
    frequency = jnp.exp(-math.log(THETA) * exponent)
    return jnp.concatenate([frequency, frequency])[None, :]


def head_norm(values, gain_vec):
    inv_rms = lax.rsqrt(jnp.mean(values * values, axis=-1, keepdims=True) + EPSILON)
    return (values * inv_rms * gain_vec, inv_rms)


def head_norm_back(cotangent, values, inv_rms, gain_vec):
    normed = values * inv_rms
    weighted = cotangent * gain_vec
    gain_grad = jnp.sum(cotangent * normed, axis=0)
    inner_mean = jnp.mean(weighted * normed, axis=-1, keepdims=True)
    return (inv_rms * (weighted - normed * inner_mean), gain_grad)


def swap_halves(values):
    half_width = values.shape[-1] // 2
    return jnp.concatenate([values[:, half_width:], values[:, :half_width]], axis=1)


def block_probability(query_block, key_rows, begins, offset, low, shift):
    score_scale = 1.0 / math.sqrt(query_block.shape[1])
    scores = dot(query_block, key_rows, 1, 1) * score_scale
    places = low + lax.broadcasted_iota(jnp.int32, scores.shape, 1)
    row_places = offset + lax.broadcasted_iota(jnp.int32, scores.shape, 0)
    allowed = (places >= begins) & (places <= row_places)
    if shift is None:
        shift = jnp.log(jnp.sum(jnp.where(allowed, jnp.exp(scores), 0.0), axis=1, keepdims=True))
    probability = jnp.where(allowed, jnp.exp(scores - shift), 0.0).astype(jnp.bfloat16)
    return probability, shift


def spans(length, longest, block):
    return [
        (offset, max(0, (offset - longest) // 128 * 128), block)
        for offset in range(0, length, block)
    ]


def local_kernel(body, args, outs, scratch=()):
    vmem = pl.BlockSpec(memory_space=pltpu.VMEM)
    return pl.pallas_call(
        body,
        out_shape=outs,
        in_specs=[vmem] * len(args),
        out_specs=[vmem] * len(outs),
        scratch_shapes=list(scratch),
    )(*args)


MESH = pl.DeviceIdType.MESH
VMEM_LIMIT = 56 * 1024 * 1024


def remote(source, target, sems, place, axis, index):
    return pltpu.make_async_remote_copy(
        src_ref=source,
        dst_ref=target,
        send_sem=sems[0].at[place],
        recv_sem=sems[1].at[place],
        device_id={axis: index},
        device_id_type=MESH,
    )


def send(source, target, sems, place, axis, index):
    copy = remote(source, target, sems, place, axis, index)
    copy.start()
    return copy


def neighbours():
    rows, row = lax.axis_size("row"), lax.axis_index("row")
    near = row + 1 - 2 * lax.rem(row, 2)
    far = lax.rem(row + rows // 2, rows)
    return near, far


def sibling():
    own = lax.axis_index("dp")
    return own + 1 - 2 * lax.rem(own, 2)


def greet(corner=False):
    cols, col = lax.axis_size("col"), lax.axis_index("col")
    near, far = neighbours()
    peers = [("col", lax.rem(col + step, cols)) for step in range(1, cols)]
    peers += [("row", near), ("row", far), ("dp", sibling())]
    if corner:
        peers.append(("row", lax.rem(near + lax.axis_size("row") // 2, lax.axis_size("row"))))
    barrier = pltpu.get_barrier_semaphore()
    for axis, index in peers:
        pl.semaphore_signal(barrier, inc=1, device_id={axis: index}, device_id_type=MESH)
    pl.semaphore_wait(barrier, len(peers))


class Gather:
    def __init__(self, block, part, sems, item):
        self.block, self.part = block, part
        self.sems, self.item = sems, item
        self.cols, self.col = lax.axis_size("col"), lax.axis_index("col")
        self.row = lax.axis_index("row")
        self.near, self.far = neighbours()

    def hop(self, origin, right):
        piece = self.block(self.row, origin)
        place = (self.item, 0 if right else 1, origin)
        return remote(piece, piece, self.sems, place, "col", self.col + (1 if right else -1))

    def cross(self, origin, kind):
        piece = self.block(self.row, origin)
        peer = (self.near, self.far)[kind]
        return remote(piece, piece, self.sems, (self.item, 2 + kind, origin), "row", peer)

    def corner(self, origin, kind):
        source, peer = ((self.near, self.far), (self.far, self.near))[kind]
        piece = self.part(source, origin, kind)
        return remote(piece, piece, self.sems, (self.item, 4 + kind, origin), "row", peer)

    def forward(self, origin, right):
        @pl.when(self.col < self.cols - 1 if right else self.col > 0)
        def _():
            self.hop(origin, right).start()

    def each(self, wave, act):
        if wave == 0:
            act(self.col, None)
            return
        for right in (True, False):
            origin = self.col - wave if right else self.col + wave

            @pl.when(self.col >= wave if right else self.col + wave < self.cols)
            def _():
                act(origin, right)

    def start(self):
        for right in (True, False):
            self.forward(self.col, right)
        for kind in range(2):
            self.cross(self.col, kind).start()

    def wave(self, wave):
        def act(origin, right):
            self.hop(origin, right).wait_recv()
            self.forward(origin, right)
            for kind in range(2):
                self.cross(origin, kind).start()

        self.each(wave, act)

    def relay(self, wave):
        def act(origin, right):
            for kind in range(2):
                self.cross(origin, kind).wait_recv()
                self.corner(origin, kind).start()

        self.each(wave, act)

    def land(self, wave):
        def act(origin, right):
            for kind in range(2):
                self.corner(origin, kind).wait_recv()

        self.each(wave, act)

    def sent(self, waves=True):
        def act(origin, right):
            for side in (True, False) if right is None else (right,):

                @pl.when(self.col < self.cols - 1 if side else self.col > 0)
                def _():
                    if waves:
                        self.hop(origin, side).wait_send()

            for kind in range(2):
                self.cross(origin, kind).wait_send()
                self.corner(origin, kind).wait_send()

        for wave in range(self.cols if waves else 1):
            self.each(wave, act)


class Swap:
    def __init__(self, source, target, sems, item, whole=False):
        self.source, self.target, self.sems, self.item = source, target, sems, item
        self.cols, self.col = lax.axis_size("col"), lax.axis_index("col")
        self.half = lax.rem(lax.axis_index("dp"), 2)
        self.lines, self.pairs, self.first = {}, {}, 0 if whole else 1

    def line(self):
        for step in range(1, self.cols):
            peer = lax.rem(self.col + step, self.cols)
            self.lines[step] = send(
                self.source(peer, self.half),
                self.target.at[self.col, self.half],
                self.sems,
                (self.item, 0, step),
                "col",
                peer,
            )

    def relay(self):
        for step in range(self.first, self.cols):
            if step:
                self.lines[step].wait_recv()
            piece = self.target.at[lax.rem(self.col + self.cols - step, self.cols), self.half]
            self.pairs[step] = send(
                piece, piece, self.sems, (self.item, 1, step), "dp", sibling()
            )

    def land(self):
        for copy in self.pairs.values():
            copy.wait_recv()

    def sent(self):
        for copies in (self.lines, self.pairs):
            for copy in copies.values():
                copy.wait_send()


def front_kernel(*refs):
    (own_in, own_grad, own_out, query, key, value, gate, up) = refs[:8]
    (attn_norm, query_norm, key_norm, seq_lengths, frequency) = refs[8:13]
    (in_all, grad_all, out_all, cat_all, wide_all, slot_all) = refs[13:19]
    (first, sums, query_rot, key_rot, value_low, low_rows, totals) = refs[19:26]
    (cosine, sine, begins) = refs[26:29]
    (slot_part, wide_part) = refs[29:31]
    gather_sems, swap_sems, pair_sems = refs[31:33], refs[33:35], refs[35:37]
    rows, cols = lax.axis_size("row"), lax.axis_size("col")
    row, col = lax.axis_index("row"), lax.axis_index("col")
    half = lax.rem(lax.axis_index("dp"), 2)
    near, far = neighbours()
    corner = lax.rem(near + rows // 2, rows)
    length, head_dim = query_rot.shape
    width = own_in.shape[1]
    local = own_in.shape[0]
    block = length // rows

    def split(ref):
        count = ref.shape[2] // 2
        return (
            lambda r, c: ref.at[r, c],
            lambda r, c, k: ref.at[r, c, pl.ds(k * count, count)],
        )

    in_all[row, col] = own_in[...]
    greet()
    inputs = Gather(*split(in_all), gather_sems, 0)
    inputs.start()
    height = query.shape[0] // 2
    for place in range(cols):
        for piece in range(2):
            lines = slice(piece * height, (piece + 1) * height)
            lanes = slice(place // 2 * head_dim, (place // 2 + 1) * head_dim)
            slot_part[place, piece, :, :head_dim] = query[
                lines, place * head_dim : (place + 1) * head_dim
            ]
            slot_part[place, piece, :, head_dim : 2 * head_dim] = key[lines, lanes]
            slot_part[place, piece, :, 2 * head_dim :] = value[lines, lanes]
    slots = Swap(lambda c, h: slot_part.at[c, h], slot_all, swap_sems, 0)
    slots.line()
    slot_all[col] = slot_part[col]
    grad_all[row, col] = own_grad[...]
    out_all[row, col] = own_out[...]
    inputs.wave(1)
    inputs.relay(0)
    inputs.wave(2)
    inputs.relay(1)
    for step in range(3, cols):
        inputs.wave(step)
    count = own_out.shape[1] // 2
    outs = Gather(
        lambda r, c: out_all.at[r, c, half],
        lambda r, c, k: out_all.at[r, c, half, pl.ds(k * count, count)],
        gather_sems,
        2,
    )
    outs.start()
    grads = Gather(*split(grad_all), gather_sems, 1)
    inputs.relay(2)
    places = lax.broadcasted_iota(jnp.int32, (length, 1), 0)
    end, begin = jnp.zeros((1, 1), jnp.int32), jnp.zeros((length, 1), jnp.int32)
    for number in range(seq_lengths.shape[1]):
        size = seq_lengths[:, number : number + 1]
        end = end + size
        begin = begin + jnp.where(places >= end, size, 0)
    begins[...] = begin
    for step in range(3, cols):
        inputs.relay(step)
    angles = (places - begin).astype(jnp.float32) * frequency[...]
    cosine[...] = jnp.cos(angles)
    grads.start()
    side = lax.broadcasted_iota(jnp.int32, angles.shape, 1)
    turned = jnp.sin(angles)
    sine[...] = jnp.where(side < head_dim // 2, -turned, turned)
    slots.relay()
    for step in range(1, cols):
        outs.wave(step)
    slots.land()

    def project(place):
        for c in range(cols):
            values = in_all[place, c].astype(jnp.float32)
            normed = head_norm(values, attn_norm[...])[0]
            first[place, c] = normed.astype(jnp.bfloat16)
        lines = pl.ds(pl.multiple_of(place * block, block), block)
        sums[lines, :] = dot(
            first[place].reshape(block, width), slot_all[...].reshape(width, 3 * head_dim)
        )

    project(row)
    project(near)
    project(far)
    for step in range(cols):
        inputs.land(step)
    project(corner)
    for place, target, gain in ((0, query_rot, query_norm), (1, key_rot, key_norm)):
        normed = head_norm(sums[:, place * head_dim : (place + 1) * head_dim], gain[...])[0]
        target[...] = (normed * cosine[...] + swap_halves(normed) * sine[...]).astype(jnp.bfloat16)
    value_low[...] = sums[:, 2 * head_dim : 3 * head_dim].astype(jnp.bfloat16)
    hidden = gate.shape[1] // cols

    def pack(place):
        for kind, source in ((0, gate), (1, up)):
            for piece in range(2):
                wide_part[place, piece, :, kind * hidden : (kind + 1) * hidden] = source[
                    piece * height : (piece + 1) * height, place * hidden : (place + 1) * hidden
                ]

    def cat(part):
        places = pl.ds(part * (rows // 2), rows // 2)
        return Gather(
            lambda r, c: cat_all.at[places, r, c],
            lambda r, c, k: cat_all.at[places, r, c, pl.ds(k * head_dim // 2, head_dim // 2)],
            gather_sems,
            3 + part,
        )

    cats = [cat(part) for part in range(2)]
    wide = Swap(lambda c, h: wide_part.at[c, h], wide_all, swap_sems, 1)
    for offset, low, _ in spans(length, length // 2, block):
        number = offset // block
        lines, keys = slice(offset, offset + block), slice(low, offset + block)
        probability, total = block_probability(
            query_rot[lines, :], key_rot[keys, :], begins[lines, :], offset, low, None
        )
        totals[lines, :] = total
        low_rows[lines, :] = dot(probability, value_low[keys, :]).astype(jnp.bfloat16)
        cat_all[number, row, col] = dot(value_low[keys, :], probability, 0, 1).astype(jnp.bfloat16)
        if number == 0:
            grads.wave(1)
            outs.relay(0)
        if number == rows // 2 - 1:
            cats[0].start()
            for step in range(1, cols):
                outs.relay(step)
            for step in range(2, cols):
                grads.wave(step)
        if number == rows // 2:
            grads.relay(0)
    cats[1].start()
    for place in range(cols):
        pack(place)
    wide.line()
    wide_all[col] = wide_part[col]
    cats[0].wave(1)
    grads.relay(1)
    for step in range(2, cols):
        cats[0].wave(step)
    for step in range(1, cols):
        cats[1].wave(step)
    for step in range(2, cols):
        grads.relay(step)
    for step in range(cols):
        cats[0].relay(step)
    pairs = []
    for step in range(cols):
        outs.land(step)
    for number, place in enumerate((near, far, corner)):
        piece = out_all.at[place, :, half]
        pairs.append(send(piece, piece, pair_sems, (number,), "dp", sibling()))
    for step in range(1, cols):
        piece = out_all.at[row, lax.rem(col + cols - step, cols), half]
        pairs.append(send(piece, piece, pair_sems, (2 + step,), "dp", sibling()))
    for step in range(cols):
        cats[1].relay(step)
    wide.relay()
    wide.land()
    for gather in [grads] + cats:
        for step in range(cols):
            gather.land(step)
    for copy in pairs:
        copy.wait()
    for item in [inputs, grads, outs, slots, wide] + cats:
        item.sent()


def front(own_in, own_grad, own_out, query, key, value, gate, up, norms, seq_lengths, number):
    rows, cols = lax.axis_size("row"), lax.axis_size("col")
    local, width = own_in.shape
    attn_norm, query_norm, key_norm = norms
    length, head_dim = local * rows * cols, query_norm.shape[0]
    hidden, height = gate.shape[1] // cols, gate.shape[0] // 2
    low = jnp.bfloat16
    blocks = jax.ShapeDtypeStruct((rows, cols, local, width), low)
    halves = own_out.shape[0] // 2
    wide = (cols, 2, height, 2 * hidden)
    slot = (cols, 2, height, 3 * head_dim)
    shape = jax.ShapeDtypeStruct
    head_rows = shape((length, head_dim), low)
    table = shape((length, head_dim), jnp.float32)
    outs = [
        blocks,
        blocks,
        shape((rows, cols, 2, halves, width), low),
        shape((rows, rows, cols, head_dim, length // rows), low),
        shape(wide, low),
        shape(slot, low),
        blocks,
        shape((length, 3 * head_dim), jnp.float32),
        head_rows,
        head_rows,
        head_rows,
        head_rows,
        shape((length, 1), jnp.float32),
        table,
        table,
        shape((length, 1), jnp.int32),
    ]
    scratch = [pltpu.VMEM(slot, low), pltpu.VMEM(wide, low)]
    scratch += dma(5, 6, cols) + dma(2, 2, cols) + dma(2 + cols)
    args = [own_in, own_grad, own_out.reshape(2, halves, width), query, key, value, gate, up]
    args += [attn_norm.reshape(1, width), query_norm.reshape(1, head_dim)]
    args += [key_norm.reshape(1, head_dim), seq_lengths, rope_frequency(head_dim)]
    return call_kernel(front_kernel, args, outs, scratch, number)


class Reduce:
    def __init__(self, part, relayed, planed, staged, lined, result, sems, item):
        self.part, self.relayed, self.planed = part, relayed, planed
        self.staged, self.lined, self.result = staged, lined, result
        self.sems, self.item = sems, item
        self.cols = part.shape[1]
        self.col = lax.axis_index("col") if self.cols > 1 else 0
        self.row = lax.axis_index("row")
        self.near, self.far = neighbours()
        self.cross = lax.rem(self.near + lax.axis_size("row") // 2, lax.axis_size("row"))
        self.count = part.shape[2] // 2
        self.relays, self.planes, self.lines = [], [], []

    def first(self):
        for kind, peer in ((0, self.near), (1, self.far)):
            self.relays.append(
                send(
                    self.part.at[self.cross, :, pl.ds(kind * self.count, self.count)],
                    self.relayed.at[kind],
                    self.sems,
                    (self.item, 1 + kind, 0),
                    "row",
                    peer,
                )
            )

    def toward(self, kind):
        peer, came = (self.near, self.far)[kind], 1 - kind
        self.relays[came].wait_recv()
        lines = slice(came * self.count, (came + 1) * self.count)
        self.part[peer, :, lines] = (
            self.part[peer, :, lines].astype(jnp.float32)
            + self.relayed[came].astype(jnp.float32)
        ).astype(jnp.bfloat16)
        self.planes.append(
            send(
                self.part.at[peer],
                self.planed.at[kind],
                self.sems,
                (self.item, 3 + kind, 0),
                "row",
                peer,
            )
        )

    def total(self, place):
        summed = self.part[self.row, place].astype(jnp.float32)
        for kind in range(2):
            summed = summed + self.planed[kind, place].astype(jnp.float32)
        return summed

    def own(self):
        for copy in self.planes:
            copy.wait_recv()
        for step in range(1, self.cols):
            place = lax.rem(self.col + step, self.cols)
            self.staged[step] = self.total(place).astype(jnp.bfloat16)
            self.lines.append(
                send(
                    self.staged.at[step],
                    self.lined.at[step],
                    self.sems,
                    (self.item, 0, step),
                    "col",
                    place,
                )
            )
        self.result[...] = self.total(self.col)

    def last(self):
        for step in range(1, self.cols):
            self.lines[step - 1].wait_recv()
            self.result[...] += self.lined[step].astype(jnp.float32)

    def sent(self):
        for copy in self.relays + self.planes + self.lines:
            copy.wait_send()


def reduce_scratch(rows, cols, local, width):
    low = jnp.bfloat16
    return [
        pltpu.VMEM((2, cols, local // 2, width), low),
        pltpu.VMEM((2, cols, local, width), low),
        pltpu.VMEM((cols, local, width), low),
        pltpu.VMEM((cols, local, width), low),
    ]


def hidden_kernel(*refs):
    in_all, grad_all, out_all, cat_all, wide_all, down, ffn_norm = refs[:7]
    query, key, value = refs[7:10]
    act_own, middle_own, down_part, slot_all = refs[10:14]
    second_all, hidden_all, wide_low = refs[14:17]
    act_parts, act_halves, middle_block, slot_part = refs[17:21]
    low_all, wide_sum, wide_came = refs[21:24]
    act_scratch, rest = (refs[24:28], refs[28:32]), refs[32:]
    sems, swap_sems, pair_sems = rest[:2], rest[2:4], rest[4:6]
    rows, cols = lax.axis_size("row"), lax.axis_size("col")
    row, col = lax.axis_index("row"), lax.axis_index("col")
    near, far = neighbours()
    cross = lax.rem(near + rows // 2, rows)
    local, width = in_all.shape[2:]
    block, hidden = cols * local, down.shape[0]
    greet()
    height, begin = query.shape[0] // 2, 0
    for source in (query, key, value):
        lanes = slice(begin, begin + source.shape[1])
        for piece in range(2):
            slot_part[piece, :, lanes] = source[piece * height : (piece + 1) * height, :]
        begin += source.shape[1]
    slots = Swap(lambda c, h: slot_part.at[h], slot_all, swap_sems, 0)
    slots.line()
    slot_all[col] = slot_part[...]
    acts = [
        Reduce(act_parts.at[side], *act_scratch[side], act_halves.at[side], sems, side)
        for side in range(2)
    ]

    def work(place):
        mixed = dot(cat_all[place].reshape(width, block), out_all[...].reshape(width, width), 0, 0)
        middle = in_all[place].reshape(block, width).astype(jnp.float32) + mixed
        middle_block[...] = middle
        second = head_norm(middle, ffn_norm[...])[0].astype(jnp.bfloat16)
        second_all[place] = second
        wide_weight = wide_all[...].reshape(width, 2 * hidden)
        wide_sums = dot(second, wide_weight)
        gating, upward = wide_sums[:, :hidden], wide_sums[:, hidden:]
        hidden_grad = dot(grad_all[place].reshape(block, width), down[...], 1, 1)
        sigmoid_gate = jax.nn.sigmoid(gating)
        activated = gating * sigmoid_gate
        hidden_low = (activated * upward).astype(jnp.bfloat16)
        gate_low = (
            hidden_grad * upward * sigmoid_gate * (1.0 + gating * (1.0 - sigmoid_gate))
        ).astype(jnp.bfloat16)
        up_low = (hidden_grad * activated).astype(jnp.bfloat16)
        hidden_all[place] = hidden_low
        low_all[place, :, :hidden] = gate_low
        low_all[place, :, hidden:] = up_low
        act = dot(low_all[place], wide_weight, 1, 1).astype(jnp.bfloat16)
        for side in range(2):
            act_parts[side, place] = act[
                :, side * (width // 2) : (side + 1) * (width // 2)
            ].reshape(cols, local, width // 2)

    def work_down(place):
        down_part[place] = (
            dot(hidden_all[place], down[...]).astype(jnp.bfloat16).reshape(cols, local, width)
        )

    work(cross)
    for item in acts:
        item.first()
    work_down(cross)
    work(near)
    for item in acts:
        item.toward(0)
    slots.relay()
    work(far)
    for item in acts:
        item.toward(1)
    work(row)
    lines = pl.ds(pl.multiple_of(col * local, local), local)
    middle_own[...] = middle_block[lines, :]
    acts[0].own()
    for place in (near, far, row):
        work_down(place)
    acts[1].own()
    wide = Paired(wide_sum, wide_came, pair_sems, 0)
    wide_sum[...] = dot(
        second_all[...].reshape(rows * block, width),
        low_all[...].reshape(rows * block, 2 * hidden),
        0,
        0,
    ).reshape(wide_sum.shape)
    wide.pair()
    acts[0].last()
    slots.land()
    wide.copy.wait_recv()
    for place in range(cols):
        total = wide.total(place).astype(jnp.bfloat16)
        for side in range(2):
            wide_low[side, place] = total[side * (height // 2) : (side + 1) * (height // 2), :]
    acts[1].last()
    for side in range(2):
        act_own[:, side * (width // 2) : (side + 1) * (width // 2)] = act_halves[side]
    for item in acts:
        item.sent()
    slots.sent()
    wide.copy.wait_send()


def hidden_pass(blocks, down, ffn_norm, query, key, value, number):
    rows, cols, local, width = blocks[0].shape
    block, hidden, height = cols * local, down.shape[0], query.shape[0] // 2
    shape = jax.ShapeDtypeStruct
    own, low, full = shape((local, width), jnp.float32), jnp.bfloat16, jnp.float32
    slot = (2, height, query.shape[1] + key.shape[1] + value.shape[1])
    outs = [own, own, shape((rows, cols, local, width), low), shape((cols,) + slot, low)]
    outs += [shape((rows, block, width), low), shape((rows, block, hidden), low)]
    outs += [shape((2, cols, height // 2, 2 * hidden), low)]
    scratch = [
        pltpu.VMEM((2, rows, cols, local, width // 2), low),
        pltpu.VMEM((2, local, width // 2), full),
        pltpu.VMEM((block, width), full),
        pltpu.VMEM(slot, low),
        pltpu.VMEM((rows, block, 2 * hidden), low),
        pltpu.VMEM((cols, 2, height, 2 * hidden), full),
        pltpu.VMEM((cols, height, 2 * hidden), full),
    ]
    scratch += reduce_scratch(rows, cols, local, width // 2) * 2
    scratch += dma(2, 5, cols) + dma(1, 2, cols) + dma(1)
    args = list(blocks) + [down, ffn_norm.reshape(1, width), query, key, value]
    return call_kernel(hidden_kernel, args, outs, scratch, number)


class Paired:
    def __init__(self, part, came, sems, item):
        self.part, self.came, self.sems, self.item = part, came, sems, item
        self.half = lax.rem(lax.axis_index("dp"), 2)

    def pair(self):
        self.copy = send(
            self.part.at[:, 1 - self.half], self.came, self.sems, (self.item,), "dp", sibling()
        )

    def total(self, place):
        return self.part[place, self.half] + self.came[place]


def back_kernel(*refs):
    own_in, own_grad, act_own, middle_own, attn_norm, ffn_norm = refs[:6]
    out_all, cat_all, grad_all, first = refs[6:10]
    hidden_all, wide_low, down_given, slot_all = refs[10:14]
    query_rot, key_rot, value_low, low_rows, totals = refs[14:19]
    sums, query_norm, key_norm, cosine, sine, begins = refs[19:25]
    outs, scratch = refs[25:32], refs[32:]
    block_out, in_grad, wide_got, head_got, out_sum, down_sum, gain_sum = outs
    mid_all, cat_part, grads_in, own_slot, slot_mine, slots_in = scratch[:6]
    head_sum, head_came, head_low = scratch[6:9]
    out_part, out_came, out_low, out_lined = scratch[9:13]
    down_grad, down_came, act_part = scratch[13:16]
    low_even, low_odd, query_acc, key_acc, value_acc = scratch[16:21]
    act_result, down_result, held, landed, down_part = scratch[21:26]
    act_scratch, down_scratch = scratch[26:30], scratch[30:34]
    sems = scratch[34:]
    mid_sems, sum_sems, swap_sems, pair_sems = sems[:2], sems[2:4], sems[4:6], sems[6:8]
    cat_sems, low_sems, out_sems, gain_sems = sems[8:10], sems[10:12], sems[12:14], sems[14:16]
    rows, cols = lax.axis_size("row"), lax.axis_size("col")
    row, col = lax.axis_index("row"), lax.axis_index("col")
    half = lax.rem(lax.axis_index("dp"), 2)
    local, width = own_in.shape
    length, head_dim = query_rot.shape
    block = cols * local
    near, far = neighbours()
    greet(corner=True)

    wides = [
        Swap(
            lambda c, h, side=side: wide_low.at[side, c],
            wide_got.at[side],
            swap_sems,
            side,
            whole=True,
        )
        for side in range(2)
    ]
    wides[0].line()
    middle = middle_own[...]
    scale_mid = head_norm(middle, ffn_norm[...])[1]
    middle_back, ffn_gain = head_norm_back(act_own[...], middle, scale_mid, ffn_norm[...])
    middle_grad = own_grad[...].astype(jnp.float32) + middle_back
    in_grad[...] = middle_grad
    mid_all[row, col] = middle_grad.astype(jnp.bfloat16)
    mid = Gather(
        lambda r, c: mid_all.at[r, c],
        lambda r, c, k: mid_all.at[r, c, pl.ds(k * (local // 2), local // 2)],
        mid_sems,
        0,
    )
    for kind in range(2):
        mid.cross(col, kind).start()
    for step in range(1, cols):
        mid_all[:, lax.rem(col + step, cols)] = jnp.zeros((rows, local, width), jnp.bfloat16)
    held[0] = jnp.zeros(held.shape[1:], jnp.float32)
    held[0, 1:2, :] = ffn_gain[None, :]

    for side in range(2):
        wide_got[side, col, half] = wide_low[side, col]
    down_part[...] = down_given[...]
    mid.relay(0)
    down_grad[...] = dot(
        hidden_all[...].reshape(length, hidden_all.shape[-1]),
        grad_all[...].reshape(length, width),
        0,
        0,
    )
    down_copy = send(down_grad, down_came, pair_sems, (3,), "dp", sibling())
    mid.land(0)

    cat_grad = dot(
        mid_all[:, col].reshape(rows * local, width),
        out_all[row].reshape(cols * head_dim, width),
        1,
        1,
    ).astype(jnp.bfloat16)
    for place in range(cols):
        piece = cat_grad[:, place * head_dim : (place + 1) * head_dim]
        cat_part[place, :, :head_dim] = piece[: rows // 2 * local]
        cat_part[place, :, head_dim:] = piece[rows // 2 * local :]

    def turn(source, target, sems):
        return [
            send(
                source(lax.rem(col + step, cols)),
                target,
                sems,
                (step,),
                "col",
                lax.rem(col + step, cols),
            )
            for step in range(1, cols)
        ]

    cats = turn(lambda c: cat_part.at[c], grads_in.at[col], cat_sems)
    grads_in[col] = cat_part[col]
    wides[1].line()
    downs = Reduce(down_part, *down_scratch, down_result, sum_sems, 0)
    downs.first()

    mixed = None
    for place in range(rows):
        term = dot(
            cat_all[place, row].reshape(cols * head_dim, block),
            mid_all[place].reshape(block, width),
        )
        mixed = term if mixed is None else mixed + term
    out = Paired(out_part, out_came, pair_sems, 2)
    out_part[...] = mixed.reshape(cols, 2, head_dim // 2, width)
    out.pair()
    for copy in cats:
        copy.wait_recv()

    score_scale = 1.0 / math.sqrt(head_dim)
    key_acc[...] = jnp.zeros_like(key_acc)
    value_acc[...] = jnp.zeros_like(value_acc)
    for offset, low, _ in spans(length, length // 2, block):
        number = offset // block
        lines, keys = slice(offset, offset + block), slice(low, offset + block)
        probability, _ = block_probability(
            query_rot[lines, :], key_rot[keys, :], begins[lines, :], offset, low, totals[lines, :]
        )
        upper, right = number % (rows // 2) * local, number // (rows // 2) * head_dim
        grad_block = grads_in[:, upper : upper + local, right : right + head_dim].reshape(
            block, head_dim
        )
        value_acc[keys, :] += dot(probability, grad_block, 0, 0)
        row_delta = jnp.sum(
            grad_block.astype(jnp.float32) * low_rows[lines, :].astype(jnp.float32),
            axis=1,
            keepdims=True,
        )
        prob_grad = dot(grad_block, value_low[keys, :], 1, 1)
        score_grad = (
            score_scale * probability.astype(jnp.float32) * (prob_grad - row_delta)
        ).astype(jnp.bfloat16)
        query_acc[lines, :] = dot(score_grad, key_rot[keys, :])
        key_acc[keys, :] += dot(score_grad, query_rot[lines, :], 0, 0)
        if number in (0, 1):
            downs.toward(number)
    slot = 3 * head_dim

    def keep(place, value):
        own_slot[:, place * head_dim : (place + 1) * head_dim] = value
        pieces = value.reshape(rows, cols, local, head_dim)
        for number in range(rows):
            upper = number % (rows // 2) * local
            begin = number // (rows // 2) * slot + place * head_dim
            slot_mine[:, upper : upper + local, begin : begin + head_dim] = pieces[number]

    for place, source, gains in ((0, query_acc, query_norm), (1, key_acc, key_norm)):
        raw = sums[:, place * head_dim : (place + 1) * head_dim]
        gain = gains[...]
        inv_rms = head_norm(raw, gain)[1]
        cotangent = source[...] * cosine[...] - swap_halves(source[...]) * sine[...]
        low_part, gain_grad = head_norm_back(cotangent, raw, inv_rms, gain)
        keep(place, low_part.astype(jnp.bfloat16))
        held[0, 2 + place : 3 + place, :head_dim] = gain_grad[None, :]
    keep(2, value_acc[...].astype(jnp.bfloat16))
    lows = turn(lambda c: slot_mine.at[c], slots_in.at[col], low_sems)
    slots_in[col] = slot_mine[col]

    head = Paired(head_sum, head_came, pair_sems, 4)
    head_grad = dot(own_slot[...], first[...].reshape(length, width), 0, 0)
    for place in range(cols):
        head_sum[place] = head_grad[
            :, place * (width // cols) : (place + 1) * (width // cols)
        ].reshape(head_sum.shape[1:])
    head.pair()
    out.copy.wait_recv()
    for place in range(cols):
        out_low[place] = out.total(place).astype(jnp.bfloat16)
    lined = [
        send(
            out_low.at[lax.rem(col + step, cols)],
            out_lined.at[step],
            out_sems,
            (step,),
            "col",
            lax.rem(col + step, cols),
        )
        for step in range(1, cols)
    ]
    for copy in lows:
        copy.wait_recv()
    for place in range(cols):
        lanes = slice(place * head_dim, (place + 1) * head_dim)
        came = jnp.concatenate([slots_in[place, :, :slot], slots_in[place, :, slot:]], axis=0)
        low_even[:, lanes] = came[:, :head_dim]
        target, offset = (low_odd, 0) if place % 2 else (low_even, cols * head_dim)
        for kind in (0, 1):
            begin = offset + (kind * (cols // 2) + place // 2) * head_dim
            target[:, begin : begin + head_dim] = came[
                :, (1 + kind) * head_dim : (2 + kind) * head_dim
            ]
    slot_weight = slot_all[...].reshape(width, slot_all.shape[-1])
    act = dot(low_even[...], slot_weight, 1, 1) + dot(
        low_odd[...], slot_weight[:, cols * head_dim :], 1, 1
    )
    act_part[...] = act.astype(jnp.bfloat16).reshape(act_part.shape)
    acts = Reduce(act_part, *act_scratch, act_result, sum_sems, 1)
    acts.first()
    head.copy.wait_recv()
    for place in range(cols):
        head_low[place] = head.total(place).astype(jnp.bfloat16)
    heads = Swap(lambda c, h: head_low.at[c], head_got, swap_sems, 2, whole=True)
    heads.line()
    head_got[col, half] = head_low[col]
    downs.own()
    acts.toward(0)
    acts.toward(1)
    wides[0].relay()
    wides[1].relay()
    acts.own()

    residual = own_in[...].astype(jnp.float32)
    scale_in = head_norm(residual, attn_norm[...])[1]
    input_back, attn_gain = head_norm_back(act_result[...], residual, scale_in, attn_norm[...])
    in_grad[...] += input_back
    held[0, 0:1, :] = attn_gain[None, :]

    def share(stage, axis, size, own):
        copies = [
            send(
                held.at[stage],
                landed.at[stage, own],
                gain_sems,
                (stage, step),
                axis,
                lax.rem(own + step, size),
            )
            for step in range(1, size)
        ]
        landed[stage, own] = held[stage]
        return copies

    def gather_up(stage, copies, size):
        for copy in copies:
            copy.wait_recv()
        total = landed[stage, 0]
        for place in range(1, size):
            total = total + landed[stage, place]
        held[stage + 1] = total

    shares = share(0, "row", rows, row)
    downs.last()
    block_out[...] = (middle_own[...] + down_result[...]).astype(jnp.bfloat16)
    gather_up(0, shares, rows)
    more = share(1, "col", cols, col)
    out_sum[half] = out.total(col)
    for step in range(1, cols):
        lined[step - 1].wait_recv()
        out_sum[half] += out_lined[step].astype(jnp.float32)
    out_copy = send(out_sum.at[half], out_sum.at[half], pair_sems, (5,), "dp", sibling())
    heads.relay()
    down_copy.wait_recv()
    down_sum[...] = down_grad[...] + down_came[...]
    gather_up(1, more, cols)
    gain_copy = send(held.at[2], landed.at[2, 0], gain_sems, (2, 0), "dp", sibling())
    for moved in wides + [heads]:
        moved.land()
    gain_copy.wait_recv()
    gain_sum[...] = held[2] + landed[2, 0]
    out_copy.wait_recv()
    for copy in cats + lows + lined + shares + more + [down_copy, out_copy, gain_copy]:
        copy.wait_send()
    for paired in (out, head):
        paired.copy.wait_send()
    mid.sent(waves=False)
    for item in [downs, acts, heads] + wides:
        item.sent()


def back_pass(args, hidden, head_dim, number):
    rows, cols = lax.axis_size("row"), lax.axis_size("col")
    local, width = args[0].shape
    length, height = rows * cols * local, width // cols // 2
    low, full = jnp.bfloat16, jnp.float32
    shape = jax.ShapeDtypeStruct
    slot, some = 3 * head_dim, head_dim // 2
    outs = [
        shape((local, width), low),
        shape((local, width), full),
        shape((2, cols, 2, height // 2, 2 * hidden), low),
        shape((cols, 2, slot // 2, width // cols), low),
        shape((2, some, width), full),
        shape((hidden, width), full),
        shape((8, width), full),
    ]

    def vmem(kind, *dims):
        return pltpu.VMEM(dims, kind)

    scratch = [
        vmem(low, rows, cols, local, width),
        vmem(low, cols, rows // 2 * local, 2 * head_dim),
        vmem(low, cols, rows // 2 * local, 2 * head_dim),
        vmem(low, length, slot),
        vmem(low, cols, rows // 2 * local, 2 * slot),
        vmem(low, cols, rows // 2 * local, 2 * slot),
        vmem(full, cols, 2, slot // 2, width // cols),
        vmem(full, cols, slot // 2, width // cols),
        vmem(low, cols, slot // 2, width // cols),
    ]
    scratch += [
        vmem(full, cols, 2, some, width),
        vmem(full, cols, some, width),
        vmem(low, cols, some, width),
        vmem(low, cols, some, width),
        vmem(full, hidden, width),
        vmem(full, hidden, width),
        vmem(low, rows, 1, local, width),
        vmem(low, rows * local, 2 * cols * head_dim),
        vmem(low, rows * local, cols * head_dim),
        vmem(full, length, head_dim),
        vmem(full, length, head_dim),
        vmem(full, length, head_dim),
        vmem(full, local, width),
        vmem(full, local, width),
        vmem(full, 3, 8, width),
        vmem(full, 3, max(rows, cols), 8, width),
        vmem(low, rows, cols, local, width),
    ]
    scratch += reduce_scratch(rows, 1, local, width) + reduce_scratch(rows, cols, local, width)
    scratch += dma(1, 6, cols) + dma(2, 5, cols) + dma(3, 2, cols) + dma(6)
    scratch += dma(cols) + dma(cols) + dma(cols) + dma(3, max(rows, cols))
    return call_kernel(back_kernel, args, outs, scratch, number)


def open_kernel(cols, head_dim, *refs):
    wide_got, head_got, block_given, in_given, out_given, down_given, gain_given = refs[:7]
    gate, up, query, key, value, block_out, in_grad, out, down = refs[7:16]
    attn_gain, ffn_gain, query_gain, key_gain = refs[16:]
    pairs = ((block_out, block_given), (in_grad, in_given), (out, out_given), (down, down_given))
    for target, source in pairs:
        target[...] = source[...]
    attn_gain[...] = gain_given[0:1, :]
    ffn_gain[...] = gain_given[1:2, :]
    query_gain[...] = gain_given[2:3, :head_dim]
    key_gain[...] = gain_given[3:4, :head_dim]
    height, part = wide_got.shape[3], wide_got.shape[4] // 2
    for col in range(cols):
        for piece in range(2):
            for side in range(2):
                begin = (2 * piece + side) * height
                lines = slice(begin, begin + height)
                lanes = slice(col * part, (col + 1) * part)
                gate[lines, lanes] = wide_got[side, col, piece, :, :part].astype(jnp.float32)
                up[lines, lanes] = wide_got[side, col, piece, :, part:].astype(jnp.float32)
    turned = []
    for col in range(cols):
        stacked = head_got[col].reshape(3 * head_dim, head_got.shape[3]).astype(jnp.float32)
        turned.append(
            [stacked[kind * head_dim : (kind + 1) * head_dim].T for kind in range(3)]
        )
        query[:, col * head_dim : (col + 1) * head_dim] = turned[col][0]
    for pair in range(cols // 2):
        for place, target in ((1, key), (2, value)):
            target[:, pair * head_dim : (pair + 1) * head_dim] = (
                turned[2 * pair][place] + turned[2 * pair + 1][place]
            )


def call_kernel(body, args, outs, scratch, number):
    vmem = pl.BlockSpec(memory_space=pltpu.VMEM)
    return pl.pallas_call(
        body,
        out_shape=outs,
        in_specs=[vmem] * len(args),
        out_specs=[vmem] * len(outs),
        scratch_shapes=scratch,
        compiler_params=pltpu.CompilerParams(
            collective_id=number, has_side_effects=True, vmem_limit_bytes=VMEM_LIMIT
        ),
    )(*args)


def dma(*shape):
    return [pltpu.SemaphoreType.DMA(shape), pltpu.SemaphoreType.DMA(shape)]


def dot(left, right, left_dim=1, right_dim=0):
    return lax.dot_general(
        left,
        right,
        (((left_dim,), (right_dim,)), ((), ())),
        preferred_element_type=jnp.float32,
    )


def shards(
    block_input,
    seq_lengths,
    out_grad,
    attn_norm,
    query_weight,
    key_weight,
    value_weight,
    query_norm,
    key_norm,
    out_weight,
    ffn_norm,
    gate_weight,
    up_weight,
    down_weight,
):
    width = block_input.shape[1]
    head_dim = query_norm.shape[0]
    cols = lax.axis_size("col")
    (
        input_blocks,
        out_blocks,
        out_weight_blocks,
        cat_blocks,
        wide_blocks,
        _,
        first_blocks,
        own_sums,
        query_rot,
        key_rot,
        value_low,
        attn_low,
        log_total,
        cosine,
        sine,
        begins,
    ) = front(
        block_input,
        out_grad,
        out_weight,
        query_weight,
        key_weight,
        value_weight,
        gate_weight,
        up_weight,
        (attn_norm, query_norm, key_norm),
        seq_lengths,
        0,
    )
    act_grad2, middle_own, down_part, slot_full, _, hidden, wide_low = hidden_pass(
        [input_blocks, out_blocks, out_weight_blocks, cat_blocks, wide_blocks],
        down_weight,
        ffn_norm,
        query_weight,
        key_weight,
        value_weight,
        1,
    )
    outs = back_pass(
        [block_input, out_grad, act_grad2, middle_own]
        + [attn_norm.reshape(1, width), ffn_norm.reshape(1, width)]
        + [out_weight_blocks, cat_blocks, out_blocks, first_blocks]
        + [hidden, wide_low, down_part, slot_full]
        + [query_rot, key_rot, value_low, attn_low, log_total]
        + [own_sums, query_norm.reshape(1, head_dim), key_norm.reshape(1, head_dim)]
        + [cosine, sine, begins],
        down_weight.shape[0],
        head_dim,
        2,
    )
    block_output, input_grad, wide_got, head_got, out_sum, grad_down, gain_sums = outs
    shape = jax.ShapeDtypeStruct
    weights = (gate_weight, up_weight, query_weight, key_weight, value_weight)
    given = (block_output, input_grad, out_sum.reshape(out_weight.shape), grad_down)
    gains = (width, width, head_dim, head_dim)
    results = local_kernel(
        functools.partial(open_kernel, cols, head_dim),
        [wide_got, head_got] + list(given) + [gain_sums],
        [shape(weight.shape, jnp.float32) for weight in weights]
        + [shape(value.shape, value.dtype) for value in given]
        + [shape((1, size), jnp.float32) for size in gains],
    )
    block_output, input_grad = results[5:7]
    sums = tuple(results[:5]) + tuple(results[7:])
    if lax.axis_size("dp") > 2:
        sums = lax.psum(tuple(0.5 * value for value in sums), "dp")
    grad_gate, grad_up, grad_query, grad_key, grad_value = sums[:5]
    grad_outweight, grad_down, grad_attnnorm, grad_ffnnorm, grad_qnorm, grad_knorm = sums[5:]
    return (
        block_output,
        input_grad,
        grad_attnnorm[0],
        grad_query,
        grad_key,
        grad_value,
        grad_qnorm[0],
        grad_knorm[0],
        grad_outweight,
        grad_ffnnorm[0],
        grad_gate,
        grad_up,
        grad_down,
    )


def solution(mesh):
    placed = (
        P(("dp", "row", "col"), None),
        P("dp", None),
        P(("dp", "row", "col"), None),
        P(),
        P("col", "row"),
        P("col", "row"),
        P("col", "row"),
        P(),
        P(),
        P(("row", "col"), None),
        P(),
        P("col", "row"),
        P("col", "row"),
        P(("row", "col"), None),
    )
    return jax.shard_map(
        shards,
        mesh=mesh,
        in_specs=placed,
        out_specs=(
            P(("dp", "row", "col"), None),
            P(("dp", "row", "col"), None),
            P(),
            P("col", "row"),
            P("col", "row"),
            P("col", "row"),
            P(),
            P(),
            P(("row", "col"), None),
            P(),
            P("col", "row"),
            P("col", "row"),
            P(("row", "col"), None),
        ),
        check_vma=False,
    )
```

```python
import functools
import math

import jax
import jax.numpy as jnp
from jax import lax
from jax.experimental import pallas as pl
from jax.experimental.pallas import tpu as pltpu
from jax.sharding import PartitionSpec as P

EPSILON = 1e-05
THETA = 1000000.0


def rope_frequency(width):
    half_width = width // 2
    exponent = jnp.arange(half_width, dtype=jnp.float32) * (2.0 / width)
    frequency = jnp.exp(-math.log(THETA) * exponent)
    return jnp.concatenate([frequency, frequency])[None, :]


def head_norm(values, gain_vec):
    inv_rms = lax.rsqrt(jnp.mean(values * values, axis=-1, keepdims=True) + EPSILON)
    return (values * inv_rms * gain_vec, inv_rms)


def head_norm_back(cotangent, values, inv_rms, gain_vec):
    normed = values * inv_rms
    weighted = cotangent * gain_vec
    gain_grad = jnp.sum(cotangent * normed, axis=0)
    inner_mean = jnp.mean(weighted * normed, axis=-1, keepdims=True)
    return (inv_rms * (weighted - normed * inner_mean), gain_grad)


def swap_halves(values):
    half_width = values.shape[-1] // 2
    return jnp.concatenate([values[:, half_width:], values[:, :half_width]], axis=1)


def block_probability(query_block, key_rows, begins, offset, low, shift):
    score_scale = 1.0 / math.sqrt(query_block.shape[1])
    scores = dot(query_block, key_rows, 1, 1) * score_scale
    places = low + lax.broadcasted_iota(jnp.int32, scores.shape, 1)
    row_places = offset + lax.broadcasted_iota(jnp.int32, scores.shape, 0)
    allowed = (places >= begins) & (places <= row_places)
    if shift is None:
        shift = jnp.log(jnp.sum(jnp.where(allowed, jnp.exp(scores), 0.0), axis=1, keepdims=True))
    probability = jnp.where(allowed, jnp.exp(scores - shift), 0.0).astype(jnp.bfloat16)
    return probability, shift


def spans(length, longest, block):
    return [
        (offset, max(0, (offset - longest) // 128 * 128), block)
        for offset in range(0, length, block)
    ]


def local_kernel(body, args, outs, scratch=()):
    vmem = pl.BlockSpec(memory_space=pltpu.VMEM)
    return pl.pallas_call(
        body,
        out_shape=outs,
        in_specs=[vmem] * len(args),
        out_specs=[vmem] * len(outs),
        scratch_shapes=list(scratch),
    )(*args)


MESH = pl.DeviceIdType.MESH
VMEM_LIMIT = 56 * 1024 * 1024


def remote(source, target, sems, place, axis, index):
    return pltpu.make_async_remote_copy(
        src_ref=source,
        dst_ref=target,
        send_sem=sems[0].at[place],
        recv_sem=sems[1].at[place],
        device_id={axis: index},
        device_id_type=MESH,
    )


def send(source, target, sems, place, axis, index):
    copy = remote(source, target, sems, place, axis, index)
    copy.start()
    return copy


def neighbours():
    rows, row = lax.axis_size("row"), lax.axis_index("row")
    near = row + 1 - 2 * lax.rem(row, 2)
    far = lax.rem(row + rows // 2, rows)
    return near, far


def sibling():
    own = lax.axis_index("dp")
    return own + 1 - 2 * lax.rem(own, 2)


def greet(corner=False):
    cols, col = lax.axis_size("col"), lax.axis_index("col")
    near, far = neighbours()
    peers = [("col", lax.rem(col + step, cols)) for step in range(1, cols)]
    peers += [("row", near), ("row", far), ("dp", sibling())]
    if corner:
        peers.append(("row", lax.rem(near + lax.axis_size("row") // 2, lax.axis_size("row"))))
    barrier = pltpu.get_barrier_semaphore()
    for axis, index in peers:
        pl.semaphore_signal(barrier, inc=1, device_id={axis: index}, device_id_type=MESH)
    pl.semaphore_wait(barrier, len(peers))


class Gather:
    def __init__(self, block, part, sems, item):
        self.block, self.part = block, part
        self.sems, self.item = sems, item
        self.cols, self.col = lax.axis_size("col"), lax.axis_index("col")
        self.row = lax.axis_index("row")
        self.near, self.far = neighbours()

    def hop(self, origin, right):
        piece = self.block(self.row, origin)
        place = (self.item, 0 if right else 1, origin)
        return remote(piece, piece, self.sems, place, "col", self.col + (1 if right else -1))

    def cross(self, origin, kind):
        piece = self.block(self.row, origin)
        peer = (self.near, self.far)[kind]
        return remote(piece, piece, self.sems, (self.item, 2 + kind, origin), "row", peer)

    def corner(self, origin, kind):
        source, peer = ((self.near, self.far), (self.far, self.near))[kind]
        piece = self.part(source, origin, kind)
        return remote(piece, piece, self.sems, (self.item, 4 + kind, origin), "row", peer)

    def forward(self, origin, right):
        @pl.when(self.col < self.cols - 1 if right else self.col > 0)
        def _():
            self.hop(origin, right).start()

    def each(self, wave, act):
        if wave == 0:
            act(self.col, None)
            return
        for right in (True, False):
            origin = self.col - wave if right else self.col + wave

            @pl.when(self.col >= wave if right else self.col + wave < self.cols)
            def _():
                act(origin, right)

    def start(self):
        for right in (True, False):
            self.forward(self.col, right)
        for kind in range(2):
            self.cross(self.col, kind).start()

    def wave(self, wave):
        def act(origin, right):
            self.hop(origin, right).wait_recv()
            self.forward(origin, right)
            for kind in range(2):
                self.cross(origin, kind).start()

        self.each(wave, act)

    def relay(self, wave):
        def act(origin, right):
            for kind in range(2):
                self.cross(origin, kind).wait_recv()
                self.corner(origin, kind).start()

        self.each(wave, act)

    def land(self, wave):
        def act(origin, right):
            for kind in range(2):
                self.corner(origin, kind).wait_recv()

        self.each(wave, act)

    def sent(self, waves=True):
        def act(origin, right):
            for side in (True, False) if right is None else (right,):

                @pl.when(self.col < self.cols - 1 if side else self.col > 0)
                def _():
                    if waves:
                        self.hop(origin, side).wait_send()

            for kind in range(2):
                self.cross(origin, kind).wait_send()
                self.corner(origin, kind).wait_send()

        for wave in range(self.cols if waves else 1):
            self.each(wave, act)


class Swap:
    def __init__(self, source, target, sems, item, whole=False):
        self.source, self.target, self.sems, self.item = source, target, sems, item
        self.cols, self.col = lax.axis_size("col"), lax.axis_index("col")
        self.half = lax.rem(lax.axis_index("dp"), 2)
        self.lines, self.pairs, self.first = {}, {}, 0 if whole else 1

    def line(self):
        for step in range(1, self.cols):
            peer = lax.rem(self.col + step, self.cols)
            self.lines[step] = send(
                self.source(peer, self.half),
                self.target.at[self.col, self.half],
                self.sems,
                (self.item, 0, step),
                "col",
                peer,
            )

    def relay(self):
        for step in range(self.first, self.cols):
            if step:
                self.lines[step].wait_recv()
            piece = self.target.at[lax.rem(self.col + self.cols - step, self.cols), self.half]
            self.pairs[step] = send(
                piece, piece, self.sems, (self.item, 1, step), "dp", sibling()
            )

    def land(self):
        for copy in self.pairs.values():
            copy.wait_recv()

    def sent(self):
        for copies in (self.lines, self.pairs):
            for copy in copies.values():
                copy.wait_send()


def front_kernel(*refs):
    (own_in, own_grad, own_out, query, key, value, gate, up) = refs[:8]
    (attn_norm, query_norm, key_norm, seq_lengths, frequency) = refs[8:13]
    (in_all, grad_all, out_all, cat_all, wide_all, slot_all) = refs[13:19]
    (first, sums, query_rot, key_rot, value_low, low_rows, totals) = refs[19:26]
    (cosine, sine, begins) = refs[26:29]
    (slot_part, wide_part) = refs[29:31]
    gather_sems, swap_sems, pair_sems = refs[31:33], refs[33:35], refs[35:37]
    rows, cols = lax.axis_size("row"), lax.axis_size("col")
    row, col = lax.axis_index("row"), lax.axis_index("col")
    half = lax.rem(lax.axis_index("dp"), 2)
    near, far = neighbours()
    corner = lax.rem(near + rows // 2, rows)
    length, head_dim = query_rot.shape
    width = own_in.shape[1]
    local = own_in.shape[0]
    block = length // rows

    def split(ref):
        count = ref.shape[2] // 2
        return (
            lambda r, c: ref.at[r, c],
            lambda r, c, k: ref.at[r, c, pl.ds(k * count, count)],
        )

    in_all[row, col] = own_in[...]
    greet()
    inputs = Gather(*split(in_all), gather_sems, 0)
    inputs.start()
    height = query.shape[0] // 2
    for place in range(cols):
        for piece in range(2):
            lines = slice(piece * height, (piece + 1) * height)
            lanes = slice(place // 2 * head_dim, (place // 2 + 1) * head_dim)
            slot_part[place, piece, :, :head_dim] = query[
                lines, place * head_dim : (place + 1) * head_dim
            ]
            slot_part[place, piece, :, head_dim : 2 * head_dim] = key[lines, lanes]
            slot_part[place, piece, :, 2 * head_dim :] = value[lines, lanes]
    slots = Swap(lambda c, h: slot_part.at[c, h], slot_all, swap_sems, 0)
    slots.line()
    slot_all[col] = slot_part[col]
    grad_all[row, col] = own_grad[...]
    out_all[row, col] = own_out[...]
    inputs.wave(1)
    inputs.relay(0)
    inputs.wave(2)
    inputs.relay(1)
    for step in range(3, cols):
        inputs.wave(step)
    count = own_out.shape[1] // 2
    outs = Gather(
        lambda r, c: out_all.at[r, c, half],
        lambda r, c, k: out_all.at[r, c, half, pl.ds(k * count, count)],
        gather_sems,
        2,
    )
    outs.start()
    grads = Gather(*split(grad_all), gather_sems, 1)
    inputs.relay(2)
    places = lax.broadcasted_iota(jnp.int32, (length, 1), 0)
    end, begin = jnp.zeros((1, 1), jnp.int32), jnp.zeros((length, 1), jnp.int32)
    for number in range(seq_lengths.shape[1]):
        size = seq_lengths[:, number : number + 1]
        end = end + size
        begin = begin + jnp.where(places >= end, size, 0)
    begins[...] = begin
    for step in range(3, cols):
        inputs.relay(step)
    angles = (places - begin).astype(jnp.float32) * frequency[...]
    cosine[...] = jnp.cos(angles)
    grads.start()
    side = lax.broadcasted_iota(jnp.int32, angles.shape, 1)
    turned = jnp.sin(angles)
    sine[...] = jnp.where(side < head_dim // 2, -turned, turned)
    slots.relay()
    for step in range(1, cols):
        outs.wave(step)
    slots.land()

    def project(place):
        for c in range(cols):
            values = in_all[place, c].astype(jnp.float32)
            normed = head_norm(values, attn_norm[...])[0]
            first[place, c] = normed.astype(jnp.bfloat16)
        lines = pl.ds(pl.multiple_of(place * block, block), block)
        sums[lines, :] = dot(
            first[place].reshape(block, width), slot_all[...].reshape(width, 3 * head_dim)
        )

    project(row)
    project(near)
    project(far)
    for step in range(cols):
        inputs.land(step)
    project(corner)
    for place, target, gain in ((0, query_rot, query_norm), (1, key_rot, key_norm)):
        normed = head_norm(sums[:, place * head_dim : (place + 1) * head_dim], gain[...])[0]
        target[...] = (normed * cosine[...] + swap_halves(normed) * sine[...]).astype(jnp.bfloat16)
    value_low[...] = sums[:, 2 * head_dim : 3 * head_dim].astype(jnp.bfloat16)
    hidden = gate.shape[1] // cols

    def pack(place):
        for kind, source in ((0, gate), (1, up)):
            for piece in range(2):
                wide_part[place, piece, :, kind * hidden : (kind + 1) * hidden] = source[
                    piece * height : (piece + 1) * height, place * hidden : (place + 1) * hidden
                ]

    def cat(part):
        places = pl.ds(part * (rows // 2), rows // 2)
        return Gather(
            lambda r, c: cat_all.at[places, r, c],
            lambda r, c, k: cat_all.at[places, r, c, pl.ds(k * head_dim // 2, head_dim // 2)],
            gather_sems,
            3 + part,
        )

    cats = [cat(part) for part in range(2)]
    wide = Swap(lambda c, h: wide_part.at[c, h], wide_all, swap_sems, 1)
    for offset, low, _ in spans(length, length // 2, block):
        number = offset // block
        lines, keys = slice(offset, offset + block), slice(low, offset + block)
        probability, total = block_probability(
            query_rot[lines, :], key_rot[keys, :], begins[lines, :], offset, low, None
        )
        totals[lines, :] = total
        low_rows[lines, :] = dot(probability, value_low[keys, :]).astype(jnp.bfloat16)
        cat_all[number, row, col] = dot(value_low[keys, :], probability, 0, 1).astype(jnp.bfloat16)
        if number == 0:
            grads.wave(1)
            outs.relay(0)
        if number == rows // 2 - 1:
            cats[0].start()
            for step in range(1, cols):
                outs.relay(step)
            for step in range(2, cols):
                grads.wave(step)
        if number == rows // 2:
            grads.relay(0)
    cats[1].start()
    for place in range(cols):
        pack(place)
    wide.line()
    wide_all[col] = wide_part[col]
    cats[0].wave(1)
    grads.relay(1)
    for step in range(2, cols):
        cats[0].wave(step)
    for step in range(1, cols):
        cats[1].wave(step)
    for step in range(2, cols):
        grads.relay(step)
    for step in range(cols):
        cats[0].relay(step)
    pairs = []
    for step in range(cols):
        outs.land(step)
    for number, place in enumerate((near, far, corner)):
        piece = out_all.at[place, :, half]
        pairs.append(send(piece, piece, pair_sems, (number,), "dp", sibling()))
    for step in range(1, cols):
        piece = out_all.at[row, lax.rem(col + cols - step, cols), half]
        pairs.append(send(piece, piece, pair_sems, (2 + step,), "dp", sibling()))
    for step in range(cols):
        cats[1].relay(step)
    wide.relay()
    wide.land()
    for gather in [grads] + cats:
        for step in range(cols):
            gather.land(step)
    for copy in pairs:
        copy.wait()
    for item in [inputs, grads, outs, slots, wide] + cats:
        item.sent()


def front(own_in, own_grad, own_out, query, key, value, gate, up, norms, seq_lengths, number):
    rows, cols = lax.axis_size("row"), lax.axis_size("col")
    local, width = own_in.shape
    attn_norm, query_norm, key_norm = norms
    length, head_dim = local * rows * cols, query_norm.shape[0]
    hidden, height = gate.shape[1] // cols, gate.shape[0] // 2
    low = jnp.bfloat16
    blocks = jax.ShapeDtypeStruct((rows, cols, local, width), low)
    halves = own_out.shape[0] // 2
    wide = (cols, 2, height, 2 * hidden)
    slot = (cols, 2, height, 3 * head_dim)
    shape = jax.ShapeDtypeStruct
    head_rows = shape((length, head_dim), low)
    table = shape((length, head_dim), jnp.float32)
    outs = [
        blocks,
        blocks,
        shape((rows, cols, 2, halves, width), low),
        shape((rows, rows, cols, head_dim, length // rows), low),
        shape(wide, low),
        shape(slot, low),
        blocks,
        shape((length, 3 * head_dim), jnp.float32),
        head_rows,
        head_rows,
        head_rows,
        head_rows,
        shape((length, 1), jnp.float32),
        table,
        table,
        shape((length, 1), jnp.int32),
    ]
    scratch = [pltpu.VMEM(slot, low), pltpu.VMEM(wide, low)]
    scratch += dma(5, 6, cols) + dma(2, 2, cols) + dma(2 + cols)
    args = [own_in, own_grad, own_out.reshape(2, halves, width), query, key, value, gate, up]
    args += [attn_norm.reshape(1, width), query_norm.reshape(1, head_dim)]
    args += [key_norm.reshape(1, head_dim), seq_lengths, rope_frequency(head_dim)]
    return call_kernel(front_kernel, args, outs, scratch, number)


class Reduce:
    def __init__(self, part, relayed, planed, staged, lined, result, sems, item):
        self.part, self.relayed, self.planed = part, relayed, planed
        self.staged, self.lined, self.result = staged, lined, result
        self.sems, self.item = sems, item
        self.cols = part.shape[1]
        self.col = lax.axis_index("col") if self.cols > 1 else 0
        self.row = lax.axis_index("row")
        self.near, self.far = neighbours()
        self.cross = lax.rem(self.near + lax.axis_size("row") // 2, lax.axis_size("row"))
        self.count = part.shape[2] // 2
        self.relays, self.planes, self.lines = [], [], []

    def first(self):
        for kind, peer in ((0, self.near), (1, self.far)):
            self.relays.append(
                send(
                    self.part.at[self.cross, :, pl.ds(kind * self.count, self.count)],
                    self.relayed.at[kind],
                    self.sems,
                    (self.item, 1 + kind, 0),
                    "row",
                    peer,
                )
            )

    def merge(self, kind):
        peer, came = (self.near, self.far)[kind], 1 - kind
        self.relays[came].wait_recv()
        lines = slice(came * self.count, (came + 1) * self.count)
        self.part[peer, :, lines] = (
            self.part[peer, :, lines].astype(jnp.float32)
            + self.relayed[came].astype(jnp.float32)
        ).astype(jnp.bfloat16)

    def ship(self, kind):
        peer = (self.near, self.far)[kind]
        self.planes.append(
            send(
                self.part.at[peer],
                self.planed.at[kind],
                self.sems,
                (self.item, 3 + kind, 0),
                "row",
                peer,
            )
        )

    def toward(self, kind):
        self.merge(kind)
        self.ship(kind)

    def total(self, place):
        summed = self.part[self.row, place].astype(jnp.float32)
        for kind in range(2):
            summed = summed + self.planed[kind, place].astype(jnp.float32)
        return summed

    def own(self):
        for copy in self.planes:
            copy.wait_recv()
        for step in range(1, self.cols):
            place = lax.rem(self.col + step, self.cols)
            self.staged[step] = self.total(place).astype(jnp.bfloat16)
            self.lines.append(
                send(
                    self.staged.at[step],
                    self.lined.at[step],
                    self.sems,
                    (self.item, 0, step),
                    "col",
                    place,
                )
            )
        self.result[...] = self.total(self.col)

    def last(self):
        for step in range(1, self.cols):
            self.lines[step - 1].wait_recv()
            self.result[...] += self.lined[step].astype(jnp.float32)

    def sent(self):
        for copy in self.relays + self.planes + self.lines:
            copy.wait_send()


def reduce_scratch(rows, cols, local, width):
    low = jnp.bfloat16
    return [
        pltpu.VMEM((2, cols, local // 2, width), low),
        pltpu.VMEM((2, cols, local, width), low),
        pltpu.VMEM((cols, local, width), low),
        pltpu.VMEM((cols, local, width), low),
    ]


def hidden_kernel(*refs):
    in_all, grad_all, out_all, cat_all, wide_all, down, ffn_norm = refs[:7]
    query, key, value = refs[7:10]
    act_own, middle_own, down_part, slot_all = refs[10:14]
    second_all, hidden_all, wide_low = refs[14:17]
    act_parts, act_halves, middle_block, slot_part = refs[17:21]
    low_all, wide_sum, wide_came, down_relayed = refs[21:25]
    act_scratch, rest = (refs[25:29], refs[29:33]), refs[33:]
    sems, swap_sems, pair_sems = rest[:2], rest[2:4], rest[4:6]
    rows, cols = lax.axis_size("row"), lax.axis_size("col")
    row, col = lax.axis_index("row"), lax.axis_index("col")
    near, far = neighbours()
    cross = lax.rem(near + rows // 2, rows)
    local, width = in_all.shape[2:]
    block, hidden = cols * local, down.shape[0]
    greet()
    height, begin = query.shape[0] // 2, 0
    for source in (query, key, value):
        lanes = slice(begin, begin + source.shape[1])
        for piece in range(2):
            slot_part[piece, :, lanes] = source[piece * height : (piece + 1) * height, :]
        begin += source.shape[1]
    slots = Swap(lambda c, h: slot_part.at[h], slot_all, swap_sems, 0)
    slots.line()
    slot_all[col] = slot_part[...]
    acts = [
        Reduce(act_parts.at[side], *act_scratch[side], act_halves.at[side], sems, side)
        for side in range(2)
    ]

    downs = Reduce(down_part, down_relayed, None, None, None, None, sems, 2)

    def work(place):
        mixed = dot(cat_all[place].reshape(width, block), out_all[...].reshape(width, width), 0, 0)
        middle = in_all[place].reshape(block, width).astype(jnp.float32) + mixed
        middle_block[...] = middle
        second = head_norm(middle, ffn_norm[...])[0].astype(jnp.bfloat16)
        second_all[place] = second
        wide_weight = wide_all[...].reshape(width, 2 * hidden)
        wide_sums = dot(second, wide_weight)
        gating, upward = wide_sums[:, :hidden], wide_sums[:, hidden:]
        hidden_grad = dot(grad_all[place].reshape(block, width), down[...], 1, 1)
        sigmoid_gate = jax.nn.sigmoid(gating)
        activated = gating * sigmoid_gate
        hidden_low = (activated * upward).astype(jnp.bfloat16)
        gate_low = (
            hidden_grad * upward * sigmoid_gate * (1.0 + gating * (1.0 - sigmoid_gate))
        ).astype(jnp.bfloat16)
        up_low = (hidden_grad * activated).astype(jnp.bfloat16)
        hidden_all[place] = hidden_low
        low_all[place, :, :hidden] = gate_low
        low_all[place, :, hidden:] = up_low
        act = dot(low_all[place], wide_weight, 1, 1).astype(jnp.bfloat16)
        for side in range(2):
            act_parts[side, place] = act[
                :, side * (width // 2) : (side + 1) * (width // 2)
            ].reshape(cols, local, width // 2)

    def work_down(place):
        down_part[place] = (
            dot(hidden_all[place], down[...]).astype(jnp.bfloat16).reshape(cols, local, width)
        )

    work(cross)
    for item in acts:
        item.first()
    work_down(cross)
    work(near)
    for item in acts:
        item.toward(0)
    slots.relay()
    work(far)
    for item in acts:
        item.toward(1)
    downs.first()
    work(row)
    lines = pl.ds(pl.multiple_of(col * local, local), local)
    middle_own[...] = middle_block[lines, :]
    acts[0].own()
    for place in (near, far, row):
        work_down(place)
    acts[1].own()
    wide = Paired(wide_sum, wide_came, pair_sems, 0)
    wide_sum[...] = dot(
        second_all[...].reshape(rows * block, width),
        low_all[...].reshape(rows * block, 2 * hidden),
        0,
        0,
    ).reshape(wide_sum.shape)
    wide.pair()
    acts[0].last()
    slots.land()
    wide.copy.wait_recv()
    for place in range(cols):
        total = wide.total(place).astype(jnp.bfloat16)
        for side in range(2):
            wide_low[side, place] = total[side * (height // 2) : (side + 1) * (height // 2), :]
    for kind in range(2):
        downs.merge(kind)
    acts[1].last()
    for side in range(2):
        act_own[:, side * (width // 2) : (side + 1) * (width // 2)] = act_halves[side]
    for item in acts + [downs]:
        item.sent()
    slots.sent()
    wide.copy.wait_send()


def hidden_pass(blocks, down, ffn_norm, query, key, value, number):
    rows, cols, local, width = blocks[0].shape
    block, hidden, height = cols * local, down.shape[0], query.shape[0] // 2
    shape = jax.ShapeDtypeStruct
    own, low, full = shape((local, width), jnp.float32), jnp.bfloat16, jnp.float32
    slot = (2, height, query.shape[1] + key.shape[1] + value.shape[1])
    outs = [own, own, shape((rows, cols, local, width), low), shape((cols,) + slot, low)]
    outs += [shape((rows, block, width), low), shape((rows, block, hidden), low)]
    outs += [shape((2, cols, height // 2, 2 * hidden), low)]
    scratch = [
        pltpu.VMEM((2, rows, cols, local, width // 2), low),
        pltpu.VMEM((2, local, width // 2), full),
        pltpu.VMEM((block, width), full),
        pltpu.VMEM(slot, low),
        pltpu.VMEM((rows, block, 2 * hidden), low),
        pltpu.VMEM((cols, 2, height, 2 * hidden), full),
        pltpu.VMEM((cols, height, 2 * hidden), full),
        pltpu.VMEM((2, cols, local // 2, width), low),
    ]
    scratch += reduce_scratch(rows, cols, local, width // 2) * 2
    scratch += dma(3, 5, cols) + dma(1, 2, cols) + dma(1)
    args = list(blocks) + [down, ffn_norm.reshape(1, width), query, key, value]
    return call_kernel(hidden_kernel, args, outs, scratch, number)


class Paired:
    def __init__(self, part, came, sems, item):
        self.part, self.came, self.sems, self.item = part, came, sems, item
        self.half = lax.rem(lax.axis_index("dp"), 2)

    def pair(self):
        self.copy = send(
            self.part.at[:, 1 - self.half], self.came, self.sems, (self.item,), "dp", sibling()
        )

    def total(self, place):
        return self.part[place, self.half] + self.came[place]


def back_kernel(*refs):
    own_in, own_grad, act_own, middle_own, attn_norm, ffn_norm = refs[:6]
    out_all, cat_all, grad_all, first = refs[6:10]
    hidden_all, wide_low, down_given, slot_all = refs[10:14]
    query_rot, key_rot, value_low, low_rows, totals = refs[14:19]
    sums, query_norm, key_norm, cosine, sine, begins = refs[19:25]
    outs, scratch = refs[25:32], refs[32:]
    block_out, in_grad, wide_got, head_got, out_sum, down_sum, gain_sum = outs
    mid_all, cat_part, grads_in, own_slot, slot_mine, slots_in = scratch[:6]
    head_sum, head_came, head_low = scratch[6:9]
    out_part, out_came, out_low, out_lined = scratch[9:13]
    down_grad, down_came, act_part = scratch[13:16]
    low_even, low_odd, query_acc, key_acc, value_acc = scratch[16:21]
    act_result, down_result, held, landed = scratch[21:25]
    act_scratch, down_scratch = scratch[25:29], (None,) + tuple(scratch[29:32])
    sems = scratch[32:]
    mid_sems, sum_sems, swap_sems, pair_sems = sems[:2], sems[2:4], sems[4:6], sems[6:8]
    cat_sems, low_sems, out_sems, gain_sems = sems[8:10], sems[10:12], sems[12:14], sems[14:16]
    rows, cols = lax.axis_size("row"), lax.axis_size("col")
    row, col = lax.axis_index("row"), lax.axis_index("col")
    half = lax.rem(lax.axis_index("dp"), 2)
    local, width = own_in.shape
    length, head_dim = query_rot.shape
    block = cols * local
    near, far = neighbours()
    greet(corner=True)

    wides = [
        Swap(
            lambda c, h, side=side: wide_low.at[side, c],
            wide_got.at[side],
            swap_sems,
            side,
            whole=True,
        )
        for side in range(2)
    ]
    wides[0].line()
    lanes = held.shape[2] // 3
    held[0] = jnp.zeros(held.shape[1:], jnp.float32)

    def pack_gain(place, gain):
        for line in range(gain.shape[1] // lanes):
            held[0, line : line + 1, place * lanes : (place + 1) * lanes] = gain[
                :, line * lanes : (line + 1) * lanes
            ]

    middle = middle_own[...]
    scale_mid = head_norm(middle, ffn_norm[...])[1]
    middle_back, ffn_gain = head_norm_back(act_own[...], middle, scale_mid, ffn_norm[...])
    middle_grad = own_grad[...].astype(jnp.float32) + middle_back
    in_grad[...] = middle_grad
    mid_all[row, col] = middle_grad.astype(jnp.bfloat16)
    mid = Gather(
        lambda r, c: mid_all.at[r, c],
        lambda r, c, k: mid_all.at[r, c, pl.ds(k * (local // 2), local // 2)],
        mid_sems,
        0,
    )
    for kind in range(2):
        mid.cross(col, kind).start()
    for step in range(1, cols):
        mid_all[:, lax.rem(col + step, cols)] = jnp.zeros((rows, local, width), jnp.bfloat16)
    pack_gain(1, ffn_gain[None, :])

    for side in range(2):
        wide_got[side, col, half] = wide_low[side, col]
    mid.relay(0)
    downs = Reduce(down_given, *down_scratch, down_result, sum_sems, 0)
    for kind in range(2):
        downs.ship(kind)
    down_grad[...] = dot(
        hidden_all[...].reshape(length, hidden_all.shape[-1]),
        grad_all[...].reshape(length, width),
        0,
        0,
    )
    down_copy = send(down_grad, down_came, pair_sems, (3,), "dp", sibling())
    mid.land(0)

    cat_grad = dot(
        mid_all[:, col].reshape(rows * local, width),
        out_all[row].reshape(cols * head_dim, width),
        1,
        1,
    ).astype(jnp.bfloat16)
    for place in range(cols):
        piece = cat_grad[:, place * head_dim : (place + 1) * head_dim]
        cat_part[place, :, :head_dim] = piece[: rows // 2 * local]
        cat_part[place, :, head_dim:] = piece[rows // 2 * local :]

    def turn(source, target, sems, place=None):
        return [
            send(
                source(lax.rem(col + step, cols)),
                place(step) if place else target,
                sems,
                (step,),
                "col",
                lax.rem(col + step, cols),
            )
            for step in range(1, cols)
        ]

    cats = turn(lambda c: cat_part.at[c], grads_in.at[col], cat_sems)
    grads_in[col] = cat_part[col]
    wides[1].line()
    mixed = None
    for place in range(rows):
        term = dot(
            cat_all[place, row].reshape(cols * head_dim, block),
            mid_all[place].reshape(block, width),
        )
        mixed = term if mixed is None else mixed + term
    out = Paired(out_part, out_came, pair_sems, 2)
    out_part[...] = mixed.reshape(cols, 2, head_dim // 2, width)
    out.pair()
    for copy in cats:
        copy.wait_recv()

    score_scale = 1.0 / math.sqrt(head_dim)
    key_acc[...] = jnp.zeros_like(key_acc)
    value_acc[...] = jnp.zeros_like(value_acc)
    for offset, low, _ in spans(length, length // 2, block):
        number = offset // block
        lines, keys = slice(offset, offset + block), slice(low, offset + block)
        probability, _ = block_probability(
            query_rot[lines, :], key_rot[keys, :], begins[lines, :], offset, low, totals[lines, :]
        )
        upper, right = number % (rows // 2) * local, number // (rows // 2) * head_dim
        grad_block = grads_in[:, upper : upper + local, right : right + head_dim].reshape(
            block, head_dim
        )
        value_acc[keys, :] += dot(probability, grad_block, 0, 0)
        row_delta = jnp.sum(
            grad_block.astype(jnp.float32) * low_rows[lines, :].astype(jnp.float32),
            axis=1,
            keepdims=True,
        )
        prob_grad = dot(grad_block, value_low[keys, :], 1, 1)
        score_grad = (
            score_scale * probability.astype(jnp.float32) * (prob_grad - row_delta)
        ).astype(jnp.bfloat16)
        query_acc[lines, :] = dot(score_grad, key_rot[keys, :])
        key_acc[keys, :] += dot(score_grad, query_rot[lines, :], 0, 0)
        if number == 0:
            out.copy.wait_recv()
            for place in range(cols):
                out_low[place] = out.total(place).astype(jnp.bfloat16)
            lined = turn(lambda c: out_low.at[c], None, out_sems, lambda step: out_lined.at[step])
    slot = 3 * head_dim

    def keep(place, value):
        own_slot[:, place * head_dim : (place + 1) * head_dim] = value
        pieces = value.reshape(rows, cols, local, head_dim)
        for number in range(rows):
            upper = number % (rows // 2) * local
            begin = number // (rows // 2) * slot + place * head_dim
            slot_mine[:, upper : upper + local, begin : begin + head_dim] = pieces[number]

    for place, source, gains in ((0, query_acc, query_norm), (1, key_acc, key_norm)):
        raw = sums[:, place * head_dim : (place + 1) * head_dim]
        gain = gains[...]
        inv_rms = head_norm(raw, gain)[1]
        cotangent = source[...] * cosine[...] - swap_halves(source[...]) * sine[...]
        low_part, gain_grad = head_norm_back(cotangent, raw, inv_rms, gain)
        keep(place, low_part.astype(jnp.bfloat16))
        held[0, place : place + 1, 2 * lanes : 2 * lanes + head_dim] = gain_grad[None, :]
    keep(2, value_acc[...].astype(jnp.bfloat16))
    lows = turn(lambda c: slot_mine.at[c], slots_in.at[col], low_sems)
    slots_in[col] = slot_mine[col]
    downs.own()

    head = Paired(head_sum, head_came, pair_sems, 4)
    head_grad = dot(own_slot[...], first[...].reshape(length, width), 0, 0)
    for place in range(cols):
        head_sum[place] = head_grad[
            :, place * (width // cols) : (place + 1) * (width // cols)
        ].reshape(head_sum.shape[1:])
    head.pair()
    for copy in lows:
        copy.wait_recv()
    for place in range(cols):
        columns = slice(place * head_dim, (place + 1) * head_dim)
        came = jnp.concatenate([slots_in[place, :, :slot], slots_in[place, :, slot:]], axis=0)
        low_even[:, columns] = came[:, :head_dim]
        target, offset = (low_odd, 0) if place % 2 else (low_even, cols * head_dim)
        for kind in (0, 1):
            begin = offset + (kind * (cols // 2) + place // 2) * head_dim
            target[:, begin : begin + head_dim] = came[
                :, (1 + kind) * head_dim : (2 + kind) * head_dim
            ]
    slot_weight = slot_all[...].reshape(width, slot_all.shape[-1])
    act = dot(low_even[...], slot_weight, 1, 1) + dot(
        low_odd[...], slot_weight[:, cols * head_dim :], 1, 1
    )
    act_part[...] = act.astype(jnp.bfloat16).reshape(act_part.shape)
    acts = Reduce(act_part, *act_scratch, act_result, sum_sems, 1)
    acts.first()
    head.copy.wait_recv()
    for place in range(cols):
        head_low[place] = head.total(place).astype(jnp.bfloat16)
    heads = Swap(lambda c, h: head_low.at[c], head_got, swap_sems, 2, whole=True)
    heads.line()
    head_got[col, half] = head_low[col]
    acts.toward(0)
    acts.toward(1)
    wides[0].relay()
    wides[1].relay()
    acts.own()

    residual = own_in[...].astype(jnp.float32)
    scale_in = head_norm(residual, attn_norm[...])[1]
    input_back, attn_gain = head_norm_back(act_result[...], residual, scale_in, attn_norm[...])
    in_grad[...] += input_back
    pack_gain(0, attn_gain[None, :])

    def share(stage, axis, size, own):
        copies = [
            send(
                held.at[stage],
                landed.at[stage, own],
                gain_sems,
                (stage, step),
                axis,
                lax.rem(own + step, size),
            )
            for step in range(1, size)
        ]
        landed[stage, own] = held[stage]
        return copies

    def gather_up(stage, copies, size):
        for copy in copies:
            copy.wait_recv()
        total = landed[stage, 0]
        for place in range(1, size):
            total = total + landed[stage, place]
        held[stage + 1] = total

    shares = share(0, "row", rows, row)
    downs.last()
    block_out[...] = (middle_own[...] + down_result[...]).astype(jnp.bfloat16)
    gather_up(0, shares, rows)
    more = share(1, "col", cols, col)
    out_sum[half] = out.total(col)
    for step in range(1, cols):
        lined[step - 1].wait_recv()
        out_sum[half] += out_lined[step].astype(jnp.float32)
    out_copy = send(out_sum.at[half], out_sum.at[half], pair_sems, (5,), "dp", sibling())
    heads.relay()
    down_copy.wait_recv()
    down_sum[...] = down_grad[...] + down_came[...]
    gather_up(1, more, cols)
    gain_copy = send(held.at[2], landed.at[2, 0], gain_sems, (2, 0), "dp", sibling())
    for moved in wides + [heads]:
        moved.land()
    gain_copy.wait_recv()
    gain_sum[...] = held[2] + landed[2, 0]
    out_copy.wait_recv()
    for copy in cats + lows + lined + shares + more + [down_copy, out_copy, gain_copy]:
        copy.wait_send()
    for paired in (out, head):
        paired.copy.wait_send()
    mid.sent(waves=False)
    for item in [downs, acts, heads] + wides:
        item.sent()


def back_pass(args, hidden, head_dim, number):
    rows, cols = lax.axis_size("row"), lax.axis_size("col")
    local, width = args[0].shape
    length, height = rows * cols * local, width // cols // 2
    low, full = jnp.bfloat16, jnp.float32
    shape = jax.ShapeDtypeStruct
    slot, some = 3 * head_dim, head_dim // 2
    outs = [
        shape((local, width), low),
        shape((local, width), full),
        shape((2, cols, 2, height // 2, 2 * hidden), low),
        shape((cols, 2, slot // 2, width // cols), low),
        shape((2, some, width), full),
        shape((hidden, width), full),
        shape((8, 3 * width // 8), full),
    ]

    def vmem(kind, *dims):
        return pltpu.VMEM(dims, kind)

    scratch = [
        vmem(low, rows, cols, local, width),
        vmem(low, cols, rows // 2 * local, 2 * head_dim),
        vmem(low, cols, rows // 2 * local, 2 * head_dim),
        vmem(low, length, slot),
        vmem(low, cols, rows // 2 * local, 2 * slot),
        vmem(low, cols, rows // 2 * local, 2 * slot),
        vmem(full, cols, 2, slot // 2, width // cols),
        vmem(full, cols, slot // 2, width // cols),
        vmem(low, cols, slot // 2, width // cols),
    ]
    scratch += [
        vmem(full, cols, 2, some, width),
        vmem(full, cols, some, width),
        vmem(low, cols, some, width),
        vmem(low, cols, some, width),
        vmem(full, hidden, width),
        vmem(full, hidden, width),
        vmem(low, rows, 1, local, width),
        vmem(low, rows * local, 2 * cols * head_dim),
        vmem(low, rows * local, cols * head_dim),
        vmem(full, length, head_dim),
        vmem(full, length, head_dim),
        vmem(full, length, head_dim),
        vmem(full, local, width),
        vmem(full, local, width),
        vmem(full, 3, 8, 3 * width // 8),
        vmem(full, 3, max(rows, cols), 8, 3 * width // 8),
    ]
    scratch += reduce_scratch(rows, 1, local, width) + reduce_scratch(rows, cols, local, width)[1:]
    scratch += dma(1, 6, cols) + dma(2, 5, cols) + dma(3, 2, cols) + dma(6)
    scratch += dma(cols) + dma(cols) + dma(cols) + dma(3, max(rows, cols))
    return call_kernel(back_kernel, args, outs, scratch, number)


def open_kernel(cols, head_dim, *refs):
    wide_got, head_got, block_given, in_given, out_given, down_given, gain_given = refs[:7]
    gate, up, query, key, value, block_out, in_grad, out, down = refs[7:16]
    attn_gain, ffn_gain, query_gain, key_gain = refs[16:]
    pairs = ((block_out, block_given), (in_grad, in_given), (out, out_given), (down, down_given))
    for target, source in pairs:
        target[...] = source[...]
    lanes = gain_given.shape[1] // 3
    for line in range(gain_given.shape[0]):
        for place, target in ((0, attn_gain), (1, ffn_gain)):
            target[:, line * lanes : (line + 1) * lanes] = gain_given[
                line : line + 1, place * lanes : (place + 1) * lanes
            ]
    query_gain[...] = gain_given[0:1, 2 * lanes : 2 * lanes + head_dim]
    key_gain[...] = gain_given[1:2, 2 * lanes : 2 * lanes + head_dim]
    height, part = wide_got.shape[3], wide_got.shape[4] // 2
    for col in range(cols):
        for piece in range(2):
            for side in range(2):
                begin = (2 * piece + side) * height
                lines = slice(begin, begin + height)
                lanes = slice(col * part, (col + 1) * part)
                gate[lines, lanes] = wide_got[side, col, piece, :, :part].astype(jnp.float32)
                up[lines, lanes] = wide_got[side, col, piece, :, part:].astype(jnp.float32)
    turned = []
    for col in range(cols):
        stacked = head_got[col].reshape(3 * head_dim, head_got.shape[3]).astype(jnp.float32)
        turned.append(
            [stacked[kind * head_dim : (kind + 1) * head_dim].T for kind in range(3)]
        )
        query[:, col * head_dim : (col + 1) * head_dim] = turned[col][0]
    for pair in range(cols // 2):
        for place, target in ((1, key), (2, value)):
            target[:, pair * head_dim : (pair + 1) * head_dim] = (
                turned[2 * pair][place] + turned[2 * pair + 1][place]
            )


def call_kernel(body, args, outs, scratch, number):
    vmem = pl.BlockSpec(memory_space=pltpu.VMEM)
    return pl.pallas_call(
        body,
        out_shape=outs,
        in_specs=[vmem] * len(args),
        out_specs=[vmem] * len(outs),
        scratch_shapes=scratch,
        compiler_params=pltpu.CompilerParams(
            collective_id=number, has_side_effects=True, vmem_limit_bytes=VMEM_LIMIT
        ),
    )(*args)


def dma(*shape):
    return [pltpu.SemaphoreType.DMA(shape), pltpu.SemaphoreType.DMA(shape)]


def dot(left, right, left_dim=1, right_dim=0):
    return lax.dot_general(
        left,
        right,
        (((left_dim,), (right_dim,)), ((), ())),
        preferred_element_type=jnp.float32,
    )


def shards(
    block_input,
    seq_lengths,
    out_grad,
    attn_norm,
    query_weight,
    key_weight,
    value_weight,
    query_norm,
    key_norm,
    out_weight,
    ffn_norm,
    gate_weight,
    up_weight,
    down_weight,
):
    width = block_input.shape[1]
    head_dim = query_norm.shape[0]
    cols = lax.axis_size("col")
    (
        input_blocks,
        out_blocks,
        out_weight_blocks,
        cat_blocks,
        wide_blocks,
        _,
        first_blocks,
        own_sums,
        query_rot,
        key_rot,
        value_low,
        attn_low,
        log_total,
        cosine,
        sine,
        begins,
    ) = front(
        block_input,
        out_grad,
        out_weight,
        query_weight,
        key_weight,
        value_weight,
        gate_weight,
        up_weight,
        (attn_norm, query_norm, key_norm),
        seq_lengths,
        0,
    )
    act_grad2, middle_own, down_part, slot_full, _, hidden, wide_low = hidden_pass(
        [input_blocks, out_blocks, out_weight_blocks, cat_blocks, wide_blocks],
        down_weight,
        ffn_norm,
        query_weight,
        key_weight,
        value_weight,
        1,
    )
    outs = back_pass(
        [block_input, out_grad, act_grad2, middle_own]
        + [attn_norm.reshape(1, width), ffn_norm.reshape(1, width)]
        + [out_weight_blocks, cat_blocks, out_blocks, first_blocks]
        + [hidden, wide_low, down_part, slot_full]
        + [query_rot, key_rot, value_low, attn_low, log_total]
        + [own_sums, query_norm.reshape(1, head_dim), key_norm.reshape(1, head_dim)]
        + [cosine, sine, begins],
        down_weight.shape[0],
        head_dim,
        2,
    )
    block_output, input_grad, wide_got, head_got, out_sum, grad_down, gain_sums = outs
    shape = jax.ShapeDtypeStruct
    weights = (gate_weight, up_weight, query_weight, key_weight, value_weight)
    given = (block_output, input_grad, out_sum.reshape(out_weight.shape), grad_down)
    gains = (width, width, head_dim, head_dim)
    results = local_kernel(
        functools.partial(open_kernel, cols, head_dim),
        [wide_got, head_got] + list(given) + [gain_sums],
        [shape(weight.shape, jnp.float32) for weight in weights]
        + [shape(value.shape, value.dtype) for value in given]
        + [shape((1, size), jnp.float32) for size in gains],
    )
    block_output, input_grad = results[5:7]
    sums = tuple(results[:5]) + tuple(results[7:])
    if lax.axis_size("dp") > 2:
        sums = lax.psum(tuple(0.5 * value for value in sums), "dp")
    grad_gate, grad_up, grad_query, grad_key, grad_value = sums[:5]
    grad_outweight, grad_down, grad_attnnorm, grad_ffnnorm, grad_qnorm, grad_knorm = sums[5:]
    return (
        block_output,
        input_grad,
        grad_attnnorm[0],
        grad_query,
        grad_key,
        grad_value,
        grad_qnorm[0],
        grad_knorm[0],
        grad_outweight,
        grad_ffnnorm[0],
        grad_gate,
        grad_up,
        grad_down,
    )


def solution(mesh):
    placed = (
        P(("dp", "row", "col"), None),
        P("dp", None),
        P(("dp", "row", "col"), None),
        P(),
        P("col", "row"),
        P("col", "row"),
        P("col", "row"),
        P(),
        P(),
        P(("row", "col"), None),
        P(),
        P("col", "row"),
        P("col", "row"),
        P(("row", "col"), None),
    )
    return jax.shard_map(
        shards,
        mesh=mesh,
        in_specs=placed,
        out_specs=(
            P(("dp", "row", "col"), None),
            P(("dp", "row", "col"), None),
            P(),
            P("col", "row"),
            P("col", "row"),
            P("col", "row"),
            P(),
            P(),
            P(("row", "col"), None),
            P(),
            P("col", "row"),
            P("col", "row"),
            P(("row", "col"), None),
        ),
        check_vma=False,
    )
```

```python
import functools
import math

import jax
import jax.numpy as jnp
from jax import lax
from jax.experimental import pallas as pl
from jax.experimental.pallas import tpu as pltpu
from jax.sharding import PartitionSpec as P

EPSILON = 1e-05
THETA = 1000000.0


def rope_frequency(width):
    half_width = width // 2
    exponent = jnp.arange(half_width, dtype=jnp.float32) * (2.0 / width)
    frequency = jnp.exp(-math.log(THETA) * exponent)
    return jnp.concatenate([frequency, frequency])[None, :]


def head_norm(values, gain_vec):
    inv_rms = lax.rsqrt(jnp.mean(values * values, axis=-1, keepdims=True) + EPSILON)
    return (values * inv_rms * gain_vec, inv_rms)


def head_norm_back(cotangent, values, inv_rms, gain_vec):
    normed = values * inv_rms
    weighted = cotangent * gain_vec
    gain_grad = jnp.sum(cotangent * normed, axis=0)
    inner_mean = jnp.mean(weighted * normed, axis=-1, keepdims=True)
    return (inv_rms * (weighted - normed * inner_mean), gain_grad)


def swap_halves(values):
    half_width = values.shape[-1] // 2
    return jnp.concatenate([values[:, half_width:], values[:, :half_width]], axis=1)


def block_probability(query_block, key_rows, begins, offset, low, shift):
    score_scale = 1.0 / math.sqrt(query_block.shape[1])
    scores = dot(query_block, key_rows, 1, 1) * score_scale
    places = low + lax.broadcasted_iota(jnp.int32, scores.shape, 1)
    row_places = offset + lax.broadcasted_iota(jnp.int32, scores.shape, 0)
    allowed = (places >= begins) & (places <= row_places)
    if shift is None:
        shift = jnp.log(jnp.sum(jnp.where(allowed, jnp.exp(scores), 0.0), axis=1, keepdims=True))
    probability = jnp.where(allowed, jnp.exp(scores - shift), 0.0).astype(jnp.bfloat16)
    return probability, shift


def spans(length, longest, block):
    return [
        (offset, max(0, (offset - longest) // 128 * 128), block)
        for offset in range(0, length, block)
    ]


def local_kernel(body, args, outs, scratch=()):
    vmem = pl.BlockSpec(memory_space=pltpu.VMEM)
    return pl.pallas_call(
        body,
        out_shape=outs,
        in_specs=[vmem] * len(args),
        out_specs=[vmem] * len(outs),
        scratch_shapes=list(scratch),
    )(*args)


MESH = pl.DeviceIdType.MESH
VMEM_LIMIT = 60 * 1024 * 1024


def remote(source, target, sems, place, axis, index):
    return pltpu.make_async_remote_copy(
        src_ref=source,
        dst_ref=target,
        send_sem=sems[0].at[place],
        recv_sem=sems[1].at[place],
        device_id={axis: index},
        device_id_type=MESH,
    )


def send(source, target, sems, place, axis, index):
    copy = remote(source, target, sems, place, axis, index)
    copy.start()
    return copy


def neighbours():
    rows, row = lax.axis_size("row"), lax.axis_index("row")
    near = row + 1 - 2 * lax.rem(row, 2)
    far = lax.rem(row + rows // 2, rows)
    return near, far


def sibling():
    own = lax.axis_index("dp")
    return own + 1 - 2 * lax.rem(own, 2)


def greet():
    cols, col = lax.axis_size("col"), lax.axis_index("col")
    near, far = neighbours()
    peers = [("col", lax.rem(col + step, cols)) for step in range(1, cols)]
    peers += [("row", near), ("row", far), ("dp", sibling())]
    peers.append(("row", lax.rem(near + lax.axis_size("row") // 2, lax.axis_size("row"))))
    barrier = pltpu.get_barrier_semaphore()
    for axis, index in peers:
        pl.semaphore_signal(barrier, inc=1, device_id={axis: index}, device_id_type=MESH)
    pl.semaphore_wait(barrier, len(peers))


class Gather:
    def __init__(self, block, part, sems, item):
        self.block, self.part = block, part
        self.sems, self.item = sems, item
        self.cols, self.col = lax.axis_size("col"), lax.axis_index("col")
        self.row = lax.axis_index("row")
        self.near, self.far = neighbours()

    def hop(self, origin, right):
        piece = self.block(self.row, origin)
        place = (self.item, 0 if right else 1, origin)
        return remote(piece, piece, self.sems, place, "col", self.col + (1 if right else -1))

    def cross(self, origin, kind):
        piece = self.block(self.row, origin)
        peer = (self.near, self.far)[kind]
        return remote(piece, piece, self.sems, (self.item, 2 + kind, origin), "row", peer)

    def corner(self, origin, kind):
        source, peer = ((self.near, self.far), (self.far, self.near))[kind]
        piece = self.part(source, origin, kind)
        return remote(piece, piece, self.sems, (self.item, 4 + kind, origin), "row", peer)

    def forward(self, origin, right):
        @pl.when(self.col < self.cols - 1 if right else self.col > 0)
        def _():
            self.hop(origin, right).start()

    def each(self, wave, act):
        if wave == 0:
            act(self.col, None)
            return
        for right in (True, False):
            origin = self.col - wave if right else self.col + wave

            @pl.when(self.col >= wave if right else self.col + wave < self.cols)
            def _():
                act(origin, right)

    def start(self):
        for right in (True, False):
            self.forward(self.col, right)
        for kind in range(2):
            self.cross(self.col, kind).start()

    def wave(self, wave):
        def act(origin, right):
            self.hop(origin, right).wait_recv()
            self.forward(origin, right)
            for kind in range(2):
                self.cross(origin, kind).start()

        self.each(wave, act)

    def relay(self, wave):
        def act(origin, right):
            for kind in range(2):
                self.cross(origin, kind).wait_recv()
                self.corner(origin, kind).start()

        self.each(wave, act)

    def land(self, wave):
        def act(origin, right):
            for kind in range(2):
                self.corner(origin, kind).wait_recv()

        self.each(wave, act)

    def sent(self, waves=True):
        def act(origin, right):
            for side in (True, False) if right is None else (right,):

                @pl.when(self.col < self.cols - 1 if side else self.col > 0)
                def _():
                    if waves:
                        self.hop(origin, side).wait_send()

            for kind in range(2):
                self.cross(origin, kind).wait_send()
                self.corner(origin, kind).wait_send()

        for wave in range(self.cols if waves else 1):
            self.each(wave, act)


class Swap:
    def __init__(self, source, target, sems, item, whole=False):
        self.source, self.target, self.sems, self.item = source, target, sems, item
        self.cols, self.col = lax.axis_size("col"), lax.axis_index("col")
        self.half = lax.rem(lax.axis_index("dp"), 2)
        self.lines, self.pairs, self.first = {}, {}, 0 if whole else 1

    def line(self):
        for step in range(1, self.cols):
            peer = lax.rem(self.col + step, self.cols)
            self.lines[step] = send(
                self.source(peer, self.half),
                self.target.at[self.col, self.half],
                self.sems,
                (self.item, 0, step),
                "col",
                peer,
            )

    def relay(self):
        for step in range(self.first, self.cols):
            if step:
                self.lines[step].wait_recv()
            piece = self.target.at[lax.rem(self.col + self.cols - step, self.cols), self.half]
            self.pairs[step] = send(
                piece, piece, self.sems, (self.item, 1, step), "dp", sibling()
            )

    def land(self):
        for copy in self.pairs.values():
            copy.wait_recv()

    def sent(self):
        for copies in (self.lines, self.pairs):
            for copy in copies.values():
                copy.wait_send()


def front_kernel(*refs):
    (own_in, own_grad, own_out, query, key, value, gate, up) = refs[:8]
    (attn_norm, query_norm, key_norm, seq_lengths, frequency) = refs[8:13]
    (in_all, grad_all, out_all, cat_all, wide_all, slot_all) = refs[13:19]
    (first, sums, query_rot, key_rot, value_low, low_rows, totals) = refs[19:26]
    (cosine, sine, begins) = refs[26:29]
    (slot_part, wide_part) = refs[29:31]
    gather_sems, swap_sems, pair_sems = refs[31:33], refs[33:35], refs[35:37]
    rows, cols = lax.axis_size("row"), lax.axis_size("col")
    row, col = lax.axis_index("row"), lax.axis_index("col")
    half = lax.rem(lax.axis_index("dp"), 2)
    near, far = neighbours()
    corner = lax.rem(near + rows // 2, rows)
    length, head_dim = query_rot.shape
    width = own_in.shape[1]
    local = own_in.shape[0]
    block = length // rows

    def split(ref):
        count = ref.shape[2] // 2
        return (
            lambda r, c: ref.at[r, c],
            lambda r, c, k: ref.at[r, c, pl.ds(k * count, count)],
        )

    in_all[row, col] = own_in[...]
    inputs = Gather(*split(in_all), gather_sems, 0)
    inputs.start()
    height = query.shape[0] // 2
    for place in range(cols):
        for piece in range(2):
            lines = slice(piece * height, (piece + 1) * height)
            lanes = slice(place // 2 * head_dim, (place // 2 + 1) * head_dim)
            slot_part[place, piece, :, :head_dim] = query[
                lines, place * head_dim : (place + 1) * head_dim
            ]
            slot_part[place, piece, :, head_dim : 2 * head_dim] = key[lines, lanes]
            slot_part[place, piece, :, 2 * head_dim :] = value[lines, lanes]
    slots = Swap(lambda c, h: slot_part.at[c, h], slot_all, swap_sems, 0)
    slots.line()
    slot_all[col] = slot_part[col]
    grad_all[row, col] = own_grad[...]
    out_all[row, col] = own_out[...]
    inputs.wave(1)
    inputs.relay(0)
    inputs.wave(2)
    inputs.relay(1)
    for step in range(3, cols):
        inputs.wave(step)
    count = own_out.shape[1] // 2
    outs = Gather(
        lambda r, c: out_all.at[r, c, half],
        lambda r, c, k: out_all.at[r, c, half, pl.ds(k * count, count)],
        gather_sems,
        2,
    )
    outs.start()
    grads = Gather(*split(grad_all), gather_sems, 1)
    inputs.relay(2)
    places = lax.broadcasted_iota(jnp.int32, (length, 1), 0)
    end, begin = jnp.zeros((1, 1), jnp.int32), jnp.zeros((length, 1), jnp.int32)
    for number in range(seq_lengths.shape[1]):
        size = seq_lengths[:, number : number + 1]
        end = end + size
        begin = begin + jnp.where(places >= end, size, 0)
    begins[...] = begin
    for step in range(3, cols):
        inputs.relay(step)
    angles = (places - begin).astype(jnp.float32) * frequency[...]
    cosine[...] = jnp.cos(angles)
    grads.start()
    side = lax.broadcasted_iota(jnp.int32, angles.shape, 1)
    turned = jnp.sin(angles)
    sine[...] = jnp.where(side < head_dim // 2, -turned, turned)
    slots.relay()
    for step in range(1, cols):
        outs.wave(step)
    slots.land()

    def project(place):
        for c in range(cols):
            values = in_all[place, c].astype(jnp.float32)
            normed = head_norm(values, attn_norm[...])[0]
            first[place, c] = normed.astype(jnp.bfloat16)
        lines = pl.ds(pl.multiple_of(place * block, block), block)
        sums[lines, :] = dot(
            first[place].reshape(block, width), slot_all[...].reshape(width, 3 * head_dim)
        )

    project(row)
    project(near)
    project(far)
    for step in range(cols):
        inputs.land(step)
    project(corner)
    for place, target, gain in ((0, query_rot, query_norm), (1, key_rot, key_norm)):
        normed = head_norm(sums[:, place * head_dim : (place + 1) * head_dim], gain[...])[0]
        target[...] = (normed * cosine[...] + swap_halves(normed) * sine[...]).astype(jnp.bfloat16)
    value_low[...] = sums[:, 2 * head_dim : 3 * head_dim].astype(jnp.bfloat16)
    hidden = gate.shape[1] // cols

    def pack(place):
        for kind, source in ((0, gate), (1, up)):
            for piece in range(2):
                wide_part[place, piece, :, kind * hidden : (kind + 1) * hidden] = source[
                    piece * height : (piece + 1) * height, place * hidden : (place + 1) * hidden
                ]

    def cat(part):
        places = pl.ds(part * (rows // 2), rows // 2)
        return Gather(
            lambda r, c: cat_all.at[places, r, c],
            lambda r, c, k: cat_all.at[places, r, c, pl.ds(k * head_dim // 2, head_dim // 2)],
            gather_sems,
            3 + part,
        )

    cats = [cat(part) for part in range(2)]
    wide = Swap(lambda c, h: wide_part.at[c, h], wide_all, swap_sems, 1)
    for offset, low, _ in spans(length, length // 2, block):
        number = offset // block
        lines, keys = slice(offset, offset + block), slice(low, offset + block)
        probability, total = block_probability(
            query_rot[lines, :], key_rot[keys, :], begins[lines, :], offset, low, None
        )
        totals[lines, :] = total
        low_rows[lines, :] = dot(probability, value_low[keys, :]).astype(jnp.bfloat16)
        cat_all[number, row, col] = dot(value_low[keys, :], probability, 0, 1).astype(jnp.bfloat16)
        if number == 0:
            grads.wave(1)
            outs.relay(0)
        if number == rows // 2 - 1:
            cats[0].start()
            for step in range(1, cols):
                outs.relay(step)
            for step in range(2, cols):
                grads.wave(step)
        if number == rows // 2:
            grads.relay(0)
    cats[1].start()
    for place in range(cols):
        pack(place)
    wide.line()
    wide_all[col] = wide_part[col]
    cats[0].wave(1)
    grads.relay(1)
    for step in range(2, cols):
        cats[0].wave(step)
    for step in range(1, cols):
        cats[1].wave(step)
    for step in range(2, cols):
        grads.relay(step)
    for step in range(cols):
        cats[0].relay(step)
    pairs = []
    for step in range(cols):
        outs.land(step)
    for number, place in enumerate((near, far, corner)):
        piece = out_all.at[place, :, half]
        pairs.append(send(piece, piece, pair_sems, (number,), "dp", sibling()))
    for step in range(1, cols):
        piece = out_all.at[row, lax.rem(col + cols - step, cols), half]
        pairs.append(send(piece, piece, pair_sems, (2 + step,), "dp", sibling()))
    for step in range(cols):
        cats[1].relay(step)
    wide.relay()
    wide.land()
    for gather in [grads] + cats:
        for step in range(cols):
            gather.land(step)
    for copy in pairs:
        copy.wait()
    for item in [inputs, grads, outs, slots, wide] + cats:
        item.sent()


def front(own_in, own_grad, own_out, query, key, value, gate, up, norms, seq_lengths):
    rows, cols = lax.axis_size("row"), lax.axis_size("col")
    local, width = own_in.shape
    attn_norm, query_norm, key_norm = norms
    length, head_dim = local * rows * cols, query_norm.shape[0]
    hidden, height = gate.shape[1] // cols, gate.shape[0] // 2
    low = jnp.bfloat16
    blocks = jax.ShapeDtypeStruct((rows, cols, local, width), low)
    halves = own_out.shape[0] // 2
    wide = (cols, 2, height, 2 * hidden)
    slot = (cols, 2, height, 3 * head_dim)
    shape = jax.ShapeDtypeStruct
    head_rows = shape((length, head_dim), low)
    table = shape((length, head_dim), jnp.float32)
    outs = [
        blocks,
        blocks,
        shape((rows, cols, 2, halves, width), low),
        shape((rows, rows, cols, head_dim, length // rows), low),
        shape(wide, low),
        shape(slot, low),
        blocks,
        shape((length, 3 * head_dim), jnp.float32),
        head_rows,
        head_rows,
        head_rows,
        head_rows,
        shape((length, 1), jnp.float32),
        table,
        table,
        shape((length, 1), jnp.int32),
    ]
    scratch = [pltpu.VMEM(slot, low), pltpu.VMEM(wide, low)]
    scratch += dma(5, 6, cols) + dma(2, 2, cols) + dma(2 + cols)
    args = [own_in, own_grad, own_out.reshape(2, halves, width), query, key, value, gate, up]
    args += [attn_norm.reshape(1, width), query_norm.reshape(1, head_dim)]
    args += [key_norm.reshape(1, head_dim), seq_lengths, rope_frequency(head_dim)]
    return args, outs, scratch


class Reduce:
    def __init__(self, part, relayed, planed, staged, lined, result, sems, item):
        self.part, self.relayed, self.planed = part, relayed, planed
        self.staged, self.lined, self.result = staged, lined, result
        self.sems, self.item = sems, item
        self.cols = part.shape[1]
        self.col = lax.axis_index("col") if self.cols > 1 else 0
        self.row = lax.axis_index("row")
        self.near, self.far = neighbours()
        self.cross = lax.rem(self.near + lax.axis_size("row") // 2, lax.axis_size("row"))
        self.count = part.shape[2] // 2
        self.relays, self.planes, self.lines = [], [], []

    def first(self):
        for kind, peer in ((0, self.near), (1, self.far)):
            self.relays.append(
                send(
                    self.part.at[self.cross, :, pl.ds(kind * self.count, self.count)],
                    self.relayed.at[kind],
                    self.sems,
                    (self.item, 1 + kind, 0),
                    "row",
                    peer,
                )
            )

    def merge(self, kind):
        peer, came = (self.near, self.far)[kind], 1 - kind
        self.relays[came].wait_recv()
        lines = slice(came * self.count, (came + 1) * self.count)
        self.part[peer, :, lines] = (
            self.part[peer, :, lines].astype(jnp.float32)
            + self.relayed[came].astype(jnp.float32)
        ).astype(jnp.bfloat16)

    def ship(self, kind):
        peer = (self.near, self.far)[kind]
        self.planes.append(
            send(
                self.part.at[peer],
                self.planed.at[kind],
                self.sems,
                (self.item, 3 + kind, 0),
                "row",
                peer,
            )
        )

    def toward(self, kind):
        self.merge(kind)
        self.ship(kind)

    def total(self, place):
        summed = self.part[self.row, place].astype(jnp.float32)
        for kind in range(2):
            summed = summed + self.planed[kind, place].astype(jnp.float32)
        return summed

    def own(self):
        for copy in self.planes:
            copy.wait_recv()
        for step in range(1, self.cols):
            place = lax.rem(self.col + step, self.cols)
            self.staged[step] = self.total(place).astype(jnp.bfloat16)
            self.lines.append(
                send(
                    self.staged.at[step],
                    self.lined.at[step],
                    self.sems,
                    (self.item, 0, step),
                    "col",
                    place,
                )
            )
        self.result[...] = self.total(self.col)

    def last(self):
        for step in range(1, self.cols):
            self.lines[step - 1].wait_recv()
            self.result[...] += self.lined[step].astype(jnp.float32)

    def sent(self):
        for copy in self.relays + self.planes + self.lines:
            copy.wait_send()


def reduce_scratch(rows, cols, local, width):
    low = jnp.bfloat16
    return [
        pltpu.VMEM((2, cols, local // 2, width), low),
        pltpu.VMEM((2, cols, local, width), low),
        pltpu.VMEM((cols, local, width), low),
        pltpu.VMEM((cols, local, width), low),
    ]


def hidden_kernel(*refs):
    in_all, grad_all, out_all, cat_all, wide_all, down, ffn_norm = refs[:7]
    query, key, value = refs[7:10]
    act_own, middle_own, down_part, slot_all = refs[10:14]
    second_all, hidden_all, wide_low = refs[14:17]
    act_parts, act_halves, middle_block, slot_part = refs[17:21]
    low_all, wide_sum, wide_came, down_relayed = refs[21:25]
    act_scratch, rest = (refs[25:29], refs[29:33]), refs[33:]
    sems, swap_sems, pair_sems = rest[:2], rest[2:4], rest[4:6]
    rows, cols = lax.axis_size("row"), lax.axis_size("col")
    row, col = lax.axis_index("row"), lax.axis_index("col")
    near, far = neighbours()
    cross = lax.rem(near + rows // 2, rows)
    local, width = in_all.shape[2:]
    block, hidden = cols * local, down.shape[0]
    height, begin = query.shape[0] // 2, 0
    for source in (query, key, value):
        lanes = slice(begin, begin + source.shape[1])
        for piece in range(2):
            slot_part[piece, :, lanes] = source[piece * height : (piece + 1) * height, :]
        begin += source.shape[1]
    slots = Swap(lambda c, h: slot_part.at[h], slot_all, swap_sems, 0)
    slots.line()
    slot_all[col] = slot_part[...]
    acts = [
        Reduce(act_parts.at[side], *act_scratch[side], act_halves.at[side], sems, side)
        for side in range(2)
    ]

    downs = Reduce(down_part, down_relayed, None, None, None, None, sems, 2)

    def work(place):
        mixed = dot(cat_all[place].reshape(width, block), out_all[...].reshape(width, width), 0, 0)
        middle = in_all[place].reshape(block, width).astype(jnp.float32) + mixed
        middle_block[...] = middle
        second = head_norm(middle, ffn_norm[...])[0].astype(jnp.bfloat16)
        second_all[place] = second
        wide_weight = wide_all[...].reshape(width, 2 * hidden)
        wide_sums = dot(second, wide_weight)
        gating, upward = wide_sums[:, :hidden], wide_sums[:, hidden:]
        hidden_grad = dot(grad_all[place].reshape(block, width), down[...], 1, 1)
        sigmoid_gate = jax.nn.sigmoid(gating)
        activated = gating * sigmoid_gate
        hidden_low = (activated * upward).astype(jnp.bfloat16)
        gate_low = (
            hidden_grad * upward * sigmoid_gate * (1.0 + gating * (1.0 - sigmoid_gate))
        ).astype(jnp.bfloat16)
        up_low = (hidden_grad * activated).astype(jnp.bfloat16)
        hidden_all[place] = hidden_low
        low_all[place, :, :hidden] = gate_low
        low_all[place, :, hidden:] = up_low
        act = dot(low_all[place], wide_weight, 1, 1).astype(jnp.bfloat16)
        for side in range(2):
            act_parts[side, place] = act[
                :, side * (width // 2) : (side + 1) * (width // 2)
            ].reshape(cols, local, width // 2)

    def work_down(place):
        down_part[place] = (
            dot(hidden_all[place], down[...]).astype(jnp.bfloat16).reshape(cols, local, width)
        )

    work(cross)
    for item in acts:
        item.first()
    work_down(cross)
    work(near)
    for item in acts:
        item.toward(0)
    slots.relay()
    work(far)
    for item in acts:
        item.toward(1)
    downs.first()
    work(row)
    lines = pl.ds(pl.multiple_of(col * local, local), local)
    middle_own[...] = middle_block[lines, :]
    acts[0].own()
    for place in (near, far, row):
        work_down(place)
    acts[1].own()
    wide = Paired(wide_sum, wide_came, pair_sems, 0)
    wide_sum[...] = dot(
        second_all[...].reshape(rows * block, width),
        low_all[...].reshape(rows * block, 2 * hidden),
        0,
        0,
    ).reshape(wide_sum.shape)
    wide.pair()
    acts[0].last()
    slots.land()
    wide.copy.wait_recv()
    for place in range(cols):
        total = wide.total(place).astype(jnp.bfloat16)
        for side in range(2):
            wide_low[side, place] = total[side * (height // 2) : (side + 1) * (height // 2), :]
    for kind in range(2):
        downs.merge(kind)
    acts[1].last()
    for side in range(2):
        act_own[:, side * (width // 2) : (side + 1) * (width // 2)] = act_halves[side]
    for item in acts + [downs]:
        item.sent()
    slots.sent()
    wide.copy.wait_send()


def hidden_pass(local, width, hidden, query, key, value):
    rows, cols = lax.axis_size("row"), lax.axis_size("col")
    block, height = cols * local, query.shape[0] // 2
    shape = jax.ShapeDtypeStruct
    own, low, full = shape((local, width), jnp.float32), jnp.bfloat16, jnp.float32
    slot = (2, height, query.shape[1] + key.shape[1] + value.shape[1])
    outs = [own, own, shape((rows, cols, local, width), low), shape((cols,) + slot, low)]
    outs += [shape((rows, block, width), low), shape((rows, block, hidden), low)]
    outs += [shape((2, cols, height // 2, 2 * hidden), low)]
    scratch = [
        pltpu.VMEM((2, rows, cols, local, width // 2), low),
        pltpu.VMEM((2, local, width // 2), full),
        pltpu.VMEM((block, width), full),
        pltpu.VMEM(slot, low),
        pltpu.VMEM((rows, block, 2 * hidden), low),
        pltpu.VMEM((cols, 2, height, 2 * hidden), full),
        pltpu.VMEM((cols, height, 2 * hidden), full),
        pltpu.VMEM((2, cols, local // 2, width), low),
    ]
    scratch += reduce_scratch(rows, cols, local, width // 2) * 2
    scratch += dma(3, 5, cols) + dma(1, 2, cols) + dma(1)
    return outs, scratch


class Paired:
    def __init__(self, part, came, sems, item):
        self.part, self.came, self.sems, self.item = part, came, sems, item
        self.half = lax.rem(lax.axis_index("dp"), 2)

    def pair(self):
        self.copy = send(
            self.part.at[:, 1 - self.half], self.came, self.sems, (self.item,), "dp", sibling()
        )

    def total(self, place):
        return self.part[place, self.half] + self.came[place]


def back_kernel(*refs):
    own_in, own_grad, act_own, middle_own, attn_norm, ffn_norm = refs[:6]
    out_all, cat_all, grad_all, first = refs[6:10]
    hidden_all, wide_low, down_given, slot_all = refs[10:14]
    query_rot, key_rot, value_low, low_rows, totals = refs[14:19]
    sums, query_norm, key_norm, cosine, sine, begins = refs[19:25]
    outs, scratch = refs[25:32], refs[32:]
    block_out, in_grad, wide_got, head_got, out_sum, down_sum, gain_sum = outs
    mid_all, cat_part, grads_in, own_slot, slot_mine, slots_in = scratch[:6]
    head_sum, head_came, head_low = scratch[6:9]
    out_part, out_came, out_low, out_lined = scratch[9:13]
    down_grad, down_came, act_part = scratch[13:16]
    low_even, low_odd, query_acc, key_acc, value_acc = scratch[16:21]
    act_result, down_result, held, landed = scratch[21:25]
    act_scratch, down_scratch = scratch[25:29], (None,) + tuple(scratch[29:32])
    sems = scratch[32:]
    mid_sems, sum_sems, swap_sems, pair_sems = sems[:2], sems[2:4], sems[4:6], sems[6:8]
    cat_sems, low_sems, out_sems, gain_sems = sems[8:10], sems[10:12], sems[12:14], sems[14:16]
    rows, cols = lax.axis_size("row"), lax.axis_size("col")
    row, col = lax.axis_index("row"), lax.axis_index("col")
    half = lax.rem(lax.axis_index("dp"), 2)
    local, width = own_in.shape
    length, head_dim = query_rot.shape
    block = cols * local
    near, far = neighbours()
    wides = [
        Swap(
            lambda c, h, side=side: wide_low.at[side, c],
            wide_got.at[side],
            swap_sems,
            side,
            whole=True,
        )
        for side in range(2)
    ]
    wides[0].line()
    lanes = held.shape[2] // 3
    held[0] = jnp.zeros(held.shape[1:], jnp.float32)

    def pack_gain(place, gain):
        for line in range(gain.shape[1] // lanes):
            held[0, line : line + 1, place * lanes : (place + 1) * lanes] = gain[
                :, line * lanes : (line + 1) * lanes
            ]

    middle = middle_own[...]
    scale_mid = head_norm(middle, ffn_norm[...])[1]
    middle_back, ffn_gain = head_norm_back(act_own[...], middle, scale_mid, ffn_norm[...])
    middle_grad = own_grad[...].astype(jnp.float32) + middle_back
    in_grad[...] = middle_grad
    mid_all[row, col] = middle_grad.astype(jnp.bfloat16)
    mid = Gather(
        lambda r, c: mid_all.at[r, c],
        lambda r, c, k: mid_all.at[r, c, pl.ds(k * (local // 2), local // 2)],
        mid_sems,
        0,
    )
    for kind in range(2):
        mid.cross(col, kind).start()
    for step in range(1, cols):
        mid_all[:, lax.rem(col + step, cols)] = jnp.zeros((rows, local, width), jnp.bfloat16)
    pack_gain(1, ffn_gain[None, :])

    for side in range(2):
        wide_got[side, col, half] = wide_low[side, col]
    mid.relay(0)
    downs = Reduce(down_given, *down_scratch, down_result, sum_sems, 0)
    for kind in range(2):
        downs.ship(kind)
    down_grad[...] = dot(
        hidden_all[...].reshape(length, hidden_all.shape[-1]),
        grad_all[...].reshape(length, width),
        0,
        0,
    )
    down_copy = send(down_grad, down_came, pair_sems, (3,), "dp", sibling())
    mid.land(0)

    cat_grad = dot(
        mid_all[:, col].reshape(rows * local, width),
        out_all[row].reshape(cols * head_dim, width),
        1,
        1,
    ).astype(jnp.bfloat16)
    for place in range(cols):
        piece = cat_grad[:, place * head_dim : (place + 1) * head_dim]
        cat_part[place, :, :head_dim] = piece[: rows // 2 * local]
        cat_part[place, :, head_dim:] = piece[rows // 2 * local :]

    def turn(source, target, sems, place=None):
        return [
            send(
                source(lax.rem(col + step, cols)),
                place(step) if place else target,
                sems,
                (step,),
                "col",
                lax.rem(col + step, cols),
            )
            for step in range(1, cols)
        ]

    cats = turn(lambda c: cat_part.at[c], grads_in.at[col], cat_sems)
    grads_in[col] = cat_part[col]
    mixed = None
    for place in range(rows):
        term = dot(
            cat_all[place, row].reshape(cols * head_dim, block),
            mid_all[place].reshape(block, width),
        )
        mixed = term if mixed is None else mixed + term
    out = Paired(out_part, out_came, pair_sems, 2)
    out_part[...] = mixed.reshape(cols, 2, head_dim // 2, width)
    out.pair()
    for copy in cats:
        copy.wait_recv()
    wides[1].line()

    score_scale = 1.0 / math.sqrt(head_dim)
    key_acc[...] = jnp.zeros_like(key_acc)
    value_acc[...] = jnp.zeros_like(value_acc)
    for offset, low, _ in spans(length, length // 2, block):
        number = offset // block
        lines, keys = slice(offset, offset + block), slice(low, offset + block)
        probability, _ = block_probability(
            query_rot[lines, :], key_rot[keys, :], begins[lines, :], offset, low, totals[lines, :]
        )
        upper, right = number % (rows // 2) * local, number // (rows // 2) * head_dim
        grad_block = grads_in[:, upper : upper + local, right : right + head_dim].reshape(
            block, head_dim
        )
        value_acc[keys, :] += dot(probability, grad_block, 0, 0)
        row_delta = jnp.sum(
            grad_block.astype(jnp.float32) * low_rows[lines, :].astype(jnp.float32),
            axis=1,
            keepdims=True,
        )
        prob_grad = dot(grad_block, value_low[keys, :], 1, 1)
        score_grad = (
            score_scale * probability.astype(jnp.float32) * (prob_grad - row_delta)
        ).astype(jnp.bfloat16)
        query_acc[lines, :] = dot(score_grad, key_rot[keys, :])
        key_acc[keys, :] += dot(score_grad, query_rot[lines, :], 0, 0)
        if number == 0:
            out.copy.wait_recv()
            for place in range(cols):
                out_low[place] = out.total(place).astype(jnp.bfloat16)
            lined = turn(lambda c: out_low.at[c], None, out_sems, lambda step: out_lined.at[step])
    slot = 3 * head_dim

    def keep(place, value):
        own_slot[:, place * head_dim : (place + 1) * head_dim] = value
        pieces = value.reshape(rows, cols, local, head_dim)
        for number in range(rows):
            upper = number % (rows // 2) * local
            begin = number // (rows // 2) * slot + place * head_dim
            slot_mine[:, upper : upper + local, begin : begin + head_dim] = pieces[number]

    for place, source, gains in ((0, query_acc, query_norm), (1, key_acc, key_norm)):
        raw = sums[:, place * head_dim : (place + 1) * head_dim]
        gain = gains[...]
        inv_rms = head_norm(raw, gain)[1]
        cotangent = source[...] * cosine[...] - swap_halves(source[...]) * sine[...]
        low_part, gain_grad = head_norm_back(cotangent, raw, inv_rms, gain)
        keep(place, low_part.astype(jnp.bfloat16))
        held[0, place : place + 1, 2 * lanes : 2 * lanes + head_dim] = gain_grad[None, :]
    keep(2, value_acc[...].astype(jnp.bfloat16))
    lows = turn(lambda c: slot_mine.at[c], slots_in.at[col], low_sems)
    slots_in[col] = slot_mine[col]

    head = Paired(head_sum, head_came, pair_sems, 4)
    head_grad = dot(own_slot[...], first[...].reshape(length, width), 0, 0)
    for place in range(cols):
        head_sum[place] = head_grad[
            :, place * (width // cols) : (place + 1) * (width // cols)
        ].reshape(head_sum.shape[1:])
    head.pair()
    for copy in lows:
        copy.wait_recv()
    downs.own()
    for place in range(cols):
        columns = slice(place * head_dim, (place + 1) * head_dim)
        came = jnp.concatenate([slots_in[place, :, :slot], slots_in[place, :, slot:]], axis=0)
        low_even[:, columns] = came[:, :head_dim]
        target, offset = (low_odd, 0) if place % 2 else (low_even, cols * head_dim)
        for kind in (0, 1):
            begin = offset + (kind * (cols // 2) + place // 2) * head_dim
            target[:, begin : begin + head_dim] = came[
                :, (1 + kind) * head_dim : (2 + kind) * head_dim
            ]
    slot_weight = slot_all[...].reshape(width, slot_all.shape[-1])
    act = dot(low_even[...], slot_weight, 1, 1) + dot(
        low_odd[...], slot_weight[:, cols * head_dim :], 1, 1
    )
    act_part[...] = act.astype(jnp.bfloat16).reshape(act_part.shape)
    acts = Reduce(act_part, *act_scratch, act_result, sum_sems, 1)
    acts.first()
    head.copy.wait_recv()
    for place in range(cols):
        head_low[place] = head.total(place).astype(jnp.bfloat16)
    heads = Swap(lambda c, h: head_low.at[c], head_got, swap_sems, 2, whole=True)
    heads.line()
    head_got[col, half] = head_low[col]
    acts.toward(0)
    acts.toward(1)
    wides[0].relay()
    wides[1].relay()
    acts.own()

    residual = own_in[...].astype(jnp.float32)
    scale_in = head_norm(residual, attn_norm[...])[1]
    input_back, attn_gain = head_norm_back(act_result[...], residual, scale_in, attn_norm[...])
    in_grad[...] += input_back
    pack_gain(0, attn_gain[None, :])

    def share(stage, axis, size, own):
        copies = [
            send(
                held.at[stage],
                landed.at[stage, own],
                gain_sems,
                (stage, step),
                axis,
                lax.rem(own + step, size),
            )
            for step in range(1, size)
        ]
        landed[stage, own] = held[stage]
        return copies

    def gather_up(stage, copies, size):
        for copy in copies:
            copy.wait_recv()
        total = landed[stage, 0]
        for place in range(1, size):
            total = total + landed[stage, place]
        held[stage + 1] = total

    shares = share(0, "row", rows, row)
    downs.last()
    block_out[...] = (middle_own[...] + down_result[...]).astype(jnp.bfloat16)
    gather_up(0, shares, rows)
    more = share(1, "col", cols, col)
    out_sum[half] = out.total(col)
    for step in range(1, cols):
        lined[step - 1].wait_recv()
        out_sum[half] += out_lined[step].astype(jnp.float32)
    out_copy = send(out_sum.at[half], out_sum.at[half], pair_sems, (5,), "dp", sibling())
    heads.relay()
    down_copy.wait_recv()
    down_sum[...] = down_grad[...] + down_came[...]
    gather_up(1, more, cols)
    gain_copy = send(held.at[2], landed.at[2, 0], gain_sems, (2, 0), "dp", sibling())
    for moved in wides + [heads]:
        moved.land()
    gain_copy.wait_recv()
    gain_sum[...] = held[2] + landed[2, 0]
    out_copy.wait_recv()
    for copy in cats + lows + lined + shares + more + [down_copy, out_copy, gain_copy]:
        copy.wait_send()
    for paired in (out, head):
        paired.copy.wait_send()
    mid.sent(waves=False)
    for item in [downs, acts, heads] + wides:
        item.sent()


def back_pass(local, width, hidden, head_dim):
    rows, cols = lax.axis_size("row"), lax.axis_size("col")
    length, height = rows * cols * local, width // cols // 2
    low, full = jnp.bfloat16, jnp.float32
    shape = jax.ShapeDtypeStruct
    slot, some = 3 * head_dim, head_dim // 2
    outs = [
        shape((local, width), low),
        shape((local, width), full),
        shape((2, cols, 2, height // 2, 2 * hidden), low),
        shape((cols, 2, slot // 2, width // cols), low),
        shape((2, some, width), full),
        shape((hidden, width), full),
        shape((8, 3 * width // 8), full),
    ]

    def vmem(kind, *dims):
        return pltpu.VMEM(dims, kind)

    scratch = [
        vmem(low, rows, cols, local, width),
        vmem(low, cols, rows // 2 * local, 2 * head_dim),
        vmem(low, cols, rows // 2 * local, 2 * head_dim),
        vmem(low, length, slot),
        vmem(low, cols, rows // 2 * local, 2 * slot),
        vmem(low, cols, rows // 2 * local, 2 * slot),
        vmem(full, cols, 2, slot // 2, width // cols),
        vmem(full, cols, slot // 2, width // cols),
        vmem(low, cols, slot // 2, width // cols),
    ]
    scratch += [
        vmem(full, cols, 2, some, width),
        vmem(full, cols, some, width),
        vmem(low, cols, some, width),
        vmem(low, cols, some, width),
        vmem(full, hidden, width),
        vmem(full, hidden, width),
        vmem(low, rows, 1, local, width),
        vmem(low, rows * local, 2 * cols * head_dim),
        vmem(low, rows * local, cols * head_dim),
        vmem(full, length, head_dim),
        vmem(full, length, head_dim),
        vmem(full, length, head_dim),
        vmem(full, local, width),
        vmem(full, local, width),
        vmem(full, 3, 8, 3 * width // 8),
        vmem(full, 3, max(rows, cols), 8, 3 * width // 8),
    ]
    scratch += reduce_scratch(rows, 1, local, width) + reduce_scratch(rows, cols, local, width)[1:]
    scratch += dma(1, 6, cols) + dma(2, 5, cols) + dma(3, 2, cols) + dma(6)
    scratch += dma(cols) + dma(cols) + dma(cols) + dma(3, max(rows, cols))
    return outs, scratch


def whole_pass(given, down, ffn_norm, head_dim):
    args, front_outs, front_scratch = front(*given)
    (local, width), hidden = args[0].shape, down.shape[0]
    hidden_outs, hidden_scratch = hidden_pass(local, width, hidden, *args[3:6])
    outs, back_scratch = back_pass(local, width, hidden, head_dim)
    front_count = len(args)
    args = args + [down, ffn_norm.reshape(1, width)]

    def body(*refs):
        refs = list(refs)

        def take(count):
            taken = refs[:count]
            del refs[:count]
            return taken

        ins, results = take(len(args)), take(len(outs))
        came, made = take(len(front_outs)), take(len(hidden_outs))
        front_own, hidden_own = take(len(front_scratch)), take(len(hidden_scratch))
        own_in, own_grad, _, query, key, value = ins[:6]
        attn_norm, query_norm, key_norm = ins[8:11]
        down_weight, ffn_gain = ins[front_count:]
        in_all, grad_all, out_all, cat_all, wide_all, _, first = came[:7]
        act_own, middle_own, down_part, slot_all, _, hidden_all, wide_low = made
        greet()
        front_kernel(*ins[:front_count], *came, *front_own)
        hidden_kernel(
            *[in_all, grad_all, out_all, cat_all, wide_all, down_weight, ffn_gain],
            *[query, key, value],
            *made,
            *hidden_own,
        )
        back_kernel(
            *[own_in, own_grad, act_own, middle_own, attn_norm, ffn_gain],
            *[out_all, cat_all, grad_all, first, hidden_all, wide_low, down_part, slot_all],
            *came[8:13],
            *[came[7], query_norm, key_norm],
            *came[13:],
            *results,
            *refs,
        )

    scratch = [pltpu.VMEM(out.shape, out.dtype) for out in front_outs + hidden_outs]
    scratch += front_scratch + hidden_scratch + back_scratch
    return call_kernel(body, args, outs, scratch, 0)


def open_kernel(cols, head_dim, *refs):
    wide_got, head_got, block_given, in_given, out_given, down_given, gain_given = refs[:7]
    gate, up, query, key, value, block_out, in_grad, out, down = refs[7:16]
    attn_gain, ffn_gain, query_gain, key_gain = refs[16:]
    pairs = ((block_out, block_given), (in_grad, in_given), (out, out_given), (down, down_given))
    for target, source in pairs:
        target[...] = source[...]
    lanes = gain_given.shape[1] // 3
    for line in range(gain_given.shape[0]):
        for place, target in ((0, attn_gain), (1, ffn_gain)):
            target[:, line * lanes : (line + 1) * lanes] = gain_given[
                line : line + 1, place * lanes : (place + 1) * lanes
            ]
    query_gain[...] = gain_given[0:1, 2 * lanes : 2 * lanes + head_dim]
    key_gain[...] = gain_given[1:2, 2 * lanes : 2 * lanes + head_dim]
    height, part = wide_got.shape[3], wide_got.shape[4] // 2
    for col in range(cols):
        for piece in range(2):
            for side in range(2):
                begin = (2 * piece + side) * height
                lines = slice(begin, begin + height)
                lanes = slice(col * part, (col + 1) * part)
                gate[lines, lanes] = wide_got[side, col, piece, :, :part].astype(jnp.float32)
                up[lines, lanes] = wide_got[side, col, piece, :, part:].astype(jnp.float32)
    turned = []
    for col in range(cols):
        stacked = head_got[col].reshape(3 * head_dim, head_got.shape[3]).astype(jnp.float32)
        turned.append(
            [stacked[kind * head_dim : (kind + 1) * head_dim].T for kind in range(3)]
        )
        query[:, col * head_dim : (col + 1) * head_dim] = turned[col][0]
    for pair in range(cols // 2):
        for place, target in ((1, key), (2, value)):
            target[:, pair * head_dim : (pair + 1) * head_dim] = (
                turned[2 * pair][place] + turned[2 * pair + 1][place]
            )


def call_kernel(body, args, outs, scratch, number):
    vmem = pl.BlockSpec(memory_space=pltpu.VMEM)
    return pl.pallas_call(
        body,
        out_shape=outs,
        in_specs=[vmem] * len(args),
        out_specs=[vmem] * len(outs),
        scratch_shapes=scratch,
        compiler_params=pltpu.CompilerParams(
            collective_id=number, has_side_effects=True, vmem_limit_bytes=VMEM_LIMIT
        ),
    )(*args)


def dma(*shape):
    return [pltpu.SemaphoreType.DMA(shape), pltpu.SemaphoreType.DMA(shape)]


def dot(left, right, left_dim=1, right_dim=0):
    return lax.dot_general(
        left,
        right,
        (((left_dim,), (right_dim,)), ((), ())),
        preferred_element_type=jnp.float32,
    )


def shards(
    block_input,
    seq_lengths,
    out_grad,
    attn_norm,
    query_weight,
    key_weight,
    value_weight,
    query_norm,
    key_norm,
    out_weight,
    ffn_norm,
    gate_weight,
    up_weight,
    down_weight,
):
    width = block_input.shape[1]
    head_dim = query_norm.shape[0]
    cols = lax.axis_size("col")
    given = [block_input, out_grad, out_weight, query_weight, key_weight, value_weight]
    given += [gate_weight, up_weight, (attn_norm, query_norm, key_norm), seq_lengths]
    outs = whole_pass(given, down_weight, ffn_norm, head_dim)
    block_output, input_grad, wide_got, head_got, out_sum, grad_down, gain_sums = outs
    shape = jax.ShapeDtypeStruct
    weights = (gate_weight, up_weight, query_weight, key_weight, value_weight)
    given = (block_output, input_grad, out_sum.reshape(out_weight.shape), grad_down)
    gains = (width, width, head_dim, head_dim)
    results = local_kernel(
        functools.partial(open_kernel, cols, head_dim),
        [wide_got, head_got] + list(given) + [gain_sums],
        [shape(weight.shape, jnp.float32) for weight in weights]
        + [shape(value.shape, value.dtype) for value in given]
        + [shape((1, size), jnp.float32) for size in gains],
    )
    block_output, input_grad = results[5:7]
    sums = tuple(results[:5]) + tuple(results[7:])
    if lax.axis_size("dp") > 2:
        sums = lax.psum(tuple(0.5 * value for value in sums), "dp")
    grad_gate, grad_up, grad_query, grad_key, grad_value = sums[:5]
    grad_outweight, grad_down, grad_attnnorm, grad_ffnnorm, grad_qnorm, grad_knorm = sums[5:]
    return (
        block_output,
        input_grad,
        grad_attnnorm[0],
        grad_query,
        grad_key,
        grad_value,
        grad_qnorm[0],
        grad_knorm[0],
        grad_outweight,
        grad_ffnnorm[0],
        grad_gate,
        grad_up,
        grad_down,
    )


def solution(mesh):
    placed = (
        P(("dp", "row", "col"), None),
        P("dp", None),
        P(("dp", "row", "col"), None),
        P(),
        P("col", "row"),
        P("col", "row"),
        P("col", "row"),
        P(),
        P(),
        P(("row", "col"), None),
        P(),
        P("col", "row"),
        P("col", "row"),
        P(("row", "col"), None),
    )
    return jax.shard_map(
        shards,
        mesh=mesh,
        in_specs=placed,
        out_specs=(
            P(("dp", "row", "col"), None),
            P(("dp", "row", "col"), None),
            P(),
            P("col", "row"),
            P("col", "row"),
            P("col", "row"),
            P(),
            P(),
            P(("row", "col"), None),
            P(),
            P("col", "row"),
            P("col", "row"),
            P(("row", "col"), None),
        ),
        check_vma=False,
    )
```

```python
import functools
import math

import jax
import jax.numpy as jnp
from jax import lax
from jax.experimental import pallas as pl
from jax.experimental.pallas import tpu as pltpu
from jax.sharding import PartitionSpec as P

EPSILON = 1e-05
THETA = 1000000.0


def rope_frequency(width):
    half_width = width // 2
    exponent = jnp.arange(half_width, dtype=jnp.float32) * (2.0 / width)
    frequency = jnp.exp(-math.log(THETA) * exponent)
    return jnp.concatenate([frequency, frequency])[None, :]


def head_norm(values, gain_vec):
    inv_rms = lax.rsqrt(jnp.mean(values * values, axis=-1, keepdims=True) + EPSILON)
    return (values * inv_rms * gain_vec, inv_rms)


def head_norm_back(cotangent, values, inv_rms, gain_vec):
    normed = values * inv_rms
    weighted = cotangent * gain_vec
    gain_grad = jnp.sum(cotangent * normed, axis=0)
    inner_mean = jnp.mean(weighted * normed, axis=-1, keepdims=True)
    return (inv_rms * (weighted - normed * inner_mean), gain_grad)


def swap_halves(values):
    half_width = values.shape[-1] // 2
    return jnp.concatenate([values[:, half_width:], values[:, :half_width]], axis=1)


def block_probability(query_block, key_rows, begins, offset, low, shift):
    score_scale = 1.0 / math.sqrt(query_block.shape[1])
    scores = dot(query_block, key_rows, 1, 1) * score_scale
    places = low + lax.broadcasted_iota(jnp.int32, scores.shape, 1)
    row_places = offset + lax.broadcasted_iota(jnp.int32, scores.shape, 0)
    allowed = (places >= begins) & (places <= row_places)
    if shift is None:
        shift = jnp.log(jnp.sum(jnp.where(allowed, jnp.exp(scores), 0.0), axis=1, keepdims=True))
    probability = jnp.where(allowed, jnp.exp(scores - shift), 0.0).astype(jnp.bfloat16)
    return probability, shift


def spans(length, longest, block):
    return [
        (offset, max(0, (offset - longest) // 128 * 128), block)
        for offset in range(0, length, block)
    ]


def local_kernel(body, args, outs, scratch=()):
    vmem = pl.BlockSpec(memory_space=pltpu.VMEM)
    return pl.pallas_call(
        body,
        out_shape=outs,
        in_specs=[vmem] * len(args),
        out_specs=[vmem] * len(outs),
        scratch_shapes=list(scratch),
    )(*args)


MESH = pl.DeviceIdType.MESH
VMEM_LIMIT = 62 * 1024 * 1024


def remote(source, target, sems, place, axis, index):
    return pltpu.make_async_remote_copy(
        src_ref=source,
        dst_ref=target,
        send_sem=sems[0].at[place],
        recv_sem=sems[1].at[place],
        device_id={axis: index},
        device_id_type=MESH,
    )


def send(source, target, sems, place, axis, index):
    copy = remote(source, target, sems, place, axis, index)
    copy.start()
    return copy


def neighbours():
    rows, row = lax.axis_size("row"), lax.axis_index("row")
    near = row + 1 - 2 * lax.rem(row, 2)
    far = lax.rem(row + rows // 2, rows)
    return near, far


def sibling():
    own = lax.axis_index("dp")
    return own + 1 - 2 * lax.rem(own, 2)


def greet():
    cols, col = lax.axis_size("col"), lax.axis_index("col")
    near, far = neighbours()
    peers = [("col", lax.rem(col + step, cols)) for step in range(1, cols)]
    peers += [("row", near), ("row", far), ("dp", sibling())]
    peers.append(("row", lax.rem(near + lax.axis_size("row") // 2, lax.axis_size("row"))))
    barrier = pltpu.get_barrier_semaphore()
    for axis, index in peers:
        pl.semaphore_signal(barrier, inc=1, device_id={axis: index}, device_id_type=MESH)
    pl.semaphore_wait(barrier, len(peers))


class Gather:
    def __init__(self, block, part, sems, item):
        self.block, self.part = block, part
        self.sems, self.item = sems, item
        self.cols, self.col = lax.axis_size("col"), lax.axis_index("col")
        self.row = lax.axis_index("row")
        self.near, self.far = neighbours()

    def hop(self, origin, right):
        piece = self.block(self.row, origin)
        place = (self.item, 0 if right else 1, origin)
        return remote(piece, piece, self.sems, place, "col", self.col + (1 if right else -1))

    def cross(self, origin, kind):
        piece = self.block(self.row, origin)
        peer = (self.near, self.far)[kind]
        return remote(piece, piece, self.sems, (self.item, 2 + kind, origin), "row", peer)

    def corner(self, origin, kind):
        source, peer = ((self.near, self.far), (self.far, self.near))[kind]
        piece = self.part(source, origin, kind)
        return remote(piece, piece, self.sems, (self.item, 4 + kind, origin), "row", peer)

    def forward(self, origin, right):
        @pl.when(self.col < self.cols - 1 if right else self.col > 0)
        def _():
            self.hop(origin, right).start()

    def each(self, wave, act):
        if wave == 0:
            act(self.col, None)
            return
        for right in (True, False):
            origin = self.col - wave if right else self.col + wave

            @pl.when(self.col >= wave if right else self.col + wave < self.cols)
            def _():
                act(origin, right)

    def start(self):
        for right in (True, False):
            self.forward(self.col, right)
        for kind in range(2):
            self.cross(self.col, kind).start()

    def wave(self, wave):
        def act(origin, right):
            self.hop(origin, right).wait_recv()
            self.forward(origin, right)
            for kind in range(2):
                self.cross(origin, kind).start()

        self.each(wave, act)

    def relay(self, wave):
        def act(origin, right):
            for kind in range(2):
                self.cross(origin, kind).wait_recv()
                self.corner(origin, kind).start()

        self.each(wave, act)

    def land(self, wave):
        def act(origin, right):
            for kind in range(2):
                self.corner(origin, kind).wait_recv()

        self.each(wave, act)

    def sent(self, waves=True):
        def act(origin, right):
            for side in (True, False) if right is None else (right,):

                @pl.when(self.col < self.cols - 1 if side else self.col > 0)
                def _():
                    if waves:
                        self.hop(origin, side).wait_send()

            for kind in range(2):
                self.cross(origin, kind).wait_send()
                self.corner(origin, kind).wait_send()

        for wave in range(self.cols if waves else 1):
            self.each(wave, act)


class Swap:
    def __init__(self, source, target, sems, item, whole=False):
        self.source, self.target, self.sems, self.item = source, target, sems, item
        self.cols, self.col = lax.axis_size("col"), lax.axis_index("col")
        self.half = lax.rem(lax.axis_index("dp"), 2)
        self.lines, self.pairs, self.first = {}, {}, 0 if whole else 1

    def line(self):
        for step in range(1, self.cols):
            peer = lax.rem(self.col + step, self.cols)
            self.lines[step] = send(
                self.source(peer, self.half),
                self.target.at[self.col, self.half],
                self.sems,
                (self.item, 0, step),
                "col",
                peer,
            )

    def relay(self):
        for step in range(self.first, self.cols):
            if step:
                self.lines[step].wait_recv()
            piece = self.target.at[lax.rem(self.col + self.cols - step, self.cols), self.half]
            self.pairs[step] = send(
                piece, piece, self.sems, (self.item, 1, step), "dp", sibling()
            )

    def land(self):
        for copy in self.pairs.values():
            copy.wait_recv()

    def sent(self):
        for copies in (self.lines, self.pairs):
            for copy in copies.values():
                copy.wait_send()


def front_kernel(*refs):
    (own_in, own_grad, own_out, query, key, value, gate, up) = refs[:8]
    (attn_norm, query_norm, key_norm, seq_lengths, frequency) = refs[8:13]
    (in_all, grad_all, out_all, cat_all, wide_all, slot_all) = refs[13:19]
    (first, sums, query_rot, key_rot, value_low, low_rows, totals) = refs[19:26]
    (cosine, sine, begins) = refs[26:29]
    (slot_part, wide_part) = refs[29:31]
    gather_sems, swap_sems, pair_sems = refs[31:33], refs[33:35], refs[35:37]
    rows, cols = lax.axis_size("row"), lax.axis_size("col")
    row, col = lax.axis_index("row"), lax.axis_index("col")
    half = lax.rem(lax.axis_index("dp"), 2)
    near, far = neighbours()
    corner = lax.rem(near + rows // 2, rows)
    length, head_dim = query_rot.shape
    width = own_in.shape[1]
    local = own_in.shape[0]
    block = length // rows

    def split(ref):
        count = ref.shape[2] // 2
        return (
            lambda r, c: ref.at[r, c],
            lambda r, c, k: ref.at[r, c, pl.ds(k * count, count)],
        )

    in_all[row, col] = own_in[...]
    inputs = Gather(*split(in_all), gather_sems, 0)
    inputs.start()
    height = query.shape[0] // 2
    for place in range(cols):
        for piece in range(2):
            lines = slice(piece * height, (piece + 1) * height)
            lanes = slice(place // 2 * head_dim, (place // 2 + 1) * head_dim)
            slot_part[place, piece, :, :head_dim] = query[
                lines, place * head_dim : (place + 1) * head_dim
            ]
            slot_part[place, piece, :, head_dim : 2 * head_dim] = key[lines, lanes]
            slot_part[place, piece, :, 2 * head_dim :] = value[lines, lanes]
    slots = Swap(lambda c, h: slot_part.at[c, h], slot_all, swap_sems, 0)
    slots.line()
    slot_all[col] = slot_part[col]
    grad_all[row, col] = own_grad[...]
    out_all[row, col] = own_out[...]
    places = lax.broadcasted_iota(jnp.int32, (length, 1), 0)
    end, begin = jnp.zeros((1, 1), jnp.int32), jnp.zeros((length, 1), jnp.int32)
    for number in range(seq_lengths.shape[1]):
        size = seq_lengths[:, number : number + 1]
        end = end + size
        begin = begin + jnp.where(places >= end, size, 0)
    begins[...] = begin
    angles = (places - begin).astype(jnp.float32) * frequency[...]
    inputs.wave(1)
    inputs.relay(0)
    cosine[...] = jnp.cos(angles)
    inputs.wave(2)
    inputs.relay(1)
    side = lax.broadcasted_iota(jnp.int32, angles.shape, 1)
    turned = jnp.sin(angles)
    sine[...] = jnp.where(side < head_dim // 2, -turned, turned)
    for step in range(3, cols):
        inputs.wave(step)
    count = own_out.shape[1] // 2
    outs = Gather(
        lambda r, c: out_all.at[r, c, half],
        lambda r, c, k: out_all.at[r, c, half, pl.ds(k * count, count)],
        gather_sems,
        2,
    )
    outs.start()
    grads = Gather(*split(grad_all), gather_sems, 1)
    inputs.relay(2)
    for step in range(3, cols):
        inputs.relay(step)
    grads.start()
    slots.relay()
    for step in range(1, cols):
        outs.wave(step)
    slots.land()

    def project(place):
        for c in range(cols):
            values = in_all[place, c].astype(jnp.float32)
            normed = head_norm(values, attn_norm[...])[0]
            first[place, c] = normed.astype(jnp.bfloat16)
        lines = pl.ds(pl.multiple_of(place * block, block), block)
        sums[lines, :] = dot(
            first[place].reshape(block, width), slot_all[...].reshape(width, 3 * head_dim)
        )

    project(row)
    project(near)
    project(far)
    for step in range(cols):
        inputs.land(step)
    project(corner)
    for place, target, gain in ((0, query_rot, query_norm), (1, key_rot, key_norm)):
        normed = head_norm(sums[:, place * head_dim : (place + 1) * head_dim], gain[...])[0]
        target[...] = (normed * cosine[...] + swap_halves(normed) * sine[...]).astype(jnp.bfloat16)
    value_low[...] = sums[:, 2 * head_dim : 3 * head_dim].astype(jnp.bfloat16)
    hidden = gate.shape[1] // cols

    def pack(place):
        for kind, source in ((0, gate), (1, up)):
            for piece in range(2):
                wide_part[place, piece, :, kind * hidden : (kind + 1) * hidden] = source[
                    piece * height : (piece + 1) * height, place * hidden : (place + 1) * hidden
                ]

    def cat(part):
        places = pl.ds(part * (rows // 2), rows // 2)
        return Gather(
            lambda r, c: cat_all.at[places, r, c],
            lambda r, c, k: cat_all.at[places, r, c, pl.ds(k * head_dim // 2, head_dim // 2)],
            gather_sems,
            3 + part,
        )

    cats = [cat(part) for part in range(2)]
    wide = Swap(lambda c, h: wide_part.at[c, h], wide_all, swap_sems, 1)
    for offset, low, _ in spans(length, length // 2, block):
        number = offset // block
        lines, keys = slice(offset, offset + block), slice(low, offset + block)
        probability, total = block_probability(
            query_rot[lines, :], key_rot[keys, :], begins[lines, :], offset, low, None
        )
        totals[lines, :] = total
        low_rows[lines, :] = dot(probability, value_low[keys, :]).astype(jnp.bfloat16)
        cat_all[number, row, col] = dot(value_low[keys, :], probability, 0, 1).astype(jnp.bfloat16)
        if number == 0:
            grads.wave(1)
            outs.relay(0)
        if number == rows // 2 - 1:
            cats[0].start()
            for step in range(1, cols):
                outs.relay(step)
        if number == rows // 2:
            grads.relay(0)
            cats[0].wave(1)
    cats[1].start()
    for place in range(cols):
        pack(place)
    wide.line()
    wide_all[col] = wide_part[col]
    for step in range(2, cols):
        cats[0].wave(step)
    for step in range(2):
        cats[0].relay(step)
    for step in range(1, cols):
        cats[1].wave(step)
    for step in range(2, cols):
        cats[0].relay(step)
    pairs = []
    for step in range(cols):
        outs.land(step)
    for number, place in enumerate((near, far, corner)):
        piece = out_all.at[place, :, half]
        pairs.append(send(piece, piece, pair_sems, (number,), "dp", sibling()))
    for step in range(1, cols):
        piece = out_all.at[row, lax.rem(col + cols - step, cols), half]
        pairs.append(send(piece, piece, pair_sems, (2 + step,), "dp", sibling()))
    for step in range(cols):
        cats[1].relay(step)
    grads.relay(1)
    wide.relay()
    for step in range(2, cols):
        grads.wave(step)
    wide.land()
    for gather in cats:
        for step in range(cols):
            gather.land(step)
    for copy in pairs:
        copy.wait()

    def spread():
        for step in range(2, cols):
            grads.relay(step)

    def finish():
        for step in range(cols):
            grads.land(step)

    def sent():
        for item in [inputs, grads, outs, slots, wide] + cats:
            item.sent()

    return spread, finish, sent


def front(own_in, own_grad, own_out, query, key, value, gate, up, norms, seq_lengths):
    rows, cols = lax.axis_size("row"), lax.axis_size("col")
    local, width = own_in.shape
    attn_norm, query_norm, key_norm = norms
    length, head_dim = local * rows * cols, query_norm.shape[0]
    hidden, height = gate.shape[1] // cols, gate.shape[0] // 2
    low = jnp.bfloat16
    blocks = jax.ShapeDtypeStruct((rows, cols, local, width), low)
    halves = own_out.shape[0] // 2
    wide = (cols, 2, height, 2 * hidden)
    slot = (cols, 2, height, 3 * head_dim)
    shape = jax.ShapeDtypeStruct
    head_rows = shape((length, head_dim), low)
    table = shape((length, head_dim), jnp.float32)
    outs = [
        blocks,
        blocks,
        shape((rows, cols, 2, halves, width), low),
        shape((rows, rows, cols, head_dim, length // rows), low),
        shape(wide, low),
        shape(slot, low),
        blocks,
        shape((length, 3 * head_dim), jnp.float32),
        head_rows,
        head_rows,
        head_rows,
        head_rows,
        shape((length, 1), jnp.float32),
        table,
        table,
        shape((length, 1), jnp.int32),
    ]
    scratch = [pltpu.VMEM(slot, low), pltpu.VMEM(wide, low)]
    scratch += dma(5, 6, cols) + dma(2, 2, cols) + dma(2 + cols)
    args = [own_in, own_grad, own_out.reshape(2, halves, width), query, key, value, gate, up]
    args += [attn_norm.reshape(1, width), query_norm.reshape(1, head_dim)]
    args += [key_norm.reshape(1, head_dim), seq_lengths, rope_frequency(head_dim)]
    return args, outs, scratch


class Reduce:
    def __init__(self, part, relayed, planed, staged, lined, result, sems, item):
        self.part, self.relayed, self.planed = part, relayed, planed
        self.staged, self.lined, self.result = staged, lined, result
        self.sems, self.item = sems, item
        self.cols = part.shape[1]
        self.col = lax.axis_index("col") if self.cols > 1 else 0
        self.row = lax.axis_index("row")
        self.near, self.far = neighbours()
        self.cross = lax.rem(self.near + lax.axis_size("row") // 2, lax.axis_size("row"))
        self.count = part.shape[2] // 2
        self.relays, self.planes, self.lines = [], [], []

    def first(self):
        for kind, peer in ((0, self.near), (1, self.far)):
            self.relays.append(
                send(
                    self.part.at[self.cross, :, pl.ds(kind * self.count, self.count)],
                    self.relayed.at[kind],
                    self.sems,
                    (self.item, 1 + kind, 0),
                    "row",
                    peer,
                )
            )

    def merge(self, kind):
        peer, came = (self.near, self.far)[kind], 1 - kind
        self.relays[came].wait_recv()
        lines = slice(came * self.count, (came + 1) * self.count)
        self.part[peer, :, lines] = (
            self.part[peer, :, lines].astype(jnp.float32)
            + self.relayed[came].astype(jnp.float32)
        ).astype(jnp.bfloat16)

    def ship(self, kind):
        peer = (self.near, self.far)[kind]
        self.planes.append(
            send(
                self.part.at[peer],
                self.planed.at[kind],
                self.sems,
                (self.item, 3 + kind, 0),
                "row",
                peer,
            )
        )

    def toward(self, kind):
        self.merge(kind)
        self.ship(kind)

    def total(self, place):
        summed = self.part[self.row, place].astype(jnp.float32)
        for kind in range(2):
            summed = summed + self.planed[kind, place].astype(jnp.float32)
        return summed

    def own(self):
        for copy in self.planes:
            copy.wait_recv()
        for step in range(1, self.cols):
            place = lax.rem(self.col + step, self.cols)
            self.staged[step] = self.total(place).astype(jnp.bfloat16)
            self.lines.append(
                send(
                    self.staged.at[step],
                    self.lined.at[step],
                    self.sems,
                    (self.item, 0, step),
                    "col",
                    place,
                )
            )
        self.result[...] = self.total(self.col)

    def last(self):
        for step in range(1, self.cols):
            self.lines[step - 1].wait_recv()
            self.result[...] += self.lined[step].astype(jnp.float32)

    def sent(self):
        for copy in self.relays + self.planes + self.lines:
            copy.wait_send()


def reduce_scratch(rows, cols, local, width):
    low = jnp.bfloat16
    return [
        pltpu.VMEM((2, cols, local // 2, width), low),
        pltpu.VMEM((2, cols, local, width), low),
        pltpu.VMEM((cols, local, width), low),
        pltpu.VMEM((cols, local, width), low),
    ]


def hidden_kernel(spread, finish, *refs):
    in_all, grad_all, out_all, cat_all, wide_all, down, ffn_norm = refs[:7]
    query, key, value = refs[7:10]
    act_own, middle_own, down_part, slot_all = refs[10:14]
    second_all, hidden_all, wide_low = refs[14:17]
    act_parts, act_halves, middle_block, slot_part = refs[17:21]
    low_all, wide_sum, wide_came, down_relayed, kept = refs[21:26]
    act_scratch, rest = (refs[26:30], refs[30:34]), refs[34:]
    sems, swap_sems, pair_sems = rest[:2], rest[2:4], rest[4:6]
    rows, cols = lax.axis_size("row"), lax.axis_size("col")
    row, col = lax.axis_index("row"), lax.axis_index("col")
    near, far = neighbours()
    cross = lax.rem(near + rows // 2, rows)
    local, width = in_all.shape[2:]
    block, hidden = cols * local, down.shape[0]
    height, begin = query.shape[0] // 2, 0
    for source in (query, key, value):
        lanes = slice(begin, begin + source.shape[1])
        for piece in range(2):
            slot_part[piece, :, lanes] = source[piece * height : (piece + 1) * height, :]
        begin += source.shape[1]
    slots = Swap(lambda c, h: slot_part.at[h], slot_all, swap_sems, 0)
    slots.line()
    slot_all[col] = slot_part[...]
    acts = [
        Reduce(act_parts.at[side], *act_scratch[side], act_halves.at[side], sems, side)
        for side in range(2)
    ]

    downs = Reduce(down_part, down_relayed, None, None, None, None, sems, 2)

    def forward(place):
        mixed = dot(cat_all[place].reshape(width, block), out_all[...].reshape(width, width), 0, 0)
        middle = in_all[place].reshape(block, width).astype(jnp.float32) + mixed
        middle_block[...] = middle
        second = head_norm(middle, ffn_norm[...])[0].astype(jnp.bfloat16)
        second_all[place] = second
        kept[place] = dot(second, wide_all[...].reshape(width, 2 * hidden))

    def work(place):
        gating, upward = kept[place, :, :hidden], kept[place, :, hidden:]
        hidden_grad = dot(grad_all[place].reshape(block, width), down[...], 1, 1)
        sigmoid_gate = jax.nn.sigmoid(gating)
        activated = gating * sigmoid_gate
        hidden_low = (activated * upward).astype(jnp.bfloat16)
        gate_low = (
            hidden_grad * upward * sigmoid_gate * (1.0 + gating * (1.0 - sigmoid_gate))
        ).astype(jnp.bfloat16)
        up_low = (hidden_grad * activated).astype(jnp.bfloat16)
        hidden_all[place] = hidden_low
        low_all[place, :, :hidden] = gate_low
        low_all[place, :, hidden:] = up_low
        wide_weight = wide_all[...].reshape(width, 2 * hidden)
        act = dot(low_all[place], wide_weight, 1, 1).astype(jnp.bfloat16)
        for side in range(2):
            act_parts[side, place] = act[
                :, side * (width // 2) : (side + 1) * (width // 2)
            ].reshape(cols, local, width // 2)

    def work_down(place):
        down_part[place] = (
            dot(hidden_all[place], down[...]).astype(jnp.bfloat16).reshape(cols, local, width)
        )

    forward(cross)
    spread()
    for place in (near, far, row):
        forward(place)
    lines = pl.ds(pl.multiple_of(col * local, local), local)
    middle_own[...] = middle_block[lines, :]
    finish()
    work(cross)
    for item in acts:
        item.first()
    work_down(cross)
    work(near)
    for item in acts:
        item.toward(0)
    slots.relay()
    work(far)
    for item in acts:
        item.toward(1)
    downs.first()
    work(row)
    acts[0].own()
    for place in (near, far, row):
        work_down(place)
    acts[1].own()
    wide = Paired(wide_sum, wide_came, pair_sems, 0)
    wide_sum[...] = dot(
        second_all[...].reshape(rows * block, width),
        low_all[...].reshape(rows * block, 2 * hidden),
        0,
        0,
    ).reshape(wide_sum.shape)
    wide.pair()
    acts[0].last()
    slots.land()
    wide.copy.wait_recv()
    for place in range(cols):
        total = wide.total(place).astype(jnp.bfloat16)
        for side in range(2):
            wide_low[side, place] = total[side * (height // 2) : (side + 1) * (height // 2), :]
    for kind in range(2):
        downs.merge(kind)
    acts[1].last()
    for side in range(2):
        act_own[:, side * (width // 2) : (side + 1) * (width // 2)] = act_halves[side]
    for item in acts + [downs]:
        item.sent()
    slots.sent()
    wide.copy.wait_send()


def hidden_pass(local, width, hidden, query, key, value):
    rows, cols = lax.axis_size("row"), lax.axis_size("col")
    block, height = cols * local, query.shape[0] // 2
    shape = jax.ShapeDtypeStruct
    own, low, full = shape((local, width), jnp.float32), jnp.bfloat16, jnp.float32
    slot = (2, height, query.shape[1] + key.shape[1] + value.shape[1])
    outs = [own, own, shape((rows, cols, local, width), low), shape((cols,) + slot, low)]
    outs += [shape((rows, block, width), low), shape((rows, block, hidden), low)]
    outs += [shape((2, cols, height // 2, 2 * hidden), low)]
    scratch = [
        pltpu.VMEM((2, rows, cols, local, width // 2), low),
        pltpu.VMEM((2, local, width // 2), full),
        pltpu.VMEM((block, width), full),
        pltpu.VMEM(slot, low),
        pltpu.VMEM((rows, block, 2 * hidden), low),
        pltpu.VMEM((cols, 2, height, 2 * hidden), full),
        pltpu.VMEM((cols, height, 2 * hidden), full),
        pltpu.VMEM((2, cols, local // 2, width), low),
        pltpu.VMEM((rows, block, 2 * hidden), full),
    ]
    scratch += reduce_scratch(rows, cols, local, width // 2) * 2
    scratch += dma(3, 5, cols) + dma(1, 2, cols) + dma(1)
    return outs, scratch


class Paired:
    def __init__(self, part, came, sems, item):
        self.part, self.came, self.sems, self.item = part, came, sems, item
        self.half = lax.rem(lax.axis_index("dp"), 2)

    def pair(self):
        self.copy = send(
            self.part.at[:, 1 - self.half], self.came, self.sems, (self.item,), "dp", sibling()
        )

    def total(self, place):
        return self.part[place, self.half] + self.came[place]


def back_kernel(*refs):
    own_in, own_grad, act_own, middle_own, attn_norm, ffn_norm = refs[:6]
    out_all, cat_all, grad_all, first = refs[6:10]
    hidden_all, wide_low, down_given, slot_all = refs[10:14]
    query_rot, key_rot, value_low, low_rows, totals = refs[14:19]
    sums, query_norm, key_norm, cosine, sine, begins = refs[19:25]
    outs, scratch = refs[25:32], refs[32:]
    block_out, in_grad, wide_got, head_got, out_sum, down_sum, gain_sum = outs
    mid_all, cat_part, grads_in, own_slot, slot_mine, slots_in = scratch[:6]
    head_sum, head_came, head_low = scratch[6:9]
    out_part, out_came, out_low, out_lined = scratch[9:13]
    down_grad, down_came, act_part = scratch[13:16]
    low_even, low_odd, query_acc, key_acc, value_acc = scratch[16:21]
    act_result, down_result, held, landed = scratch[21:25]
    act_scratch, down_scratch = scratch[25:29], (None,) + tuple(scratch[29:32])
    sems = scratch[32:]
    mid_sems, sum_sems, swap_sems, pair_sems = sems[:2], sems[2:4], sems[4:6], sems[6:8]
    cat_sems, low_sems, out_sems, gain_sems = sems[8:10], sems[10:12], sems[12:14], sems[14:16]
    rows, cols = lax.axis_size("row"), lax.axis_size("col")
    row, col = lax.axis_index("row"), lax.axis_index("col")
    half = lax.rem(lax.axis_index("dp"), 2)
    local, width = own_in.shape
    length, head_dim = query_rot.shape
    block = cols * local
    near, far = neighbours()
    wides = [
        Swap(
            lambda c, h, side=side: wide_low.at[side, c],
            wide_got.at[side],
            swap_sems,
            side,
            whole=True,
        )
        for side in range(2)
    ]
    wides[0].line()
    lanes = held.shape[2] // 3
    held[0] = jnp.zeros(held.shape[1:], jnp.float32)

    def pack_gain(place, gain):
        for line in range(gain.shape[1] // lanes):
            held[0, line : line + 1, place * lanes : (place + 1) * lanes] = gain[
                :, line * lanes : (line + 1) * lanes
            ]

    middle = middle_own[...]
    scale_mid = head_norm(middle, ffn_norm[...])[1]
    middle_back, ffn_gain = head_norm_back(act_own[...], middle, scale_mid, ffn_norm[...])
    middle_grad = own_grad[...].astype(jnp.float32) + middle_back
    in_grad[...] = middle_grad
    mid_all[row, col] = middle_grad.astype(jnp.bfloat16)
    mid = Gather(
        lambda r, c: mid_all.at[r, c],
        lambda r, c, k: mid_all.at[r, c, pl.ds(k * (local // 2), local // 2)],
        mid_sems,
        0,
    )
    for kind in range(2):
        mid.cross(col, kind).start()
    for step in range(1, cols):
        mid_all[:, lax.rem(col + step, cols)] = jnp.zeros((rows, local, width), jnp.bfloat16)
    pack_gain(1, ffn_gain[None, :])

    for side in range(2):
        wide_got[side, col, half] = wide_low[side, col]
    mid.relay(0)
    downs = Reduce(down_given, *down_scratch, down_result, sum_sems, 0)
    for kind in range(2):
        downs.ship(kind)
    down_grad[...] = dot(
        hidden_all[...].reshape(length, hidden_all.shape[-1]),
        grad_all[...].reshape(length, width),
        0,
        0,
    )
    down_copy = send(down_grad, down_came, pair_sems, (3,), "dp", sibling())
    mid.land(0)

    cat_grad = dot(
        mid_all[:, col].reshape(rows * local, width),
        out_all[row].reshape(cols * head_dim, width),
        1,
        1,
    ).astype(jnp.bfloat16)
    for place in range(cols):
        piece = cat_grad[:, place * head_dim : (place + 1) * head_dim]
        cat_part[place, :, :head_dim] = piece[: rows // 2 * local]
        cat_part[place, :, head_dim:] = piece[rows // 2 * local :]

    def turn(source, target, sems, place=None):
        return [
            send(
                source(lax.rem(col + step, cols)),
                place(step) if place else target,
                sems,
                (step,),
                "col",
                lax.rem(col + step, cols),
            )
            for step in range(1, cols)
        ]

    cats = turn(lambda c: cat_part.at[c], grads_in.at[col], cat_sems)
    grads_in[col] = cat_part[col]
    mixed = None
    for place in range(rows):
        term = dot(
            cat_all[place, row].reshape(cols * head_dim, block),
            mid_all[place].reshape(block, width),
        )
        mixed = term if mixed is None else mixed + term
    out = Paired(out_part, out_came, pair_sems, 2)
    out_part[...] = mixed.reshape(cols, 2, head_dim // 2, width)
    out.pair()
    for copy in cats:
        copy.wait_recv()
    wides[1].line()

    score_scale = 1.0 / math.sqrt(head_dim)
    key_acc[...] = jnp.zeros_like(key_acc)
    value_acc[...] = jnp.zeros_like(value_acc)
    for offset, low, _ in spans(length, length // 2, block):
        number = offset // block
        lines, keys = slice(offset, offset + block), slice(low, offset + block)
        probability, _ = block_probability(
            query_rot[lines, :], key_rot[keys, :], begins[lines, :], offset, low, totals[lines, :]
        )
        upper, right = number % (rows // 2) * local, number // (rows // 2) * head_dim
        grad_block = grads_in[:, upper : upper + local, right : right + head_dim].reshape(
            block, head_dim
        )
        value_acc[keys, :] += dot(probability, grad_block, 0, 0)
        row_delta = jnp.sum(
            grad_block.astype(jnp.float32) * low_rows[lines, :].astype(jnp.float32),
            axis=1,
            keepdims=True,
        )
        prob_grad = dot(grad_block, value_low[keys, :], 1, 1)
        score_grad = (
            score_scale * probability.astype(jnp.float32) * (prob_grad - row_delta)
        ).astype(jnp.bfloat16)
        query_acc[lines, :] = dot(score_grad, key_rot[keys, :])
        key_acc[keys, :] += dot(score_grad, query_rot[lines, :], 0, 0)
        if number == 0:
            out.copy.wait_recv()
            for place in range(cols):
                out_low[place] = out.total(place).astype(jnp.bfloat16)
            lined = turn(lambda c: out_low.at[c], None, out_sems, lambda step: out_lined.at[step])
    slot = 3 * head_dim

    def keep(place, value):
        own_slot[:, place * head_dim : (place + 1) * head_dim] = value
        pieces = value.reshape(rows, cols, local, head_dim)
        for number in range(rows):
            upper = number % (rows // 2) * local
            begin = number // (rows // 2) * slot + place * head_dim
            slot_mine[:, upper : upper + local, begin : begin + head_dim] = pieces[number]

    for place, source, gains in ((0, query_acc, query_norm), (1, key_acc, key_norm)):
        raw = sums[:, place * head_dim : (place + 1) * head_dim]
        gain = gains[...]
        inv_rms = head_norm(raw, gain)[1]
        cotangent = source[...] * cosine[...] - swap_halves(source[...]) * sine[...]
        low_part, gain_grad = head_norm_back(cotangent, raw, inv_rms, gain)
        keep(place, low_part.astype(jnp.bfloat16))
        held[0, place : place + 1, 2 * lanes : 2 * lanes + head_dim] = gain_grad[None, :]
    keep(2, value_acc[...].astype(jnp.bfloat16))
    lows = turn(lambda c: slot_mine.at[c], slots_in.at[col], low_sems)
    slots_in[col] = slot_mine[col]

    head = Paired(head_sum, head_came, pair_sems, 4)
    head_grad = dot(own_slot[...], first[...].reshape(length, width), 0, 0)
    for place in range(cols):
        head_sum[place] = head_grad[
            :, place * (width // cols) : (place + 1) * (width // cols)
        ].reshape(head_sum.shape[1:])
    head.pair()
    for copy in lows:
        copy.wait_recv()
    downs.own()
    for place in range(cols):
        columns = slice(place * head_dim, (place + 1) * head_dim)
        came = jnp.concatenate([slots_in[place, :, :slot], slots_in[place, :, slot:]], axis=0)
        low_even[:, columns] = came[:, :head_dim]
        target, offset = (low_odd, 0) if place % 2 else (low_even, cols * head_dim)
        for kind in (0, 1):
            begin = offset + (kind * (cols // 2) + place // 2) * head_dim
            target[:, begin : begin + head_dim] = came[
                :, (1 + kind) * head_dim : (2 + kind) * head_dim
            ]
    slot_weight = slot_all[...].reshape(width, slot_all.shape[-1])
    act = dot(low_even[...], slot_weight, 1, 1) + dot(
        low_odd[...], slot_weight[:, cols * head_dim :], 1, 1
    )
    act_part[...] = act.astype(jnp.bfloat16).reshape(act_part.shape)
    acts = Reduce(act_part, *act_scratch, act_result, sum_sems, 1)
    acts.first()
    head.copy.wait_recv()
    for place in range(cols):
        head_low[place] = head.total(place).astype(jnp.bfloat16)
    heads = Swap(lambda c, h: head_low.at[c], head_got, swap_sems, 2, whole=True)
    heads.line()
    head_got[col, half] = head_low[col]
    acts.toward(0)
    acts.toward(1)
    wides[0].relay()
    wides[1].relay()
    acts.own()

    residual = own_in[...].astype(jnp.float32)
    scale_in = head_norm(residual, attn_norm[...])[1]
    input_back, attn_gain = head_norm_back(act_result[...], residual, scale_in, attn_norm[...])
    in_grad[...] += input_back
    pack_gain(0, attn_gain[None, :])

    def share(stage, axis, size, own):
        copies = [
            send(
                held.at[stage],
                landed.at[stage, own],
                gain_sems,
                (stage, step),
                axis,
                lax.rem(own + step, size),
            )
            for step in range(1, size)
        ]
        landed[stage, own] = held[stage]
        return copies

    def gather_up(stage, copies, size):
        for copy in copies:
            copy.wait_recv()
        total = landed[stage, 0]
        for place in range(1, size):
            total = total + landed[stage, place]
        held[stage + 1] = total

    shares = share(0, "row", rows, row)
    downs.last()
    block_out[...] = (middle_own[...] + down_result[...]).astype(jnp.bfloat16)
    gather_up(0, shares, rows)
    more = share(1, "col", cols, col)
    out_sum[half] = out.total(col)
    for step in range(1, cols):
        lined[step - 1].wait_recv()
        out_sum[half] += out_lined[step].astype(jnp.float32)
    out_copy = send(out_sum.at[half], out_sum.at[half], pair_sems, (5,), "dp", sibling())
    heads.relay()
    down_copy.wait_recv()
    down_sum[...] = down_grad[...] + down_came[...]
    gather_up(1, more, cols)
    gain_copy = send(held.at[2], landed.at[2, 0], gain_sems, (2, 0), "dp", sibling())
    for moved in wides + [heads]:
        moved.land()
    gain_copy.wait_recv()
    gain_sum[...] = held[2] + landed[2, 0]
    out_copy.wait_recv()
    for copy in cats + lows + lined + shares + more + [down_copy, out_copy, gain_copy]:
        copy.wait_send()
    for paired in (out, head):
        paired.copy.wait_send()
    mid.sent(waves=False)
    for item in [downs, acts, heads] + wides:
        item.sent()


def back_pass(local, width, hidden, head_dim):
    rows, cols = lax.axis_size("row"), lax.axis_size("col")
    length, height = rows * cols * local, width // cols // 2
    low, full = jnp.bfloat16, jnp.float32
    shape = jax.ShapeDtypeStruct
    slot, some = 3 * head_dim, head_dim // 2
    outs = [
        shape((local, width), low),
        shape((local, width), full),
        shape((2, cols, 2, height // 2, 2 * hidden), low),
        shape((cols, 2, slot // 2, width // cols), low),
        shape((2, some, width), full),
        shape((hidden, width), full),
        shape((8, 3 * width // 8), full),
    ]

    def vmem(kind, *dims):
        return pltpu.VMEM(dims, kind)

    scratch = [
        vmem(low, rows, cols, local, width),
        vmem(low, cols, rows // 2 * local, 2 * head_dim),
        vmem(low, cols, rows // 2 * local, 2 * head_dim),
        vmem(low, length, slot),
        vmem(low, cols, rows // 2 * local, 2 * slot),
        vmem(low, cols, rows // 2 * local, 2 * slot),
        vmem(full, cols, 2, slot // 2, width // cols),
        vmem(full, cols, slot // 2, width // cols),
        vmem(low, cols, slot // 2, width // cols),
    ]
    scratch += [
        vmem(full, cols, 2, some, width),
        vmem(full, cols, some, width),
        vmem(low, cols, some, width),
        vmem(low, cols, some, width),
        vmem(full, hidden, width),
        vmem(full, hidden, width),
        vmem(low, rows, 1, local, width),
        vmem(low, rows * local, 2 * cols * head_dim),
        vmem(low, rows * local, cols * head_dim),
        vmem(full, length, head_dim),
        vmem(full, length, head_dim),
        vmem(full, length, head_dim),
        vmem(full, local, width),
        vmem(full, local, width),
        vmem(full, 3, 8, 3 * width // 8),
        vmem(full, 3, max(rows, cols), 8, 3 * width // 8),
    ]
    scratch += reduce_scratch(rows, 1, local, width) + reduce_scratch(rows, cols, local, width)[1:]
    scratch += dma(1, 6, cols) + dma(2, 5, cols) + dma(3, 2, cols) + dma(6)
    scratch += dma(cols) + dma(cols) + dma(cols) + dma(3, max(rows, cols))
    return outs, scratch


def whole_pass(given, down, ffn_norm, head_dim):
    args, front_outs, front_scratch = front(*given)
    (local, width), hidden = args[0].shape, down.shape[0]
    hidden_outs, hidden_scratch = hidden_pass(local, width, hidden, *args[3:6])
    outs, back_scratch = back_pass(local, width, hidden, head_dim)
    front_count = len(args)
    args = args + [down, ffn_norm.reshape(1, width)]

    def body(*refs):
        refs = list(refs)

        def take(count):
            taken = refs[:count]
            del refs[:count]
            return taken

        ins, results = take(len(args)), take(len(outs))
        came, made = take(len(front_outs)), take(len(hidden_outs))
        front_own, hidden_own = take(len(front_scratch)), take(len(hidden_scratch))
        own_in, own_grad, _, query, key, value = ins[:6]
        attn_norm, query_norm, key_norm = ins[8:11]
        down_weight, ffn_gain = ins[front_count:]
        in_all, grad_all, out_all, cat_all, wide_all, _, first = came[:7]
        act_own, middle_own, down_part, slot_all, _, hidden_all, wide_low = made
        greet()
        spread, finish, sent = front_kernel(*ins[:front_count], *came, *front_own)
        hidden_kernel(
            spread,
            finish,
            *[in_all, grad_all, out_all, cat_all, wide_all, down_weight, ffn_gain],
            *[query, key, value],
            *made,
            *hidden_own,
        )
        back_kernel(
            *[own_in, own_grad, act_own, middle_own, attn_norm, ffn_gain],
            *[out_all, cat_all, grad_all, first, hidden_all, wide_low, down_part, slot_all],
            *came[8:13],
            *[came[7], query_norm, key_norm],
            *came[13:],
            *results,
            *refs,
        )
        sent()

    scratch = [pltpu.VMEM(out.shape, out.dtype) for out in front_outs + hidden_outs]
    scratch += front_scratch + hidden_scratch + back_scratch
    return call_kernel(body, args, outs, scratch, 0)


def open_kernel(cols, head_dim, *refs):
    wide_got, head_got, block_given, in_given, out_given, down_given, gain_given = refs[:7]
    gate, up, query, key, value, block_out, in_grad, out, down = refs[7:16]
    attn_gain, ffn_gain, query_gain, key_gain = refs[16:]
    pairs = ((block_out, block_given), (in_grad, in_given), (out, out_given), (down, down_given))
    for target, source in pairs:
        target[...] = source[...]
    lanes = gain_given.shape[1] // 3
    for line in range(gain_given.shape[0]):
        for place, target in ((0, attn_gain), (1, ffn_gain)):
            target[:, line * lanes : (line + 1) * lanes] = gain_given[
                line : line + 1, place * lanes : (place + 1) * lanes
            ]
    query_gain[...] = gain_given[0:1, 2 * lanes : 2 * lanes + head_dim]
    key_gain[...] = gain_given[1:2, 2 * lanes : 2 * lanes + head_dim]
    height, part = wide_got.shape[3], wide_got.shape[4] // 2
    for col in range(cols):
        for piece in range(2):
            for side in range(2):
                begin = (2 * piece + side) * height
                lines = slice(begin, begin + height)
                lanes = slice(col * part, (col + 1) * part)
                gate[lines, lanes] = wide_got[side, col, piece, :, :part].astype(jnp.float32)
                up[lines, lanes] = wide_got[side, col, piece, :, part:].astype(jnp.float32)
    turned = []
    for col in range(cols):
        stacked = head_got[col].reshape(3 * head_dim, head_got.shape[3]).astype(jnp.float32)
        turned.append(
            [stacked[kind * head_dim : (kind + 1) * head_dim].T for kind in range(3)]
        )
        query[:, col * head_dim : (col + 1) * head_dim] = turned[col][0]
    for pair in range(cols // 2):
        for place, target in ((1, key), (2, value)):
            target[:, pair * head_dim : (pair + 1) * head_dim] = (
                turned[2 * pair][place] + turned[2 * pair + 1][place]
            )


def call_kernel(body, args, outs, scratch, number):
    vmem = pl.BlockSpec(memory_space=pltpu.VMEM)
    return pl.pallas_call(
        body,
        out_shape=outs,
        in_specs=[vmem] * len(args),
        out_specs=[vmem] * len(outs),
        scratch_shapes=scratch,
        compiler_params=pltpu.CompilerParams(
            collective_id=number, has_side_effects=True, vmem_limit_bytes=VMEM_LIMIT
        ),
    )(*args)


def dma(*shape):
    return [pltpu.SemaphoreType.DMA(shape), pltpu.SemaphoreType.DMA(shape)]


def dot(left, right, left_dim=1, right_dim=0):
    return lax.dot_general(
        left,
        right,
        (((left_dim,), (right_dim,)), ((), ())),
        preferred_element_type=jnp.float32,
    )


def shards(
    block_input,
    seq_lengths,
    out_grad,
    attn_norm,
    query_weight,
    key_weight,
    value_weight,
    query_norm,
    key_norm,
    out_weight,
    ffn_norm,
    gate_weight,
    up_weight,
    down_weight,
):
    width = block_input.shape[1]
    head_dim = query_norm.shape[0]
    cols = lax.axis_size("col")
    given = [block_input, out_grad, out_weight, query_weight, key_weight, value_weight]
    given += [gate_weight, up_weight, (attn_norm, query_norm, key_norm), seq_lengths]
    outs = whole_pass(given, down_weight, ffn_norm, head_dim)
    block_output, input_grad, wide_got, head_got, out_sum, grad_down, gain_sums = outs
    shape = jax.ShapeDtypeStruct
    weights = (gate_weight, up_weight, query_weight, key_weight, value_weight)
    given = (block_output, input_grad, out_sum.reshape(out_weight.shape), grad_down)
    gains = (width, width, head_dim, head_dim)
    results = local_kernel(
        functools.partial(open_kernel, cols, head_dim),
        [wide_got, head_got] + list(given) + [gain_sums],
        [shape(weight.shape, jnp.float32) for weight in weights]
        + [shape(value.shape, value.dtype) for value in given]
        + [shape((1, size), jnp.float32) for size in gains],
    )
    block_output, input_grad = results[5:7]
    sums = tuple(results[:5]) + tuple(results[7:])
    if lax.axis_size("dp") > 2:
        sums = lax.psum(tuple(0.5 * value for value in sums), "dp")
    grad_gate, grad_up, grad_query, grad_key, grad_value = sums[:5]
    grad_outweight, grad_down, grad_attnnorm, grad_ffnnorm, grad_qnorm, grad_knorm = sums[5:]
    return (
        block_output,
        input_grad,
        grad_attnnorm[0],
        grad_query,
        grad_key,
        grad_value,
        grad_qnorm[0],
        grad_knorm[0],
        grad_outweight,
        grad_ffnnorm[0],
        grad_gate,
        grad_up,
        grad_down,
    )


def solution(mesh):
    placed = (
        P(("dp", "row", "col"), None),
        P("dp", None),
        P(("dp", "row", "col"), None),
        P(),
        P("col", "row"),
        P("col", "row"),
        P("col", "row"),
        P(),
        P(),
        P(("row", "col"), None),
        P(),
        P("col", "row"),
        P("col", "row"),
        P(("row", "col"), None),
    )
    return jax.shard_map(
        shards,
        mesh=mesh,
        in_specs=placed,
        out_specs=(
            P(("dp", "row", "col"), None),
            P(("dp", "row", "col"), None),
            P(),
            P("col", "row"),
            P("col", "row"),
            P("col", "row"),
            P(),
            P(),
            P(("row", "col"), None),
            P(),
            P("col", "row"),
            P("col", "row"),
            P(("row", "col"), None),
        ),
        check_vma=False,
    )
```

```python
import functools
import math

import jax
import jax.numpy as jnp
from jax import lax
from jax.experimental import pallas as pl
from jax.experimental.pallas import tpu as pltpu
from jax.sharding import PartitionSpec as P

EPSILON = 1e-05
THETA = 1000000.0


def rope_frequency(width):
    half_width = width // 2
    exponent = jnp.arange(half_width, dtype=jnp.float32) * (2.0 / width)
    frequency = jnp.exp(-math.log(THETA) * exponent)
    return jnp.concatenate([frequency, frequency])[None, :]


def head_norm(values, gain_vec):
    inv_rms = lax.rsqrt(jnp.mean(values * values, axis=-1, keepdims=True) + EPSILON)
    return (values * inv_rms * gain_vec, inv_rms)


def head_norm_back(cotangent, values, inv_rms, gain_vec):
    normed = values * inv_rms
    weighted = cotangent * gain_vec
    gain_grad = jnp.sum(cotangent * normed, axis=0)
    inner_mean = jnp.mean(weighted * normed, axis=-1, keepdims=True)
    return (inv_rms * (weighted - normed * inner_mean), gain_grad)


def swap_halves(values):
    half_width = values.shape[-1] // 2
    return jnp.concatenate([values[:, half_width:], values[:, :half_width]], axis=1)


def block_probability(query_block, key_rows, begins, offset, low, shift):
    score_scale = 1.0 / math.sqrt(query_block.shape[1])
    scores = dot(query_block, key_rows, 1, 1) * score_scale
    places = low + lax.broadcasted_iota(jnp.int32, scores.shape, 1)
    row_places = offset + lax.broadcasted_iota(jnp.int32, scores.shape, 0)
    allowed = (places >= begins) & (places <= row_places)
    if shift is None:
        shift = jnp.log(jnp.sum(jnp.where(allowed, jnp.exp(scores), 0.0), axis=1, keepdims=True))
    probability = jnp.where(allowed, jnp.exp(scores - shift), 0.0).astype(jnp.bfloat16)
    return probability, shift


def spans(length, longest, block):
    return [
        (offset, max(0, (offset - longest) // 128 * 128), block)
        for offset in range(0, length, block)
    ]


def local_kernel(body, args, outs, scratch=()):
    vmem = pl.BlockSpec(memory_space=pltpu.VMEM)
    return pl.pallas_call(
        body,
        out_shape=outs,
        in_specs=[vmem] * len(args),
        out_specs=[vmem] * len(outs),
        scratch_shapes=list(scratch),
    )(*args)


MESH = pl.DeviceIdType.MESH
VMEM_LIMIT = 60 * 1024 * 1024


def remote(source, target, sems, place, axis, index):
    return pltpu.make_async_remote_copy(
        src_ref=source,
        dst_ref=target,
        send_sem=sems[0].at[place],
        recv_sem=sems[1].at[place],
        device_id={axis: index},
        device_id_type=MESH,
    )


def send(source, target, sems, place, axis, index):
    copy = remote(source, target, sems, place, axis, index)
    copy.start()
    return copy


def neighbours():
    rows, row = lax.axis_size("row"), lax.axis_index("row")
    near = row + 1 - 2 * lax.rem(row, 2)
    far = lax.rem(row + rows // 2, rows)
    return near, far


def sibling():
    own = lax.axis_index("dp")
    return own + 1 - 2 * lax.rem(own, 2)


def greet():
    cols, col = lax.axis_size("col"), lax.axis_index("col")
    near, far = neighbours()
    peers = [("col", lax.rem(col + step, cols)) for step in range(1, cols)]
    peers += [("row", near), ("row", far), ("dp", sibling())]
    peers.append(("row", lax.rem(near + lax.axis_size("row") // 2, lax.axis_size("row"))))
    barrier = pltpu.get_barrier_semaphore()
    for axis, index in peers:
        pl.semaphore_signal(barrier, inc=1, device_id={axis: index}, device_id_type=MESH)
    pl.semaphore_wait(barrier, len(peers))


class Gather:
    def __init__(self, block, part, sems, item):
        self.block, self.part = block, part
        self.sems, self.item = sems, item
        self.cols, self.col = lax.axis_size("col"), lax.axis_index("col")
        self.row = lax.axis_index("row")
        self.near, self.far = neighbours()

    def hop(self, origin, right):
        piece = self.block(self.row, origin)
        place = (self.item, 0 if right else 1, origin)
        return remote(piece, piece, self.sems, place, "col", self.col + (1 if right else -1))

    def cross(self, origin, kind):
        piece = self.block(self.row, origin)
        peer = (self.near, self.far)[kind]
        return remote(piece, piece, self.sems, (self.item, 2 + kind, origin), "row", peer)

    def corner(self, origin, kind):
        source, peer = ((self.near, self.far), (self.far, self.near))[kind]
        piece = self.part(source, origin, kind)
        return remote(piece, piece, self.sems, (self.item, 4 + kind, origin), "row", peer)

    def forward(self, origin, right):
        @pl.when(self.col < self.cols - 1 if right else self.col > 0)
        def _():
            self.hop(origin, right).start()

    def each(self, wave, act):
        if wave == 0:
            act(self.col, None)
            return
        for right in (True, False):
            origin = self.col - wave if right else self.col + wave

            @pl.when(self.col >= wave if right else self.col + wave < self.cols)
            def _():
                act(origin, right)

    def start(self):
        for right in (True, False):
            self.forward(self.col, right)
        for kind in range(2):
            self.cross(self.col, kind).start()

    def wave(self, wave):
        def act(origin, right):
            self.hop(origin, right).wait_recv()
            self.forward(origin, right)
            for kind in range(2):
                self.cross(origin, kind).start()

        self.each(wave, act)

    def relay(self, wave):
        def act(origin, right):
            for kind in range(2):
                self.cross(origin, kind).wait_recv()
                self.corner(origin, kind).start()

        self.each(wave, act)

    def land(self, wave):
        def act(origin, right):
            for kind in range(2):
                self.corner(origin, kind).wait_recv()

        self.each(wave, act)

    def sent(self, waves=True):
        def act(origin, right):
            for side in (True, False) if right is None else (right,):

                @pl.when(self.col < self.cols - 1 if side else self.col > 0)
                def _():
                    if waves:
                        self.hop(origin, side).wait_send()

            for kind in range(2):
                self.cross(origin, kind).wait_send()
                self.corner(origin, kind).wait_send()

        for wave in range(self.cols if waves else 1):
            self.each(wave, act)


class Swap:
    def __init__(self, source, target, sems, item, whole=False):
        self.source, self.target, self.sems, self.item = source, target, sems, item
        self.cols, self.col = lax.axis_size("col"), lax.axis_index("col")
        self.half = lax.rem(lax.axis_index("dp"), 2)
        self.lines, self.pairs, self.first = {}, {}, 0 if whole else 1

    def line(self):
        for step in range(1, self.cols):
            peer = lax.rem(self.col + step, self.cols)
            self.lines[step] = send(
                self.source(peer, self.half),
                self.target.at[self.col, self.half],
                self.sems,
                (self.item, 0, step),
                "col",
                peer,
            )

    def relay(self):
        for step in range(self.first, self.cols):
            if step:
                self.lines[step].wait_recv()
            piece = self.target.at[lax.rem(self.col + self.cols - step, self.cols), self.half]
            self.pairs[step] = send(
                piece, piece, self.sems, (self.item, 1, step), "dp", sibling()
            )

    def land(self):
        for copy in self.pairs.values():
            copy.wait_recv()

    def sent(self):
        for copies in (self.lines, self.pairs):
            for copy in copies.values():
                copy.wait_send()


def front_kernel(*refs):
    (own_in, own_grad, own_out, query, key, value, gate, up) = refs[:8]
    (attn_norm, query_norm, key_norm, seq_lengths, frequency) = refs[8:13]
    (in_all, grad_all, out_all, cat_all, wide_all, slot_all) = refs[13:19]
    (first, sums, query_rot, key_rot, value_low, low_rows, totals) = refs[19:26]
    (cosine, sine, begins) = refs[26:29]
    (slot_part, wide_part) = refs[29:31]
    gather_sems, swap_sems, pair_sems = refs[31:33], refs[33:35], refs[35:37]
    rows, cols = lax.axis_size("row"), lax.axis_size("col")
    row, col = lax.axis_index("row"), lax.axis_index("col")
    half = lax.rem(lax.axis_index("dp"), 2)
    near, far = neighbours()
    corner = lax.rem(near + rows // 2, rows)
    length, head_dim = query_rot.shape
    width = own_in.shape[1]
    local = own_in.shape[0]
    block = length // rows

    def split(ref):
        count = ref.shape[2] // 2
        return (
            lambda r, c: ref.at[r, c],
            lambda r, c, k: ref.at[r, c, pl.ds(k * count, count)],
        )

    in_all[row, col] = own_in[...]
    inputs = Gather(*split(in_all), gather_sems, 0)
    inputs.start()
    height = query.shape[0] // 2
    for place in range(cols):
        for piece in range(2):
            lines = slice(piece * height, (piece + 1) * height)
            lanes = slice(place // 2 * head_dim, (place // 2 + 1) * head_dim)
            slot_part[place, piece, :, :head_dim] = query[
                lines, place * head_dim : (place + 1) * head_dim
            ]
            slot_part[place, piece, :, head_dim : 2 * head_dim] = key[lines, lanes]
            slot_part[place, piece, :, 2 * head_dim :] = value[lines, lanes]
    slots = Swap(lambda c, h: slot_part.at[c, h], slot_all, swap_sems, 0)
    slots.line()
    slot_all[col] = slot_part[col]
    grad_all[row, col] = own_grad[...]
    out_all[row, col] = own_out[...]
    places = lax.broadcasted_iota(jnp.int32, (length, 1), 0)
    end, begin = jnp.zeros((1, 1), jnp.int32), jnp.zeros((length, 1), jnp.int32)
    for number in range(seq_lengths.shape[1]):
        size = seq_lengths[:, number : number + 1]
        end = end + size
        begin = begin + jnp.where(places >= end, size, 0)
    begins[...] = begin
    angles = (places - begin).astype(jnp.float32) * frequency[...]
    inputs.wave(1)
    inputs.relay(0)
    cosine[...] = jnp.cos(angles)
    inputs.wave(2)
    inputs.relay(1)
    side = lax.broadcasted_iota(jnp.int32, angles.shape, 1)
    turned = jnp.sin(angles)
    sine[...] = jnp.where(side < head_dim // 2, -turned, turned)
    for step in range(3, cols):
        inputs.wave(step)
    count = own_out.shape[1] // 2
    outs = Gather(
        lambda r, c: out_all.at[r, c, half],
        lambda r, c, k: out_all.at[r, c, half, pl.ds(k * count, count)],
        gather_sems,
        2,
    )
    outs.start()
    grads = Gather(*split(grad_all), gather_sems, 1)
    inputs.relay(2)
    for step in range(3, cols):
        inputs.relay(step)
    grads.start()
    slots.relay()
    for step in range(1, cols):
        outs.wave(step)
    slots.land()

    def project(place):
        for c in range(cols):
            values = in_all[place, c].astype(jnp.float32)
            normed = head_norm(values, attn_norm[...])[0]
            first[place, c] = normed.astype(jnp.bfloat16)
        lines = pl.ds(pl.multiple_of(place * block, block), block)
        sums[lines, :] = dot(
            first[place].reshape(block, width), slot_all[...].reshape(width, 3 * head_dim)
        )

    project(row)
    project(near)
    project(far)
    for step in range(cols):
        inputs.land(step)
    project(corner)
    for place, target, gain in ((0, query_rot, query_norm), (1, key_rot, key_norm)):
        normed = head_norm(sums[:, place * head_dim : (place + 1) * head_dim], gain[...])[0]
        target[...] = (normed * cosine[...] + swap_halves(normed) * sine[...]).astype(jnp.bfloat16)
    value_low[...] = sums[:, 2 * head_dim : 3 * head_dim].astype(jnp.bfloat16)
    hidden = gate.shape[1] // cols

    def pack(place):
        for kind, source in ((0, gate), (1, up)):
            for piece in range(2):
                wide_part[place, piece, :, kind * hidden : (kind + 1) * hidden] = source[
                    piece * height : (piece + 1) * height, place * hidden : (place + 1) * hidden
                ]

    def cat(part):
        places = pl.ds(part * (rows // 2), rows // 2)
        return Gather(
            lambda r, c: cat_all.at[places, r, c],
            lambda r, c, k: cat_all.at[places, r, c, pl.ds(k * head_dim // 2, head_dim // 2)],
            gather_sems,
            3 + part,
        )

    cats = [cat(part) for part in range(2)]
    wide = Swap(lambda c, h: wide_part.at[c, h], wide_all, swap_sems, 1)
    for offset, low, _ in spans(length, length // 2, block):
        number = offset // block
        lines, keys = slice(offset, offset + block), slice(low, offset + block)
        probability, total = block_probability(
            query_rot[lines, :], key_rot[keys, :], begins[lines, :], offset, low, None
        )
        totals[lines, :] = total
        low_rows[lines, :] = dot(probability, value_low[keys, :]).astype(jnp.bfloat16)
        cat_all[number, row, col] = dot(value_low[keys, :], probability, 0, 1).astype(jnp.bfloat16)
        if number == 0:
            grads.wave(1)
            outs.relay(0)
        if number == rows // 2 - 1:
            cats[0].start()
            for step in range(1, cols):
                outs.relay(step)
            for step in range(2, cols):
                grads.wave(step)
        if number == rows // 2:
            grads.relay(0)
    cats[1].start()
    for place in range(cols):
        pack(place)
    wide.line()
    wide_all[col] = wide_part[col]
    cats[0].wave(1)
    grads.relay(1)
    for step in range(2, cols):
        cats[0].wave(step)
    for step in range(1, cols):
        cats[1].wave(step)
    for step in range(2, cols):
        grads.relay(step)
    for step in range(cols):
        cats[0].relay(step)
    pairs = []
    for step in range(cols):
        outs.land(step)
    for number, place in enumerate((near, far, corner)):
        piece = out_all.at[place, :, half]
        pairs.append(send(piece, piece, pair_sems, (number,), "dp", sibling()))
    for step in range(1, cols):
        piece = out_all.at[row, lax.rem(col + cols - step, cols), half]
        pairs.append(send(piece, piece, pair_sems, (2 + step,), "dp", sibling()))
    for step in range(cols):
        cats[1].relay(step)
    wide.relay()
    wide.land()
    for gather in [grads] + cats:
        for step in range(cols):
            gather.land(step)
    for copy in pairs:
        copy.wait()

    def sent():
        for item in [inputs, grads, outs, slots, wide] + cats:
            item.sent()

    return sent


def front(own_in, own_grad, own_out, query, key, value, gate, up, norms, seq_lengths):
    rows, cols = lax.axis_size("row"), lax.axis_size("col")
    local, width = own_in.shape
    attn_norm, query_norm, key_norm = norms
    length, head_dim = local * rows * cols, query_norm.shape[0]
    hidden, height = gate.shape[1] // cols, gate.shape[0] // 2
    low = jnp.bfloat16
    blocks = jax.ShapeDtypeStruct((rows, cols, local, width), low)
    halves = own_out.shape[0] // 2
    wide = (cols, 2, height, 2 * hidden)
    slot = (cols, 2, height, 3 * head_dim)
    shape = jax.ShapeDtypeStruct
    head_rows = shape((length, head_dim), low)
    table = shape((length, head_dim), jnp.float32)
    outs = [
        blocks,
        blocks,
        shape((rows, cols, 2, halves, width), low),
        shape((rows, rows, cols, head_dim, length // rows), low),
        shape(wide, low),
        shape(slot, low),
        blocks,
        shape((length, 3 * head_dim), jnp.float32),
        head_rows,
        head_rows,
        head_rows,
        head_rows,
        shape((length, 1), jnp.float32),
        table,
        table,
        shape((length, 1), jnp.int32),
    ]
    scratch = [pltpu.VMEM(slot, low), pltpu.VMEM(wide, low)]
    scratch += dma(5, 6, cols) + dma(2, 2, cols) + dma(2 + cols)
    args = [own_in, own_grad, own_out.reshape(2, halves, width), query, key, value, gate, up]
    args += [attn_norm.reshape(1, width), query_norm.reshape(1, head_dim)]
    args += [key_norm.reshape(1, head_dim), seq_lengths, rope_frequency(head_dim)]
    return args, outs, scratch


class Reduce:
    def __init__(self, part, relayed, planed, staged, lined, result, sems, item):
        self.part, self.relayed, self.planed = part, relayed, planed
        self.staged, self.lined, self.result = staged, lined, result
        self.sems, self.item = sems, item
        self.cols = part.shape[1]
        self.col = lax.axis_index("col") if self.cols > 1 else 0
        self.row = lax.axis_index("row")
        self.near, self.far = neighbours()
        self.cross = lax.rem(self.near + lax.axis_size("row") // 2, lax.axis_size("row"))
        self.count = part.shape[2] // 2
        self.relays, self.planes, self.lines = [], [], []

    def first(self):
        for kind, peer in ((0, self.near), (1, self.far)):
            self.relays.append(
                send(
                    self.part.at[self.cross, :, pl.ds(kind * self.count, self.count)],
                    self.relayed.at[kind],
                    self.sems,
                    (self.item, 1 + kind, 0),
                    "row",
                    peer,
                )
            )

    def merge(self, kind):
        peer, came = (self.near, self.far)[kind], 1 - kind
        self.relays[came].wait_recv()
        lines = slice(came * self.count, (came + 1) * self.count)
        self.part[peer, :, lines] = (
            self.part[peer, :, lines].astype(jnp.float32)
            + self.relayed[came].astype(jnp.float32)
        ).astype(jnp.bfloat16)

    def ship(self, kind):
        peer = (self.near, self.far)[kind]
        self.planes.append(
            send(
                self.part.at[peer],
                self.planed.at[kind],
                self.sems,
                (self.item, 3 + kind, 0),
                "row",
                peer,
            )
        )

    def toward(self, kind):
        self.merge(kind)
        self.ship(kind)

    def total(self, place):
        summed = self.part[self.row, place].astype(jnp.float32)
        for kind in range(2):
            summed = summed + self.planed[kind, place].astype(jnp.float32)
        return summed

    def own(self):
        for copy in self.planes:
            copy.wait_recv()
        for step in range(1, self.cols):
            place = lax.rem(self.col + step, self.cols)
            self.staged[step] = self.total(place).astype(jnp.bfloat16)
            self.lines.append(
                send(
                    self.staged.at[step],
                    self.lined.at[step],
                    self.sems,
                    (self.item, 0, step),
                    "col",
                    place,
                )
            )
        self.result[...] = self.total(self.col)

    def last(self):
        for step in range(1, self.cols):
            self.lines[step - 1].wait_recv()
            self.result[...] += self.lined[step].astype(jnp.float32)

    def sent(self):
        for copy in self.relays + self.planes + self.lines:
            copy.wait_send()


def reduce_scratch(rows, cols, local, width):
    low = jnp.bfloat16
    return [
        pltpu.VMEM((2, cols, local // 2, width), low),
        pltpu.VMEM((2, cols, local, width), low),
        pltpu.VMEM((cols, local, width), low),
        pltpu.VMEM((cols, local, width), low),
    ]


def hidden_kernel(*refs):
    in_all, grad_all, out_all, cat_all, wide_all, down, ffn_norm = refs[:7]
    query, key, value = refs[7:10]
    act_own, middle_own, down_part, slot_all = refs[10:14]
    second_all, hidden_all, wide_low = refs[14:17]
    act_parts, act_halves, middle_block, slot_part = refs[17:21]
    low_all, wide_sum, wide_came, down_relayed = refs[21:25]
    act_scratch, rest = (refs[25:29], refs[29:33]), refs[33:]
    sems, swap_sems, pair_sems = rest[:2], rest[2:4], rest[4:6]
    rows, cols = lax.axis_size("row"), lax.axis_size("col")
    row, col = lax.axis_index("row"), lax.axis_index("col")
    near, far = neighbours()
    cross = lax.rem(near + rows // 2, rows)
    local, width = in_all.shape[2:]
    block, hidden = cols * local, down.shape[0]
    height, begin = query.shape[0] // 2, 0
    for source in (query, key, value):
        lanes = slice(begin, begin + source.shape[1])
        for piece in range(2):
            slot_part[piece, :, lanes] = source[piece * height : (piece + 1) * height, :]
        begin += source.shape[1]
    slots = Swap(lambda c, h: slot_part.at[h], slot_all, swap_sems, 0)
    slots.line()
    slot_all[col] = slot_part[...]
    acts = [
        Reduce(act_parts.at[side], *act_scratch[side], act_halves.at[side], sems, side)
        for side in range(2)
    ]

    downs = Reduce(down_part, down_relayed, None, None, None, None, sems, 2)

    def work(place):
        mixed = dot(cat_all[place].reshape(width, block), out_all[...].reshape(width, width), 0, 0)
        middle = in_all[place].reshape(block, width).astype(jnp.float32) + mixed
        middle_block[...] = middle
        second = head_norm(middle, ffn_norm[...])[0].astype(jnp.bfloat16)
        second_all[place] = second
        wide_weight = wide_all[...].reshape(width, 2 * hidden)
        wide_sums = dot(second, wide_weight)
        gating, upward = wide_sums[:, :hidden], wide_sums[:, hidden:]
        hidden_grad = dot(grad_all[place].reshape(block, width), down[...], 1, 1)
        sigmoid_gate = jax.nn.sigmoid(gating)
        activated = gating * sigmoid_gate
        hidden_low = (activated * upward).astype(jnp.bfloat16)
        gate_low = (
            hidden_grad * upward * sigmoid_gate * (1.0 + gating * (1.0 - sigmoid_gate))
        ).astype(jnp.bfloat16)
        up_low = (hidden_grad * activated).astype(jnp.bfloat16)
        hidden_all[place] = hidden_low
        low_all[place, :, :hidden] = gate_low
        low_all[place, :, hidden:] = up_low
        act = dot(low_all[place], wide_weight, 1, 1).astype(jnp.bfloat16)
        for side in range(2):
            act_parts[side, place] = act[
                :, side * (width // 2) : (side + 1) * (width // 2)
            ].reshape(cols, local, width // 2)

    def work_down(place):
        down_part[place] = (
            dot(hidden_all[place], down[...]).astype(jnp.bfloat16).reshape(cols, local, width)
        )

    work(cross)
    for item in acts:
        item.first()
    work_down(cross)
    work(near)
    for item in acts:
        item.toward(0)
    slots.relay()
    work(far)
    for item in acts:
        item.toward(1)
    downs.first()
    work(row)
    lines = pl.ds(pl.multiple_of(col * local, local), local)
    middle_own[...] = middle_block[lines, :]
    acts[0].own()
    for place in (near, far, row):
        work_down(place)
    acts[1].own()
    wide = Paired(wide_sum, wide_came, pair_sems, 0)
    wide_sum[...] = dot(
        second_all[...].reshape(rows * block, width),
        low_all[...].reshape(rows * block, 2 * hidden),
        0,
        0,
    ).reshape(wide_sum.shape)
    wide.pair()
    acts[0].last()
    slots.land()
    wide.copy.wait_recv()
    for place in range(cols):
        total = wide.total(place).astype(jnp.bfloat16)
        for side in range(2):
            wide_low[side, place] = total[side * (height // 2) : (side + 1) * (height // 2), :]
    for kind in range(2):
        downs.merge(kind)
    acts[1].last()
    for side in range(2):
        act_own[:, side * (width // 2) : (side + 1) * (width // 2)] = act_halves[side]
    for item in acts + [downs]:
        item.sent()
    slots.sent()
    wide.copy.wait_send()


def hidden_pass(local, width, hidden, query, key, value):
    rows, cols = lax.axis_size("row"), lax.axis_size("col")
    block, height = cols * local, query.shape[0] // 2
    shape = jax.ShapeDtypeStruct
    own, low, full = shape((local, width), jnp.float32), jnp.bfloat16, jnp.float32
    slot = (2, height, query.shape[1] + key.shape[1] + value.shape[1])
    outs = [own, own, shape((rows, cols, local, width), low), shape((cols,) + slot, low)]
    outs += [shape((rows, block, width), low), shape((rows, block, hidden), low)]
    outs += [shape((2, cols, height // 2, 2 * hidden), low)]
    scratch = [
        pltpu.VMEM((2, rows, cols, local, width // 2), low),
        pltpu.VMEM((2, local, width // 2), full),
        pltpu.VMEM((block, width), full),
        pltpu.VMEM(slot, low),
        pltpu.VMEM((rows, block, 2 * hidden), low),
        pltpu.VMEM((cols, 2, height, 2 * hidden), full),
        pltpu.VMEM((cols, height, 2 * hidden), full),
        pltpu.VMEM((2, cols, local // 2, width), low),
    ]
    scratch += reduce_scratch(rows, cols, local, width // 2) * 2
    scratch += dma(3, 5, cols) + dma(1, 2, cols) + dma(1)
    return outs, scratch


class Paired:
    def __init__(self, part, came, sems, item):
        self.part, self.came, self.sems, self.item = part, came, sems, item
        self.half = lax.rem(lax.axis_index("dp"), 2)

    def pair(self):
        self.copy = send(
            self.part.at[:, 1 - self.half], self.came, self.sems, (self.item,), "dp", sibling()
        )

    def total(self, place):
        return self.part[place, self.half] + self.came[place]


def back_kernel(*refs):
    own_in, own_grad, act_own, middle_own, attn_norm, ffn_norm = refs[:6]
    out_all, cat_all, grad_all, first = refs[6:10]
    hidden_all, wide_low, down_given, slot_all = refs[10:14]
    query_rot, key_rot, value_low, low_rows, totals = refs[14:19]
    sums, query_norm, key_norm, cosine, sine, begins = refs[19:25]
    outs, scratch = refs[25:32], refs[32:]
    block_out, in_grad, wide_got, head_got, out_sum, down_sum, gain_sum = outs
    mid_all, cat_part, grads_in, own_slot, slot_mine, slots_in = scratch[:6]
    head_sum, head_came, head_low = scratch[6:9]
    out_part, out_came, out_low, out_lined = scratch[9:13]
    down_grad, down_came, act_part = scratch[13:16]
    low_even, low_odd, query_acc, key_acc, value_acc = scratch[16:21]
    act_result, down_result, held, landed = scratch[21:25]
    act_scratch, down_scratch = scratch[25:29], (None,) + tuple(scratch[29:32])
    sems = scratch[32:]
    mid_sems, sum_sems, swap_sems, pair_sems = sems[:2], sems[2:4], sems[4:6], sems[6:8]
    cat_sems, low_sems, out_sems, gain_sems = sems[8:10], sems[10:12], sems[12:14], sems[14:16]
    rows, cols = lax.axis_size("row"), lax.axis_size("col")
    row, col = lax.axis_index("row"), lax.axis_index("col")
    half = lax.rem(lax.axis_index("dp"), 2)
    local, width = own_in.shape
    length, head_dim = query_rot.shape
    block = cols * local
    near, far = neighbours()
    wides = [
        Swap(
            lambda c, h, side=side: wide_low.at[side, c],
            wide_got.at[side],
            swap_sems,
            side,
            whole=True,
        )
        for side in range(2)
    ]
    wides[0].line()
    lanes = held.shape[2] // 3
    held[0] = jnp.zeros(held.shape[1:], jnp.float32)

    def pack_gain(place, gain):
        for line in range(gain.shape[1] // lanes):
            held[0, line : line + 1, place * lanes : (place + 1) * lanes] = gain[
                :, line * lanes : (line + 1) * lanes
            ]

    middle = middle_own[...]
    scale_mid = head_norm(middle, ffn_norm[...])[1]
    middle_back, ffn_gain = head_norm_back(act_own[...], middle, scale_mid, ffn_norm[...])
    middle_grad = own_grad[...].astype(jnp.float32) + middle_back
    in_grad[...] = middle_grad
    mid_all[row, col] = middle_grad.astype(jnp.bfloat16)
    mid = Gather(
        lambda r, c: mid_all.at[r, c],
        lambda r, c, k: mid_all.at[r, c, pl.ds(k * (local // 2), local // 2)],
        mid_sems,
        0,
    )
    for kind in range(2):
        mid.cross(col, kind).start()
    for step in range(1, cols):
        mid_all[:, lax.rem(col + step, cols)] = jnp.zeros((rows, local, width), jnp.bfloat16)
    pack_gain(1, ffn_gain[None, :])

    for side in range(2):
        wide_got[side, col, half] = wide_low[side, col]
    mid.relay(0)
    downs = Reduce(down_given, *down_scratch, down_result, sum_sems, 0)
    for kind in range(2):
        downs.ship(kind)
    down_grad[...] = dot(
        hidden_all[...].reshape(length, hidden_all.shape[-1]),
        grad_all[...].reshape(length, width),
        0,
        0,
    )
    down_copy = send(down_grad, down_came, pair_sems, (3,), "dp", sibling())
    mid.land(0)

    cat_grad = dot(
        mid_all[:, col].reshape(rows * local, width),
        out_all[row].reshape(cols * head_dim, width),
        1,
        1,
    ).astype(jnp.bfloat16)
    for place in range(cols):
        piece = cat_grad[:, place * head_dim : (place + 1) * head_dim]
        cat_part[place, :, :head_dim] = piece[: rows // 2 * local]
        cat_part[place, :, head_dim:] = piece[rows // 2 * local :]

    def turn(source, target, sems, place=None):
        return [
            send(
                source(lax.rem(col + step, cols)),
                place(step) if place else target,
                sems,
                (step,),
                "col",
                lax.rem(col + step, cols),
            )
            for step in range(1, cols)
        ]

    cats = turn(lambda c: cat_part.at[c], grads_in.at[col], cat_sems)
    grads_in[col] = cat_part[col]
    mixed = None
    for place in range(rows):
        term = dot(
            cat_all[place, row].reshape(cols * head_dim, block),
            mid_all[place].reshape(block, width),
        )
        mixed = term if mixed is None else mixed + term
    out = Paired(out_part, out_came, pair_sems, 2)
    out_part[...] = mixed.reshape(cols, 2, head_dim // 2, width)
    out.pair()
    for copy in cats:
        copy.wait_recv()
    wides[1].line()

    score_scale = 1.0 / math.sqrt(head_dim)
    key_acc[...] = jnp.zeros_like(key_acc)
    value_acc[...] = jnp.zeros_like(value_acc)
    for offset, low, _ in spans(length, length // 2, block):
        number = offset // block
        lines, keys = slice(offset, offset + block), slice(low, offset + block)
        probability, _ = block_probability(
            query_rot[lines, :], key_rot[keys, :], begins[lines, :], offset, low, totals[lines, :]
        )
        upper, right = number % (rows // 2) * local, number // (rows // 2) * head_dim
        grad_block = grads_in[:, upper : upper + local, right : right + head_dim].reshape(
            block, head_dim
        )
        value_acc[keys, :] += dot(probability, grad_block, 0, 0)
        row_delta = jnp.sum(
            grad_block.astype(jnp.float32) * low_rows[lines, :].astype(jnp.float32),
            axis=1,
            keepdims=True,
        )
        prob_grad = dot(grad_block, value_low[keys, :], 1, 1)
        score_grad = (
            score_scale * probability.astype(jnp.float32) * (prob_grad - row_delta)
        ).astype(jnp.bfloat16)
        query_acc[lines, :] = dot(score_grad, key_rot[keys, :])
        key_acc[keys, :] += dot(score_grad, query_rot[lines, :], 0, 0)
        if number == 0:
            out.copy.wait_recv()
            for place in range(cols):
                out_low[place] = out.total(place).astype(jnp.bfloat16)
            lined = turn(lambda c: out_low.at[c], None, out_sems, lambda step: out_lined.at[step])
    slot = 3 * head_dim

    def keep(place, value):
        own_slot[:, place * head_dim : (place + 1) * head_dim] = value
        pieces = value.reshape(rows, cols, local, head_dim)
        for number in range(rows):
            upper = number % (rows // 2) * local
            begin = number // (rows // 2) * slot + place * head_dim
            slot_mine[:, upper : upper + local, begin : begin + head_dim] = pieces[number]

    for place, source, gains in ((0, query_acc, query_norm), (1, key_acc, key_norm)):
        raw = sums[:, place * head_dim : (place + 1) * head_dim]
        gain = gains[...]
        inv_rms = head_norm(raw, gain)[1]
        cotangent = source[...] * cosine[...] - swap_halves(source[...]) * sine[...]
        low_part, gain_grad = head_norm_back(cotangent, raw, inv_rms, gain)
        keep(place, low_part.astype(jnp.bfloat16))
        held[0, place : place + 1, 2 * lanes : 2 * lanes + head_dim] = gain_grad[None, :]
    keep(2, value_acc[...].astype(jnp.bfloat16))
    lows = turn(lambda c: slot_mine.at[c], slots_in.at[col], low_sems)
    slots_in[col] = slot_mine[col]

    head = Paired(head_sum, head_came, pair_sems, 4)
    head_grad = dot(own_slot[...], first[...].reshape(length, width), 0, 0)
    for place in range(cols):
        head_sum[place] = head_grad[
            :, place * (width // cols) : (place + 1) * (width // cols)
        ].reshape(head_sum.shape[1:])
    head.pair()
    for copy in lows:
        copy.wait_recv()
    downs.own()
    for place in range(cols):
        columns = slice(place * head_dim, (place + 1) * head_dim)
        came = jnp.concatenate([slots_in[place, :, :slot], slots_in[place, :, slot:]], axis=0)
        low_even[:, columns] = came[:, :head_dim]
        target, offset = (low_odd, 0) if place % 2 else (low_even, cols * head_dim)
        for kind in (0, 1):
            begin = offset + (kind * (cols // 2) + place // 2) * head_dim
            target[:, begin : begin + head_dim] = came[
                :, (1 + kind) * head_dim : (2 + kind) * head_dim
            ]
    slot_weight = slot_all[...].reshape(width, slot_all.shape[-1])
    act = dot(low_even[...], slot_weight, 1, 1) + dot(
        low_odd[...], slot_weight[:, cols * head_dim :], 1, 1
    )
    act_part[...] = act.astype(jnp.bfloat16).reshape(act_part.shape)
    acts = Reduce(act_part, *act_scratch, act_result, sum_sems, 1)
    acts.first()
    head.copy.wait_recv()
    for place in range(cols):
        head_low[place] = head.total(place).astype(jnp.bfloat16)
    heads = Swap(lambda c, h: head_low.at[c], head_got, swap_sems, 2, whole=True)
    heads.line()
    head_got[col, half] = head_low[col]
    acts.toward(0)
    acts.toward(1)
    wides[0].relay()
    wides[1].relay()
    acts.own()

    residual = own_in[...].astype(jnp.float32)
    scale_in = head_norm(residual, attn_norm[...])[1]
    input_back, attn_gain = head_norm_back(act_result[...], residual, scale_in, attn_norm[...])
    in_grad[...] += input_back
    pack_gain(0, attn_gain[None, :])

    def share(stage, axis, size, own):
        copies = [
            send(
                held.at[stage],
                landed.at[stage, own],
                gain_sems,
                (stage, step),
                axis,
                lax.rem(own + step, size),
            )
            for step in range(1, size)
        ]
        landed[stage, own] = held[stage]
        return copies

    def gather_up(stage, copies, size):
        for copy in copies:
            copy.wait_recv()
        total = landed[stage, 0]
        for place in range(1, size):
            total = total + landed[stage, place]
        held[stage + 1] = total

    shares = share(0, "row", rows, row)
    downs.last()
    block_out[...] = (middle_own[...] + down_result[...]).astype(jnp.bfloat16)
    gather_up(0, shares, rows)
    more = share(1, "col", cols, col)
    out_sum[half] = out.total(col)
    for step in range(1, cols):
        lined[step - 1].wait_recv()
        out_sum[half] += out_lined[step].astype(jnp.float32)
    out_copy = send(out_sum.at[half], out_sum.at[half], pair_sems, (5,), "dp", sibling())
    heads.relay()
    down_copy.wait_recv()
    down_sum[...] = down_grad[...] + down_came[...]
    gather_up(1, more, cols)
    gain_copy = send(held.at[2], landed.at[2, 0], gain_sems, (2, 0), "dp", sibling())
    for moved in wides + [heads]:
        moved.land()
    gain_copy.wait_recv()
    gain_sum[...] = held[2] + landed[2, 0]
    out_copy.wait_recv()
    for copy in cats + lows + lined + shares + more + [down_copy, out_copy, gain_copy]:
        copy.wait_send()
    for paired in (out, head):
        paired.copy.wait_send()
    mid.sent(waves=False)
    for item in [downs, acts, heads] + wides:
        item.sent()


def back_pass(local, width, hidden, head_dim):
    rows, cols = lax.axis_size("row"), lax.axis_size("col")
    length, height = rows * cols * local, width // cols // 2
    low, full = jnp.bfloat16, jnp.float32
    shape = jax.ShapeDtypeStruct
    slot, some = 3 * head_dim, head_dim // 2
    outs = [
        shape((local, width), low),
        shape((local, width), full),
        shape((2, cols, 2, height // 2, 2 * hidden), low),
        shape((cols, 2, slot // 2, width // cols), low),
        shape((2, some, width), full),
        shape((hidden, width), full),
        shape((8, 3 * width // 8), full),
    ]

    def vmem(kind, *dims):
        return pltpu.VMEM(dims, kind)

    scratch = [
        vmem(low, rows, cols, local, width),
        vmem(low, cols, rows // 2 * local, 2 * head_dim),
        vmem(low, cols, rows // 2 * local, 2 * head_dim),
        vmem(low, length, slot),
        vmem(low, cols, rows // 2 * local, 2 * slot),
        vmem(low, cols, rows // 2 * local, 2 * slot),
        vmem(full, cols, 2, slot // 2, width // cols),
        vmem(full, cols, slot // 2, width // cols),
        vmem(low, cols, slot // 2, width // cols),
    ]
    scratch += [
        vmem(full, cols, 2, some, width),
        vmem(full, cols, some, width),
        vmem(low, cols, some, width),
        vmem(low, cols, some, width),
        vmem(full, hidden, width),
        vmem(full, hidden, width),
        vmem(low, rows, 1, local, width),
        vmem(low, rows * local, 2 * cols * head_dim),
        vmem(low, rows * local, cols * head_dim),
        vmem(full, length, head_dim),
        vmem(full, length, head_dim),
        vmem(full, length, head_dim),
        vmem(full, local, width),
        vmem(full, local, width),
        vmem(full, 3, 8, 3 * width // 8),
        vmem(full, 3, max(rows, cols), 8, 3 * width // 8),
    ]
    scratch += reduce_scratch(rows, 1, local, width) + reduce_scratch(rows, cols, local, width)[1:]
    scratch += dma(1, 6, cols) + dma(2, 5, cols) + dma(3, 2, cols) + dma(6)
    scratch += dma(cols) + dma(cols) + dma(cols) + dma(3, max(rows, cols))
    return outs, scratch


def whole_pass(given, down, ffn_norm, head_dim):
    args, front_outs, front_scratch = front(*given)
    (local, width), hidden = args[0].shape, down.shape[0]
    hidden_outs, hidden_scratch = hidden_pass(local, width, hidden, *args[3:6])
    outs, back_scratch = back_pass(local, width, hidden, head_dim)
    front_count = len(args)
    args = args + [down, ffn_norm.reshape(1, width)]

    def body(*refs):
        refs = list(refs)

        def take(count):
            taken = refs[:count]
            del refs[:count]
            return taken

        ins, results = take(len(args)), take(len(outs))
        came, made = take(len(front_outs)), take(len(hidden_outs))
        front_own, hidden_own = take(len(front_scratch)), take(len(hidden_scratch))
        own_in, own_grad, _, query, key, value = ins[:6]
        attn_norm, query_norm, key_norm = ins[8:11]
        down_weight, ffn_gain = ins[front_count:]
        in_all, grad_all, out_all, cat_all, wide_all, _, first = came[:7]
        act_own, middle_own, down_part, slot_all, _, hidden_all, wide_low = made
        greet()
        sent = front_kernel(*ins[:front_count], *came, *front_own)
        hidden_kernel(
            *[in_all, grad_all, out_all, cat_all, wide_all, down_weight, ffn_gain],
            *[query, key, value],
            *made,
            *hidden_own,
        )
        back_kernel(
            *[own_in, own_grad, act_own, middle_own, attn_norm, ffn_gain],
            *[out_all, cat_all, grad_all, first, hidden_all, wide_low, down_part, slot_all],
            *came[8:13],
            *[came[7], query_norm, key_norm],
            *came[13:],
            *results,
            *refs,
        )
        sent()

    scratch = [pltpu.VMEM(out.shape, out.dtype) for out in front_outs + hidden_outs]
    scratch += front_scratch + hidden_scratch + back_scratch
    return call_kernel(body, args, outs, scratch, 0)


def open_kernel(cols, head_dim, *refs):
    wide_got, head_got, block_given, in_given, out_given, down_given, gain_given = refs[:7]
    gate, up, query, key, value, block_out, in_grad, out, down = refs[7:16]
    attn_gain, ffn_gain, query_gain, key_gain = refs[16:]
    pairs = ((block_out, block_given), (in_grad, in_given), (out, out_given), (down, down_given))
    for target, source in pairs:
        target[...] = source[...]
    lanes = gain_given.shape[1] // 3
    for line in range(gain_given.shape[0]):
        for place, target in ((0, attn_gain), (1, ffn_gain)):
            target[:, line * lanes : (line + 1) * lanes] = gain_given[
                line : line + 1, place * lanes : (place + 1) * lanes
            ]
    query_gain[...] = gain_given[0:1, 2 * lanes : 2 * lanes + head_dim]
    key_gain[...] = gain_given[1:2, 2 * lanes : 2 * lanes + head_dim]
    height, part = wide_got.shape[3], wide_got.shape[4] // 2
    for col in range(cols):
        for piece in range(2):
            for side in range(2):
                begin = (2 * piece + side) * height
                lines = slice(begin, begin + height)
                lanes = slice(col * part, (col + 1) * part)
                gate[lines, lanes] = wide_got[side, col, piece, :, :part].astype(jnp.float32)
                up[lines, lanes] = wide_got[side, col, piece, :, part:].astype(jnp.float32)
    turned = []
    for col in range(cols):
        stacked = head_got[col].reshape(3 * head_dim, head_got.shape[3]).astype(jnp.float32)
        turned.append(
            [stacked[kind * head_dim : (kind + 1) * head_dim].T for kind in range(3)]
        )
        query[:, col * head_dim : (col + 1) * head_dim] = turned[col][0]
    for pair in range(cols // 2):
        for place, target in ((1, key), (2, value)):
            target[:, pair * head_dim : (pair + 1) * head_dim] = (
                turned[2 * pair][place] + turned[2 * pair + 1][place]
            )


def call_kernel(body, args, outs, scratch, number):
    vmem = pl.BlockSpec(memory_space=pltpu.VMEM)
    return pl.pallas_call(
        body,
        out_shape=outs,
        in_specs=[vmem] * len(args),
        out_specs=[vmem] * len(outs),
        scratch_shapes=scratch,
        compiler_params=pltpu.CompilerParams(
            collective_id=number, has_side_effects=True, vmem_limit_bytes=VMEM_LIMIT
        ),
    )(*args)


def dma(*shape):
    return [pltpu.SemaphoreType.DMA(shape), pltpu.SemaphoreType.DMA(shape)]


def dot(left, right, left_dim=1, right_dim=0):
    return lax.dot_general(
        left,
        right,
        (((left_dim,), (right_dim,)), ((), ())),
        preferred_element_type=jnp.float32,
    )


def shards(
    block_input,
    seq_lengths,
    out_grad,
    attn_norm,
    query_weight,
    key_weight,
    value_weight,
    query_norm,
    key_norm,
    out_weight,
    ffn_norm,
    gate_weight,
    up_weight,
    down_weight,
):
    width = block_input.shape[1]
    head_dim = query_norm.shape[0]
    cols = lax.axis_size("col")
    given = [block_input, out_grad, out_weight, query_weight, key_weight, value_weight]
    given += [gate_weight, up_weight, (attn_norm, query_norm, key_norm), seq_lengths]
    outs = whole_pass(given, down_weight, ffn_norm, head_dim)
    block_output, input_grad, wide_got, head_got, out_sum, grad_down, gain_sums = outs
    shape = jax.ShapeDtypeStruct
    weights = (gate_weight, up_weight, query_weight, key_weight, value_weight)
    given = (block_output, input_grad, out_sum.reshape(out_weight.shape), grad_down)
    gains = (width, width, head_dim, head_dim)
    results = local_kernel(
        functools.partial(open_kernel, cols, head_dim),
        [wide_got, head_got] + list(given) + [gain_sums],
        [shape(weight.shape, jnp.float32) for weight in weights]
        + [shape(value.shape, value.dtype) for value in given]
        + [shape((1, size), jnp.float32) for size in gains],
    )
    block_output, input_grad = results[5:7]
    sums = tuple(results[:5]) + tuple(results[7:])
    if lax.axis_size("dp") > 2:
        sums = lax.psum(tuple(0.5 * value for value in sums), "dp")
    grad_gate, grad_up, grad_query, grad_key, grad_value = sums[:5]
    grad_outweight, grad_down, grad_attnnorm, grad_ffnnorm, grad_qnorm, grad_knorm = sums[5:]
    return (
        block_output,
        input_grad,
        grad_attnnorm[0],
        grad_query,
        grad_key,
        grad_value,
        grad_qnorm[0],
        grad_knorm[0],
        grad_outweight,
        grad_ffnnorm[0],
        grad_gate,
        grad_up,
        grad_down,
    )


def solution(mesh):
    placed = (
        P(("dp", "row", "col"), None),
        P("dp", None),
        P(("dp", "row", "col"), None),
        P(),
        P("col", "row"),
        P("col", "row"),
        P("col", "row"),
        P(),
        P(),
        P(("row", "col"), None),
        P(),
        P("col", "row"),
        P("col", "row"),
        P(("row", "col"), None),
    )
    return jax.shard_map(
        shards,
        mesh=mesh,
        in_specs=placed,
        out_specs=(
            P(("dp", "row", "col"), None),
            P(("dp", "row", "col"), None),
            P(),
            P("col", "row"),
            P("col", "row"),
            P("col", "row"),
            P(),
            P(),
            P(("row", "col"), None),
            P(),
            P("col", "row"),
            P("col", "row"),
            P(("row", "col"), None),
        ),
        check_vma=False,
    )
```
